32 devices in a mesh: frame: 16 (over z, y, x), row: 2 (over core).
Axes of the slice: x: 2, y: 2, z: 4, core: 2. Of those that a mesh axis runs over, the one named last changes fastest.
Arguments:
- tokens: bfloat16 [16, 2, 128, 2048], P('frame', 'row'), may hold values from -6 to 6
- cotangent: bfloat16 [16, 2, 128, 2048], P('frame', 'row'), may hold values from -6 to 6
- timestep: int32 [1], replicated, may hold values from 0 to 999
- mod_weight: bfloat16 [256, 4096], P(None, 'frame'), may hold values from -0.375 to 0.375
- proj_weight: bfloat16 [2048, 256], P('frame'), may hold values from -0.125 to 0.125
- step_weight: bfloat16 [2048, 32], P('frame'), may hold values from -0.125 to 0.125
- step_bias: float32 [32], replicated, may hold values from -1 to 1
- rate_space: float32 [32], replicated, may hold values from 0.001171875 to 0.05
- rate_time: float32 [32], replicated, may hold values from 0.01875 to 1
- skip_gain: float32 [32], replicated, may hold values from 0.5 to 1.5
Outputs:
- mixed: bfloat16 [16, 2, 128, 2048], P('frame', 'row')
- d_tokens: bfloat16 [16, 2, 128, 2048], P('frame', 'row')
- grad_proj: float32 [2048, 256], P('frame')
- grad_step: float32 [2048, 32], P('frame')
- grad_mod: float32 [256, 4096], P(None, 'frame')
The draws below stay inside these ranges and needn't reach their ends.
All inputs are finite; a program needn't handle non-finite values.
Results may differ from the reference program's by a relative error of at most 0.015.
Values may be sent and summed in bfloat16 or wider, within the bound.
No kernel may reach another device: no remote copies, remote signals or barrier semaphores. Data moves between devices by JAX's collectives and lax.ppermute only.
A program may use at most 64 MiB of HBM per device.

```python
import math
import jax
import jax.numpy as jnp
from jax import lax

HEADS = 32
HEAD_DIM = 64
WIDTH = 2048
STATE = 128
EMBED = 256
CLIP_LEN = 16
COLS = 128
ROWS_DEV = 1
LATENT_ROWS = 2
FRAMES = 16
CLIPS = 1
TOKENS = 4096


def steps_of(own_key, extent, cuts, smallest, high):
    gain = 1.0
    for dim, shards_of in cuts:
        draws = jax.random.uniform(jax.random.fold_in(jax.random.fold_in(own_key, 6), dim), (shards_of,), jnp.float32, smallest / len(cuts), high / len(cuts))
        gain = gain * jnp.repeat(jnp.exp(draws), extent[dim] // shards_of).reshape((-1,) + (1,) * (len(extent) - 1 - dim))
    return gain


def gaussian(stream_key, extent, scale, limit, cuts=(), kind=jnp.bfloat16):
    values = jax.random.normal(stream_key, extent, jnp.float32) * scale
    if len(cuts) > 0:
        values = steps_of(stream_key, extent, cuts, -0.22, 0.18) * values
    return jnp.clip(values, min=-limit, max=limit).astype(kind)


def setup_inputs(seed: int = 0) -> dict:
    keys = jax.random.split(jax.random.key(seed), 11)
    return {
        "tokens": gaussian(keys[0], (FRAMES, LATENT_ROWS, COLS, WIDTH), 1.0, 6.0, ((0, 16), (1, 2))),
        "cotangent": gaussian(keys[1], (FRAMES, LATENT_ROWS, COLS, WIDTH), 1.0, 6.0, ((0, 16), (1, 2))),
        "timestep": jax.random.randint(keys[2], (CLIPS,), 0, 1000).astype(jnp.int32),
        "mod_weight": gaussian(keys[3], (EMBED, 2 * WIDTH), EMBED ** -0.5, 0.375, ((1, 16),)),
        "proj_weight": gaussian(keys[4], (WIDTH, 2 * STATE), WIDTH ** -0.5, 0.125, ((0, 16),)),
        "step_weight": gaussian(keys[5], (WIDTH, HEADS), WIDTH ** -0.5, 0.125, ((0, 16),)),
        "step_bias": jnp.clip(jax.random.uniform(keys[6], (HEADS,), jnp.float32, -1.0, 1.0), -1.0, 1.0),
        "rate_space": jnp.clip(jnp.exp(jax.random.uniform(keys[7], (HEADS,), jnp.float32, math.log(0.001171875), math.log(0.05))), 0.001171875, 0.05),
        "rate_time": jnp.clip(jnp.exp(jax.random.uniform(keys[8], (HEADS,), jnp.float32, math.log(0.01875), math.log(1.0))), 0.01875, 1.0),
        "skip_gain": jnp.clip(jax.random.uniform(keys[9], (HEADS,), jnp.float32, 0.5, 1.5), 0.5, 1.5),
    }


norm_eps = 1e-05

def time_embed(timestep, embed_dim):
    half_dim = embed_dim // 2
    frequency = jnp.exp(-math.log(10000.0) * jnp.arange(half_dim, dtype=jnp.float32) / half_dim)
    angles = timestep.astype(jnp.float32)[:, None] * frequency[None, :]
    return jax.nn.silu(jnp.concatenate([jnp.cos(angles), jnp.sin(angles)], axis=1))

def normalize(values):
    return values * lax.rsqrt(lax.optimization_barrier(jnp.mean(values * values, axis=-1, keepdims=True)) + norm_eps)

def block_parts(normed, coeffs, logits, step_bias, decay_rate, need_end):
    seq_count, length, feat_width = normed.shape
    head_count = decay_rate.shape[0]
    inputs = normed.reshape(seq_count, length, head_count, feat_width // head_count)
    state_size = coeffs.shape[-1] // 2
    b_part = coeffs[..., :state_size]
    c_part = coeffs[..., state_size:]
    step_size = jax.nn.softplus(logits.astype(jnp.float32) + step_bias)
    cum_log = jnp.cumsum(-step_size * decay_rate, axis=1)
    scores = jnp.einsum('stn,sun->stu', c_part, b_part, preferred_element_type=jnp.float32) / state_size
    lag_rows = jnp.swapaxes(cum_log, 1, 2)
    causal = jnp.tril(jnp.ones((length, length), dtype=bool))
    differences = lag_rows[:, :, :, None] - lag_rows[:, :, None, :]
    decays = jnp.where(causal, jnp.exp(jnp.where(causal, differences, 0.0)), 0.0)
    spread = jnp.swapaxes(step_size, 1, 2)
    weights = (scores[:, None, :, :] * decays * spread[:, :, None, :]).astype(jnp.bfloat16)
    inner_out = jnp.einsum('shtu,suhp->sthp', weights, inputs, preferred_element_type=jnp.float32)
    inner_out = inner_out.reshape(seq_count, length, feat_width)
    if need_end:
        end_log = cum_log[:, -1:, :]
        lead_decay = jnp.exp(end_log - cum_log) * step_size
        scaled = (inputs.astype(jnp.float32) * lead_decay[..., None]).astype(jnp.bfloat16)
        end_local = jnp.einsum('sthp,stn->shpn', scaled, b_part, preferred_element_type=jnp.float32)
    else:
        end_local = jnp.zeros((seq_count, head_count, feat_width // head_count, state_size), jnp.float32)
    return (inner_out, end_local, cum_log, c_part)

def carry_term(cum_log, c_part, state_in):
    seq_count, length, head_count = cum_log.shape
    state_size = c_part.shape[-1]
    reached = jnp.einsum('stn,shpn->sthp', c_part.astype(jnp.float32), state_in, precision=lax.Precision.HIGHEST)
    return (reached * jnp.exp(cum_log)[..., None] / state_size).reshape(seq_count, length, -1)

def reference(tokens, cotangent, timestep, mod_weight, proj_weight, step_weight, step_bias, rate_space, rate_time, skip_gain):
    site_total = LATENT_ROWS * COLS
    band_len = ROWS_DEV * COLS
    band_count = LATENT_ROWS // ROWS_DEV
    activated = time_embed(timestep, EMBED).astype(jnp.bfloat16)
    modulation = jnp.dot(activated, mod_weight, preferred_element_type=jnp.float32)
    shift_vec = modulation[:, :WIDTH][:, None, :]
    scale_vec = modulation[:, WIDTH:][:, None, :]
    tokens_wide = tokens.reshape(CLIPS, CLIP_LEN * site_total, WIDTH).astype(jnp.float32)
    unit_rows = normalize(tokens_wide)
    normed = (unit_rows * (1.0 + scale_vec) + shift_vec).astype(jnp.bfloat16).reshape(-1, WIDTH)
    projected = jnp.dot(normed, proj_weight, preferred_element_type=jnp.float32).astype(jnp.bfloat16)
    logits = jnp.dot(normed, step_weight, preferred_element_type=jnp.float32).astype(jnp.bfloat16)
    skip_full = jnp.repeat(skip_gain, HEAD_DIM)

    def space_frame(pieces):

        def one_band(state_in, band_in):
            inner_out, end_local, cum_log, c_part = block_parts(band_in[0], band_in[1], band_in[2], step_bias, rate_space, True)
            output = inner_out + carry_term(cum_log, c_part, state_in)
            state_out = jnp.exp(cum_log[:, -1, :])[:, :, None, None] * state_in + end_local
            return (state_out, output)
        banded = tuple((member.reshape(band_count, 1, band_len, member.shape[-1]) for member in pieces))
        initial = jnp.zeros((1, HEADS, HEAD_DIM, STATE), jnp.float32)
        unused, outputs = lax.scan(one_band, initial, banded)
        return outputs.reshape(site_total, WIDTH)

    def time_rows(pieces):
        sequences = tuple((jnp.swapaxes(member, 0, 1) for member in pieces))
        inner_out = block_parts(sequences[0], sequences[1], sequences[2], step_bias, rate_time, False)[0]
        return jnp.swapaxes(inner_out.astype(jnp.bfloat16), 0, 1)

    def core(normed_s, proj_s, logit_s, normed_t, proj_t, logit_t):
        frame_view = tuple((member.reshape(FRAMES, site_total, member.shape[-1]) for member in (normed_s, proj_s, logit_s)))
        space_out = lax.map(jax.checkpoint(space_frame), frame_view).reshape(-1, WIDTH)
        row_view = tuple((member.reshape(FRAMES, LATENT_ROWS, COLS, member.shape[-1]).transpose(1, 0, 2, 3) for member in (normed_t, proj_t, logit_t)))
        time_out = lax.map(jax.checkpoint(time_rows), row_view)
        time_out = time_out.transpose(1, 0, 2, 3).reshape(-1, WIDTH)
        return space_out + time_out.astype(jnp.float32) + skip_full * normed_s.astype(jnp.float32)
    output, core_pull = jax.vjp(core, normed, projected, logits, normed, projected, logits)
    mixed = output.astype(jnp.bfloat16).reshape(tokens.shape)
    grads = core_pull(cotangent.reshape(-1, WIDTH).astype(jnp.float32))
    space_dnorm, space_dproj, space_dlogit, time_dnorm, time_dproj, time_dlogit = grads
    time_back = (time_dnorm.astype(jnp.float32) + jnp.dot(time_dproj, proj_weight.T, preferred_element_type=jnp.float32) + jnp.dot(time_dlogit, step_weight.T, preferred_element_type=jnp.float32)).astype(jnp.bfloat16)
    pre_grad = space_dnorm.astype(jnp.float32) + jnp.dot(space_dproj, proj_weight.T, preferred_element_type=jnp.float32) + jnp.dot(space_dlogit, step_weight.T, preferred_element_type=jnp.float32) + time_back.astype(jnp.float32)
    factor = TOKENS ** (-0.5)
    grad_proj = (jnp.dot(normed.T, space_dproj, preferred_element_type=jnp.float32) + jnp.dot(normed.T, time_dproj, preferred_element_type=jnp.float32)) * factor
    grad_step = (jnp.dot(normed.T, space_dlogit, preferred_element_type=jnp.float32) + jnp.dot(normed.T, time_dlogit, preferred_element_type=jnp.float32)) * factor
    pre_clip = pre_grad.reshape(CLIPS, -1, WIDTH)
    shift_grad = lax.optimization_barrier(jnp.sum(pre_clip, axis=1))
    scale_grad = lax.optimization_barrier(jnp.sum(pre_clip * unit_rows, axis=1))
    mod_grad = jnp.concatenate([shift_grad, scale_grad], axis=1)
    grad_mod = jnp.dot(activated.astype(jnp.float32).T, mod_grad, precision=lax.Precision.HIGHEST) * factor
    unused, norm_pull = jax.vjp(normalize, tokens_wide)
    tokens_grad, = norm_pull(pre_clip * (1.0 + scale_vec))
    d_tokens = tokens_grad.astype(jnp.bfloat16).reshape(tokens.shape)
    return (mixed, d_tokens, grad_proj, grad_step, grad_mod)
```

```python
import functools
import math

import jax
import jax.numpy as jnp
from jax import lax
from jax.experimental import pallas as pl
from jax.experimental.pallas import tpu as pltpu
from jax.sharding import PartitionSpec as P

norm_eps = 1e-05
LANES = 128
f32 = jnp.float32
bf16 = jnp.bfloat16
EXACT = lax.Precision.HIGHEST


def time_embed(timestep, embed_dim):
    half_dim = embed_dim // 2
    frequency = jnp.exp(-math.log(10000.0) * jnp.arange(half_dim, dtype=f32) / half_dim)
    angles = timestep.astype(f32)[:, None] * frequency[None, :]
    return jax.nn.silu(jnp.concatenate([jnp.cos(angles), jnp.sin(angles)], axis=1))


def to_tiles(a):
    f, r, c = a.shape
    if r % 8 == 0 and c % LANES == 0:
        a = a.reshape(f, r // 8, 8, c // LANES, LANES).transpose(0, 1, 3, 2, 4)
    return a.reshape(f, r * c // LANES, LANES)


def from_tiles(a, r, c):
    f = a.shape[0]
    if r % 8 == 0 and c % LANES == 0:
        a = a.reshape(f, r // 8, c // LANES, 8, LANES).transpose(0, 1, 3, 2, 4)
    return a.reshape(f, r, c)


def exchange(packed):
    return lax.all_to_all(packed, "frame", split_axis=0, concat_axis=0, tiled=True)


def mm(a, b, ca, cb):
    return lax.dot_general(a, b, (((ca,), (cb,)), ((), ())), preferred_element_type=f32)


def exact(a, b, ca, cb):
    return lax.dot_general(
        a, b, (((ca,), (cb,)), ((), ())), preferred_element_type=f32, precision=EXACT
    )


def split(a):
    high = a.astype(bf16)
    return high, (a - high.astype(f32)).astype(bf16)


def head_map(heads, width):
    size = width // heads
    own = lax.broadcasted_iota(jnp.int32, (heads, width), 0)
    lane = lax.broadcasted_iota(jnp.int32, (heads, width), 1)
    return jnp.where(lane // size == own, 1.0, 0.0).astype(bf16)


def sequence_mask(length, sites):
    later = lax.broadcasted_iota(jnp.int32, (length, length), 0)
    earlier = lax.broadcasted_iota(jnp.int32, (length, length), 1)
    keep = later >= earlier
    if sites > 1:
        keep = keep & (later % sites == earlier % sites)
    return jnp.where(keep, 1.0, 0.0).astype(f32)


def blocks(width):
    return [(j, slice(j * LANES, (j + 1) * LANES)) for j in range(width // LANES)]


def spread_rows(rows, length):
    count = rows.shape[0]
    if count == 1:
        return rows
    part = (length // count, rows.shape[1])
    return jnp.concatenate([jnp.broadcast_to(rows[c : c + 1], part) for c in range(count)], axis=0)


def normalize_into(tok_ref, shift_ref, gain_ref, x_ref):
    length, width = tok_ref.shape
    total = jnp.zeros((length, LANES), f32)
    for _, sl in blocks(width):
        v = tok_ref[:, sl].astype(f32)
        total = total + v * v
    mean = jnp.sum(total, axis=1, keepdims=True) / width
    inverse = lax.rsqrt(mean + norm_eps)
    for _, sl in blocks(width):
        unit = tok_ref[:, sl].astype(f32) * inverse
        gain = spread_rows(gain_ref[:, sl], length)
        shift = spread_rows(shift_ref[:, sl], length)
        x_ref[:, sl] = (unit * (1.0 + gain) + shift).astype(bf16)
    return inverse


def steps_of(logits, bias, rate, mask):
    z = logits.astype(f32) + bias
    step = jnp.maximum(z, 0.0) + jnp.log1p(jnp.exp(-jnp.abs(z)))
    log_decay = -step * rate
    cum = exact(mask, log_decay, 1, 0)
    cum_rows = exact(log_decay, mask, 0, 1)
    return z, step, cum, cum_rows


def expand(parts, lanes_of):
    return mm(parts[0], lanes_of, 1, 0) + mm(parts[1], lanes_of, 1, 0)


def scan_block(j, x, grad, step_wide, scores, cum, cum_rows, heads, width, d_scores):
    size = width // heads
    per_block = LANES // size
    stepped = (x.astype(f32) * step_wide).astype(bf16)
    lane = lax.broadcasted_iota(jnp.int32, x.shape, 1)
    weights, steppeds, grads = [], [], []
    for i in range(per_block):
        h = j * per_block + i
        decay = jnp.exp(jnp.minimum(cum[:, h : h + 1] - cum_rows[h : h + 1, :], 0.0))
        inside = lane // size == i
        own_grad = jnp.where(inside, grad, jnp.zeros_like(grad))
        d_weight = mm(own_grad, stepped, 1, 1)
        d_scores = d_scores + d_weight * decay
        weights.append((scores * decay).astype(bf16))
        steppeds.append(jnp.where(inside, stepped, jnp.zeros_like(stepped)))
        grads.append(own_grad)
    out = mm(jnp.concatenate(weights, axis=1), jnp.concatenate(steppeds, axis=0), 1, 0)
    d_stepped = mm(jnp.concatenate(weights, axis=0), jnp.concatenate(grads, axis=0), 0, 0)
    return stepped, out, d_stepped, d_scores


def head_sums(high_ref, low_ref, lanes_of):
    return mm(high_ref[...], lanes_of, 1, 1) + mm(low_ref[...], lanes_of, 1, 1)


def put(refs, sl, value):
    high, low = split(value)
    refs[0][:, sl] = high
    refs[1][:, sl] = low


def site_kernel(
    sites,
    tok_ref,
    grad_ref,
    shift_ref,
    gain_ref,
    proj_ref,
    step_ref,
    bias_ref,
    rate_ref,
    out_ref,
    back_ref,
    gproj_ref,
    gstep_ref,
    gmod_ref,
    x_ref,
    dn_ref,
    a_hi,
    a_lo,
    b_hi,
    b_lo,
):
    length, width = tok_ref.shape
    heads = step_ref.shape[0]
    state = proj_ref.shape[1] // 2
    clips = shift_ref.shape[0]
    inverse = normalize_into(tok_ref, shift_ref, gain_ref, x_ref)
    lanes_of = head_map(heads, width)
    mask = sequence_mask(length, sites)
    coeffs = mm(x_ref[...], proj_ref[...], 1, 0).astype(bf16)
    logits = mm(x_ref[...], step_ref[...], 1, 1).astype(bf16)
    rate = rate_ref[...]
    z, step, cum, cum_rows = steps_of(logits, bias_ref[...], rate, mask)
    b_part, c_part = coeffs[:, :state], coeffs[:, state:]
    scores = mm(c_part, b_part, 1, 1) * (mask / state)
    step_parts = split(step)
    d_scores = jnp.zeros((length, length), f32)
    for j, sl in blocks(width):
        x, grad = x_ref[:, sl], grad_ref[:, sl]
        step_wide = expand(step_parts, lanes_of[:, sl])
        stepped, out, d_stepped, d_scores = scan_block(
            j, x, grad, step_wide, scores, cum, cum_rows, heads, width, d_scores
        )
        out_ref[:, sl] = out.astype(bf16)
        dn_ref[:, sl] = (step_wide * d_stepped).astype(bf16)
        put((a_hi, a_lo), sl, grad.astype(f32) * out - stepped.astype(f32) * d_stepped)
        put((b_hi, b_lo), sl, x.astype(f32) * d_stepped)
    d_cum = head_sums(a_hi, a_lo, lanes_of)
    d_step = head_sums(b_hi, b_lo, lanes_of)
    d_log = exact(mask, d_cum, 0, 0)
    d_logits = (jax.nn.sigmoid(z) * (d_step - rate * d_log)).astype(bf16)
    d_scores = (d_scores * (mask / state)).astype(bf16)
    d_coeffs = jnp.concatenate(
        [mm(d_scores, c_part, 0, 0), mm(d_scores, b_part, 1, 0)], axis=1
    ).astype(bf16)
    for _, sl in blocks(width):
        back = (
            dn_ref[:, sl].astype(f32)
            + mm(d_coeffs, proj_ref[sl, :], 1, 1)
            + mm(d_logits, step_ref[:, sl], 1, 0)
        ).astype(bf16)
        back_ref[:, sl] = back
        back = back.astype(f32)
        scaled = back * (tok_ref[:, sl].astype(f32) * inverse)
        for c in range(clips):
            rows = slice(c * (length // clips), (c + 1) * (length // clips))
            gmod_ref[c : c + 1, sl] = jnp.sum(back[rows], axis=0, keepdims=True)
            gmod_ref[clips + c : clips + c + 1, sl] = jnp.sum(scaled[rows], axis=0, keepdims=True)
        gproj_ref[sl, :] = mm(x_ref[:, sl], d_coeffs, 0, 0)
        gstep_ref[:, sl] = mm(d_logits, x_ref[:, sl], 0, 0)


def band_kernel(
    tok_ref,
    grad_ref,
    shift_ref,
    gain_ref,
    proj_ref,
    step_ref,
    bias_ref,
    rate_ref,
    x_ref,
    coeffs_ref,
    logits_ref,
    inverse_ref,
    decay_ref,
    end_ref,
    own_ref,
):
    length, width = tok_ref.shape
    heads = step_ref.shape[0]
    state = proj_ref.shape[1] // 2
    inverse_ref[...] = normalize_into(tok_ref, shift_ref, gain_ref, x_ref)
    lanes_of = head_map(heads, width)
    mask = sequence_mask(length, 1)
    coeffs = mm(x_ref[...], proj_ref[...], 1, 0).astype(bf16)
    logits = mm(x_ref[...], step_ref[...], 1, 1).astype(bf16)
    coeffs_ref[...] = coeffs
    logits_ref[...] = logits
    _, step, cum, _ = steps_of(logits, bias_ref[...], rate_ref[...], mask)
    last = cum[length - 1 : length, :]
    decay_ref[...] = jnp.exp(last)
    lead = split(jnp.exp(last - cum) * step)
    reach = split(jnp.exp(cum) / state)
    b_part, c_part = coeffs[:, :state], coeffs[:, state:]
    for _, sl in blocks(width):
        lead_wide = expand(lead, lanes_of[:, sl])
        reach_wide = expand(reach, lanes_of[:, sl])
        scaled = (x_ref[:, sl].astype(f32) * lead_wide).astype(bf16)
        faded = (grad_ref[:, sl].astype(f32) * reach_wide).astype(bf16)
        end_ref[sl, :] = mm(scaled, b_part, 0, 0).astype(bf16)
        own_ref[sl, :] = mm(faded, c_part, 0, 0).astype(bf16)


def space_kernel(
    tok_ref,
    grad_ref,
    x_ref,
    coeffs_ref,
    logits_ref,
    inverse_ref,
    proj_ref,
    step_ref,
    bias_ref,
    rate_ref,
    skip_ref,
    state_ref,
    later_ref,
    gproj_in,
    gstep_in,
    mix_ref,
    pre_ref,
    gproj_ref,
    gstep_ref,
    gmod_ref,
    dn_ref,
    a_hi,
    a_lo,
    b_hi,
    b_lo,
    c_hi,
    c_lo,
):
    length, width = tok_ref.shape
    heads = step_ref.shape[0]
    state = proj_ref.shape[1] // 2
    lanes_of = head_map(heads, width)
    mask = sequence_mask(length, 1)
    coeffs = coeffs_ref[...]
    rate = rate_ref[...]
    z, step, cum, cum_rows = steps_of(logits_ref[...], bias_ref[...], rate, mask)
    last = cum[length - 1 : length, :]
    rest = jnp.exp(last - cum)
    lead = rest * step
    b_part, c_part = coeffs[:, :state], coeffs[:, state:]
    scores = mm(c_part, b_part, 1, 1) * (mask / state)
    step_parts, lead_parts, reach_parts = split(step), split(lead), split(jnp.exp(cum) / state)
    d_scores = jnp.zeros((length, length), f32)
    d_b = jnp.zeros((length, state), f32)
    d_c = jnp.zeros((length, state), f32)
    d_end = jnp.zeros((heads, state), f32)
    for j, sl in blocks(width):
        x, grad = x_ref[:, sl], grad_ref[:, sl]
        wide_map = lanes_of[:, sl]
        step_wide = expand(step_parts, wide_map)
        lead_wide = expand(lead_parts, wide_map)
        reach_wide = expand(reach_parts, wide_map)
        stepped, out, d_stepped, d_scores = scan_block(
            j, x, grad, step_wide, scores, cum, cum_rows, heads, width, d_scores
        )
        x, wide = x.astype(f32), grad.astype(f32)
        before, later = state_ref[sl, :], later_ref[sl, :]
        carried = mm(c_part, before, 1, 1) * reach_wide
        d_c = d_c + mm((wide * reach_wide).astype(bf16), before, 1, 0)
        d_b = d_b + mm((x * lead_wide).astype(bf16), later, 1, 0)
        d_scaled = mm(b_part, later, 1, 1)
        both = split(before.astype(f32) * later.astype(f32))
        d_end = d_end + mm(wide_map, both[0], 1, 0) + mm(wide_map, both[1], 1, 0)
        total = out + carried
        skip = skip_ref[:, sl]
        mix_ref[:, sl] = total + skip * x
        d_x = (step_wide * d_stepped + d_scaled * lead_wide).astype(bf16)
        dn_ref[:, sl] = d_x + (wide * skip).astype(bf16)
        put((a_hi, a_lo), sl, wide * total - stepped.astype(f32) * d_stepped)
        put((b_hi, b_lo), sl, x * d_stepped)
        put((c_hi, c_lo), sl, x * d_scaled)
    d_lead = head_sums(c_hi, c_lo, lanes_of)
    d_step = head_sums(b_hi, b_lo, lanes_of) + d_lead * rest
    fall = d_lead * lead
    d_cum = head_sums(a_hi, a_lo, lanes_of) - fall
    ones = jnp.ones((8, state), f32)
    end_sum = exact(ones, d_end, 1, 1)[0:1, :] * jnp.exp(last)
    end_sum = end_sum + jnp.sum(fall, axis=0, keepdims=True)
    d_log = exact(mask, d_cum, 0, 0) + end_sum
    d_logits = (jax.nn.sigmoid(z) * (d_step - rate * d_log)).astype(bf16)
    d_scores = (d_scores * (mask / state)).astype(bf16)
    d_coeffs = jnp.concatenate(
        [mm(d_scores, c_part, 0, 0) + d_b, mm(d_scores, b_part, 1, 0) + d_c], axis=1
    ).astype(bf16)
    inverse = inverse_ref[...]
    for _, sl in blocks(width):
        pre = (
            dn_ref[:, sl].astype(f32)
            + mm(d_coeffs, proj_ref[sl, :], 1, 1)
            + mm(d_logits, step_ref[:, sl], 1, 0)
        )
        pre_ref[:, sl] = pre
        scaled = pre * (tok_ref[:, sl].astype(f32) * inverse)
        gmod_ref[0:1, sl] = jnp.sum(pre, axis=0, keepdims=True)
        gmod_ref[1:2, sl] = jnp.sum(scaled, axis=0, keepdims=True)
        gproj_ref[sl, :] = (gproj_in[sl, :] + mm(x_ref[:, sl], d_coeffs, 0, 0)).astype(bf16)
        gstep_ref[:, sl] = (gstep_in[:, sl] + mm(d_logits, x_ref[:, sl], 0, 0)).astype(bf16)


def last_kernel(tok_ref, inverse_ref, gain_ref, mix_ref, pre_ref, time_ref, back_ref, out_ref, dtok_ref):
    length, width = tok_ref.shape
    inverse = inverse_ref[...]
    total = jnp.zeros((length, LANES), f32)
    for _, sl in blocks(width):
        out_ref[:, sl] = (mix_ref[:, sl] + time_ref[:, sl].astype(f32)).astype(bf16)
        grad = (pre_ref[:, sl] + back_ref[:, sl].astype(f32)) * (1.0 + gain_ref[:, sl])
        total = total + grad * tok_ref[:, sl].astype(f32)
    inner = jnp.sum(total, axis=1, keepdims=True) / width
    inner = inner * inverse * inverse * inverse
    for _, sl in blocks(width):
        grad = (pre_ref[:, sl] + back_ref[:, sl].astype(f32)) * (1.0 + gain_ref[:, sl])
        dtok_ref[:, sl] = (grad * inverse - tok_ref[:, sl].astype(f32) * inner).astype(bf16)


def call(kernel, outs, scratch=(), name=None):
    shapes = [jax.ShapeDtypeStruct(s, d) for s, d in outs]
    return pl.pallas_call(
        kernel,
        out_shape=shapes,
        scratch_shapes=[pltpu.VMEM(s, d) for s, d in scratch],
        compiler_params=pltpu.CompilerParams(vmem_limit_bytes=48 << 20),
        name=name,
    )


def rows_in_order(part):
    if lax.axis_size("row") != 2:
        return lax.all_gather(part, "row")
    other = lax.ppermute(part, "row", [(0, 1), (1, 0)])
    first = lax.axis_index("row") == 0
    return jnp.stack([jnp.where(first, part, other), jnp.where(first, other, part)])


def rows_sum(part):
    if lax.axis_size("row") != 2:
        return lax.psum(part, "row")
    return part + lax.ppermute(part, "row", [(0, 1), (1, 0)])


def chain(own, decay, forward):
    count = lax.axis_size("row")
    hops = [(i, i + 1) if forward else (i + 1, i) for i in range(count - 1)]
    if count == 1:
        return jnp.zeros_like(own)
    arrived = lax.ppermute(own, "row", hops)
    wide = jnp.repeat(decay[0], own.shape[0] // decay.shape[1])[:, None]
    for _ in range(count - 2):
        passed = wide * arrived.astype(f32) + own.astype(f32)
        arrived = lax.ppermute(passed.astype(bf16), "row", hops)
    return arrived


def per_device(
    tokens,
    cotangent,
    timestep,
    mod_weight,
    proj_weight,
    step_weight,
    step_bias,
    rate_space,
    rate_time,
    skip_gain,
):
    frames = lax.axis_size("frame")
    rows = lax.axis_size("row")
    frame_id = lax.axis_index("frame")
    row_id = lax.axis_index("row")
    width = tokens.shape[-1]
    length = tokens.shape[1] * tokens.shape[2]
    clips = timestep.shape[0]
    clip_id = frame_id // (frames // clips)
    sites = length // frames
    heads = rate_space.shape[0]
    depth, pair = proj_weight.shape
    state = pair // 2
    mod_cols = mod_weight.shape[1]
    factor = (frames * rows * length) ** (-0.5)
    tok = tokens.reshape(length, width)
    grad = cotangent.reshape(length, width)

    activated = time_embed(timestep, mod_weight.shape[0]).astype(bf16)
    own_mod = jnp.dot(activated, mod_weight, preferred_element_type=f32)
    high = lax.reduce_precision(own_mod, 8, 7)
    own_mod = jnp.stack([high, own_mod - high]).astype(bf16)

    part = depth // rows
    own_proj = lax.dynamic_slice_in_dim(proj_weight, row_id * part, part, 0)
    to_all = [
        to_tiles(own_proj[None]),
        to_tiles(step_weight.T[None]),
        own_mod.reshape(1, -1, LANES),
    ]
    to_all = jnp.concatenate(to_all, axis=1)
    to_all = jnp.pad(to_all, ((0, 0), (0, -to_all.shape[1] % 8), (0, 0)))
    count = sites * width // LANES
    got = exchange(
        jnp.concatenate(
            [
                to_tiles(tok.reshape(frames, sites, width)),
                to_tiles(grad.reshape(frames, sites, width)),
                jnp.broadcast_to(to_all, (frames,) + to_all.shape[1:]),
            ],
            axis=1,
        )
    )
    site_tok = from_tiles(got[:, :count], sites, width).reshape(length, width)
    site_grad = from_tiles(got[:, count : 2 * count], sites, width).reshape(length, width)
    at = 2 * count
    size = part * pair // LANES
    proj_full = rows_in_order(got[:, at : at + size])
    proj_full = from_tiles(proj_full.reshape(rows * frames, size, LANES), part, pair)
    proj_full = proj_full.reshape(rows, frames, part, pair).transpose(1, 0, 2, 3)
    proj_full = proj_full.reshape(width, pair)
    at += size
    size = heads * depth // LANES
    step_full = from_tiles(got[:, at : at + size], heads, depth)
    step_full = step_full.transpose(1, 0, 2).reshape(heads, width)
    at += size
    size = 2 * clips * mod_cols // LANES
    mod_full = got[:, at : at + size].reshape(frames, 2, clips, mod_cols).astype(f32)
    mod_full = (mod_full[:, 0] + mod_full[:, 1]).transpose(1, 0, 2).reshape(clips, 2 * width)
    shift, gain = mod_full[:, :width], mod_full[:, width:]

    bias = step_bias[None]
    wide = (length, width)
    site_out, site_back, gproj, gstep, site_gmod = call(
        functools.partial(site_kernel, sites),
        [(wide, bf16), (wide, bf16), ((width, pair), f32), ((heads, width), f32), ((2 * clips, width), f32)],
        [(wide, bf16)] * 6,
        name="site",
    )(site_tok, site_grad, shift, gain, proj_full, step_full, bias, rate_time[None])

    came = exchange(
        jnp.concatenate(
            [
                to_tiles(site_out.reshape(frames, sites, width)),
                to_tiles(site_back.reshape(frames, sites, width)),
            ],
            axis=1,
        )
    )
    time_out = from_tiles(came[:, :count], sites, width).reshape(length, width)
    time_back = from_tiles(came[:, count:], sites, width).reshape(length, width)

    own_shift = lax.dynamic_slice_in_dim(shift, clip_id, 1, 0)
    own_gain = lax.dynamic_slice_in_dim(gain, clip_id, 1, 0)
    normed, coeffs, logits, inverse, decay, end_own, start_grad = call(
        band_kernel,
        [
            (wide, bf16),
            ((length, pair), bf16),
            ((length, heads), bf16),
            ((length, 1), f32),
            ((1, heads), f32),
            ((width, state), bf16),
            ((width, state), bf16),
        ],
        name="band",
    )(tok, grad, own_shift, own_gain, proj_full, step_full, bias, rate_space[None])
    state_in = chain(end_own, decay, True)
    later_grad = chain(start_grad, decay, False)
    skip = jnp.repeat(skip_gain, width // heads)[None]
    mix, pre, gproj, gstep, gmod = call(
        space_kernel,
        [(wide, f32), (wide, f32), ((width, pair), bf16), ((heads, width), bf16), ((2, width), f32)],
        [(wide, bf16)] * 7,
        name="space",
    )(
        tok,
        grad,
        normed,
        coeffs,
        logits,
        inverse,
        proj_full,
        step_full,
        bias,
        rate_space[None],
        skip,
        state_in,
        later_grad,
        gproj,
        gstep,
    )

    picked = (jnp.arange(clips) == clip_id).astype(f32)[:, None]
    gmod = jnp.concatenate(
        [site_gmod[:clips] + picked * gmod[0:1], site_gmod[clips:] + picked * gmod[1:2]], axis=1
    )
    gmod = gmod.reshape(clips, frames, mod_cols).transpose(1, 0, 2).astype(bf16)
    sent = jnp.concatenate(
        [
            to_tiles(gproj.reshape(frames, depth, pair)),
            to_tiles(gstep.reshape(heads, frames, depth).transpose(1, 0, 2)),
            gmod.reshape(frames, -1, LANES) if (clips * mod_cols) % LANES == 0 else gmod,
        ],
        axis=1,
    )
    size = sent.shape[1]
    sent = jnp.pad(sent, ((0, 0), (0, -size % 8), (0, 0)))
    sums = jnp.sum(exchange(sent).astype(f32), axis=0, keepdims=True)
    sums = rows_sum(sums) * factor
    at = depth * pair // LANES
    grad_proj = from_tiles(sums[:, :at], depth, pair)[0]
    size = heads * depth // LANES
    grad_step = from_tiles(sums[:, at : at + size], heads, depth)[0].T
    at += size
    size = clips * mod_cols // LANES
    mod_sum = sums[0, at : at + size].reshape(clips, mod_cols)
    grad_mod = jnp.dot(activated.astype(f32).T, mod_sum, precision=EXACT)

    mixed, d_tokens = call(last_kernel, [(wide, bf16), (wide, bf16)], name="last")(
        tok, inverse, own_gain, mix, pre, time_out, time_back
    )
    return (mixed.reshape(tokens.shape), d_tokens.reshape(tokens.shape), grad_proj, grad_step, grad_mod)


def solution(mesh):
    placed = (
        P("frame", "row", None, None),
        P("frame", "row", None, None),
        P(),
        P(None, "frame"),
        P("frame", None),
        P("frame", None),
        P(),
        P(),
        P(),
        P(),
    )
    return jax.shard_map(
        per_device,
        mesh=mesh,
        in_specs=placed,
        out_specs=(
            P("frame", "row", None, None),
            P("frame", "row", None, None),
            P("frame", None),
            P("frame", None),
            P(None, "frame"),
        ),
        check_vma=False,
    )
```

```python
import functools
import math

import jax
import jax.numpy as jnp
from jax import lax
from jax.experimental import pallas as pl
from jax.experimental.pallas import tpu as pltpu
from jax.sharding import PartitionSpec as P

norm_eps = 1e-05
LANES = 128
f32 = jnp.float32
bf16 = jnp.bfloat16
EXACT = lax.Precision.HIGHEST


def time_embed(timestep, embed_dim):
    half_dim = embed_dim // 2
    frequency = jnp.exp(-math.log(10000.0) * jnp.arange(half_dim, dtype=f32) / half_dim)
    angles = timestep.astype(f32)[:, None] * frequency[None, :]
    return jax.nn.silu(jnp.concatenate([jnp.cos(angles), jnp.sin(angles)], axis=1))


def to_tiles(a):
    f, r, c = a.shape
    if r % 8 == 0 and c % LANES == 0:
        a = a.reshape(f, r // 8, 8, c // LANES, LANES).transpose(0, 1, 3, 2, 4)
    return a.reshape(f, r * c // LANES, LANES)


def from_tiles(a, r, c):
    f = a.shape[0]
    if r % 8 == 0 and c % LANES == 0:
        a = a.reshape(f, r // 8, c // LANES, 8, LANES).transpose(0, 1, 3, 2, 4)
    return a.reshape(f, r, c)


def exchange(packed):
    return lax.all_to_all(packed, "frame", split_axis=0, concat_axis=0, tiled=True)


def mm(a, b, ca, cb):
    return lax.dot_general(a, b, (((ca,), (cb,)), ((), ())), preferred_element_type=f32)


def exact(a, b, ca, cb):
    return lax.dot_general(
        a, b, (((ca,), (cb,)), ((), ())), preferred_element_type=f32, precision=EXACT
    )


def split(a):
    high = a.astype(bf16)
    return high, (a - high.astype(f32)).astype(bf16)


def head_map(heads, width):
    size = width // heads
    own = lax.broadcasted_iota(jnp.int32, (heads, width), 0)
    lane = lax.broadcasted_iota(jnp.int32, (heads, width), 1)
    return jnp.where(lane // size == own, 1.0, 0.0).astype(bf16)


def sequence_mask(length, sites):
    later = lax.broadcasted_iota(jnp.int32, (length, length), 0)
    earlier = lax.broadcasted_iota(jnp.int32, (length, length), 1)
    keep = later >= earlier
    if sites > 1:
        keep = keep & (later % sites == earlier % sites)
    return jnp.where(keep, 1.0, 0.0).astype(f32)


def blocks(width):
    return [(j, slice(j * LANES, (j + 1) * LANES)) for j in range(width // LANES)]


def spread_rows(rows, length):
    count = rows.shape[0]
    if count == 1:
        return rows
    part = (length // count, rows.shape[1])
    return jnp.concatenate([jnp.broadcast_to(rows[c : c + 1], part) for c in range(count)], axis=0)


def normalize_into(tok_ref, shift_ref, gain_ref, x_ref):
    length, width = tok_ref.shape
    total = jnp.zeros((length, LANES), f32)
    for _, sl in blocks(width):
        v = tok_ref[:, sl].astype(f32)
        total = total + v * v
    mean = jnp.sum(total, axis=1, keepdims=True) / width
    inverse = lax.rsqrt(mean + norm_eps)
    for _, sl in blocks(width):
        unit = tok_ref[:, sl].astype(f32) * inverse
        gain = spread_rows(gain_ref[:, sl], length)
        shift = spread_rows(shift_ref[:, sl], length)
        x_ref[:, sl] = (unit * (1.0 + gain) + shift).astype(bf16)
    return inverse


def steps_of(logits, bias, rate, mask):
    z = logits.astype(f32) + bias
    step = jnp.maximum(z, 0.0) + jnp.log1p(jnp.exp(-jnp.abs(z)))
    log_decay = -step * rate
    cum = exact(mask, log_decay, 1, 0)
    cum_rows = exact(log_decay, mask, 0, 1)
    return z, step, cum, cum_rows


def expand(parts, lanes_of):
    return mm(parts[0], lanes_of, 1, 0) + mm(parts[1], lanes_of, 1, 0)


def scan_block(j, x, grad, step_wide, scores, cum, cum_rows, heads, width, d_scores):
    size = width // heads
    per_block = LANES // size
    stepped = (x.astype(f32) * step_wide).astype(bf16)
    lane = lax.broadcasted_iota(jnp.int32, x.shape, 1)
    weights, steppeds, grads = [], [], []
    for i in range(per_block):
        h = j * per_block + i
        decay = jnp.exp(jnp.minimum(cum[:, h : h + 1] - cum_rows[h : h + 1, :], 0.0))
        inside = lane // size == i
        own_grad = jnp.where(inside, grad, jnp.zeros_like(grad))
        d_weight = mm(own_grad, stepped, 1, 1)
        d_scores = d_scores + d_weight * decay
        weights.append((scores * decay).astype(bf16))
        steppeds.append(jnp.where(inside, stepped, jnp.zeros_like(stepped)))
        grads.append(own_grad)
    out = mm(jnp.concatenate(weights, axis=1), jnp.concatenate(steppeds, axis=0), 1, 0)
    d_stepped = mm(jnp.concatenate(weights, axis=0), jnp.concatenate(grads, axis=0), 0, 0)
    return stepped, out, d_stepped, d_scores


def head_sums(high_ref, low_ref, lanes_of):
    return mm(high_ref[...], lanes_of, 1, 1) + mm(low_ref[...], lanes_of, 1, 1)


def put(refs, sl, value):
    high, low = split(value)
    refs[0][:, sl] = high
    refs[1][:, sl] = low


def from_sites(ref, j, sites, base):
    rows = slice(base + j * sites, base + (j + 1) * sites)
    return ref[:, rows, :].astype(f32).reshape(ref.shape[0] * sites, LANES)


def to_sites(ref, j, sites, base, value):
    rows = slice(base + j * sites, base + (j + 1) * sites)
    ref[:, rows, :] = value.astype(f32).reshape(ref.shape[0], sites, LANES).astype(bf16)


def pack_kernel(sites, tok_ref, grad_ref, sent_ref):
    base = sent_ref.shape[1] // 2
    for j, sl in blocks(tok_ref.shape[1]):
        to_sites(sent_ref, j, sites, 0, tok_ref[:, sl])
        to_sites(sent_ref, j, sites, base, grad_ref[:, sl])


def payload_kernel(ids_ref, proj_ref, step_ref, active_ref, mod_ref, sent_ref):
    row = ids_ref[1]
    part, pair = proj_ref.shape[0] // 2, proj_ref.shape[1]
    own = proj_ref[pl.ds(pl.multiple_of(row * part, part), part), :]
    at = 0
    for _, sl in blocks(pair):
        sent_ref[at : at + part, :] = own[:, sl]
        at += part
    part = step_ref.shape[0] // 2
    sent_ref[at : at + part, :] = step_ref[pl.ds(pl.multiple_of(row * part, part), part), :]
    at += part
    own = mm(active_ref[...], mod_ref[...], 1, 0)
    high = own.astype(bf16).astype(f32)
    pieces = [piece[:, sl] for piece in (high, own - high) for _, sl in blocks(own.shape[1])]
    pieces.append(jnp.zeros((8 - len(pieces), LANES), f32))
    sent_ref[at : at + 8, :] = jnp.concatenate(pieces, axis=0).astype(bf16)


def unpack_kernel(radix, ids_ref, own_ref, other_ref, proj_ref, step_ref, shift_ref, gain_ref):
    me, row = ids_ref[0], ids_ref[1]
    width, pair = proj_ref.shape
    frames = own_ref.shape[0]
    depth = width // frames
    part, heads = depth // 2, step_ref.shape[0] // 2
    cols = 2 * width // frames
    for i in range(frames):
        source = jnp.bitwise_xor(me, (i % radix) * radix + i // radix)
        for ref, half in ((own_ref, row), (other_ref, 1 - row)):
            rows = pl.ds(pl.multiple_of(source * depth + half * part, part), part)
            at = 0
            for _, sl in blocks(pair):
                proj_ref[rows, sl] = ref[i, at : at + part, :]
                at += part
            rows = pl.ds(pl.multiple_of(half * heads, heads), heads)
            lanes = pl.ds(pl.multiple_of(source * depth, depth), depth)
            step_ref[rows, lanes] = ref[i, at : at + heads, :]
            at += heads
        own = own_ref[i, at : at + 8, :].astype(f32)
        count = cols // LANES
        lanes_at = jnp.bitwise_and(source, frames // 2 - 1) * cols
        for k in range(count):
            value = own[k : k + 1, :] + own[count + k : count + k + 1, :]
            lanes = pl.ds(pl.multiple_of(lanes_at + k * LANES, LANES), LANES)

            @pl.when(source < frames // 2)
            def _():
                shift_ref[:, lanes] = value

            @pl.when(source >= frames // 2)
            def _():
                gain_ref[:, lanes] = value


def finish_kernel(factor, ids_ref, own_ref, other_ref, active_ref, proj_ref, step_ref, mod_ref):
    row = ids_ref[1]
    pair = proj_ref.shape[1]
    part, heads = proj_ref.shape[0] // 2, step_ref.shape[0] // 2
    for ref, half in ((own_ref, row), (other_ref, 1 - row)):
        rows = pl.ds(pl.multiple_of(half * part, part), part)
        at = 0
        for _, sl in blocks(pair):
            proj_ref[rows, sl] = ref[at : at + part, :] * factor
            at += part
        step_ref[pl.ds(pl.multiple_of(half * heads, heads), heads), :] = ref[at : at + heads, :] * factor
        at += heads
    for k, sl in blocks(mod_ref.shape[1]):
        mod_ref[:, sl] = active_ref[...] * (own_ref[at + k : at + k + 1, :] * factor)


def site_fast_kernel(sites, got_ref, *refs):
    inputs, outs, tok_ref, grad_ref, scratch = refs[:6], refs[6:10], refs[10], refs[11], refs[12:]
    base = got_ref.shape[1] // 2
    for j, sl in blocks(tok_ref.shape[1]):
        tok_ref[:, sl] = from_sites(got_ref, j, sites, 0).astype(bf16)
        grad_ref[:, sl] = from_sites(got_ref, j, sites, base).astype(bf16)
    sent_ref = outs[0]

    class Packed:
        def __init__(self, base):
            self.base = base

        def __setitem__(self, at, value):
            to_sites(sent_ref, at[1].start // LANES, sites, self.base, value)

    site_kernel(sites, tok_ref, grad_ref, *inputs, Packed(0), Packed(base), *outs[1:], *scratch)


def site_kernel(
    sites,
    tok_ref,
    grad_ref,
    shift_ref,
    gain_ref,
    proj_ref,
    step_ref,
    bias_ref,
    rate_ref,
    out_ref,
    back_ref,
    gproj_ref,
    gstep_ref,
    gmod_ref,
    x_ref,
    dn_ref,
    a_hi,
    a_lo,
    b_hi,
    b_lo,
):
    length, width = tok_ref.shape
    heads = step_ref.shape[0]
    state = proj_ref.shape[1] // 2
    clips = shift_ref.shape[0]
    inverse = normalize_into(tok_ref, shift_ref, gain_ref, x_ref)
    lanes_of = head_map(heads, width)
    mask = sequence_mask(length, sites)
    coeffs = mm(x_ref[...], proj_ref[...], 1, 0).astype(bf16)
    logits = mm(x_ref[...], step_ref[...], 1, 1).astype(bf16)
    rate = rate_ref[...]
    z, step, cum, cum_rows = steps_of(logits, bias_ref[...], rate, mask)
    b_part, c_part = coeffs[:, :state], coeffs[:, state:]
    scores = mm(c_part, b_part, 1, 1) * (mask / state)
    step_parts = split(step)
    d_scores = jnp.zeros((length, length), f32)
    for j, sl in blocks(width):
        x, grad = x_ref[:, sl], grad_ref[:, sl]
        step_wide = expand(step_parts, lanes_of[:, sl])
        stepped, out, d_stepped, d_scores = scan_block(
            j, x, grad, step_wide, scores, cum, cum_rows, heads, width, d_scores
        )
        out_ref[:, sl] = out.astype(bf16)
        dn_ref[:, sl] = (step_wide * d_stepped).astype(bf16)
        put((a_hi, a_lo), sl, grad.astype(f32) * out - stepped.astype(f32) * d_stepped)
        put((b_hi, b_lo), sl, x.astype(f32) * d_stepped)
    d_cum = head_sums(a_hi, a_lo, lanes_of)
    d_step = head_sums(b_hi, b_lo, lanes_of)
    d_log = exact(mask, d_cum, 0, 0)
    d_logits = (jax.nn.sigmoid(z) * (d_step - rate * d_log)).astype(bf16)
    d_scores = (d_scores * (mask / state)).astype(bf16)
    d_coeffs = jnp.concatenate(
        [mm(d_scores, c_part, 0, 0), mm(d_scores, b_part, 1, 0)], axis=1
    ).astype(bf16)
    for _, sl in blocks(width):
        back = (
            dn_ref[:, sl].astype(f32)
            + mm(d_coeffs, proj_ref[sl, :], 1, 1)
            + mm(d_logits, step_ref[:, sl], 1, 0)
        ).astype(bf16)
        back_ref[:, sl] = back
        back = back.astype(f32)
        scaled = back * (tok_ref[:, sl].astype(f32) * inverse)
        for c in range(clips):
            rows = slice(c * (length // clips), (c + 1) * (length // clips))
            gmod_ref[c : c + 1, sl] = jnp.sum(back[rows], axis=0, keepdims=True)
            gmod_ref[clips + c : clips + c + 1, sl] = jnp.sum(scaled[rows], axis=0, keepdims=True)
        gproj_ref[sl, :] = mm(x_ref[:, sl], d_coeffs, 0, 0)
        gstep_ref[:, sl] = mm(d_logits, x_ref[:, sl], 0, 0)


def band_kernel(
    tok_ref,
    grad_ref,
    shift_ref,
    gain_ref,
    proj_ref,
    step_ref,
    bias_ref,
    rate_ref,
    x_ref,
    coeffs_ref,
    logits_ref,
    inverse_ref,
    decay_ref,
    end_ref,
    own_ref,
):
    length, width = tok_ref.shape
    heads = step_ref.shape[0]
    state = proj_ref.shape[1] // 2
    inverse_ref[...] = normalize_into(tok_ref, shift_ref, gain_ref, x_ref)
    lanes_of = head_map(heads, width)
    mask = sequence_mask(length, 1)
    coeffs = mm(x_ref[...], proj_ref[...], 1, 0).astype(bf16)
    logits = mm(x_ref[...], step_ref[...], 1, 1).astype(bf16)
    coeffs_ref[...] = coeffs
    logits_ref[...] = logits
    _, step, cum, _ = steps_of(logits, bias_ref[...], rate_ref[...], mask)
    last = cum[length - 1 : length, :]
    decay_ref[...] = jnp.exp(last)
    lead = split(jnp.exp(last - cum) * step)
    reach = split(jnp.exp(cum) / state)
    b_part, c_part = coeffs[:, :state], coeffs[:, state:]
    for _, sl in blocks(width):
        lead_wide = expand(lead, lanes_of[:, sl])
        reach_wide = expand(reach, lanes_of[:, sl])
        scaled = (x_ref[:, sl].astype(f32) * lead_wide).astype(bf16)
        faded = (grad_ref[:, sl].astype(f32) * reach_wide).astype(bf16)
        end_ref[sl, :] = mm(scaled, b_part, 0, 0).astype(bf16)
        own_ref[sl, :] = mm(faded, c_part, 0, 0).astype(bf16)


def space_fast_kernel(ids_ref, gmod_in, *refs):
    inputs, mix_ref, pre_ref, keep_ref, give_ref = refs[:15], *refs[15:19]
    gmod_ref, scratch = refs[19], refs[20:]
    first = ids_ref[1] == 0
    pair = inputs[6].shape[1]
    part, heads = LANES // 2, inputs[7].shape[0] // 2
    proj_rows = part * pair // LANES

    class Halves:
        def __init__(self, at, part):
            self.at, self.part = at, part

        def __setitem__(self, where, value):
            value = value.astype(f32)
            j = max(0 if w.start is None else w.start for w in where) // LANES
            own = jnp.where(first, value[: self.part], value[self.part :]).astype(bf16)
            other = jnp.where(first, value[self.part :], value[: self.part]).astype(bf16)
            for k, sl in blocks(value.shape[1]):
                rows = slice(self.at + k * self.part, self.at + (k + 1) * self.part)
                keep_ref[j, rows, :] = own[:, sl]
                give_ref[j, rows, :] = other[:, sl]

    space_kernel(
        *inputs, mix_ref, pre_ref, Halves(0, part), Halves(proj_rows, heads), gmod_ref, *scratch
    )
    at = proj_rows + heads
    count = pre_ref.shape[1] // LANES
    for j in range(keep_ref.shape[0]):
        rows = []
        for k in range(2 * count // keep_ref.shape[0]):
            n = j * (2 * count // keep_ref.shape[0]) + k
            which, sl = n // count, slice(n % count * LANES, (n % count + 1) * LANES)
            rows.append(gmod_ref[which : which + 1, sl] + gmod_in[which : which + 1, sl])
        rows.append(jnp.zeros((8 - len(rows), LANES), f32))
        rows = jnp.concatenate(rows, axis=0).astype(bf16)
        keep_ref[j, at : at + 8, :] = rows
        give_ref[j, at : at + 8, :] = rows


def space_kernel(
    tok_ref,
    grad_ref,
    x_ref,
    coeffs_ref,
    logits_ref,
    inverse_ref,
    proj_ref,
    step_ref,
    bias_ref,
    rate_ref,
    skip_ref,
    state_ref,
    later_ref,
    gproj_in,
    gstep_in,
    mix_ref,
    pre_ref,
    gproj_ref,
    gstep_ref,
    gmod_ref,
    dn_ref,
    a_hi,
    a_lo,
    b_hi,
    b_lo,
    c_hi,
    c_lo,
):
    length, width = tok_ref.shape
    heads = step_ref.shape[0]
    state = proj_ref.shape[1] // 2
    lanes_of = head_map(heads, width)
    mask = sequence_mask(length, 1)
    coeffs = coeffs_ref[...]
    rate = rate_ref[...]
    z, step, cum, cum_rows = steps_of(logits_ref[...], bias_ref[...], rate, mask)
    last = cum[length - 1 : length, :]
    rest = jnp.exp(last - cum)
    lead = rest * step
    b_part, c_part = coeffs[:, :state], coeffs[:, state:]
    scores = mm(c_part, b_part, 1, 1) * (mask / state)
    step_parts, lead_parts, reach_parts = split(step), split(lead), split(jnp.exp(cum) / state)
    skip_parts = split(jnp.broadcast_to(skip_ref[...], (8, heads)))
    d_scores = jnp.zeros((length, length), f32)
    d_b = jnp.zeros((length, state), f32)
    d_c = jnp.zeros((length, state), f32)
    d_end = jnp.zeros((heads, state), f32)
    for j, sl in blocks(width):
        x, grad = x_ref[:, sl], grad_ref[:, sl]
        wide_map = lanes_of[:, sl]
        step_wide = expand(step_parts, wide_map)
        lead_wide = expand(lead_parts, wide_map)
        reach_wide = expand(reach_parts, wide_map)
        stepped, out, d_stepped, d_scores = scan_block(
            j, x, grad, step_wide, scores, cum, cum_rows, heads, width, d_scores
        )
        x, wide = x.astype(f32), grad.astype(f32)
        before, later = state_ref[sl, :], later_ref[sl, :]
        carried = mm(c_part, before, 1, 1) * reach_wide
        d_c = d_c + mm((wide * reach_wide).astype(bf16), before, 1, 0)
        d_b = d_b + mm((x * lead_wide).astype(bf16), later, 1, 0)
        d_scaled = mm(b_part, later, 1, 1)
        both = split(before.astype(f32) * later.astype(f32))
        d_end = d_end + mm(wide_map, both[0], 1, 0) + mm(wide_map, both[1], 1, 0)
        total = out + carried
        skip = expand(skip_parts, wide_map)[0:1, :]
        mix_ref[:, sl] = total + skip * x
        d_x = (step_wide * d_stepped + d_scaled * lead_wide).astype(bf16)
        dn_ref[:, sl] = d_x + (wide * skip).astype(bf16)
        put((a_hi, a_lo), sl, wide * total - stepped.astype(f32) * d_stepped)
        put((b_hi, b_lo), sl, x * d_stepped)
        put((c_hi, c_lo), sl, x * d_scaled)
    d_lead = head_sums(c_hi, c_lo, lanes_of)
    d_step = head_sums(b_hi, b_lo, lanes_of) + d_lead * rest
    fall = d_lead * lead
    d_cum = head_sums(a_hi, a_lo, lanes_of) - fall
    ones = jnp.ones((8, state), f32)
    end_sum = exact(ones, d_end, 1, 1)[0:1, :] * jnp.exp(last)
    end_sum = end_sum + jnp.sum(fall, axis=0, keepdims=True)
    d_log = exact(mask, d_cum, 0, 0) + end_sum
    d_logits = (jax.nn.sigmoid(z) * (d_step - rate * d_log)).astype(bf16)
    d_scores = (d_scores * (mask / state)).astype(bf16)
    d_coeffs = jnp.concatenate(
        [mm(d_scores, c_part, 0, 0) + d_b, mm(d_scores, b_part, 1, 0) + d_c], axis=1
    ).astype(bf16)
    inverse = inverse_ref[...]
    for _, sl in blocks(width):
        pre = (
            dn_ref[:, sl].astype(f32)
            + mm(d_coeffs, proj_ref[sl, :], 1, 1)
            + mm(d_logits, step_ref[:, sl], 1, 0)
        )
        pre_ref[:, sl] = pre
        scaled = pre * (tok_ref[:, sl].astype(f32) * inverse)
        gmod_ref[0:1, sl] = jnp.sum(pre, axis=0, keepdims=True)
        gmod_ref[1:2, sl] = jnp.sum(scaled, axis=0, keepdims=True)
        gproj_ref[sl, :] = (gproj_in[sl, :] + mm(x_ref[:, sl], d_coeffs, 0, 0)).astype(bf16)
        gstep_ref[:, sl] = (gstep_in[:, sl] + mm(d_logits, x_ref[:, sl], 0, 0)).astype(bf16)


def last_kernel(tok_ref, inverse_ref, gain_ref, mix_ref, pre_ref, time_ref, back_ref, out_ref, dtok_ref):
    length, width = tok_ref.shape
    inverse = inverse_ref[...]
    total = jnp.zeros((length, LANES), f32)
    for _, sl in blocks(width):
        out_ref[:, sl] = (mix_ref[:, sl] + time_ref[:, sl].astype(f32)).astype(bf16)
        grad = (pre_ref[:, sl] + back_ref[:, sl].astype(f32)) * (1.0 + gain_ref[:, sl])
        total = total + grad * tok_ref[:, sl].astype(f32)
    inner = jnp.sum(total, axis=1, keepdims=True) / width
    inner = inner * inverse * inverse * inverse
    for _, sl in blocks(width):
        grad = (pre_ref[:, sl] + back_ref[:, sl].astype(f32)) * (1.0 + gain_ref[:, sl])
        dtok_ref[:, sl] = (grad * inverse - tok_ref[:, sl].astype(f32) * inner).astype(bf16)


def last_fast_kernel(sites, tok_ref, inverse_ref, gain_ref, mix_ref, pre_ref, came_ref, *outs):
    base = came_ref.shape[1] // 2

    class Packed:
        def __init__(self, base):
            self.base = base

        def __getitem__(self, at):
            return from_sites(came_ref, at[1].start // LANES, sites, self.base)

    last_kernel(tok_ref, inverse_ref, gain_ref, mix_ref, pre_ref, Packed(0), Packed(base), *outs)


def call(kernel, outs, scratch=(), name=None, ids=0):
    shapes = [jax.ShapeDtypeStruct(s, d) for s, d in outs]
    if ids:
        whole = pl.BlockSpec(memory_space=pltpu.VMEM)
        specs = [pl.BlockSpec(memory_space=pltpu.SMEM)] + [whole] * ids
        specs = {"in_specs": specs, "out_specs": [whole] * len(outs)}
    else:
        specs = {}
    return pl.pallas_call(
        kernel,
        out_shape=shapes,
        **specs,
        scratch_shapes=[pltpu.VMEM(s, d) for s, d in scratch],
        compiler_params=pltpu.CompilerParams(vmem_limit_bytes=48 << 20),
        name=name,
    )


def rows_in_order(part):
    if lax.axis_size("row") != 2:
        return lax.all_gather(part, "row")
    other = lax.ppermute(part, "row", [(0, 1), (1, 0)])
    first = lax.axis_index("row") == 0
    return jnp.stack([jnp.where(first, part, other), jnp.where(first, other, part)])


def rows_sum(part):
    if lax.axis_size("row") != 2:
        return lax.psum(part, "row")
    return part + lax.ppermute(part, "row", [(0, 1), (1, 0)])


def chain(own, decay, forward):
    count = lax.axis_size("row")
    hops = [(i, i + 1) if forward else (i + 1, i) for i in range(count - 1)]
    if count == 1:
        return jnp.zeros_like(own)
    arrived = lax.ppermute(own, "row", hops)
    wide = jnp.repeat(decay[0], own.shape[0] // decay.shape[1])[:, None]
    for _ in range(count - 2):
        passed = wide * arrived.astype(f32) + own.astype(f32)
        arrived = lax.ppermute(passed.astype(bf16), "row", hops)
    return arrived


def per_device(
    tokens,
    cotangent,
    timestep,
    mod_weight,
    proj_weight,
    step_weight,
    step_bias,
    rate_space,
    rate_time,
    skip_gain,
):
    frames = lax.axis_size("frame")
    rows = lax.axis_size("row")
    frame_id = lax.axis_index("frame")
    row_id = lax.axis_index("row")
    width = tokens.shape[-1]
    length = tokens.shape[1] * tokens.shape[2]
    clips = timestep.shape[0]
    clip_id = frame_id // (frames // clips)
    sites = length // frames
    heads = rate_space.shape[0]
    depth, pair = proj_weight.shape
    state = pair // 2
    mod_cols = mod_weight.shape[1]
    factor = (frames * rows * length) ** (-0.5)
    tok = tokens.reshape(length, width)
    grad = cotangent.reshape(length, width)

    activated = time_embed(timestep, mod_weight.shape[0]).astype(bf16)
    own_mod = jnp.dot(activated, mod_weight, preferred_element_type=f32)
    high = lax.reduce_precision(own_mod, 8, 7)
    own_mod = jnp.stack([high, own_mod - high]).astype(bf16)

    part = depth // rows
    own_proj = lax.dynamic_slice_in_dim(proj_weight, row_id * part, part, 0)
    to_all = [
        to_tiles(own_proj[None]),
        to_tiles(step_weight.T[None]),
        own_mod.reshape(1, -1, LANES),
    ]
    to_all = jnp.concatenate(to_all, axis=1)
    to_all = jnp.pad(to_all, ((0, 0), (0, -to_all.shape[1] % 8), (0, 0)))
    count = sites * width // LANES
    got = exchange(
        jnp.concatenate(
            [
                to_tiles(tok.reshape(frames, sites, width)),
                to_tiles(grad.reshape(frames, sites, width)),
                jnp.broadcast_to(to_all, (frames,) + to_all.shape[1:]),
            ],
            axis=1,
        )
    )
    site_tok = from_tiles(got[:, :count], sites, width).reshape(length, width)
    site_grad = from_tiles(got[:, count : 2 * count], sites, width).reshape(length, width)
    at = 2 * count
    size = part * pair // LANES
    proj_full = rows_in_order(got[:, at : at + size])
    proj_full = from_tiles(proj_full.reshape(rows * frames, size, LANES), part, pair)
    proj_full = proj_full.reshape(rows, frames, part, pair).transpose(1, 0, 2, 3)
    proj_full = proj_full.reshape(width, pair)
    at += size
    size = heads * depth // LANES
    step_full = from_tiles(got[:, at : at + size], heads, depth)
    step_full = step_full.transpose(1, 0, 2).reshape(heads, width)
    at += size
    size = 2 * clips * mod_cols // LANES
    mod_full = got[:, at : at + size].reshape(frames, 2, clips, mod_cols).astype(f32)
    mod_full = (mod_full[:, 0] + mod_full[:, 1]).transpose(1, 0, 2).reshape(clips, 2 * width)
    shift, gain = mod_full[:, :width], mod_full[:, width:]

    bias = step_bias[None]
    wide = (length, width)
    site_out, site_back, gproj, gstep, site_gmod = call(
        functools.partial(site_kernel, sites),
        [(wide, bf16), (wide, bf16), ((width, pair), f32), ((heads, width), f32), ((2 * clips, width), f32)],
        [(wide, bf16)] * 6,
        name="site",
    )(site_tok, site_grad, shift, gain, proj_full, step_full, bias, rate_time[None])

    came = exchange(
        jnp.concatenate(
            [
                to_tiles(site_out.reshape(frames, sites, width)),
                to_tiles(site_back.reshape(frames, sites, width)),
            ],
            axis=1,
        )
    )
    time_out = from_tiles(came[:, :count], sites, width).reshape(length, width)
    time_back = from_tiles(came[:, count:], sites, width).reshape(length, width)

    own_shift = lax.dynamic_slice_in_dim(shift, clip_id, 1, 0)
    own_gain = lax.dynamic_slice_in_dim(gain, clip_id, 1, 0)
    normed, coeffs, logits, inverse, decay, end_own, start_grad = call(
        band_kernel,
        [
            (wide, bf16),
            ((length, pair), bf16),
            ((length, heads), bf16),
            ((length, 1), f32),
            ((1, heads), f32),
            ((width, state), bf16),
            ((width, state), bf16),
        ],
        name="band",
    )(tok, grad, own_shift, own_gain, proj_full, step_full, bias, rate_space[None])
    state_in = chain(end_own, decay, True)
    later_grad = chain(start_grad, decay, False)
    mix, pre, gproj, gstep, gmod = call(
        space_kernel,
        [(wide, f32), (wide, f32), ((width, pair), bf16), ((heads, width), bf16), ((2, width), f32)],
        [(wide, bf16)] * 7,
        name="space",
    )(
        tok,
        grad,
        normed,
        coeffs,
        logits,
        inverse,
        proj_full,
        step_full,
        bias,
        rate_space[None],
        skip_gain[None],
        state_in,
        later_grad,
        gproj,
        gstep,
    )

    picked = (jnp.arange(clips) == clip_id).astype(f32)[:, None]
    gmod = jnp.concatenate(
        [site_gmod[:clips] + picked * gmod[0:1], site_gmod[clips:] + picked * gmod[1:2]], axis=1
    )
    gmod = gmod.reshape(clips, frames, mod_cols).transpose(1, 0, 2).astype(bf16)
    sent = jnp.concatenate(
        [
            to_tiles(gproj.reshape(frames, depth, pair)),
            to_tiles(gstep.reshape(heads, frames, depth).transpose(1, 0, 2)),
            gmod.reshape(frames, -1, LANES) if (clips * mod_cols) % LANES == 0 else gmod,
        ],
        axis=1,
    )
    size = sent.shape[1]
    sent = jnp.pad(sent, ((0, 0), (0, -size % 8), (0, 0)))
    sums = jnp.sum(exchange(sent).astype(f32), axis=0, keepdims=True)
    sums = rows_sum(sums) * factor
    at = depth * pair // LANES
    grad_proj = from_tiles(sums[:, :at], depth, pair)[0]
    size = heads * depth // LANES
    grad_step = from_tiles(sums[:, at : at + size], heads, depth)[0].T
    at += size
    size = clips * mod_cols // LANES
    mod_sum = sums[0, at : at + size].reshape(clips, mod_cols)
    grad_mod = jnp.dot(activated.astype(f32).T, mod_sum, precision=EXACT)

    mixed, d_tokens = call(last_kernel, [(wide, bf16), (wide, bf16)], name="last")(
        tok, inverse, own_gain, mix, pre, time_out, time_back
    )
    return (mixed.reshape(tokens.shape), d_tokens.reshape(tokens.shape), grad_proj, grad_step, grad_mod)


def fits(mesh, tokens, timestep, proj_weight, step_weight):
    frames, rows = mesh.shape["frame"], mesh.shape["row"]
    length, width = tokens.shape[2] * tokens.shape[1] // rows, tokens.shape[3]
    return (
        rows == 2
        and frames == 16
        and timestep.shape[0] == 1
        and length == LANES
        and length // frames == 8
        and width // frames == LANES
        and proj_weight.shape[1] == 2 * LANES
        and step_weight.shape[1] % 32 == 0
    )


def spread_over_frames(own, radix=4):
    frames = radix * radix

    def others(piece, stride):
        return [piece] + [
            lax.ppermute(piece, "frame", [(i, i ^ (d * stride)) for i in range(frames)])
            for d in range(1, radix)
        ]

    far = jnp.stack(others(own, radix))
    return jnp.concatenate(others(far, 1))


def per_device_fast(
    tokens,
    cotangent,
    timestep,
    mod_weight,
    proj_weight,
    step_weight,
    step_bias,
    rate_space,
    rate_time,
    skip_gain,
):
    frames = lax.axis_size("frame")
    rows = lax.axis_size("row")
    ids = jnp.stack([lax.axis_index("frame"), lax.axis_index("row")]).astype(jnp.int32)
    width = tokens.shape[-1]
    length = tokens.shape[1] * tokens.shape[2]
    sites = length // frames
    heads = rate_space.shape[0]
    depth, pair = proj_weight.shape
    state = pair // 2
    mod_cols = mod_weight.shape[1]
    factor = (frames * rows * length) ** (-0.5)
    tok = tokens.reshape(length, width)
    grad = cotangent.reshape(length, width)
    wide = (length, width)
    bias = step_bias[None]
    swap = [(0, 1), (1, 0)]

    packed = (frames, 2 * sites * width // LANES, LANES)
    (sent,) = call(functools.partial(pack_kernel, sites), [(packed, bf16)], name="pack")(tok, grad)

    timestep, sent = lax.optimization_barrier((timestep, sent))
    got = exchange(sent)
    activated = time_embed(timestep, mod_weight.shape[0]).astype(bf16)
    size = depth // 2 * pair // LANES + heads // 2 + 8
    (payload,) = call(payload_kernel, [((size, LANES), bf16)], name="payload", ids=4)(
        ids, proj_weight, step_weight.T, activated, mod_weight
    )
    payload = spread_over_frames(payload)
    other = lax.ppermute(payload, "row", swap)
    proj_full, step_full, shift, gain = call(
        functools.partial(unpack_kernel, 4),
        [((width, pair), bf16), ((heads, width), bf16), ((1, width), f32), ((1, width), f32)],
        name="unpack",
        ids=2,
    )(ids, payload, other)

    sent, gproj, gstep, site_gmod = call(
        functools.partial(site_fast_kernel, sites),
        [(packed, bf16), ((width, pair), f32), ((heads, width), f32), ((2, width), f32)],
        [(wide, bf16)] * 8,
        name="site",
    )(got, shift, gain, proj_full, step_full, bias, rate_time[None])
    came = exchange(sent)

    normed, coeffs, logits, inverse, decay, end_own, start_grad = call(
        band_kernel,
        [
            (wide, bf16),
            ((length, pair), bf16),
            ((length, heads), bf16),
            ((length, 1), f32),
            ((1, heads), f32),
            ((width, state), bf16),
            ((width, state), bf16),
        ],
        name="band",
    )(tok, grad, shift, gain, proj_full, step_full, bias, rate_space[None])
    state_in = chain(end_own, decay, True)
    later_grad = chain(start_grad, decay, False)
    halves = (frames, size, LANES)
    mix, pre, keep, give, _ = call(
        space_fast_kernel,
        [(wide, f32), (wide, f32), (halves, bf16), (halves, bf16), ((2, width), f32)],
        [(wide, bf16)] * 7,
        name="space",
        ids=16,
    )(
        ids,
        site_gmod,
        tok,
        grad,
        normed,
        coeffs,
        logits,
        inverse,
        proj_full,
        step_full,
        bias,
        rate_space[None],
        skip_gain[None],
        state_in,
        later_grad,
        gproj,
        gstep,
    )
    given = lax.ppermute(give, "row", swap)
    terms = (keep.astype(f32) + given.astype(f32)).astype(bf16)
    terms, came = lax.optimization_barrier((terms, came))
    sums = jnp.sum(exchange(terms).astype(f32), axis=0)
    other = lax.ppermute(sums, "row", swap)
    grad_proj, grad_step, grad_mod = call(
        functools.partial(finish_kernel, factor),
        [((depth, pair), f32), ((heads, depth), f32), ((mod_weight.shape[0], mod_cols), f32)],
        name="finish",
        ids=3,
    )(ids, sums, other, activated.astype(f32).T)
    mixed, d_tokens = call(
        functools.partial(last_fast_kernel, sites), [(wide, bf16), (wide, bf16)], name="last"
    )(tok, inverse, gain, mix, pre, came)
    return (mixed.reshape(tokens.shape), d_tokens.reshape(tokens.shape), grad_proj, grad_step.T, grad_mod)


def solution(mesh):
    placed = (
        P("frame", "row", None, None),
        P("frame", "row", None, None),
        P(),
        P(None, "frame"),
        P("frame", None),
        P("frame", None),
        P(),
        P(),
        P(),
        P(),
    )
    outs = (
        P("frame", "row", None, None),
        P("frame", "row", None, None),
        P("frame", None),
        P("frame", None),
        P(None, "frame"),
    )

    def step(tokens, cotangent, timestep, mod_weight, proj_weight, step_weight, *rest):
        fast = fits(mesh, tokens, timestep, proj_weight, step_weight)
        body = per_device_fast if fast else per_device
        return jax.shard_map(
            body, mesh=mesh, in_specs=placed, out_specs=outs, check_vma=False
        )(tokens, cotangent, timestep, mod_weight, proj_weight, step_weight, *rest)

    return step
```

```python
import functools
import math

import jax
import jax.numpy as jnp
from jax import lax
from jax.experimental import pallas as pl
from jax.experimental.pallas import tpu as pltpu
from jax.sharding import PartitionSpec as P

norm_eps = 1e-05
LANES = 128
f32 = jnp.float32
bf16 = jnp.bfloat16
EXACT = lax.Precision.HIGHEST


def time_embed(timestep, embed_dim):
    half_dim = embed_dim // 2
    frequency = jnp.exp(-math.log(10000.0) * jnp.arange(half_dim, dtype=f32) / half_dim)
    angles = timestep.astype(f32)[:, None] * frequency[None, :]
    return jax.nn.silu(jnp.concatenate([jnp.cos(angles), jnp.sin(angles)], axis=1))


def to_tiles(a):
    f, r, c = a.shape
    if r % 8 == 0 and c % LANES == 0:
        a = a.reshape(f, r // 8, 8, c // LANES, LANES).transpose(0, 1, 3, 2, 4)
    return a.reshape(f, r * c // LANES, LANES)


def from_tiles(a, r, c):
    f = a.shape[0]
    if r % 8 == 0 and c % LANES == 0:
        a = a.reshape(f, r // 8, c // LANES, 8, LANES).transpose(0, 1, 3, 2, 4)
    return a.reshape(f, r, c)


def exchange(packed):
    return lax.all_to_all(packed, "frame", split_axis=0, concat_axis=0, tiled=True)


def mm(a, b, ca, cb):
    return lax.dot_general(a, b, (((ca,), (cb,)), ((), ())), preferred_element_type=f32)


def exact(a, b, ca, cb):
    return lax.dot_general(
        a, b, (((ca,), (cb,)), ((), ())), preferred_element_type=f32, precision=EXACT
    )


def split(a):
    high = a.astype(bf16)
    return high, (a - high.astype(f32)).astype(bf16)


def head_map(heads, width):
    size = width // heads
    own = lax.broadcasted_iota(jnp.int32, (heads, width), 0)
    lane = lax.broadcasted_iota(jnp.int32, (heads, width), 1)
    return jnp.where(lane // size == own, 1.0, 0.0).astype(bf16)


def sequence_mask(length, sites):
    later = lax.broadcasted_iota(jnp.int32, (length, length), 0)
    earlier = lax.broadcasted_iota(jnp.int32, (length, length), 1)
    keep = later >= earlier
    if sites > 1:
        keep = keep & (later % sites == earlier % sites)
    return jnp.where(keep, 1.0, 0.0).astype(f32)


def blocks(width):
    return [(j, slice(j * LANES, (j + 1) * LANES)) for j in range(width // LANES)]


def spread_rows(rows, length):
    count = rows.shape[0]
    if count == 1:
        return rows
    part = (length // count, rows.shape[1])
    return jnp.concatenate([jnp.broadcast_to(rows[c : c + 1], part) for c in range(count)], axis=0)


def normalize_into(tok_ref, shift_ref, gain_ref, x_ref):
    length, width = tok_ref.shape
    total = jnp.zeros((length, LANES), f32)
    for _, sl in blocks(width):
        v = tok_ref[:, sl].astype(f32)
        total = total + v * v
    mean = jnp.sum(total, axis=1, keepdims=True) / width
    inverse = lax.rsqrt(mean + norm_eps)
    for _, sl in blocks(width):
        unit = tok_ref[:, sl].astype(f32) * inverse
        gain = spread_rows(gain_ref[:, sl], length)
        shift = spread_rows(shift_ref[:, sl], length)
        x_ref[:, sl] = (unit * (1.0 + gain) + shift).astype(bf16)
    return inverse


def steps_of(logits, bias, rate, mask):
    z = logits.astype(f32) + bias
    step = jnp.maximum(z, 0.0) + jnp.log1p(jnp.exp(-jnp.abs(z)))
    log_decay = -step * rate
    cum = exact(mask, log_decay, 1, 0)
    cum_rows = exact(log_decay, mask, 0, 1)
    return z, step, cum, cum_rows


def expand(parts, lanes_of):
    return mm(parts[0], lanes_of, 1, 0) + mm(parts[1], lanes_of, 1, 0)


def scan_block(j, x, grad, step_wide, scores, cum, cum_rows, heads, width, d_scores):
    size = width // heads
    per_block = LANES // size
    stepped = (x.astype(f32) * step_wide).astype(bf16)
    lane = lax.broadcasted_iota(jnp.int32, x.shape, 1)
    weights, steppeds, grads = [], [], []
    for i in range(per_block):
        h = j * per_block + i
        decay = jnp.exp(jnp.minimum(cum[:, h : h + 1] - cum_rows[h : h + 1, :], 0.0))
        inside = lane // size == i
        own_grad = jnp.where(inside, grad, jnp.zeros_like(grad))
        d_weight = mm(own_grad, stepped, 1, 1)
        d_scores = d_scores + d_weight * decay
        weights.append((scores * decay).astype(bf16))
        steppeds.append(jnp.where(inside, stepped, jnp.zeros_like(stepped)))
        grads.append(own_grad)
    out = mm(jnp.concatenate(weights, axis=1), jnp.concatenate(steppeds, axis=0), 1, 0)
    d_stepped = mm(jnp.concatenate(weights, axis=0), jnp.concatenate(grads, axis=0), 0, 0)
    return stepped, out, d_stepped, d_scores


def head_sums(high_ref, low_ref, lanes_of):
    return mm(high_ref[...], lanes_of, 1, 1) + mm(low_ref[...], lanes_of, 1, 1)


def put(refs, sl, value):
    high, low = split(value)
    refs[0][:, sl] = high
    refs[1][:, sl] = low


def start_kernel(ids_ref, tok_ref, grad_ref, proj_hbm, step_hbm, mod_hbm, active_ref, sent_ref, pay_ref,
                 proj_ref, step_ref, mod_ref, sems):
    copies = [
        pltpu.make_async_copy(src, dst, sems.at[n])
        for n, (src, dst) in enumerate(
            [
                (proj_hbm, proj_ref),
                (step_hbm, step_ref),
                (mod_hbm, mod_ref),
                (tok_ref, sent_ref.at[:, 0]),
                (grad_ref, sent_ref.at[:, 1]),
            ]
        )
    ]
    for copy in copies:
        copy.start()
    row = ids_ref[1]
    part, pair = proj_ref.shape[0] // 2, proj_ref.shape[1]
    copies[0].wait()
    own = proj_ref[pl.ds(pl.multiple_of(row * part, part), part), :]
    at = 0
    for _, sl in blocks(pair):
        pay_ref[at : at + part, :] = own[:, sl]
        at += part
    copies[1].wait()
    part = step_ref.shape[0] // 2
    pay_ref[at : at + part, :] = step_ref[pl.ds(pl.multiple_of(row * part, part), part), :]
    at += part
    copies[2].wait()
    own = mm(active_ref[...], mod_ref[...], 1, 0)
    high = own.astype(bf16).astype(f32)
    pieces = [piece[:, sl] for piece in (high, own - high) for _, sl in blocks(own.shape[1])]
    pieces.append(jnp.zeros((8 - len(pieces), LANES), f32))
    pay_ref[at : at + 8, :] = jnp.concatenate(pieces, axis=0).astype(bf16)
    copies[3].wait()
    copies[4].wait()


def unpack_kernel(radix, ids_ref, own_ref, other_ref, proj_ref, step_ref, shift_ref, gain_ref):
    me, row = ids_ref[0], ids_ref[1]
    width, pair = proj_ref.shape
    frames = own_ref.shape[0]
    depth = width // frames
    part, heads = depth // 2, step_ref.shape[0] // 2
    cols = 2 * width // frames
    for i in range(frames):
        source = jnp.bitwise_xor(me, (i % radix) * radix + i // radix)
        for ref, half in ((own_ref, row), (other_ref, 1 - row)):
            rows = pl.ds(pl.multiple_of(source * depth + half * part, part), part)
            at = 0
            for _, sl in blocks(pair):
                proj_ref[rows, sl] = ref[i, at : at + part, :]
                at += part
            rows = pl.ds(pl.multiple_of(half * heads, heads), heads)
            lanes = pl.ds(pl.multiple_of(source * depth, depth), depth)
            step_ref[rows, lanes] = ref[i, at : at + heads, :]
            at += heads
        own = own_ref[i, at : at + 8, :].astype(f32)
        count = cols // LANES
        lanes_at = jnp.bitwise_and(source, frames // 2 - 1) * cols
        for k in range(count):
            value = own[k : k + 1, :] + own[count + k : count + k + 1, :]
            lanes = pl.ds(pl.multiple_of(lanes_at + k * LANES, LANES), LANES)

            @pl.when(source < frames // 2)
            def _():
                shift_ref[:, lanes] = value

            @pl.when(source >= frames // 2)
            def _():
                gain_ref[:, lanes] = value


def finish_kernel(factor, ids_ref, own_ref, other_ref, active_ref, proj_ref, step_ref, mod_ref):
    row = ids_ref[1]
    pair = proj_ref.shape[1]
    part, heads = proj_ref.shape[0] // 2, step_ref.shape[0] // 2
    for ref, half in ((own_ref, row), (other_ref, 1 - row)):
        rows = pl.ds(pl.multiple_of(half * part, part), part)
        at = 0
        for _, sl in blocks(pair):
            proj_ref[rows, sl] = ref[at : at + part, :] * factor
            at += part
        step_ref[pl.ds(pl.multiple_of(half * heads, heads), heads), :] = ref[at : at + heads, :] * factor
        at += heads
    for k, sl in blocks(mod_ref.shape[1]):
        mod_ref[:, sl] = active_ref[...] * (own_ref[at + k : at + k + 1, :] * factor)


def site_fast_kernel(sites, got_ref, *refs):
    inputs, (sent_hbm, x_ref, dc_ref, dl_ref, gmod_ref) = refs[:6], refs[6:11]
    tok_ref, grad_ref, sent_ref, sems = refs[11:15]
    scratch = refs[15:]
    frames, width = got_ref.shape[0], got_ref.shape[3]
    for _, sl in blocks(width):
        for ref, which in ((tok_ref, 0), (grad_ref, 1)):
            value = got_ref[:, which, :, sl].astype(f32)
            ref[:, sl] = value.reshape(frames * sites, LANES).astype(bf16)

    parts = 2
    share = width // parts
    copies = []

    def send(which, p):
        at = (slice(None), which, slice(None), slice(p * share, (p + 1) * share))
        copy = pltpu.make_async_copy(sent_ref.at[at], sent_hbm.at[at], sems.at[len(copies)])
        copy.start()
        copies.append(copy)

    class Packed:
        def __init__(self, which):
            self.which = which

        def __setitem__(self, at, value):
            value = value.astype(f32).reshape(frames, sites, LANES)
            sent_ref[:, self.which, :, at[1]] = value.astype(bf16)
            if at[1].stop % share == 0:
                send(self.which, at[1].stop // share - 1)

    site_kernel(
        sites, tok_ref, grad_ref, *inputs, Packed(0), Packed(1), dc_ref, dl_ref, gmod_ref, x_ref, *scratch
    )
    for copy in copies:
        copy.wait()


def site_kernel(
    sites,
    tok_ref,
    grad_ref,
    shift_ref,
    gain_ref,
    proj_ref,
    step_ref,
    bias_ref,
    rate_ref,
    out_ref,
    back_ref,
    gproj_ref,
    gstep_ref,
    gmod_ref,
    x_ref,
    dn_ref,
    a_hi,
    a_lo,
    b_hi,
    b_lo,
):
    length, width = tok_ref.shape
    heads = step_ref.shape[0]
    state = proj_ref.shape[1] // 2
    clips = shift_ref.shape[0]
    inverse = normalize_into(tok_ref, shift_ref, gain_ref, x_ref)
    lanes_of = head_map(heads, width)
    mask = sequence_mask(length, sites)
    coeffs = mm(x_ref[...], proj_ref[...], 1, 0).astype(bf16)
    logits = mm(x_ref[...], step_ref[...], 1, 1).astype(bf16)
    rate = rate_ref[...]
    z, step, cum, cum_rows = steps_of(logits, bias_ref[...], rate, mask)
    b_part, c_part = coeffs[:, :state], coeffs[:, state:]
    scores = mm(c_part, b_part, 1, 1) * (mask / state)
    step_parts = split(step)
    d_scores = jnp.zeros((length, length), f32)
    for j, sl in blocks(width):
        x, grad = x_ref[:, sl], grad_ref[:, sl]
        step_wide = expand(step_parts, lanes_of[:, sl])
        stepped, out, d_stepped, d_scores = scan_block(
            j, x, grad, step_wide, scores, cum, cum_rows, heads, width, d_scores
        )
        out_ref[:, sl] = out.astype(bf16)
        dn_ref[:, sl] = (step_wide * d_stepped).astype(bf16)
        put((a_hi, a_lo), sl, grad.astype(f32) * out - stepped.astype(f32) * d_stepped)
        put((b_hi, b_lo), sl, x.astype(f32) * d_stepped)
    d_cum = head_sums(a_hi, a_lo, lanes_of)
    d_step = head_sums(b_hi, b_lo, lanes_of)
    d_log = exact(mask, d_cum, 0, 0)
    d_logits = (jax.nn.sigmoid(z) * (d_step - rate * d_log)).astype(bf16)
    d_scores = (d_scores * (mask / state)).astype(bf16)
    d_coeffs = jnp.concatenate(
        [mm(d_scores, c_part, 0, 0), mm(d_scores, b_part, 1, 0)], axis=1
    ).astype(bf16)
    for _, sl in blocks(width):
        back = (
            dn_ref[:, sl].astype(f32)
            + mm(d_coeffs, proj_ref[sl, :], 1, 1)
            + mm(d_logits, step_ref[:, sl], 1, 0)
        ).astype(bf16)
        back_ref[:, sl] = back
        back = back.astype(f32)
        scaled = back * (tok_ref[:, sl].astype(f32) * inverse)
        for c in range(clips):
            rows = slice(c * (length // clips), (c + 1) * (length // clips))
            gmod_ref[c : c + 1, sl] = jnp.sum(back[rows], axis=0, keepdims=True)
            gmod_ref[clips + c : clips + c + 1, sl] = jnp.sum(scaled[rows], axis=0, keepdims=True)
        if gproj_ref.shape == (width, 2 * state):
            gproj_ref[sl, :] = mm(x_ref[:, sl], d_coeffs, 0, 0)
            gstep_ref[:, sl] = mm(d_logits, x_ref[:, sl], 0, 0)
    if gproj_ref.shape != (width, 2 * state):
        gproj_ref[...] = d_coeffs
        gstep_ref[...] = d_logits


def band_fast_kernel(ids_ref, *refs):
    give_ref = refs[-1]
    band_kernel(*refs[:-1], None, give_ref, first=ids_ref[1] == 0)


def band_kernel(
    tok_ref,
    grad_ref,
    shift_ref,
    gain_ref,
    proj_ref,
    step_ref,
    bias_ref,
    rate_ref,
    x_ref,
    coeffs_ref,
    logits_ref,
    inverse_ref,
    decay_ref,
    end_ref,
    own_ref,
    first=None,
):
    length, width = tok_ref.shape
    heads = step_ref.shape[0]
    state = proj_ref.shape[1] // 2
    inverse_ref[...] = normalize_into(tok_ref, shift_ref, gain_ref, x_ref)
    lanes_of = head_map(heads, width)
    mask = sequence_mask(length, 1)
    coeffs = mm(x_ref[...], proj_ref[...], 1, 0).astype(bf16)
    logits = mm(x_ref[...], step_ref[...], 1, 1).astype(bf16)
    coeffs_ref[...] = coeffs
    logits_ref[...] = logits
    _, step, cum, _ = steps_of(logits, bias_ref[...], rate_ref[...], mask)
    last = cum[length - 1 : length, :]
    decay_ref[...] = jnp.exp(last)
    lead = split(jnp.exp(last - cum) * step)
    reach = split(jnp.exp(cum) / state)
    b_part, c_part = coeffs[:, :state], coeffs[:, state:]
    if first is not None:
        gain = split(jnp.where(first, jnp.exp(last - cum) * step, jnp.exp(cum) / state))
        other = jnp.where(first, b_part, c_part)
        for _, sl in blocks(width):
            value = jnp.where(first, x_ref[:, sl], grad_ref[:, sl]).astype(f32)
            value = (value * expand(gain, lanes_of[:, sl])).astype(bf16)
            own_ref[sl, :] = mm(value, other, 0, 0).astype(bf16)
        return
    for _, sl in blocks(width):
        lead_wide = expand(lead, lanes_of[:, sl])
        reach_wide = expand(reach, lanes_of[:, sl])
        scaled = (x_ref[:, sl].astype(f32) * lead_wide).astype(bf16)
        faded = (grad_ref[:, sl].astype(f32) * reach_wide).astype(bf16)
        end_ref[sl, :] = mm(scaled, b_part, 0, 0).astype(bf16)
        own_ref[sl, :] = mm(faded, c_part, 0, 0).astype(bf16)


def space_fast_kernel(radix, ids_ref, gmod_in, site_x, site_dc, site_dl, arrived_ref, *refs):
    inputs, mix_ref, pre_ref, keep_ref, give_ref = refs[:11], *refs[11:15]
    gmod_ref, scratch = refs[15], refs[16:]
    me, first = ids_ref[0], ids_ref[1] == 0
    pair = inputs[6].shape[1]
    part, heads = LANES // 2, inputs[7].shape[0] // 2
    proj_rows = part * pair // LANES

    def place(j):
        offset = jnp.bitwise_xor(me, j)
        return jnp.bitwise_and(offset, radix - 1) * radix + offset // radix

    class Halves:
        def __init__(self, at, part):
            self.at, self.part = at, part

        def __setitem__(self, where, value):
            j = max(0 if w.start is None else w.start for w in where) // LANES
            own = jnp.where(first, value[: self.part], value[self.part :]).astype(bf16)
            other = jnp.where(first, value[self.part :], value[: self.part]).astype(bf16)
            j = place(j)
            for k, sl in blocks(value.shape[1]):
                rows = slice(self.at + k * self.part, self.at + (k + 1) * self.part)
                keep_ref[j, rows, :] = own[:, sl]
                give_ref[j, rows, :] = other[:, sl]

    class Arrived:
        def __init__(self, wanted):
            self.wanted = wanted

        def __getitem__(self, at):
            value = arrived_ref[at]
            return jnp.where(self.wanted, value, jnp.zeros_like(value))

    space_kernel(
        *inputs,
        Arrived(jnp.logical_not(first)),
        Arrived(first),
        (site_x, site_dc, site_dl),
        None,
        mix_ref,
        pre_ref,
        Halves(0, part),
        Halves(proj_rows, heads),
        gmod_ref,
        *scratch,
    )
    at = proj_rows + heads
    count = pre_ref.shape[1] // LANES
    frames = keep_ref.shape[0]
    for j in range(frames):
        rows = []
        for k in range(2 * count // frames):
            n = j * (2 * count // frames) + k
            which, sl = n // count, slice(n % count * LANES, (n % count + 1) * LANES)
            rows.append(gmod_ref[which : which + 1, sl] + gmod_in[which : which + 1, sl])
        rows.append(jnp.zeros((8 - len(rows), LANES), f32))
        rows = jnp.concatenate(rows, axis=0).astype(bf16)
        keep_ref[place(j), at : at + 8, :] = rows
        give_ref[place(j), at : at + 8, :] = rows


def space_kernel(
    tok_ref,
    grad_ref,
    x_ref,
    coeffs_ref,
    logits_ref,
    inverse_ref,
    proj_ref,
    step_ref,
    bias_ref,
    rate_ref,
    skip_ref,
    state_ref,
    later_ref,
    gproj_in,
    gstep_in,
    mix_ref,
    pre_ref,
    gproj_ref,
    gstep_ref,
    gmod_ref,
    dn_ref,
    a_hi,
    a_lo,
    b_hi,
    b_lo,
    c_hi,
    c_lo,
):
    length, width = tok_ref.shape
    heads = step_ref.shape[0]
    state = proj_ref.shape[1] // 2
    lanes_of = head_map(heads, width)
    mask = sequence_mask(length, 1)
    coeffs = coeffs_ref[...]
    rate = rate_ref[...]
    z, step, cum, cum_rows = steps_of(logits_ref[...], bias_ref[...], rate, mask)
    last = cum[length - 1 : length, :]
    rest = jnp.exp(last - cum)
    lead = rest * step
    b_part, c_part = coeffs[:, :state], coeffs[:, state:]
    scores = mm(c_part, b_part, 1, 1) * (mask / state)
    step_parts, lead_parts, reach_parts = split(step), split(lead), split(jnp.exp(cum) / state)
    skip_parts = split(jnp.broadcast_to(skip_ref[...], (8, heads)))
    d_scores = jnp.zeros((length, length), f32)
    d_b = jnp.zeros((length, state), f32)
    d_c = jnp.zeros((length, state), f32)
    d_end = jnp.zeros((heads, state), f32)
    for j, sl in blocks(width):
        x, grad = x_ref[:, sl], grad_ref[:, sl]
        wide_map = lanes_of[:, sl]
        step_wide = expand(step_parts, wide_map)
        lead_wide = expand(lead_parts, wide_map)
        reach_wide = expand(reach_parts, wide_map)
        stepped, out, d_stepped, d_scores = scan_block(
            j, x, grad, step_wide, scores, cum, cum_rows, heads, width, d_scores
        )
        x, wide = x.astype(f32), grad.astype(f32)
        before, later = state_ref[sl, :], later_ref[sl, :]
        carried = mm(c_part, before, 1, 1) * reach_wide
        d_c = d_c + mm((wide * reach_wide).astype(bf16), before, 1, 0)
        d_b = d_b + mm((x * lead_wide).astype(bf16), later, 1, 0)
        d_scaled = mm(b_part, later, 1, 1)
        both = split(before.astype(f32) * later.astype(f32))
        d_end = d_end + mm(wide_map, both[0], 1, 0) + mm(wide_map, both[1], 1, 0)
        total = out + carried
        skip = expand(skip_parts, wide_map)[0:1, :]
        mix_ref[:, sl] = total + skip * x
        d_x = (step_wide * d_stepped + d_scaled * lead_wide).astype(bf16)
        dn_ref[:, sl] = d_x + (wide * skip).astype(bf16)
        put((a_hi, a_lo), sl, wide * total - stepped.astype(f32) * d_stepped)
        put((b_hi, b_lo), sl, x * d_stepped)
        put((c_hi, c_lo), sl, x * d_scaled)
    d_lead = head_sums(c_hi, c_lo, lanes_of)
    d_step = head_sums(b_hi, b_lo, lanes_of) + d_lead * rest
    fall = d_lead * lead
    d_cum = head_sums(a_hi, a_lo, lanes_of) - fall
    ones = jnp.ones((8, state), f32)
    end_sum = exact(ones, d_end, 1, 1)[0:1, :] * jnp.exp(last)
    end_sum = end_sum + jnp.sum(fall, axis=0, keepdims=True)
    d_log = exact(mask, d_cum, 0, 0) + end_sum
    d_logits = (jax.nn.sigmoid(z) * (d_step - rate * d_log)).astype(bf16)
    d_scores = (d_scores * (mask / state)).astype(bf16)
    d_coeffs = jnp.concatenate(
        [mm(d_scores, c_part, 0, 0) + d_b, mm(d_scores, b_part, 1, 0) + d_c], axis=1
    ).astype(bf16)
    inverse = inverse_ref[...]
    if gstep_in is None:
        tall_coeffs = jnp.concatenate([gproj_in[1][...], d_coeffs], axis=0)
        tall_logits = jnp.concatenate([gproj_in[2][...], d_logits], axis=0)
    for _, sl in blocks(width):
        pre = (
            dn_ref[:, sl].astype(f32)
            + mm(d_coeffs, proj_ref[sl, :], 1, 1)
            + mm(d_logits, step_ref[:, sl], 1, 0)
        )
        pre_ref[:, sl] = pre
        scaled = pre * (tok_ref[:, sl].astype(f32) * inverse)
        gmod_ref[0:1, sl] = jnp.sum(pre, axis=0, keepdims=True)
        gmod_ref[1:2, sl] = jnp.sum(scaled, axis=0, keepdims=True)
        if gstep_in is None:
            tall = jnp.concatenate([gproj_in[0][:, sl], x_ref[:, sl]], axis=0)
            gproj_ref[sl, :] = mm(tall, tall_coeffs, 0, 0)
            gstep_ref[:, sl] = mm(tall_logits, tall, 0, 0)
        else:
            gproj_ref[sl, :] = (gproj_in[sl, :] + mm(x_ref[:, sl], d_coeffs, 0, 0)).astype(bf16)
            gstep_ref[:, sl] = (gstep_in[:, sl] + mm(d_logits, x_ref[:, sl], 0, 0)).astype(bf16)


def last_kernel(tok_ref, inverse_ref, gain_ref, mix_ref, pre_ref, time_ref, back_ref, out_ref, dtok_ref):
    length, width = tok_ref.shape
    inverse = inverse_ref[...]
    total = jnp.zeros((length, LANES), f32)
    for _, sl in blocks(width):
        out_ref[:, sl] = (mix_ref[:, sl] + time_ref[:, sl].astype(f32)).astype(bf16)
        grad = (pre_ref[:, sl] + back_ref[:, sl].astype(f32)) * (1.0 + gain_ref[:, sl])
        total = total + grad * tok_ref[:, sl].astype(f32)
    inner = jnp.sum(total, axis=1, keepdims=True) / width
    inner = inner * inverse * inverse * inverse
    for _, sl in blocks(width):
        grad = (pre_ref[:, sl] + back_ref[:, sl].astype(f32)) * (1.0 + gain_ref[:, sl])
        dtok_ref[:, sl] = (grad * inverse - tok_ref[:, sl].astype(f32) * inner).astype(bf16)


def last_fast_kernel(tok_ref, inverse_ref, gain_ref, mix_ref, pre_ref, came_ref, *outs):
    class Packed:
        def __init__(self, which):
            self.which = which

        def __getitem__(self, at):
            value = came_ref[:, self.which, :, at[1]].astype(f32)
            return value.reshape(value.shape[0] * value.shape[1], LANES)

    last_kernel(tok_ref, inverse_ref, gain_ref, mix_ref, pre_ref, Packed(0), Packed(1), *outs)


def in_hbm(array):
    return pltpu.with_memory_space_constraint(array, pltpu.MemorySpace.HBM)


def call(kernel, outs, scratch=(), name=None, specs=None, hbm_outs=()):
    shapes = [
        pltpu.MemorySpace.HBM(s, d) if n in hbm_outs else jax.ShapeDtypeStruct(s, d)
        for n, (s, d) in enumerate(outs)
    ]
    where = {"s": pltpu.SMEM, "v": pltpu.VMEM, "h": pltpu.MemorySpace.HBM}
    spaces = {}
    if specs:
        spaces["in_specs"] = [pl.BlockSpec(memory_space=where[c]) for c in specs]
        spaces["out_specs"] = [
            pl.BlockSpec(memory_space=where["h" if n in hbm_outs else "v"]) for n in range(len(outs))
        ]
    return pl.pallas_call(
        kernel,
        out_shape=shapes,
        **spaces,
        scratch_shapes=[pltpu.VMEM(*s) if isinstance(s, tuple) else s for s in scratch],
        compiler_params=pltpu.CompilerParams(vmem_limit_bytes=48 << 20),
        name=name,
    )


def rows_in_order(part):
    if lax.axis_size("row") != 2:
        return lax.all_gather(part, "row")
    other = lax.ppermute(part, "row", [(0, 1), (1, 0)])
    first = lax.axis_index("row") == 0
    return jnp.stack([jnp.where(first, part, other), jnp.where(first, other, part)])


def rows_sum(part):
    if lax.axis_size("row") != 2:
        return lax.psum(part, "row")
    return part + lax.ppermute(part, "row", [(0, 1), (1, 0)])


def chain(own, decay, forward):
    count = lax.axis_size("row")
    hops = [(i, i + 1) if forward else (i + 1, i) for i in range(count - 1)]
    if count == 1:
        return jnp.zeros_like(own)
    arrived = lax.ppermute(own, "row", hops)
    wide = jnp.repeat(decay[0], own.shape[0] // decay.shape[1])[:, None]
    for _ in range(count - 2):
        passed = wide * arrived.astype(f32) + own.astype(f32)
        arrived = lax.ppermute(passed.astype(bf16), "row", hops)
    return arrived


def per_device(
    tokens,
    cotangent,
    timestep,
    mod_weight,
    proj_weight,
    step_weight,
    step_bias,
    rate_space,
    rate_time,
    skip_gain,
):
    frames = lax.axis_size("frame")
    rows = lax.axis_size("row")
    frame_id = lax.axis_index("frame")
    row_id = lax.axis_index("row")
    width = tokens.shape[-1]
    length = tokens.shape[1] * tokens.shape[2]
    clips = timestep.shape[0]
    clip_id = frame_id // (frames // clips)
    sites = length // frames
    heads = rate_space.shape[0]
    depth, pair = proj_weight.shape
    state = pair // 2
    mod_cols = mod_weight.shape[1]
    factor = (frames * rows * length) ** (-0.5)
    tok = tokens.reshape(length, width)
    grad = cotangent.reshape(length, width)

    activated = time_embed(timestep, mod_weight.shape[0]).astype(bf16)
    own_mod = jnp.dot(activated, mod_weight, preferred_element_type=f32)
    high = lax.reduce_precision(own_mod, 8, 7)
    own_mod = jnp.stack([high, own_mod - high]).astype(bf16)

    part = depth // rows
    own_proj = lax.dynamic_slice_in_dim(proj_weight, row_id * part, part, 0)
    to_all = [
        to_tiles(own_proj[None]),
        to_tiles(step_weight.T[None]),
        own_mod.reshape(1, -1, LANES),
    ]
    to_all = jnp.concatenate(to_all, axis=1)
    to_all = jnp.pad(to_all, ((0, 0), (0, -to_all.shape[1] % 8), (0, 0)))
    count = sites * width // LANES
    got = exchange(
        jnp.concatenate(
            [
                to_tiles(tok.reshape(frames, sites, width)),
                to_tiles(grad.reshape(frames, sites, width)),
                jnp.broadcast_to(to_all, (frames,) + to_all.shape[1:]),
            ],
            axis=1,
        )
    )
    site_tok = from_tiles(got[:, :count], sites, width).reshape(length, width)
    site_grad = from_tiles(got[:, count : 2 * count], sites, width).reshape(length, width)
    at = 2 * count
    size = part * pair // LANES
    proj_full = rows_in_order(got[:, at : at + size])
    proj_full = from_tiles(proj_full.reshape(rows * frames, size, LANES), part, pair)
    proj_full = proj_full.reshape(rows, frames, part, pair).transpose(1, 0, 2, 3)
    proj_full = proj_full.reshape(width, pair)
    at += size
    size = heads * depth // LANES
    step_full = from_tiles(got[:, at : at + size], heads, depth)
    step_full = step_full.transpose(1, 0, 2).reshape(heads, width)
    at += size
    size = 2 * clips * mod_cols // LANES
    mod_full = got[:, at : at + size].reshape(frames, 2, clips, mod_cols).astype(f32)
    mod_full = (mod_full[:, 0] + mod_full[:, 1]).transpose(1, 0, 2).reshape(clips, 2 * width)
    shift, gain = mod_full[:, :width], mod_full[:, width:]

    bias = step_bias[None]
    wide = (length, width)
    site_out, site_back, gproj, gstep, site_gmod = call(
        functools.partial(site_kernel, sites),
        [(wide, bf16), (wide, bf16), ((width, pair), f32), ((heads, width), f32), ((2 * clips, width), f32)],
        [(wide, bf16)] * 6,
        name="site",
    )(site_tok, site_grad, shift, gain, proj_full, step_full, bias, rate_time[None])

    came = exchange(
        jnp.concatenate(
            [
                to_tiles(site_out.reshape(frames, sites, width)),
                to_tiles(site_back.reshape(frames, sites, width)),
            ],
            axis=1,
        )
    )
    time_out = from_tiles(came[:, :count], sites, width).reshape(length, width)
    time_back = from_tiles(came[:, count:], sites, width).reshape(length, width)

    own_shift = lax.dynamic_slice_in_dim(shift, clip_id, 1, 0)
    own_gain = lax.dynamic_slice_in_dim(gain, clip_id, 1, 0)
    normed, coeffs, logits, inverse, decay, end_own, start_grad = call(
        band_kernel,
        [
            (wide, bf16),
            ((length, pair), bf16),
            ((length, heads), bf16),
            ((length, 1), f32),
            ((1, heads), f32),
            ((width, state), bf16),
            ((width, state), bf16),
        ],
        name="band",
    )(tok, grad, own_shift, own_gain, proj_full, step_full, bias, rate_space[None])
    state_in = chain(end_own, decay, True)
    later_grad = chain(start_grad, decay, False)
    mix, pre, gproj, gstep, gmod = call(
        space_kernel,
        [(wide, f32), (wide, f32), ((width, pair), bf16), ((heads, width), bf16), ((2, width), f32)],
        [(wide, bf16)] * 7,
        name="space",
    )(
        tok,
        grad,
        normed,
        coeffs,
        logits,
        inverse,
        proj_full,
        step_full,
        bias,
        rate_space[None],
        skip_gain[None],
        state_in,
        later_grad,
        gproj,
        gstep,
    )

    picked = (jnp.arange(clips) == clip_id).astype(f32)[:, None]
    gmod = jnp.concatenate(
        [site_gmod[:clips] + picked * gmod[0:1], site_gmod[clips:] + picked * gmod[1:2]], axis=1
    )
    gmod = gmod.reshape(clips, frames, mod_cols).transpose(1, 0, 2).astype(bf16)
    sent = jnp.concatenate(
        [
            to_tiles(gproj.reshape(frames, depth, pair)),
            to_tiles(gstep.reshape(heads, frames, depth).transpose(1, 0, 2)),
            gmod.reshape(frames, -1, LANES) if (clips * mod_cols) % LANES == 0 else gmod,
        ],
        axis=1,
    )
    size = sent.shape[1]
    sent = jnp.pad(sent, ((0, 0), (0, -size % 8), (0, 0)))
    sums = jnp.sum(exchange(sent).astype(f32), axis=0, keepdims=True)
    sums = rows_sum(sums) * factor
    at = depth * pair // LANES
    grad_proj = from_tiles(sums[:, :at], depth, pair)[0]
    size = heads * depth // LANES
    grad_step = from_tiles(sums[:, at : at + size], heads, depth)[0].T
    at += size
    size = clips * mod_cols // LANES
    mod_sum = sums[0, at : at + size].reshape(clips, mod_cols)
    grad_mod = jnp.dot(activated.astype(f32).T, mod_sum, precision=EXACT)

    mixed, d_tokens = call(last_kernel, [(wide, bf16), (wide, bf16)], name="last")(
        tok, inverse, own_gain, mix, pre, time_out, time_back
    )
    return (mixed.reshape(tokens.shape), d_tokens.reshape(tokens.shape), grad_proj, grad_step, grad_mod)


def fits(mesh, tokens, timestep, proj_weight, step_weight):
    frames, rows = mesh.shape["frame"], mesh.shape["row"]
    length, width = tokens.shape[2] * tokens.shape[1] // rows, tokens.shape[3]
    return (
        rows == 2
        and frames == 16
        and timestep.shape[0] == 1
        and length == LANES
        and length // frames == 8
        and width // frames == LANES
        and proj_weight.shape[1] == 2 * LANES
        and step_weight.shape[1] % 32 == 0
    )


def spread_over_frames(own, radix=4):
    frames = radix * radix

    def others(piece, stride):
        return [piece] + [
            lax.ppermute(piece, "frame", [(i, i ^ (d * stride)) for i in range(frames)])
            for d in range(1, radix)
        ]

    far = jnp.stack(others(own, radix))
    return jnp.concatenate(others(far, 1))


def sum_over_frames(keep, given, radix):
    def gathered(pieces, stride):
        frames = radix * radix
        return [pieces[0]] + [
            lax.ppermute(pieces[d], "frame", [(i, i ^ (d * stride)) for i in range(frames)])
            for d in range(1, radix)
        ]

    def total(pieces):
        value = pieces[0].astype(f32)
        for piece in pieces[1:]:
            value = value + piece.astype(f32)
        return value

    parts = [slice(d * radix, (d + 1) * radix) for d in range(radix)]
    near = [total([keep[p], given[p]]).astype(bf16) for p in parts]
    near = total(gathered(near, 1)).astype(bf16)
    return total(gathered([near[d] for d in range(radix)], radix))


def per_device_fast(
    tokens,
    cotangent,
    timestep,
    mod_weight,
    proj_weight,
    step_weight,
    step_bias,
    rate_space,
    rate_time,
    skip_gain,
):
    frames = lax.axis_size("frame")
    rows = lax.axis_size("row")
    ids = jnp.stack([lax.axis_index("frame"), lax.axis_index("row")]).astype(jnp.int32)
    width = tokens.shape[-1]
    length = tokens.shape[1] * tokens.shape[2]
    sites = length // frames
    heads = rate_space.shape[0]
    depth, pair = proj_weight.shape
    state = pair // 2
    mod_cols = mod_weight.shape[1]
    factor = (frames * rows * length) ** (-0.5)
    tok = tokens.reshape(length, width)
    grad = cotangent.reshape(length, width)
    wide = (length, width)
    bias = step_bias[None]
    swap = [(0, 1), (1, 0)]

    packed = (frames, 2, sites, width)
    size = depth // 2 * pair // LANES + heads // 2 + 8
    activated = time_embed(timestep, mod_weight.shape[0]).astype(bf16)
    sent, payload = call(
        start_kernel,
        [(packed, bf16), ((size, LANES), bf16)],
        [
            ((depth, pair), bf16),
            ((heads, depth), bf16),
            (mod_weight.shape, bf16),
            pltpu.SemaphoreType.DMA((5,)),
        ],
        name="start",
        specs="shhhhhv",
        hbm_outs=(0,),
    )(
        ids,
        in_hbm(tok.reshape(frames, sites, width)),
        in_hbm(grad.reshape(frames, sites, width)),
        in_hbm(proj_weight),
        in_hbm(step_weight.T),
        in_hbm(mod_weight),
        activated,
    )
    got = exchange(sent)
    payload = spread_over_frames(payload)
    other = lax.ppermute(payload, "row", swap)
    proj_full, step_full, shift, gain = call(
        functools.partial(unpack_kernel, 4),
        [((width, pair), bf16), ((heads, width), bf16), ((1, width), f32), ((1, width), f32)],
        name="unpack",
        specs="svv",
    )(ids, payload, other)

    sent, site_x, site_dc, site_dl, site_gmod = call(
        functools.partial(site_fast_kernel, sites),
        [
            (packed, bf16),
            (wide, bf16),
            ((length, pair), bf16),
            ((length, heads), bf16),
            ((2, width), f32),
        ],
        [(wide, bf16), (wide, bf16), (packed, bf16), pltpu.SemaphoreType.DMA((4,))]
        + [(wide, bf16)] * 5,
        name="site",
        specs="vvvvvvv",
        hbm_outs=(0,),
    )(got, shift, gain, proj_full, step_full, bias, rate_time[None])
    came = exchange(sent)

    normed, coeffs, logits, inverse, _, give = call(
        band_fast_kernel,
        [
            (wide, bf16),
            ((length, pair), bf16),
            ((length, heads), bf16),
            ((length, 1), f32),
            ((1, heads), f32),
            ((width, state), bf16),
        ],
        name="band",
        specs="svvvvvvvv",
    )(ids, tok, grad, shift, gain, proj_full, step_full, bias, rate_space[None])
    arrived = lax.ppermute(give, "row", swap)
    halves = (frames, size, LANES)
    mix, pre, keep, give, _ = call(
        functools.partial(space_fast_kernel, 4),
        [(wide, f32), (wide, f32), (halves, bf16), (halves, bf16), ((2, width), f32)],
        [(wide, bf16)] * 7,
        name="space",
        specs="s" + "v" * 16,
    )(
        ids,
        site_gmod,
        site_x,
        site_dc,
        site_dl,
        arrived,
        tok,
        grad,
        normed,
        coeffs,
        logits,
        inverse,
        proj_full,
        step_full,
        bias,
        rate_space[None],
        skip_gain[None],
    )
    given = lax.ppermute(give, "row", swap)
    terms = sum_over_frames(keep, given, 4)
    other = lax.ppermute(terms, "row", swap)
    grad_proj, grad_step, grad_mod = call(
        functools.partial(finish_kernel, factor),
        [((depth, pair), f32), ((heads, depth), f32), ((mod_weight.shape[0], mod_cols), f32)],
        name="finish",
        specs="svvv",
    )(ids, terms, other, activated.astype(f32).T)
    mixed, d_tokens = call(last_fast_kernel, [(wide, bf16), (wide, bf16)], name="last")(
        tok, inverse, gain, mix, pre, came
    )
    return (mixed.reshape(tokens.shape), d_tokens.reshape(tokens.shape), grad_proj, grad_step.T, grad_mod)


def solution(mesh):
    placed = (
        P("frame", "row", None, None),
        P("frame", "row", None, None),
        P(),
        P(None, "frame"),
        P("frame", None),
        P("frame", None),
        P(),
        P(),
        P(),
        P(),
    )
    outs = (
        P("frame", "row", None, None),
        P("frame", "row", None, None),
        P("frame", None),
        P("frame", None),
        P(None, "frame"),
    )

    def step(tokens, cotangent, timestep, mod_weight, proj_weight, step_weight, *rest):
        fast = fits(mesh, tokens, timestep, proj_weight, step_weight)
        body = per_device_fast if fast else per_device
        return jax.shard_map(
            body, mesh=mesh, in_specs=placed, out_specs=outs, check_vma=False
        )(tokens, cotangent, timestep, mod_weight, proj_weight, step_weight, *rest)

    return step
```

```python
import functools
import math

import jax
import jax.numpy as jnp
from jax import lax
from jax.experimental import pallas as pl
from jax.experimental.pallas import tpu as pltpu
from jax.sharding import PartitionSpec as P


norm_eps = 1e-05
LANES = 128
f32 = jnp.float32
bf16 = jnp.bfloat16
EXACT = lax.Precision.HIGHEST


def time_embed(timestep, embed_dim):
    half_dim = embed_dim // 2
    frequency = jnp.exp(-math.log(10000.0) * jnp.arange(half_dim, dtype=f32) / half_dim)
    angles = timestep.astype(f32)[:, None] * frequency[None, :]
    return jax.nn.silu(jnp.concatenate([jnp.cos(angles), jnp.sin(angles)], axis=1))


def to_tiles(a):
    f, r, c = a.shape
    if r % 8 == 0 and c % LANES == 0:
        a = a.reshape(f, r // 8, 8, c // LANES, LANES).transpose(0, 1, 3, 2, 4)
    return a.reshape(f, r * c // LANES, LANES)


def from_tiles(a, r, c):
    f = a.shape[0]
    if r % 8 == 0 and c % LANES == 0:
        a = a.reshape(f, r // 8, c // LANES, 8, LANES).transpose(0, 1, 3, 2, 4)
    return a.reshape(f, r, c)


def exchange(packed):
    return lax.all_to_all(packed, "frame", split_axis=0, concat_axis=0, tiled=True)


def mm(a, b, ca, cb):
    return lax.dot_general(a, b, (((ca,), (cb,)), ((), ())), preferred_element_type=f32)


def exact(a, b, ca, cb):
    return lax.dot_general(
        a, b, (((ca,), (cb,)), ((), ())), preferred_element_type=f32, precision=EXACT
    )


def split(a):
    high = a.astype(bf16)
    return high, (a - high.astype(f32)).astype(bf16)


def head_map(heads, width):
    size = width // heads
    own = lax.broadcasted_iota(jnp.int32, (heads, width), 0)
    lane = lax.broadcasted_iota(jnp.int32, (heads, width), 1)
    return jnp.where(lane // size == own, 1.0, 0.0).astype(bf16)


def sequence_mask(length, sites):
    later = lax.broadcasted_iota(jnp.int32, (length, length), 0)
    earlier = lax.broadcasted_iota(jnp.int32, (length, length), 1)
    keep = later >= earlier
    if sites > 1:
        keep = keep & (later % sites == earlier % sites)
    return jnp.where(keep, 1.0, 0.0).astype(f32)


def blocks(width):
    return [(j, slice(j * LANES, (j + 1) * LANES)) for j in range(width // LANES)]


def spread_rows(rows, length):
    count = rows.shape[0]
    if count == 1:
        return rows
    part = (length // count, rows.shape[1])
    return jnp.concatenate([jnp.broadcast_to(rows[c : c + 1], part) for c in range(count)], axis=0)


def normalize_into(tok_ref, shift_ref, gain_ref, x_ref):
    length, width = tok_ref.shape
    total = jnp.zeros((length, LANES), f32)
    for _, sl in blocks(width):
        v = tok_ref[:, sl].astype(f32)
        total = total + v * v
    mean = jnp.sum(total, axis=1, keepdims=True) / width
    inverse = lax.rsqrt(mean + norm_eps)
    for _, sl in blocks(width):
        unit = tok_ref[:, sl].astype(f32) * inverse
        gain = spread_rows(gain_ref[:, sl], length)
        shift = spread_rows(shift_ref[:, sl], length)
        x_ref[:, sl] = (unit * (1.0 + gain) + shift).astype(bf16)
    return inverse


def steps_of(logits, bias, rate, mask):
    z = logits.astype(f32) + bias
    step = jnp.maximum(z, 0.0) + jnp.log1p(jnp.exp(-jnp.abs(z)))
    log_decay = -step * rate
    cum = exact(mask, log_decay, 1, 0)
    cum_rows = exact(log_decay, mask, 0, 1)
    return z, step, cum, cum_rows


def expand(parts, lanes_of):
    return mm(parts[0], lanes_of, 1, 0) + mm(parts[1], lanes_of, 1, 0)


def scan_block(j, x, grad, step_wide, scores, cum, cum_rows, heads, width, d_scores):
    size = width // heads
    per_block = LANES // size
    stepped = (x.astype(f32) * step_wide).astype(bf16)
    lane = lax.broadcasted_iota(jnp.int32, x.shape, 1)
    weights, steppeds, grads = [], [], []
    for i in range(per_block):
        h = j * per_block + i
        decay = jnp.exp(jnp.minimum(cum[:, h : h + 1] - cum_rows[h : h + 1, :], 0.0))
        inside = lane // size == i
        own_grad = jnp.where(inside, grad, jnp.zeros_like(grad))
        d_weight = mm(own_grad, stepped, 1, 1)
        d_scores = d_scores + d_weight * decay
        weights.append((scores * decay).astype(bf16))
        steppeds.append(jnp.where(inside, stepped, jnp.zeros_like(stepped)))
        grads.append(own_grad)
    out = mm(jnp.concatenate(weights, axis=1), jnp.concatenate(steppeds, axis=0), 1, 0)
    d_stepped = mm(jnp.concatenate(weights, axis=0), jnp.concatenate(grads, axis=0), 0, 0)
    return stepped, out, d_stepped, d_scores


def head_sums(high_ref, low_ref, lanes_of):
    return mm(high_ref[...], lanes_of, 1, 1) + mm(low_ref[...], lanes_of, 1, 1)


def put(refs, sl, value):
    high, low = split(value)
    refs[0][:, sl] = high
    refs[1][:, sl] = low


def start_kernel(ids_ref, tok_ref, grad_ref, proj_hbm, step_hbm, mod_hbm, active_ref, sent_ref, pay_ref,
                 proj_ref, step_ref, mod_ref, both_ref, sems):
    copies = [
        pltpu.make_async_copy(src, dst, sems.at[n])
        for n, (src, dst) in enumerate(
            [
                (proj_hbm, proj_ref),
                (step_hbm, step_ref),
                (mod_hbm, mod_ref),
                (tok_ref, both_ref.at[:, 0]),
                (grad_ref, both_ref.at[:, 1]),
                (both_ref.at[:, 0], sent_ref.at[:, 0]),
                (both_ref.at[:, 1], sent_ref.at[:, 1]),
            ]
        )
    ]
    for copy in copies[:5]:
        copy.start()
    copies[3].wait()
    copies[5].start()
    copies[4].wait()
    copies[6].start()
    row = ids_ref[1]
    part, pair = proj_ref.shape[0] // 2, proj_ref.shape[1]
    copies[0].wait()
    own = proj_ref[pl.ds(pl.multiple_of(row * part, part), part), :]
    at = 0
    for _, sl in blocks(pair):
        pay_ref[at : at + part, :] = own[:, sl]
        at += part
    copies[1].wait()
    part = step_ref.shape[0] // 2
    pay_ref[at : at + part, :] = step_ref[pl.ds(pl.multiple_of(row * part, part), part), :]
    at += part
    copies[2].wait()
    own = mm(active_ref[...], mod_ref[...], 1, 0)
    high = own.astype(bf16).astype(f32)
    pieces = [piece[:, sl] for piece in (high, own - high) for _, sl in blocks(own.shape[1])]
    pieces.append(jnp.zeros((8 - len(pieces), LANES), f32))
    pay_ref[at : at + 8, :] = jnp.concatenate(pieces, axis=0).astype(bf16)
    copies[5].wait()
    copies[6].wait()


def unpack_kernel(radix, ids_ref, own_ref, other_ref, proj_ref, step_ref, shift_ref, gain_ref):
    me, row = ids_ref[0], ids_ref[1]
    width, pair = proj_ref.shape
    frames = own_ref.shape[0]
    depth = width // frames
    part, heads = depth // 2, step_ref.shape[0] // 2
    cols = 2 * width // frames
    for i in range(frames):
        source = jnp.bitwise_xor(me, (i % radix) * radix + i // radix)
        for ref, half in ((own_ref, row), (other_ref, 1 - row)):
            rows = pl.ds(pl.multiple_of(source * depth + half * part, part), part)
            at = 0
            for _, sl in blocks(pair):
                proj_ref[rows, sl] = ref[i, at : at + part, :]
                at += part
            rows = pl.ds(pl.multiple_of(half * heads, heads), heads)
            lanes = pl.ds(pl.multiple_of(source * depth, depth), depth)
            step_ref[rows, lanes] = ref[i, at : at + heads, :]
            at += heads
        own = own_ref[i, at : at + 8, :].astype(f32)
        count = cols // LANES
        lanes_at = jnp.bitwise_and(source, frames // 2 - 1) * cols
        for k in range(count):
            value = own[k : k + 1, :] + own[count + k : count + k + 1, :]
            lanes = pl.ds(pl.multiple_of(lanes_at + k * LANES, LANES), LANES)

            @pl.when(source < frames // 2)
            def _():
                shift_ref[:, lanes] = value

            @pl.when(source >= frames // 2)
            def _():
                gain_ref[:, lanes] = value


def finish_kernel(factor, ids_ref, own_ref, other_ref, active_ref, proj_ref, step_ref, mod_ref):
    row = ids_ref[1]
    pair = proj_ref.shape[1]
    part, heads = proj_ref.shape[0] // 2, step_ref.shape[0] // 2
    for ref, half in ((own_ref, row), (other_ref, 1 - row)):
        rows = pl.ds(pl.multiple_of(half * part, part), part)
        at = 0
        for _, sl in blocks(pair):
            proj_ref[rows, sl] = ref[at : at + part, :] * factor
            at += part
        step_ref[pl.ds(pl.multiple_of(half * heads, heads), heads), :] = ref[at : at + heads, :] * factor
        at += heads
    for k, sl in blocks(mod_ref.shape[1]):
        mod_ref[:, sl] = active_ref[...] * (own_ref[at + k : at + k + 1, :] * factor)


def site_fast_kernel(sites, got_ref, *refs):
    inputs, (sent_hbm, x_hbm, gmod_hbm, dc_ref, dl_ref) = refs[:6], refs[6:11]
    tok_ref, grad_ref, sent_ref, x_ref, gmod_ref, sems = refs[11:17]
    scratch = refs[17:]
    frames, width = got_ref.shape[0], got_ref.shape[3]
    for _, sl in blocks(width):
        for ref, which in ((tok_ref, 0), (grad_ref, 1)):
            value = got_ref[:, which, :, sl].astype(f32)
            ref[:, sl] = value.reshape(frames * sites, LANES).astype(bf16)

    parts = 2
    share = width // parts
    copies = []

    def begin(source, target):
        copy = pltpu.make_async_copy(source, target, sems.at[len(copies)])
        copy.start()
        copies.append(copy)

    def send(which, p):
        at = (slice(None), which, slice(None), slice(p * share, (p + 1) * share))
        begin(sent_ref.at[at], sent_hbm.at[at])

    class Packed:
        def __init__(self, which):
            self.which = which

        def __setitem__(self, at, value):
            if not copies:
                begin(x_ref, x_hbm)
            value = value.astype(f32).reshape(frames, sites, LANES)
            sent_ref[:, self.which, :, at[1]] = value.astype(bf16)
            if at[1].stop % share == 0:
                send(self.which, at[1].stop // share - 1)

    site_kernel(
        sites, tok_ref, grad_ref, *inputs, Packed(0), Packed(1), dc_ref, dl_ref, gmod_ref, x_ref, *scratch
    )
    begin(gmod_ref, gmod_hbm)
    for copy in copies:
        copy.wait()


def site_kernel(
    sites,
    tok_ref,
    grad_ref,
    shift_ref,
    gain_ref,
    proj_ref,
    step_ref,
    bias_ref,
    rate_ref,
    out_ref,
    back_ref,
    gproj_ref,
    gstep_ref,
    gmod_ref,
    x_ref,
    dn_ref,
    a_hi,
    a_lo,
    b_hi,
    b_lo,
):
    length, width = tok_ref.shape
    heads = step_ref.shape[0]
    state = proj_ref.shape[1] // 2
    clips = shift_ref.shape[0]
    inverse = normalize_into(tok_ref, shift_ref, gain_ref, x_ref)
    lanes_of = head_map(heads, width)
    mask = sequence_mask(length, sites)
    coeffs = mm(x_ref[...], proj_ref[...], 1, 0).astype(bf16)
    logits = mm(x_ref[...], step_ref[...], 1, 1).astype(bf16)
    rate = rate_ref[...]
    z, step, cum, cum_rows = steps_of(logits, bias_ref[...], rate, mask)
    b_part, c_part = coeffs[:, :state], coeffs[:, state:]
    scores = mm(c_part, b_part, 1, 1) * (mask / state)
    step_parts = split(step)
    d_scores = jnp.zeros((length, length), f32)
    for j, sl in blocks(width):
        x, grad = x_ref[:, sl], grad_ref[:, sl]
        step_wide = expand(step_parts, lanes_of[:, sl])
        stepped, out, d_stepped, d_scores = scan_block(
            j, x, grad, step_wide, scores, cum, cum_rows, heads, width, d_scores
        )
        out_ref[:, sl] = out.astype(bf16)
        dn_ref[:, sl] = (step_wide * d_stepped).astype(bf16)
        put((a_hi, a_lo), sl, grad.astype(f32) * out - stepped.astype(f32) * d_stepped)
        put((b_hi, b_lo), sl, x.astype(f32) * d_stepped)
    d_cum = head_sums(a_hi, a_lo, lanes_of)
    d_step = head_sums(b_hi, b_lo, lanes_of)
    d_log = exact(mask, d_cum, 0, 0)
    d_logits = (jax.nn.sigmoid(z) * (d_step - rate * d_log)).astype(bf16)
    d_scores = (d_scores * (mask / state)).astype(bf16)
    d_coeffs = jnp.concatenate(
        [mm(d_scores, c_part, 0, 0), mm(d_scores, b_part, 1, 0)], axis=1
    ).astype(bf16)
    for _, sl in blocks(width):
        back = (
            dn_ref[:, sl].astype(f32)
            + mm(d_coeffs, proj_ref[sl, :], 1, 1)
            + mm(d_logits, step_ref[:, sl], 1, 0)
        ).astype(bf16)
        back_ref[:, sl] = back
        back = back.astype(f32)
        scaled = back * (tok_ref[:, sl].astype(f32) * inverse)
        for c in range(clips):
            rows = slice(c * (length // clips), (c + 1) * (length // clips))
            gmod_ref[c : c + 1, sl] = jnp.sum(back[rows], axis=0, keepdims=True)
            gmod_ref[clips + c : clips + c + 1, sl] = jnp.sum(scaled[rows], axis=0, keepdims=True)
        if gproj_ref.shape == (width, 2 * state):
            gproj_ref[sl, :] = mm(x_ref[:, sl], d_coeffs, 0, 0)
            gstep_ref[:, sl] = mm(d_logits, x_ref[:, sl], 0, 0)
    if gproj_ref.shape != (width, 2 * state):
        gproj_ref[...] = d_coeffs
        gstep_ref[...] = d_logits


def band_fast_kernel(ids_ref, *refs):
    give_ref = refs[-1]
    band_kernel(*refs[:-1], None, give_ref, first=ids_ref[1] == 0)


def band_kernel(
    tok_ref,
    grad_ref,
    shift_ref,
    gain_ref,
    proj_ref,
    step_ref,
    bias_ref,
    rate_ref,
    x_ref,
    coeffs_ref,
    logits_ref,
    inverse_ref,
    decay_ref,
    end_ref,
    own_ref,
    first=None,
):
    length, width = tok_ref.shape
    heads = step_ref.shape[0]
    state = proj_ref.shape[1] // 2
    inverse_ref[...] = normalize_into(tok_ref, shift_ref, gain_ref, x_ref)
    lanes_of = head_map(heads, width)
    mask = sequence_mask(length, 1)
    coeffs = mm(x_ref[...], proj_ref[...], 1, 0).astype(bf16)
    logits = mm(x_ref[...], step_ref[...], 1, 1).astype(bf16)
    coeffs_ref[...] = coeffs
    logits_ref[...] = logits
    _, step, cum, _ = steps_of(logits, bias_ref[...], rate_ref[...], mask)
    last = cum[length - 1 : length, :]
    decay_ref[...] = jnp.exp(last)
    lead = split(jnp.exp(last - cum) * step)
    reach = split(jnp.exp(cum) / state)
    b_part, c_part = coeffs[:, :state], coeffs[:, state:]
    if first is not None:
        gain = split(jnp.where(first, jnp.exp(last - cum) * step, jnp.exp(cum) / state))
        other = jnp.where(first, b_part, c_part)
        for _, sl in blocks(width):
            value = jnp.where(first, x_ref[:, sl], grad_ref[:, sl]).astype(f32)
            value = (value * expand(gain, lanes_of[:, sl])).astype(bf16)
            own_ref[sl, :] = mm(value, other, 0, 0).astype(bf16)
        return
    for _, sl in blocks(width):
        lead_wide = expand(lead, lanes_of[:, sl])
        reach_wide = expand(reach, lanes_of[:, sl])
        scaled = (x_ref[:, sl].astype(f32) * lead_wide).astype(bf16)
        faded = (grad_ref[:, sl].astype(f32) * reach_wide).astype(bf16)
        end_ref[sl, :] = mm(scaled, b_part, 0, 0).astype(bf16)
        own_ref[sl, :] = mm(faded, c_part, 0, 0).astype(bf16)


def terms_kernel(radix, ids_ref, x_ref, dc_ref, dl_ref, gmod_ref, site_x, site_dc, site_dl, site_gmod,
                 keep_ref, give_ref):
    me, first = ids_ref[0], ids_ref[1] == 0
    width = x_ref.shape[1]
    coeffs = jnp.concatenate([dc_ref[...], site_dc[...]], axis=0)
    logits = jnp.concatenate([dl_ref[...], site_dl[...]], axis=0)
    frames = keep_ref.shape[0]
    share = 2 * width // LANES // frames

    def put_halves(j, at, value):
        part = value.shape[0] // 2
        own = jnp.where(first, value[:part], value[part:]).astype(bf16)
        other = jnp.where(first, value[part:], value[:part]).astype(bf16)
        for _, sl in blocks(value.shape[1]):
            keep_ref[j, at : at + part, :] = own[:, sl]
            give_ref[j, at : at + part, :] = other[:, sl]
            at += part
        return at

    for j, sl in blocks(width):
        offset = jnp.bitwise_xor(me, j)
        place = jnp.bitwise_and(offset, radix - 1) * radix + offset // radix
        tall = jnp.concatenate([x_ref[:, sl], site_x[:, sl]], axis=0)
        at = put_halves(place, 0, mm(tall, coeffs, 0, 0))
        at = put_halves(place, at, mm(logits, tall, 0, 0))
        rows = []
        for n in range(j * share, (j + 1) * share):
            which, at_lane = n // (width // LANES), n % (width // LANES) * LANES
            lanes = slice(at_lane, at_lane + LANES)
            rows.append(gmod_ref[which : which + 1, lanes] + site_gmod[which : which + 1, lanes])
        rows.append(jnp.zeros((8 - len(rows), LANES), f32))
        rows = jnp.concatenate(rows, axis=0).astype(bf16)
        keep_ref[place, at : at + 8, :] = rows
        give_ref[place, at : at + 8, :] = rows


def space_fast_kernel(ids_ref, arrived_ref, *refs):
    inputs, outs = refs[:11], refs[11:]
    first = ids_ref[1] == 0

    class Arrived:
        def __init__(self, wanted):
            self.wanted = wanted

        def __getitem__(self, at):
            value = arrived_ref[at]
            return jnp.where(self.wanted, value, jnp.zeros_like(value))

    space_kernel(*inputs, Arrived(jnp.logical_not(first)), Arrived(first), None, None, *outs)


def space_kernel(
    tok_ref,
    grad_ref,
    x_ref,
    coeffs_ref,
    logits_ref,
    inverse_ref,
    proj_ref,
    step_ref,
    bias_ref,
    rate_ref,
    skip_ref,
    state_ref,
    later_ref,
    gproj_in,
    gstep_in,
    mix_ref,
    pre_ref,
    gproj_ref,
    gstep_ref,
    gmod_ref,
    dn_ref,
    a_hi,
    a_lo,
    b_hi,
    b_lo,
    c_hi,
    c_lo,
):
    length, width = tok_ref.shape
    heads = step_ref.shape[0]
    state = proj_ref.shape[1] // 2
    lanes_of = head_map(heads, width)
    mask = sequence_mask(length, 1)
    coeffs = coeffs_ref[...]
    rate = rate_ref[...]
    z, step, cum, cum_rows = steps_of(logits_ref[...], bias_ref[...], rate, mask)
    last = cum[length - 1 : length, :]
    rest = jnp.exp(last - cum)
    lead = rest * step
    b_part, c_part = coeffs[:, :state], coeffs[:, state:]
    scores = mm(c_part, b_part, 1, 1) * (mask / state)
    step_parts, lead_parts, reach_parts = split(step), split(lead), split(jnp.exp(cum) / state)
    skip_parts = split(jnp.broadcast_to(skip_ref[...], (8, heads)))
    d_scores = jnp.zeros((length, length), f32)
    d_b = jnp.zeros((length, state), f32)
    d_c = jnp.zeros((length, state), f32)
    d_end = jnp.zeros((heads, state), f32)
    for j, sl in blocks(width):
        x, grad = x_ref[:, sl], grad_ref[:, sl]
        wide_map = lanes_of[:, sl]
        step_wide = expand(step_parts, wide_map)
        lead_wide = expand(lead_parts, wide_map)
        reach_wide = expand(reach_parts, wide_map)
        stepped, out, d_stepped, d_scores = scan_block(
            j, x, grad, step_wide, scores, cum, cum_rows, heads, width, d_scores
        )
        x, wide = x.astype(f32), grad.astype(f32)
        before, later = state_ref[sl, :], later_ref[sl, :]
        carried = mm(c_part, before, 1, 1) * reach_wide
        d_c = d_c + mm((wide * reach_wide).astype(bf16), before, 1, 0)
        d_b = d_b + mm((x * lead_wide).astype(bf16), later, 1, 0)
        d_scaled = mm(b_part, later, 1, 1)
        both = split(before.astype(f32) * later.astype(f32))
        d_end = d_end + mm(wide_map, both[0], 1, 0) + mm(wide_map, both[1], 1, 0)
        total = out + carried
        skip = expand(skip_parts, wide_map)[0:1, :]
        mix_ref[:, sl] = total + skip * x
        d_x = (step_wide * d_stepped + d_scaled * lead_wide).astype(bf16)
        dn_ref[:, sl] = d_x + (wide * skip).astype(bf16)
        put((a_hi, a_lo), sl, wide * total - stepped.astype(f32) * d_stepped)
        put((b_hi, b_lo), sl, x * d_stepped)
        put((c_hi, c_lo), sl, x * d_scaled)
    d_lead = head_sums(c_hi, c_lo, lanes_of)
    d_step = head_sums(b_hi, b_lo, lanes_of) + d_lead * rest
    fall = d_lead * lead
    d_cum = head_sums(a_hi, a_lo, lanes_of) - fall
    ones = jnp.ones((8, state), f32)
    end_sum = exact(ones, d_end, 1, 1)[0:1, :] * jnp.exp(last)
    end_sum = end_sum + jnp.sum(fall, axis=0, keepdims=True)
    d_log = exact(mask, d_cum, 0, 0) + end_sum
    d_logits = (jax.nn.sigmoid(z) * (d_step - rate * d_log)).astype(bf16)
    d_scores = (d_scores * (mask / state)).astype(bf16)
    d_coeffs = jnp.concatenate(
        [mm(d_scores, c_part, 0, 0) + d_b, mm(d_scores, b_part, 1, 0) + d_c], axis=1
    ).astype(bf16)
    inverse = inverse_ref[...]
    if gproj_in is None:
        gproj_ref[...] = d_coeffs
        gstep_ref[...] = d_logits
    for _, sl in blocks(width):
        pre = (
            dn_ref[:, sl].astype(f32)
            + mm(d_coeffs, proj_ref[sl, :], 1, 1)
            + mm(d_logits, step_ref[:, sl], 1, 0)
        )
        pre_ref[:, sl] = pre
        scaled = pre * (tok_ref[:, sl].astype(f32) * inverse)
        gmod_ref[0:1, sl] = jnp.sum(pre, axis=0, keepdims=True)
        gmod_ref[1:2, sl] = jnp.sum(scaled, axis=0, keepdims=True)
        if gproj_in is not None:
            gproj_ref[sl, :] = (gproj_in[sl, :] + mm(x_ref[:, sl], d_coeffs, 0, 0)).astype(bf16)
            gstep_ref[:, sl] = (gstep_in[:, sl] + mm(d_logits, x_ref[:, sl], 0, 0)).astype(bf16)


def last_kernel(tok_ref, inverse_ref, gain_ref, mix_ref, pre_ref, time_ref, back_ref, out_ref, dtok_ref):
    length, width = tok_ref.shape
    inverse = inverse_ref[...]
    total = jnp.zeros((length, LANES), f32)
    for _, sl in blocks(width):
        out_ref[:, sl] = (mix_ref[:, sl] + time_ref[:, sl].astype(f32)).astype(bf16)
        grad = (pre_ref[:, sl] + back_ref[:, sl].astype(f32)) * (1.0 + gain_ref[:, sl])
        total = total + grad * tok_ref[:, sl].astype(f32)
    inner = jnp.sum(total, axis=1, keepdims=True) / width
    inner = inner * inverse * inverse * inverse
    for _, sl in blocks(width):
        grad = (pre_ref[:, sl] + back_ref[:, sl].astype(f32)) * (1.0 + gain_ref[:, sl])
        dtok_ref[:, sl] = (grad * inverse - tok_ref[:, sl].astype(f32) * inner).astype(bf16)


def last_fast_kernel(tok_ref, inverse_ref, gain_ref, mix_ref, pre_ref, came_ref, *outs):
    class Packed:
        def __init__(self, which):
            self.which = which

        def __getitem__(self, at):
            value = came_ref[:, self.which, :, at[1]].astype(f32)
            return value.reshape(value.shape[0] * value.shape[1], LANES)

    last_kernel(tok_ref, inverse_ref, gain_ref, mix_ref, pre_ref, Packed(0), Packed(1), *outs)


def in_hbm(array):
    return pltpu.with_memory_space_constraint(array, pltpu.MemorySpace.HBM)


def call(kernel, outs, scratch=(), specs=None, hbm_outs=()):
    shapes = [
        pltpu.MemorySpace.HBM(s, d) if n in hbm_outs else jax.ShapeDtypeStruct(s, d)
        for n, (s, d) in enumerate(outs)
    ]
    where = {"s": pltpu.SMEM, "v": pltpu.VMEM, "h": pltpu.MemorySpace.HBM}
    spaces = {}
    if specs:
        spaces["in_specs"] = [pl.BlockSpec(memory_space=where[c]) for c in specs]
        spaces["out_specs"] = [
            pl.BlockSpec(memory_space=where["h" if n in hbm_outs else "v"]) for n in range(len(outs))
        ]
    return pl.pallas_call(
        kernel,
        out_shape=shapes,
        **spaces,
        scratch_shapes=[pltpu.VMEM(*s) if isinstance(s, tuple) else s for s in scratch],
        compiler_params=pltpu.CompilerParams(vmem_limit_bytes=24 << 20),
    )


def rows_in_order(part):
    if lax.axis_size("row") != 2:
        return lax.all_gather(part, "row")
    other = lax.ppermute(part, "row", [(0, 1), (1, 0)])
    first = lax.axis_index("row") == 0
    return jnp.stack([jnp.where(first, part, other), jnp.where(first, other, part)])


def rows_sum(part):
    if lax.axis_size("row") != 2:
        return lax.psum(part, "row")
    return part + lax.ppermute(part, "row", [(0, 1), (1, 0)])


def chain(own, decay, forward):
    count = lax.axis_size("row")
    hops = [(i, i + 1) if forward else (i + 1, i) for i in range(count - 1)]
    if count == 1:
        return jnp.zeros_like(own)
    arrived = lax.ppermute(own, "row", hops)
    wide = jnp.repeat(decay[0], own.shape[0] // decay.shape[1])[:, None]
    for _ in range(count - 2):
        passed = wide * arrived.astype(f32) + own.astype(f32)
        arrived = lax.ppermute(passed.astype(bf16), "row", hops)
    return arrived


def per_device(
    tokens,
    cotangent,
    timestep,
    mod_weight,
    proj_weight,
    step_weight,
    step_bias,
    rate_space,
    rate_time,
    skip_gain,
):
    frames = lax.axis_size("frame")
    rows = lax.axis_size("row")
    frame_id = lax.axis_index("frame")
    row_id = lax.axis_index("row")
    width = tokens.shape[-1]
    length = tokens.shape[1] * tokens.shape[2]
    clips = timestep.shape[0]
    clip_id = frame_id // (frames // clips)
    sites = length // frames
    heads = rate_space.shape[0]
    depth, pair = proj_weight.shape
    state = pair // 2
    mod_cols = mod_weight.shape[1]
    factor = (frames * rows * length) ** (-0.5)
    tok = tokens.reshape(length, width)
    grad = cotangent.reshape(length, width)

    activated = time_embed(timestep, mod_weight.shape[0]).astype(bf16)
    own_mod = jnp.dot(activated, mod_weight, preferred_element_type=f32)
    high = lax.reduce_precision(own_mod, 8, 7)
    own_mod = jnp.stack([high, own_mod - high]).astype(bf16)

    part = depth // rows
    own_proj = lax.dynamic_slice_in_dim(proj_weight, row_id * part, part, 0)
    to_all = [
        to_tiles(own_proj[None]),
        to_tiles(step_weight.T[None]),
        own_mod.reshape(1, -1, LANES),
    ]
    to_all = jnp.concatenate(to_all, axis=1)
    to_all = jnp.pad(to_all, ((0, 0), (0, -to_all.shape[1] % 8), (0, 0)))
    count = sites * width // LANES
    got = exchange(
        jnp.concatenate(
            [
                to_tiles(tok.reshape(frames, sites, width)),
                to_tiles(grad.reshape(frames, sites, width)),
                jnp.broadcast_to(to_all, (frames,) + to_all.shape[1:]),
            ],
            axis=1,
        )
    )
    site_tok = from_tiles(got[:, :count], sites, width).reshape(length, width)
    site_grad = from_tiles(got[:, count : 2 * count], sites, width).reshape(length, width)
    at = 2 * count
    size = part * pair // LANES
    proj_full = rows_in_order(got[:, at : at + size])
    proj_full = from_tiles(proj_full.reshape(rows * frames, size, LANES), part, pair)
    proj_full = proj_full.reshape(rows, frames, part, pair).transpose(1, 0, 2, 3)
    proj_full = proj_full.reshape(width, pair)
    at += size
    size = heads * depth // LANES
    step_full = from_tiles(got[:, at : at + size], heads, depth)
    step_full = step_full.transpose(1, 0, 2).reshape(heads, width)
    at += size
    size = 2 * clips * mod_cols // LANES
    mod_full = got[:, at : at + size].reshape(frames, 2, clips, mod_cols).astype(f32)
    mod_full = (mod_full[:, 0] + mod_full[:, 1]).transpose(1, 0, 2).reshape(clips, 2 * width)
    shift, gain = mod_full[:, :width], mod_full[:, width:]

    bias = step_bias[None]
    wide = (length, width)
    site_out, site_back, gproj, gstep, site_gmod = call(
        functools.partial(site_kernel, sites),
        [(wide, bf16), (wide, bf16), ((width, pair), f32), ((heads, width), f32), ((2 * clips, width), f32)],
        [(wide, bf16)] * 6,
    )(site_tok, site_grad, shift, gain, proj_full, step_full, bias, rate_time[None])

    came = exchange(
        jnp.concatenate(
            [
                to_tiles(site_out.reshape(frames, sites, width)),
                to_tiles(site_back.reshape(frames, sites, width)),
            ],
            axis=1,
        )
    )
    time_out = from_tiles(came[:, :count], sites, width).reshape(length, width)
    time_back = from_tiles(came[:, count:], sites, width).reshape(length, width)

    own_shift = lax.dynamic_slice_in_dim(shift, clip_id, 1, 0)
    own_gain = lax.dynamic_slice_in_dim(gain, clip_id, 1, 0)
    normed, coeffs, logits, inverse, decay, end_own, start_grad = call(
        band_kernel,
        [
            (wide, bf16),
            ((length, pair), bf16),
            ((length, heads), bf16),
            ((length, 1), f32),
            ((1, heads), f32),
            ((width, state), bf16),
            ((width, state), bf16),
        ],
    )(tok, grad, own_shift, own_gain, proj_full, step_full, bias, rate_space[None])
    state_in = chain(end_own, decay, True)
    later_grad = chain(start_grad, decay, False)
    mix, pre, gproj, gstep, gmod = call(
        space_kernel,
        [(wide, f32), (wide, f32), ((width, pair), bf16), ((heads, width), bf16), ((2, width), f32)],
        [(wide, bf16)] * 7,
    )(
        tok,
        grad,
        normed,
        coeffs,
        logits,
        inverse,
        proj_full,
        step_full,
        bias,
        rate_space[None],
        skip_gain[None],
        state_in,
        later_grad,
        gproj,
        gstep,
    )

    picked = (jnp.arange(clips) == clip_id).astype(f32)[:, None]
    gmod = jnp.concatenate(
        [site_gmod[:clips] + picked * gmod[0:1], site_gmod[clips:] + picked * gmod[1:2]], axis=1
    )
    gmod = gmod.reshape(clips, frames, mod_cols).transpose(1, 0, 2).astype(bf16)
    sent = jnp.concatenate(
        [
            to_tiles(gproj.reshape(frames, depth, pair)),
            to_tiles(gstep.reshape(heads, frames, depth).transpose(1, 0, 2)),
            gmod.reshape(frames, -1, LANES) if (clips * mod_cols) % LANES == 0 else gmod,
        ],
        axis=1,
    )
    size = sent.shape[1]
    sent = jnp.pad(sent, ((0, 0), (0, -size % 8), (0, 0)))
    sums = jnp.sum(exchange(sent).astype(f32), axis=0, keepdims=True)
    sums = rows_sum(sums) * factor
    at = depth * pair // LANES
    grad_proj = from_tiles(sums[:, :at], depth, pair)[0]
    size = heads * depth // LANES
    grad_step = from_tiles(sums[:, at : at + size], heads, depth)[0].T
    at += size
    size = clips * mod_cols // LANES
    mod_sum = sums[0, at : at + size].reshape(clips, mod_cols)
    grad_mod = jnp.dot(activated.astype(f32).T, mod_sum, precision=EXACT)

    mixed, d_tokens = call(last_kernel, [(wide, bf16), (wide, bf16)])(
        tok, inverse, own_gain, mix, pre, time_out, time_back
    )
    return (mixed.reshape(tokens.shape), d_tokens.reshape(tokens.shape), grad_proj, grad_step, grad_mod)


def fits(mesh, tokens, timestep, proj_weight, step_weight):
    frames, rows = mesh.shape["frame"], mesh.shape["row"]
    length, width = tokens.shape[2] * tokens.shape[1] // rows, tokens.shape[3]
    return (
        rows == 2
        and frames == 16
        and timestep.shape[0] == 1
        and length == LANES
        and length // frames == 8
        and width // frames == LANES
        and proj_weight.shape[1] == 2 * LANES
        and step_weight.shape[1] % 32 == 0
    )


def spread_over_frames(own, sent, radix=4):
    frames = radix * radix

    def others(piece, stride):
        return [piece] + [
            lax.ppermute(piece, "frame", [(i, i ^ (d * stride)) for i in range(frames)])
            for d in range(1, radix)
        ]

    far = jnp.stack(others(own, radix))
    far, sent = lax.optimization_barrier((far, sent))
    pieces = others(far, 1)
    got = exchange(sent)
    return jnp.concatenate(pieces), got


def sum_over_frames(keep, given, radix):
    def gathered(pieces, stride):
        frames = radix * radix
        return [pieces[0]] + [
            lax.ppermute(pieces[d], "frame", [(i, i ^ (d * stride)) for i in range(frames)])
            for d in range(1, radix)
        ]

    def total(pieces):
        value = pieces[0].astype(f32)
        for piece in pieces[1:]:
            value = value + piece.astype(f32)
        return value

    parts = [slice(d * radix, (d + 1) * radix) for d in range(radix)]
    near = [total([keep[p], given[p]]).astype(bf16) for p in parts]
    near = total(gathered(near, 1)).astype(bf16)
    return total(gathered([near[d] for d in range(radix)], radix))


def per_device_fast(
    tokens,
    cotangent,
    timestep,
    mod_weight,
    proj_weight,
    step_weight,
    step_bias,
    rate_space,
    rate_time,
    skip_gain,
):
    frames = lax.axis_size("frame")
    rows = lax.axis_size("row")
    ids = jnp.stack([lax.axis_index("frame"), lax.axis_index("row")]).astype(jnp.int32)
    width = tokens.shape[-1]
    length = tokens.shape[1] * tokens.shape[2]
    sites = length // frames
    heads = rate_space.shape[0]
    depth, pair = proj_weight.shape
    state = pair // 2
    mod_cols = mod_weight.shape[1]
    factor = (frames * rows * length) ** (-0.5)
    tok = tokens.reshape(length, width)
    grad = cotangent.reshape(length, width)
    wide = (length, width)
    bias = step_bias[None]
    swap = [(0, 1), (1, 0)]

    packed = (frames, 2, sites, width)
    size = depth // 2 * pair // LANES + heads // 2 + 8
    activated = time_embed(timestep, mod_weight.shape[0]).astype(bf16)
    sent, payload = call(
        start_kernel,
        [(packed, bf16), ((size, LANES), bf16)],
        [
            ((depth, pair), bf16),
            ((heads, depth), bf16),
            (mod_weight.shape, bf16),
            (packed, bf16),
            pltpu.SemaphoreType.DMA((7,)),
        ],
        specs="shhhhhv",
        hbm_outs=(0,),
    )(
        ids,
        in_hbm(tok.reshape(frames, sites, width)),
        in_hbm(grad.reshape(frames, sites, width)),
        in_hbm(proj_weight),
        in_hbm(step_weight.T),
        in_hbm(mod_weight),
        activated,
    )
    payload, got = spread_over_frames(payload, sent)
    other = lax.ppermute(payload, "row", swap)
    proj_full, step_full, shift, gain = call(
        functools.partial(unpack_kernel, 4),
        [((width, pair), bf16), ((heads, width), bf16), ((1, width), f32), ((1, width), f32)],
        specs="svv",
    )(ids, payload, other)

    normed, coeffs, logits, inverse, _, give = call(
        band_fast_kernel,
        [
            (wide, bf16),
            ((length, pair), bf16),
            ((length, heads), bf16),
            ((length, 1), f32),
            ((1, heads), f32),
            ((width, state), bf16),
        ],
        specs="svvvvvvvv",
    )(ids, tok, grad, shift, gain, proj_full, step_full, bias, rate_space[None])
    arrived = lax.ppermute(give, "row", swap)
    halves = (frames, size, LANES)
    mix, pre, own_dc, own_dl, gmod = call(
        space_fast_kernel,
        [(wide, f32), (wide, f32), ((length, pair), bf16), ((length, heads), bf16), ((2, width), f32)],
        [(wide, bf16)] * 7,
        specs="s" + "v" * 12,
    )(
        ids,
        arrived,
        tok,
        grad,
        normed,
        coeffs,
        logits,
        inverse,
        proj_full,
        step_full,
        bias,
        rate_space[None],
        skip_gain[None],
    )
    got, own_dc = lax.optimization_barrier((got, own_dc))
    sent, site_x, site_gmod, site_dc, site_dl = call(
        functools.partial(site_fast_kernel, sites),
        [
            (packed, bf16),
            (wide, bf16),
            ((2, width), f32),
            ((length, pair), bf16),
            ((length, heads), bf16),
        ],
        [
            (wide, bf16),
            (wide, bf16),
            (packed, bf16),
            (wide, bf16),
            ((2, width), f32),
            pltpu.SemaphoreType.DMA((6,)),
        ]
        + [(wide, bf16)] * 5,
        specs="vvvvvvv",
        hbm_outs=(0, 1, 2),
    )(got, shift, gain, proj_full, step_full, bias, rate_time[None])
    came = exchange(sent)

    keep, give = call(
        functools.partial(terms_kernel, 4), [(halves, bf16), (halves, bf16)], specs="svvvvvvvv"
    )(ids, normed, own_dc, own_dl, gmod, site_x, site_dc, site_dl, site_gmod)
    given = lax.ppermute(give, "row", swap)
    terms = sum_over_frames(keep, given, 4)
    other = lax.ppermute(terms, "row", swap)
    grad_proj, grad_step, grad_mod = call(
        functools.partial(finish_kernel, factor),
        [((depth, pair), f32), ((heads, depth), f32), ((mod_weight.shape[0], mod_cols), f32)],
        specs="svvv",
    )(ids, terms, other, activated.astype(f32).T)
    mixed, d_tokens = call(last_fast_kernel, [(wide, bf16), (wide, bf16)])(
        tok, inverse, gain, mix, pre, came
    )
    return (mixed.reshape(tokens.shape), d_tokens.reshape(tokens.shape), grad_proj, grad_step.T, grad_mod)


def solution(mesh):
    placed = (
        P("frame", "row", None, None),
        P("frame", "row", None, None),
        P(),
        P(None, "frame"),
        P("frame", None),
        P("frame", None),
        P(),
        P(),
        P(),
        P(),
    )
    outs = (
        P("frame", "row", None, None),
        P("frame", "row", None, None),
        P("frame", None),
        P("frame", None),
        P(None, "frame"),
    )

    def step(tokens, cotangent, timestep, mod_weight, proj_weight, step_weight, *rest):
        fast = fits(mesh, tokens, timestep, proj_weight, step_weight)
        body = per_device_fast if fast else per_device
        return jax.shard_map(
            body, mesh=mesh, in_specs=placed, out_specs=outs, check_vma=False
        )(tokens, cotangent, timestep, mod_weight, proj_weight, step_weight, *rest)

    return step
```

```python
import functools
import math

import jax
import jax.numpy as jnp
from jax import lax
from jax.experimental import pallas as pl
from jax.experimental.pallas import tpu as pltpu
from jax.sharding import PartitionSpec as P

norm_eps = 1e-05
LANES = 128
f32 = jnp.float32
bf16 = jnp.bfloat16
EXACT = lax.Precision.HIGHEST


def time_embed(timestep, embed_dim):
    half_dim = embed_dim // 2
    frequency = jnp.exp(-math.log(10000.0) * jnp.arange(half_dim, dtype=f32) / half_dim)
    angles = timestep.astype(f32)[:, None] * frequency[None, :]
    return jax.nn.silu(jnp.concatenate([jnp.cos(angles), jnp.sin(angles)], axis=1))


def to_tiles(a):
    f, r, c = a.shape
    if r % 8 == 0 and c % LANES == 0:
        a = a.reshape(f, r // 8, 8, c // LANES, LANES).transpose(0, 1, 3, 2, 4)
    return a.reshape(f, r * c // LANES, LANES)


def from_tiles(a, r, c):
    f = a.shape[0]
    if r % 8 == 0 and c % LANES == 0:
        a = a.reshape(f, r // 8, c // LANES, 8, LANES).transpose(0, 1, 3, 2, 4)
    return a.reshape(f, r, c)


def exchange(packed):
    return lax.all_to_all(packed, "frame", split_axis=0, concat_axis=0, tiled=True)


def mm(a, b, ca, cb):
    return lax.dot_general(a, b, (((ca,), (cb,)), ((), ())), preferred_element_type=f32)


def exact(a, b, ca, cb):
    return lax.dot_general(
        a, b, (((ca,), (cb,)), ((), ())), preferred_element_type=f32, precision=EXACT
    )


def split(a):
    high = a.astype(bf16)
    return high, (a - high.astype(f32)).astype(bf16)


def head_map(heads, width):
    size = width // heads
    own = lax.broadcasted_iota(jnp.int32, (heads, width), 0)
    lane = lax.broadcasted_iota(jnp.int32, (heads, width), 1)
    return jnp.where(lane // size == own, 1.0, 0.0).astype(bf16)


def sequence_mask(length, sites):
    later = lax.broadcasted_iota(jnp.int32, (length, length), 0)
    earlier = lax.broadcasted_iota(jnp.int32, (length, length), 1)
    keep = later >= earlier
    if sites > 1:
        keep = keep & (later % sites == earlier % sites)
    return jnp.where(keep, 1.0, 0.0).astype(f32)


def blocks(width):
    return [(j, slice(j * LANES, (j + 1) * LANES)) for j in range(width // LANES)]


def spread_rows(rows, length):
    count = rows.shape[0]
    if count == 1:
        return rows
    part = (length // count, rows.shape[1])
    return jnp.concatenate([jnp.broadcast_to(rows[c : c + 1], part) for c in range(count)], axis=0)


def normalize_into(tok_ref, shift_ref, gain_ref, x_ref):
    length, width = tok_ref.shape
    total = jnp.zeros((length, LANES), f32)
    for _, sl in blocks(width):
        v = tok_ref[:, sl].astype(f32)
        total = total + v * v
    mean = jnp.sum(total, axis=1, keepdims=True) / width
    inverse = lax.rsqrt(mean + norm_eps)
    for _, sl in blocks(width):
        unit = tok_ref[:, sl].astype(f32) * inverse
        gain = spread_rows(gain_ref[:, sl], length)
        shift = spread_rows(shift_ref[:, sl], length)
        x_ref[:, sl] = (unit * (1.0 + gain) + shift).astype(bf16)
    return inverse


def steps_of(logits, bias, rate, mask):
    z = logits.astype(f32) + bias
    step = jnp.maximum(z, 0.0) + jnp.log1p(jnp.exp(-jnp.abs(z)))
    log_decay = -step * rate
    cum = exact(mask, log_decay, 1, 0)
    cum_rows = exact(log_decay, mask, 0, 1)
    return z, step, cum, cum_rows


def expand(parts, lanes_of):
    return mm(parts[0], lanes_of, 1, 0) + mm(parts[1], lanes_of, 1, 0)


def scan_block(j, x, grad, step_wide, scores, cum, cum_rows, heads, width, d_scores):
    size = width // heads
    per_block = LANES // size
    stepped = (x.astype(f32) * step_wide).astype(bf16)
    lane = lax.broadcasted_iota(jnp.int32, x.shape, 1)
    weights, steppeds, grads = [], [], []
    for i in range(per_block):
        h = j * per_block + i
        decay = jnp.exp(jnp.minimum(cum[:, h : h + 1] - cum_rows[h : h + 1, :], 0.0))
        inside = lane // size == i
        own_grad = jnp.where(inside, grad, jnp.zeros_like(grad))
        d_weight = mm(own_grad, stepped, 1, 1)
        d_scores = d_scores + d_weight * decay
        weights.append((scores * decay).astype(bf16))
        steppeds.append(jnp.where(inside, stepped, jnp.zeros_like(stepped)))
        grads.append(own_grad)
    out = mm(jnp.concatenate(weights, axis=1), jnp.concatenate(steppeds, axis=0), 1, 0)
    d_stepped = mm(jnp.concatenate(weights, axis=0), jnp.concatenate(grads, axis=0), 0, 0)
    return stepped, out, d_stepped, d_scores


def head_sums(high_ref, low_ref, lanes_of):
    return mm(high_ref[...], lanes_of, 1, 1) + mm(low_ref[...], lanes_of, 1, 1)


def put(refs, sl, value):
    high, low = split(value)
    refs[0][:, sl] = high
    refs[1][:, sl] = low


def start_kernel(ids_ref, tok_ref, grad_ref, proj_hbm, step_hbm, mod_hbm, active_ref, sent_ref, pay_ref,
                 proj_ref, step_ref, mod_ref, both_ref, sems):
    copies = [
        pltpu.make_async_copy(src, dst, sems.at[n])
        for n, (src, dst) in enumerate(
            [
                (proj_hbm, proj_ref),
                (step_hbm, step_ref),
                (mod_hbm, mod_ref),
                (tok_ref, both_ref.at[:, 0]),
                (grad_ref, both_ref.at[:, 1]),
                (both_ref.at[:, 0], sent_ref.at[:, 0]),
                (both_ref.at[:, 1], sent_ref.at[:, 1]),
            ]
        )
    ]
    for copy in copies[:5]:
        copy.start()
    copies[3].wait()
    copies[5].start()
    copies[4].wait()
    copies[6].start()
    row = ids_ref[1]
    part, pair = proj_ref.shape[0] // 2, proj_ref.shape[1]
    copies[0].wait()
    own = proj_ref[pl.ds(pl.multiple_of(row * part, part), part), :]
    at = 0
    for _, sl in blocks(pair):
        pay_ref[at : at + part, :] = own[:, sl]
        at += part
    copies[1].wait()
    part = step_ref.shape[0] // 2
    pay_ref[at : at + part, :] = step_ref[pl.ds(pl.multiple_of(row * part, part), part), :]
    at += part
    copies[2].wait()
    own = mm(active_ref[...], mod_ref[...], 1, 0)
    high = own.astype(bf16).astype(f32)
    pieces = [piece[:, sl] for piece in (high, own - high) for _, sl in blocks(own.shape[1])]
    pieces.append(jnp.zeros((8 - len(pieces), LANES), f32))
    pay_ref[at : at + 8, :] = jnp.concatenate(pieces, axis=0).astype(bf16)
    copies[5].wait()
    copies[6].wait()


def unpack_kernel(radix, ids_ref, own_ref, other_ref, proj_ref, step_ref, shift_ref, gain_ref):
    me, row = ids_ref[0], ids_ref[1]
    width, pair = proj_ref.shape
    frames = own_ref.shape[0]
    depth = width // frames
    part, heads = depth // 2, step_ref.shape[0] // 2
    cols = 2 * width // frames
    for i in range(frames):
        source = jnp.bitwise_xor(me, (i % radix) * radix + i // radix)
        for ref, half in ((own_ref, row), (other_ref, 1 - row)):
            rows = pl.ds(pl.multiple_of(source * depth + half * part, part), part)
            at = 0
            for _, sl in blocks(pair):
                proj_ref[rows, sl] = ref[i, at : at + part, :]
                at += part
            rows = pl.ds(pl.multiple_of(half * heads, heads), heads)
            lanes = pl.ds(pl.multiple_of(source * depth, depth), depth)
            step_ref[rows, lanes] = ref[i, at : at + heads, :]
            at += heads
        own = own_ref[i, at : at + 8, :].astype(f32)
        count = cols // LANES
        lanes_at = jnp.bitwise_and(source, frames // 2 - 1) * cols
        for k in range(count):
            value = own[k : k + 1, :] + own[count + k : count + k + 1, :]
            lanes = pl.ds(pl.multiple_of(lanes_at + k * LANES, LANES), LANES)

            @pl.when(source < frames // 2)
            def _():
                shift_ref[:, lanes] = value

            @pl.when(source >= frames // 2)
            def _():
                gain_ref[:, lanes] = value


def finish_kernel(factor, ids_ref, own_ref, other_ref, active_ref, proj_ref, step_ref, mod_ref):
    row = ids_ref[1]
    pair = proj_ref.shape[1]
    part, heads = proj_ref.shape[0] // 2, step_ref.shape[0] // 2
    for ref, half in ((own_ref, row), (other_ref, 1 - row)):
        rows = pl.ds(pl.multiple_of(half * part, part), part)
        at = 0
        for _, sl in blocks(pair):
            proj_ref[rows, sl] = ref[at : at + part, :] * factor
            at += part
        step_ref[pl.ds(pl.multiple_of(half * heads, heads), heads), :] = ref[at : at + heads, :] * factor
        at += heads
    for k, sl in blocks(mod_ref.shape[1]):
        mod_ref[:, sl] = active_ref[...] * (own_ref[at + k : at + k + 1, :] * factor)


def site_fast_kernel(sites, got_ref, *refs):
    inputs, (sent_hbm, x_hbm, gmod_hbm, dc_ref, dl_ref) = refs[:6], refs[6:11]
    tok_ref, grad_ref, sent_ref, x_ref, gmod_ref, sems = refs[11:17]
    scratch = refs[17:]
    frames, width = got_ref.shape[0], got_ref.shape[3]
    for _, sl in blocks(width):
        for ref, which in ((tok_ref, 0), (grad_ref, 1)):
            value = got_ref[:, which, :, sl].astype(f32)
            ref[:, sl] = value.reshape(frames * sites, LANES).astype(bf16)

    parts = 2
    share = width // parts
    copies = []

    def begin(source, target):
        copy = pltpu.make_async_copy(source, target, sems.at[len(copies)])
        copy.start()
        copies.append(copy)

    def send(which, p):
        at = (slice(None), which, slice(None), slice(p * share, (p + 1) * share))
        begin(sent_ref.at[at], sent_hbm.at[at])

    class Packed:
        def __init__(self, which):
            self.which = which

        def __setitem__(self, at, value):
            if not copies:
                begin(x_ref, x_hbm)
            value = value.astype(f32).reshape(frames, sites, LANES)
            sent_ref[:, self.which, :, at[1]] = value.astype(bf16)
            if at[1].stop % share == 0:
                send(self.which, at[1].stop // share - 1)

    site_kernel(
        sites, tok_ref, grad_ref, *inputs, Packed(0), Packed(1), dc_ref, dl_ref, gmod_ref, x_ref, *scratch
    )
    begin(gmod_ref, gmod_hbm)
    for copy in copies:
        copy.wait()


def site_kernel(
    sites,
    tok_ref,
    grad_ref,
    shift_ref,
    gain_ref,
    proj_ref,
    step_ref,
    bias_ref,
    rate_ref,
    out_ref,
    back_ref,
    gproj_ref,
    gstep_ref,
    gmod_ref,
    x_ref,
    dn_ref,
    a_hi,
    a_lo,
    b_hi,
    b_lo,
):
    length, width = tok_ref.shape
    heads = step_ref.shape[0]
    state = proj_ref.shape[1] // 2
    clips = shift_ref.shape[0]
    inverse = normalize_into(tok_ref, shift_ref, gain_ref, x_ref)
    lanes_of = head_map(heads, width)
    mask = sequence_mask(length, sites)
    coeffs = mm(x_ref[...], proj_ref[...], 1, 0).astype(bf16)
    logits = mm(x_ref[...], step_ref[...], 1, 1).astype(bf16)
    rate = rate_ref[...]
    z, step, cum, cum_rows = steps_of(logits, bias_ref[...], rate, mask)
    b_part, c_part = coeffs[:, :state], coeffs[:, state:]
    scores = mm(c_part, b_part, 1, 1) * (mask / state)
    step_parts = split(step)
    d_scores = jnp.zeros((length, length), f32)
    for j, sl in blocks(width):
        x, grad = x_ref[:, sl], grad_ref[:, sl]
        step_wide = expand(step_parts, lanes_of[:, sl])
        stepped, out, d_stepped, d_scores = scan_block(
            j, x, grad, step_wide, scores, cum, cum_rows, heads, width, d_scores
        )
        out_ref[:, sl] = out.astype(bf16)
        dn_ref[:, sl] = (step_wide * d_stepped).astype(bf16)
        put((a_hi, a_lo), sl, grad.astype(f32) * out - stepped.astype(f32) * d_stepped)
        put((b_hi, b_lo), sl, x.astype(f32) * d_stepped)
    d_cum = head_sums(a_hi, a_lo, lanes_of)
    d_step = head_sums(b_hi, b_lo, lanes_of)
    d_log = exact(mask, d_cum, 0, 0)
    d_logits = (jax.nn.sigmoid(z) * (d_step - rate * d_log)).astype(bf16)
    d_scores = (d_scores * (mask / state)).astype(bf16)
    d_coeffs = jnp.concatenate(
        [mm(d_scores, c_part, 0, 0), mm(d_scores, b_part, 1, 0)], axis=1
    ).astype(bf16)
    for _, sl in blocks(width):
        back = (
            dn_ref[:, sl].astype(f32)
            + mm(d_coeffs, proj_ref[sl, :], 1, 1)
            + mm(d_logits, step_ref[:, sl], 1, 0)
        ).astype(bf16)
        back_ref[:, sl] = back
        back = back.astype(f32)
        scaled = back * (tok_ref[:, sl].astype(f32) * inverse)
        for c in range(clips):
            rows = slice(c * (length // clips), (c + 1) * (length // clips))
            gmod_ref[c : c + 1, sl] = jnp.sum(back[rows], axis=0, keepdims=True)
            gmod_ref[clips + c : clips + c + 1, sl] = jnp.sum(scaled[rows], axis=0, keepdims=True)
        if gproj_ref.shape == (width, 2 * state):
            gproj_ref[sl, :] = mm(x_ref[:, sl], d_coeffs, 0, 0)
            gstep_ref[:, sl] = mm(d_logits, x_ref[:, sl], 0, 0)
    if gproj_ref.shape != (width, 2 * state):
        gproj_ref[...] = d_coeffs
        gstep_ref[...] = d_logits


def band_fast_kernel(ids_ref, *refs):
    give_ref = refs[-1]
    band_kernel(*refs[:-1], None, give_ref, first=ids_ref[1] == 0)


def band_kernel(
    tok_ref,
    grad_ref,
    shift_ref,
    gain_ref,
    proj_ref,
    step_ref,
    bias_ref,
    rate_ref,
    x_ref,
    coeffs_ref,
    logits_ref,
    inverse_ref,
    decay_ref,
    end_ref,
    own_ref,
    first=None,
):
    length, width = tok_ref.shape
    heads = step_ref.shape[0]
    state = proj_ref.shape[1] // 2
    inverse_ref[...] = normalize_into(tok_ref, shift_ref, gain_ref, x_ref)
    lanes_of = head_map(heads, width)
    mask = sequence_mask(length, 1)
    coeffs = mm(x_ref[...], proj_ref[...], 1, 0).astype(bf16)
    logits = mm(x_ref[...], step_ref[...], 1, 1).astype(bf16)
    coeffs_ref[...] = coeffs
    logits_ref[...] = logits
    _, step, cum, _ = steps_of(logits, bias_ref[...], rate_ref[...], mask)
    last = cum[length - 1 : length, :]
    decay_ref[...] = jnp.exp(last)
    lead = split(jnp.exp(last - cum) * step)
    reach = split(jnp.exp(cum) / state)
    b_part, c_part = coeffs[:, :state], coeffs[:, state:]
    if first is not None:
        gain = split(jnp.where(first, jnp.exp(last - cum) * step, jnp.exp(cum) / state))
        other = jnp.where(first, b_part, c_part)
        for _, sl in blocks(width):
            value = jnp.where(first, x_ref[:, sl], grad_ref[:, sl]).astype(f32)
            value = (value * expand(gain, lanes_of[:, sl])).astype(bf16)
            own_ref[sl, :] = mm(value, other, 0, 0).astype(bf16)
        return
    for _, sl in blocks(width):
        lead_wide = expand(lead, lanes_of[:, sl])
        reach_wide = expand(reach, lanes_of[:, sl])
        scaled = (x_ref[:, sl].astype(f32) * lead_wide).astype(bf16)
        faded = (grad_ref[:, sl].astype(f32) * reach_wide).astype(bf16)
        end_ref[sl, :] = mm(scaled, b_part, 0, 0).astype(bf16)
        own_ref[sl, :] = mm(faded, c_part, 0, 0).astype(bf16)


def terms_kernel(radix, ids_ref, x_ref, dc_ref, dl_ref, gmod_ref, site_x, site_dc, site_dl, site_gmod,
                 keep_ref, give_ref):
    me, first = ids_ref[0], ids_ref[1] == 0
    width = x_ref.shape[1]
    coeffs = jnp.concatenate([dc_ref[...], site_dc[...]], axis=0)
    logits = jnp.concatenate([dl_ref[...], site_dl[...]], axis=0)
    frames = keep_ref.shape[0]
    share = 2 * width // LANES // frames

    def put_halves(j, at, value):
        part = value.shape[0] // 2
        own = jnp.where(first, value[:part], value[part:]).astype(bf16)
        other = jnp.where(first, value[part:], value[:part]).astype(bf16)
        for _, sl in blocks(value.shape[1]):
            keep_ref[j, at : at + part, :] = own[:, sl]
            give_ref[j, at : at + part, :] = other[:, sl]
            at += part
        return at

    for j, sl in blocks(width):
        offset = jnp.bitwise_xor(me, j)
        place = jnp.bitwise_and(offset, radix - 1) * radix + offset // radix
        tall = jnp.concatenate([x_ref[:, sl], site_x[:, sl]], axis=0)
        at = put_halves(place, 0, mm(tall, coeffs, 0, 0))
        at = put_halves(place, at, mm(logits, tall, 0, 0))
        rows = []
        for n in range(j * share, (j + 1) * share):
            which, at_lane = n // (width // LANES), n % (width // LANES) * LANES
            lanes = slice(at_lane, at_lane + LANES)
            rows.append(gmod_ref[which : which + 1, lanes] + site_gmod[which : which + 1, lanes])
        rows.append(jnp.zeros((8 - len(rows), LANES), f32))
        rows = jnp.concatenate(rows, axis=0).astype(bf16)
        keep_ref[place, at : at + 8, :] = rows
        give_ref[place, at : at + 8, :] = rows


def space_fast_kernel(ids_ref, arrived_ref, *refs):
    inputs, outs = refs[:11], refs[11:]
    first = ids_ref[1] == 0

    class Arrived:
        def __init__(self, wanted):
            self.wanted = wanted

        def __getitem__(self, at):
            value = arrived_ref[at]
            return jnp.where(self.wanted, value, jnp.zeros_like(value))

    space_kernel(*inputs, Arrived(jnp.logical_not(first)), Arrived(first), None, None, *outs)


def space_kernel(
    tok_ref,
    grad_ref,
    x_ref,
    coeffs_ref,
    logits_ref,
    inverse_ref,
    proj_ref,
    step_ref,
    bias_ref,
    rate_ref,
    skip_ref,
    state_ref,
    later_ref,
    gproj_in,
    gstep_in,
    mix_ref,
    pre_ref,
    gproj_ref,
    gstep_ref,
    gmod_ref,
    dn_ref,
    a_hi,
    a_lo,
    b_hi,
    b_lo,
    c_hi,
    c_lo,
):
    length, width = tok_ref.shape
    heads = step_ref.shape[0]
    state = proj_ref.shape[1] // 2
    lanes_of = head_map(heads, width)
    mask = sequence_mask(length, 1)
    coeffs = coeffs_ref[...]
    rate = rate_ref[...]
    z, step, cum, cum_rows = steps_of(logits_ref[...], bias_ref[...], rate, mask)
    last = cum[length - 1 : length, :]
    rest = jnp.exp(last - cum)
    lead = rest * step
    b_part, c_part = coeffs[:, :state], coeffs[:, state:]
    scores = mm(c_part, b_part, 1, 1) * (mask / state)
    step_parts, lead_parts, reach_parts = split(step), split(lead), split(jnp.exp(cum) / state)
    skip_parts = split(jnp.broadcast_to(skip_ref[...], (8, heads)))
    d_scores = jnp.zeros((length, length), f32)
    d_b = jnp.zeros((length, state), f32)
    d_c = jnp.zeros((length, state), f32)
    d_end = jnp.zeros((heads, state), f32)
    for j, sl in blocks(width):
        x, grad = x_ref[:, sl], grad_ref[:, sl]
        wide_map = lanes_of[:, sl]
        step_wide = expand(step_parts, wide_map)
        lead_wide = expand(lead_parts, wide_map)
        reach_wide = expand(reach_parts, wide_map)
        stepped, out, d_stepped, d_scores = scan_block(
            j, x, grad, step_wide, scores, cum, cum_rows, heads, width, d_scores
        )
        x, wide = x.astype(f32), grad.astype(f32)
        before, later = state_ref[sl, :], later_ref[sl, :]
        carried = mm(c_part, before, 1, 1) * reach_wide
        d_c = d_c + mm((wide * reach_wide).astype(bf16), before, 1, 0)
        d_b = d_b + mm((x * lead_wide).astype(bf16), later, 1, 0)
        d_scaled = mm(b_part, later, 1, 1)
        both = split(before.astype(f32) * later.astype(f32))
        d_end = d_end + mm(wide_map, both[0], 1, 0) + mm(wide_map, both[1], 1, 0)
        total = out + carried
        skip = expand(skip_parts, wide_map)[0:1, :]
        mix_ref[:, sl] = total + skip * x
        d_x = (step_wide * d_stepped + d_scaled * lead_wide).astype(bf16)
        dn_ref[:, sl] = d_x + (wide * skip).astype(bf16)
        put((a_hi, a_lo), sl, wide * total - stepped.astype(f32) * d_stepped)
        put((b_hi, b_lo), sl, x * d_stepped)
        put((c_hi, c_lo), sl, x * d_scaled)
    d_lead = head_sums(c_hi, c_lo, lanes_of)
    d_step = head_sums(b_hi, b_lo, lanes_of) + d_lead * rest
    fall = d_lead * lead
    d_cum = head_sums(a_hi, a_lo, lanes_of) - fall
    ones = jnp.ones((8, state), f32)
    end_sum = exact(ones, d_end, 1, 1)[0:1, :] * jnp.exp(last)
    end_sum = end_sum + jnp.sum(fall, axis=0, keepdims=True)
    d_log = exact(mask, d_cum, 0, 0) + end_sum
    d_logits = (jax.nn.sigmoid(z) * (d_step - rate * d_log)).astype(bf16)
    d_scores = (d_scores * (mask / state)).astype(bf16)
    d_coeffs = jnp.concatenate(
        [mm(d_scores, c_part, 0, 0) + d_b, mm(d_scores, b_part, 1, 0) + d_c], axis=1
    ).astype(bf16)
    inverse = inverse_ref[...]
    if gproj_in is None:
        gproj_ref[...] = d_coeffs
        gstep_ref[...] = d_logits
    for _, sl in blocks(width):
        pre = (
            dn_ref[:, sl].astype(f32)
            + mm(d_coeffs, proj_ref[sl, :], 1, 1)
            + mm(d_logits, step_ref[:, sl], 1, 0)
        )
        pre_ref[:, sl] = pre
        scaled = pre * (tok_ref[:, sl].astype(f32) * inverse)
        gmod_ref[0:1, sl] = jnp.sum(pre, axis=0, keepdims=True)
        gmod_ref[1:2, sl] = jnp.sum(scaled, axis=0, keepdims=True)
        if gproj_in is not None:
            gproj_ref[sl, :] = (gproj_in[sl, :] + mm(x_ref[:, sl], d_coeffs, 0, 0)).astype(bf16)
            gstep_ref[:, sl] = (gstep_in[:, sl] + mm(d_logits, x_ref[:, sl], 0, 0)).astype(bf16)


def last_kernel(tok_ref, inverse_ref, gain_ref, mix_ref, pre_ref, time_ref, back_ref, out_ref, dtok_ref):
    length, width = tok_ref.shape
    inverse = inverse_ref[...]
    total = jnp.zeros((length, LANES), f32)
    for _, sl in blocks(width):
        out_ref[:, sl] = (mix_ref[:, sl] + time_ref[:, sl].astype(f32)).astype(bf16)
        grad = (pre_ref[:, sl] + back_ref[:, sl].astype(f32)) * (1.0 + gain_ref[:, sl])
        total = total + grad * tok_ref[:, sl].astype(f32)
    inner = jnp.sum(total, axis=1, keepdims=True) / width
    inner = inner * inverse * inverse * inverse
    for _, sl in blocks(width):
        grad = (pre_ref[:, sl] + back_ref[:, sl].astype(f32)) * (1.0 + gain_ref[:, sl])
        dtok_ref[:, sl] = (grad * inverse - tok_ref[:, sl].astype(f32) * inner).astype(bf16)


def last_fast_kernel(tok_ref, inverse_ref, gain_ref, mix_ref, pre_ref, came_ref, *outs):
    class Packed:
        def __init__(self, which):
            self.which = which

        def __getitem__(self, at):
            value = came_ref[:, self.which, :, at[1]].astype(f32)
            return value.reshape(value.shape[0] * value.shape[1], LANES)

    last_kernel(tok_ref, inverse_ref, gain_ref, mix_ref, pre_ref, Packed(0), Packed(1), *outs)


def in_hbm(array):
    return pltpu.with_memory_space_constraint(array, pltpu.MemorySpace.HBM)


def call(kernel, outs, scratch=(), name=None, specs=None, hbm_outs=()):
    shapes = [
        pltpu.MemorySpace.HBM(s, d) if n in hbm_outs else jax.ShapeDtypeStruct(s, d)
        for n, (s, d) in enumerate(outs)
    ]
    where = {"s": pltpu.SMEM, "v": pltpu.VMEM, "h": pltpu.MemorySpace.HBM}
    spaces = {}
    if specs:
        spaces["in_specs"] = [pl.BlockSpec(memory_space=where[c]) for c in specs]
        spaces["out_specs"] = [
            pl.BlockSpec(memory_space=where["h" if n in hbm_outs else "v"]) for n in range(len(outs))
        ]
    return pl.pallas_call(
        kernel,
        out_shape=shapes,
        **spaces,
        scratch_shapes=[pltpu.VMEM(*s) if isinstance(s, tuple) else s for s in scratch],
        compiler_params=pltpu.CompilerParams(vmem_limit_bytes=24 << 20),
        name=name,
    )


def rows_in_order(part):
    if lax.axis_size("row") != 2:
        return lax.all_gather(part, "row")
    other = lax.ppermute(part, "row", [(0, 1), (1, 0)])
    first = lax.axis_index("row") == 0
    return jnp.stack([jnp.where(first, part, other), jnp.where(first, other, part)])


def rows_sum(part):
    if lax.axis_size("row") != 2:
        return lax.psum(part, "row")
    return part + lax.ppermute(part, "row", [(0, 1), (1, 0)])


def chain(own, decay, forward):
    count = lax.axis_size("row")
    hops = [(i, i + 1) if forward else (i + 1, i) for i in range(count - 1)]
    if count == 1:
        return jnp.zeros_like(own)
    arrived = lax.ppermute(own, "row", hops)
    wide = jnp.repeat(decay[0], own.shape[0] // decay.shape[1])[:, None]
    for _ in range(count - 2):
        passed = wide * arrived.astype(f32) + own.astype(f32)
        arrived = lax.ppermute(passed.astype(bf16), "row", hops)
    return arrived


def per_device(
    tokens,
    cotangent,
    timestep,
    mod_weight,
    proj_weight,
    step_weight,
    step_bias,
    rate_space,
    rate_time,
    skip_gain,
):
    frames = lax.axis_size("frame")
    rows = lax.axis_size("row")
    frame_id = lax.axis_index("frame")
    row_id = lax.axis_index("row")
    width = tokens.shape[-1]
    length = tokens.shape[1] * tokens.shape[2]
    clips = timestep.shape[0]
    clip_id = frame_id // (frames // clips)
    sites = length // frames
    heads = rate_space.shape[0]
    depth, pair = proj_weight.shape
    state = pair // 2
    mod_cols = mod_weight.shape[1]
    factor = (frames * rows * length) ** (-0.5)
    tok = tokens.reshape(length, width)
    grad = cotangent.reshape(length, width)

    activated = time_embed(timestep, mod_weight.shape[0]).astype(bf16)
    own_mod = jnp.dot(activated, mod_weight, preferred_element_type=f32)
    high = lax.reduce_precision(own_mod, 8, 7)
    own_mod = jnp.stack([high, own_mod - high]).astype(bf16)

    part = depth // rows
    own_proj = lax.dynamic_slice_in_dim(proj_weight, row_id * part, part, 0)
    to_all = [
        to_tiles(own_proj[None]),
        to_tiles(step_weight.T[None]),
        own_mod.reshape(1, -1, LANES),
    ]
    to_all = jnp.concatenate(to_all, axis=1)
    to_all = jnp.pad(to_all, ((0, 0), (0, -to_all.shape[1] % 8), (0, 0)))
    count = sites * width // LANES
    got = exchange(
        jnp.concatenate(
            [
                to_tiles(tok.reshape(frames, sites, width)),
                to_tiles(grad.reshape(frames, sites, width)),
                jnp.broadcast_to(to_all, (frames,) + to_all.shape[1:]),
            ],
            axis=1,
        )
    )
    site_tok = from_tiles(got[:, :count], sites, width).reshape(length, width)
    site_grad = from_tiles(got[:, count : 2 * count], sites, width).reshape(length, width)
    at = 2 * count
    size = part * pair // LANES
    proj_full = rows_in_order(got[:, at : at + size])
    proj_full = from_tiles(proj_full.reshape(rows * frames, size, LANES), part, pair)
    proj_full = proj_full.reshape(rows, frames, part, pair).transpose(1, 0, 2, 3)
    proj_full = proj_full.reshape(width, pair)
    at += size
    size = heads * depth // LANES
    step_full = from_tiles(got[:, at : at + size], heads, depth)
    step_full = step_full.transpose(1, 0, 2).reshape(heads, width)
    at += size
    size = 2 * clips * mod_cols // LANES
    mod_full = got[:, at : at + size].reshape(frames, 2, clips, mod_cols).astype(f32)
    mod_full = (mod_full[:, 0] + mod_full[:, 1]).transpose(1, 0, 2).reshape(clips, 2 * width)
    shift, gain = mod_full[:, :width], mod_full[:, width:]

    bias = step_bias[None]
    wide = (length, width)
    site_out, site_back, gproj, gstep, site_gmod = call(
        functools.partial(site_kernel, sites),
        [(wide, bf16), (wide, bf16), ((width, pair), f32), ((heads, width), f32), ((2 * clips, width), f32)],
        [(wide, bf16)] * 6,
        name="site",
    )(site_tok, site_grad, shift, gain, proj_full, step_full, bias, rate_time[None])

    came = exchange(
        jnp.concatenate(
            [
                to_tiles(site_out.reshape(frames, sites, width)),
                to_tiles(site_back.reshape(frames, sites, width)),
            ],
            axis=1,
        )
    )
    time_out = from_tiles(came[:, :count], sites, width).reshape(length, width)
    time_back = from_tiles(came[:, count:], sites, width).reshape(length, width)

    own_shift = lax.dynamic_slice_in_dim(shift, clip_id, 1, 0)
    own_gain = lax.dynamic_slice_in_dim(gain, clip_id, 1, 0)
    normed, coeffs, logits, inverse, decay, end_own, start_grad = call(
        band_kernel,
        [
            (wide, bf16),
            ((length, pair), bf16),
            ((length, heads), bf16),
            ((length, 1), f32),
            ((1, heads), f32),
            ((width, state), bf16),
            ((width, state), bf16),
        ],
        name="band",
    )(tok, grad, own_shift, own_gain, proj_full, step_full, bias, rate_space[None])
    state_in = chain(end_own, decay, True)
    later_grad = chain(start_grad, decay, False)
    mix, pre, gproj, gstep, gmod = call(
        space_kernel,
        [(wide, f32), (wide, f32), ((width, pair), bf16), ((heads, width), bf16), ((2, width), f32)],
        [(wide, bf16)] * 7,
        name="space",
    )(
        tok,
        grad,
        normed,
        coeffs,
        logits,
        inverse,
        proj_full,
        step_full,
        bias,
        rate_space[None],
        skip_gain[None],
        state_in,
        later_grad,
        gproj,
        gstep,
    )

    picked = (jnp.arange(clips) == clip_id).astype(f32)[:, None]
    gmod = jnp.concatenate(
        [site_gmod[:clips] + picked * gmod[0:1], site_gmod[clips:] + picked * gmod[1:2]], axis=1
    )
    gmod = gmod.reshape(clips, frames, mod_cols).transpose(1, 0, 2).astype(bf16)
    sent = jnp.concatenate(
        [
            to_tiles(gproj.reshape(frames, depth, pair)),
            to_tiles(gstep.reshape(heads, frames, depth).transpose(1, 0, 2)),
            gmod.reshape(frames, -1, LANES) if (clips * mod_cols) % LANES == 0 else gmod,
        ],
        axis=1,
    )
    size = sent.shape[1]
    sent = jnp.pad(sent, ((0, 0), (0, -size % 8), (0, 0)))
    sums = jnp.sum(exchange(sent).astype(f32), axis=0, keepdims=True)
    sums = rows_sum(sums) * factor
    at = depth * pair // LANES
    grad_proj = from_tiles(sums[:, :at], depth, pair)[0]
    size = heads * depth // LANES
    grad_step = from_tiles(sums[:, at : at + size], heads, depth)[0].T
    at += size
    size = clips * mod_cols // LANES
    mod_sum = sums[0, at : at + size].reshape(clips, mod_cols)
    grad_mod = jnp.dot(activated.astype(f32).T, mod_sum, precision=EXACT)

    mixed, d_tokens = call(last_kernel, [(wide, bf16), (wide, bf16)], name="last")(
        tok, inverse, own_gain, mix, pre, time_out, time_back
    )
    return (mixed.reshape(tokens.shape), d_tokens.reshape(tokens.shape), grad_proj, grad_step, grad_mod)


def fits(mesh, tokens, timestep, proj_weight, step_weight):
    frames, rows = mesh.shape["frame"], mesh.shape["row"]
    length, width = tokens.shape[2] * tokens.shape[1] // rows, tokens.shape[3]
    return (
        rows == 2
        and frames == 16
        and timestep.shape[0] == 1
        and length == LANES
        and length // frames == 8
        and width // frames == LANES
        and proj_weight.shape[1] == 2 * LANES
        and step_weight.shape[1] % 32 == 0
    )


def spread_over_frames(own, radix=4):
    frames = radix * radix

    def others(piece, stride):
        return [piece] + [
            lax.ppermute(piece, "frame", [(i, i ^ (d * stride)) for i in range(frames)])
            for d in range(1, radix)
        ]

    far = jnp.stack(others(own, radix))
    return jnp.concatenate(others(far, 1))


def sum_over_frames(keep, given, radix, ahead):
    def gathered(pieces, stride):
        frames = radix * radix
        return [pieces[0]] + [
            lax.ppermute(pieces[d], "frame", [(i, i ^ (d * stride)) for i in range(frames)])
            for d in range(1, radix)
        ]

    def total(pieces):
        value = pieces[0].astype(f32)
        for piece in pieces[1:]:
            value = value + piece.astype(f32)
        return value

    parts = [slice(d * radix, (d + 1) * radix) for d in range(radix)]
    near = [total([keep[p], given[p]]).astype(bf16) for p in parts]
    near, *ahead = lax.optimization_barrier((total(gathered(near, 1)).astype(bf16), *ahead))
    return total(gathered([near[d] for d in range(radix)], radix)), *ahead


def per_device_fast(
    tokens,
    cotangent,
    timestep,
    mod_weight,
    proj_weight,
    step_weight,
    step_bias,
    rate_space,
    rate_time,
    skip_gain,
):
    frames = lax.axis_size("frame")
    rows = lax.axis_size("row")
    ids = jnp.stack([lax.axis_index("frame"), lax.axis_index("row")]).astype(jnp.int32)
    width = tokens.shape[-1]
    length = tokens.shape[1] * tokens.shape[2]
    sites = length // frames
    heads = rate_space.shape[0]
    depth, pair = proj_weight.shape
    state = pair // 2
    mod_cols = mod_weight.shape[1]
    factor = (frames * rows * length) ** (-0.5)
    tok = tokens.reshape(length, width)
    grad = cotangent.reshape(length, width)
    wide = (length, width)
    bias = step_bias[None]
    swap = [(0, 1), (1, 0)]

    packed = (frames, 2, sites, width)
    size = depth // 2 * pair // LANES + heads // 2 + 8
    activated = time_embed(timestep, mod_weight.shape[0]).astype(bf16)
    sent, payload = call(
        start_kernel,
        [(packed, bf16), ((size, LANES), bf16)],
        [
            ((depth, pair), bf16),
            ((heads, depth), bf16),
            (mod_weight.shape, bf16),
            (packed, bf16),
            pltpu.SemaphoreType.DMA((7,)),
        ],
        name="start",
        specs="shhhhhv",
        hbm_outs=(0,),
    )(
        ids,
        in_hbm(tok.reshape(frames, sites, width)),
        in_hbm(grad.reshape(frames, sites, width)),
        in_hbm(proj_weight),
        in_hbm(step_weight.T),
        in_hbm(mod_weight),
        activated,
    )
    got = exchange(sent)
    payload = spread_over_frames(payload)
    other = lax.ppermute(payload, "row", swap)
    proj_full, step_full, shift, gain = call(
        functools.partial(unpack_kernel, 4),
        [((width, pair), bf16), ((heads, width), bf16), ((1, width), f32), ((1, width), f32)],
        name="unpack",
        specs="svv",
    )(ids, payload, other)

    sent, site_x, site_gmod, site_dc, site_dl = call(
        functools.partial(site_fast_kernel, sites),
        [
            (packed, bf16),
            (wide, bf16),
            ((2, width), f32),
            ((length, pair), bf16),
            ((length, heads), bf16),
        ],
        [
            (wide, bf16),
            (wide, bf16),
            (packed, bf16),
            (wide, bf16),
            ((2, width), f32),
            pltpu.SemaphoreType.DMA((6,)),
        ]
        + [(wide, bf16)] * 5,
        name="site",
        specs="vvvvvvv",
        hbm_outs=(0, 1, 2),
    )(got, shift, gain, proj_full, step_full, bias, rate_time[None])
    sent, proj_full = lax.optimization_barrier((sent, proj_full))
    came = exchange(sent)

    normed, coeffs, logits, inverse, _, give = call(
        band_fast_kernel,
        [
            (wide, bf16),
            ((length, pair), bf16),
            ((length, heads), bf16),
            ((length, 1), f32),
            ((1, heads), f32),
            ((width, state), bf16),
        ],
        name="band",
        specs="svvvvvvvv",
    )(ids, tok, grad, shift, gain, proj_full, step_full, bias, rate_space[None])
    arrived = lax.ppermute(give, "row", swap)
    halves = (frames, size, LANES)
    mix, pre, own_dc, own_dl, gmod = call(
        space_fast_kernel,
        [(wide, f32), (wide, f32), ((length, pair), bf16), ((length, heads), bf16), ((2, width), f32)],
        [(wide, bf16)] * 7,
        name="space",
        specs="s" + "v" * 12,
    )(
        ids,
        arrived,
        tok,
        grad,
        normed,
        coeffs,
        logits,
        inverse,
        proj_full,
        step_full,
        bias,
        rate_space[None],
        skip_gain[None],
    )
    keep, give = call(
        functools.partial(terms_kernel, 4),
        [(halves, bf16), (halves, bf16)],
        name="terms",
        specs="svvvvvvvv",
    )(ids, normed, own_dc, own_dl, gmod, site_x, site_dc, site_dl, site_gmod)
    given = lax.ppermute(give, "row", swap)
    mixed, d_tokens = call(last_fast_kernel, [(wide, bf16), (wide, bf16)], name="last")(
        tok, inverse, gain, mix, pre, came
    )
    terms, mixed, d_tokens = sum_over_frames(keep, given, 4, (mixed, d_tokens))
    other = lax.ppermute(terms, "row", swap)
    grad_proj, grad_step, grad_mod = call(
        functools.partial(finish_kernel, factor),
        [((depth, pair), f32), ((heads, depth), f32), ((mod_weight.shape[0], mod_cols), f32)],
        name="finish",
        specs="svvv",
    )(ids, terms, other, activated.astype(f32).T)
    return (mixed.reshape(tokens.shape), d_tokens.reshape(tokens.shape), grad_proj, grad_step.T, grad_mod)


def solution(mesh):
    placed = (
        P("frame", "row", None, None),
        P("frame", "row", None, None),
        P(),
        P(None, "frame"),
        P("frame", None),
        P("frame", None),
        P(),
        P(),
        P(),
        P(),
    )
    outs = (
        P("frame", "row", None, None),
        P("frame", "row", None, None),
        P("frame", None),
        P("frame", None),
        P(None, "frame"),
    )

    def step(tokens, cotangent, timestep, mod_weight, proj_weight, step_weight, *rest):
        fast = fits(mesh, tokens, timestep, proj_weight, step_weight)
        body = per_device_fast if fast else per_device
        return jax.shard_map(
            body, mesh=mesh, in_specs=placed, out_specs=outs, check_vma=False
        )(tokens, cotangent, timestep, mod_weight, proj_weight, step_weight, *rest)

    return step
```

```python
import functools
import math

import jax
import jax.numpy as jnp
from jax import lax
from jax.experimental import pallas as pl
from jax.experimental.pallas import tpu as pltpu
from jax.sharding import PartitionSpec as P

norm_eps = 1e-05
LANES = 128
f32 = jnp.float32
bf16 = jnp.bfloat16
EXACT = lax.Precision.HIGHEST


def time_embed(timestep, embed_dim):
    half_dim = embed_dim // 2
    frequency = jnp.exp(-math.log(10000.0) * jnp.arange(half_dim, dtype=f32) / half_dim)
    angles = timestep.astype(f32)[:, None] * frequency[None, :]
    return jax.nn.silu(jnp.concatenate([jnp.cos(angles), jnp.sin(angles)], axis=1))


def to_tiles(a):
    f, r, c = a.shape
    if r % 8 == 0 and c % LANES == 0:
        a = a.reshape(f, r // 8, 8, c // LANES, LANES).transpose(0, 1, 3, 2, 4)
    return a.reshape(f, r * c // LANES, LANES)


def from_tiles(a, r, c):
    f = a.shape[0]
    if r % 8 == 0 and c % LANES == 0:
        a = a.reshape(f, r // 8, c // LANES, 8, LANES).transpose(0, 1, 3, 2, 4)
    return a.reshape(f, r, c)


def exchange(packed):
    return lax.all_to_all(packed, "frame", split_axis=0, concat_axis=0, tiled=True)


def mm(a, b, ca, cb):
    return lax.dot_general(a, b, (((ca,), (cb,)), ((), ())), preferred_element_type=f32)


def exact(a, b, ca, cb):
    return lax.dot_general(
        a, b, (((ca,), (cb,)), ((), ())), preferred_element_type=f32, precision=EXACT
    )


def split(a):
    high = a.astype(bf16)
    return high, (a - high.astype(f32)).astype(bf16)


def head_map(heads, width):
    size = width // heads
    own = lax.broadcasted_iota(jnp.int32, (heads, width), 0)
    lane = lax.broadcasted_iota(jnp.int32, (heads, width), 1)
    return jnp.where(lane // size == own, 1.0, 0.0).astype(bf16)


def sequence_mask(length, sites):
    later = lax.broadcasted_iota(jnp.int32, (length, length), 0)
    earlier = lax.broadcasted_iota(jnp.int32, (length, length), 1)
    keep = later >= earlier
    if sites > 1:
        keep = keep & (later % sites == earlier % sites)
    return jnp.where(keep, 1.0, 0.0).astype(f32)


def blocks(width):
    return [(j, slice(j * LANES, (j + 1) * LANES)) for j in range(width // LANES)]


def spread_rows(rows, length):
    count = rows.shape[0]
    if count == 1:
        return rows
    part = (length // count, rows.shape[1])
    return jnp.concatenate([jnp.broadcast_to(rows[c : c + 1], part) for c in range(count)], axis=0)


def normalize_into(tok_ref, shift_ref, gain_ref, x_ref):
    length, width = tok_ref.shape
    total = jnp.zeros((length, LANES), f32)
    for _, sl in blocks(width):
        v = tok_ref[:, sl].astype(f32)
        total = total + v * v
    mean = jnp.sum(total, axis=1, keepdims=True) / width
    inverse = lax.rsqrt(mean + norm_eps)
    for _, sl in blocks(width):
        unit = tok_ref[:, sl].astype(f32) * inverse
        gain = spread_rows(gain_ref[:, sl], length)
        shift = spread_rows(shift_ref[:, sl], length)
        x_ref[:, sl] = (unit * (1.0 + gain) + shift).astype(bf16)
    return inverse


def steps_of(logits, bias, rate, mask):
    z = logits.astype(f32) + bias
    step = jnp.maximum(z, 0.0) + jnp.log1p(jnp.exp(-jnp.abs(z)))
    log_decay = -step * rate
    cum = exact(mask, log_decay, 1, 0)
    cum_rows = exact(log_decay, mask, 0, 1)
    return z, step, cum, cum_rows


def expand(parts, lanes_of):
    return mm(parts[0], lanes_of, 1, 0) + mm(parts[1], lanes_of, 1, 0)


def scan_block(j, x, grad, step_wide, scores, cum, cum_rows, heads, width, d_scores):
    size = width // heads
    per_block = LANES // size
    stepped = (x.astype(f32) * step_wide).astype(bf16)
    lane = lax.broadcasted_iota(jnp.int32, x.shape, 1)
    weights, steppeds, grads = [], [], []
    for i in range(per_block):
        h = j * per_block + i
        decay = jnp.exp(jnp.minimum(cum[:, h : h + 1] - cum_rows[h : h + 1, :], 0.0))
        inside = lane // size == i
        own_grad = jnp.where(inside, grad, jnp.zeros_like(grad))
        d_weight = mm(own_grad, stepped, 1, 1)
        d_scores = d_scores + d_weight * decay
        weights.append((scores * decay).astype(bf16))
        steppeds.append(jnp.where(inside, stepped, jnp.zeros_like(stepped)))
        grads.append(own_grad)
    out = mm(jnp.concatenate(weights, axis=1), jnp.concatenate(steppeds, axis=0), 1, 0)
    d_stepped = mm(jnp.concatenate(weights, axis=0), jnp.concatenate(grads, axis=0), 0, 0)
    return stepped, out, d_stepped, d_scores


def head_sums(high_ref, low_ref, lanes_of):
    return mm(high_ref[...], lanes_of, 1, 1) + mm(low_ref[...], lanes_of, 1, 1)


def put(refs, sl, value):
    high, low = split(value)
    refs[0][:, sl] = high
    refs[1][:, sl] = low


def start_kernel(ids_ref, tok_ref, grad_ref, proj_hbm, step_hbm, mod_hbm, active_ref, sent_ref, pay_ref,
                 proj_ref, step_ref, mod_ref, both_ref, sems):
    copies = [
        pltpu.make_async_copy(src, dst, sems.at[n])
        for n, (src, dst) in enumerate(
            [
                (proj_hbm, proj_ref),
                (step_hbm, step_ref),
                (mod_hbm, mod_ref),
                (tok_ref, both_ref.at[:, 0]),
                (grad_ref, both_ref.at[:, 1]),
                (both_ref.at[:, 0], sent_ref.at[:, 0]),
                (both_ref.at[:, 1], sent_ref.at[:, 1]),
            ]
        )
    ]
    for copy in copies[:5]:
        copy.start()
    copies[3].wait()
    copies[5].start()
    copies[4].wait()
    copies[6].start()
    row = ids_ref[1]
    part, pair = proj_ref.shape[0] // 2, proj_ref.shape[1]
    copies[0].wait()
    own = proj_ref[pl.ds(pl.multiple_of(row * part, part), part), :]
    at = 0
    for _, sl in blocks(pair):
        pay_ref[at : at + part, :] = own[:, sl]
        at += part
    copies[1].wait()
    part = step_ref.shape[0] // 2
    pay_ref[at : at + part, :] = step_ref[pl.ds(pl.multiple_of(row * part, part), part), :]
    at += part
    copies[2].wait()
    own = mm(active_ref[...], mod_ref[...], 1, 0)
    high = own.astype(bf16).astype(f32)
    pieces = [piece[:, sl] for piece in (high, own - high) for _, sl in blocks(own.shape[1])]
    pieces.append(jnp.zeros((8 - len(pieces), LANES), f32))
    pay_ref[at : at + 8, :] = jnp.concatenate(pieces, axis=0).astype(bf16)
    copies[5].wait()
    copies[6].wait()


def unpack_kernel(radix, ids_ref, own_ref, other_ref, proj_ref, step_ref, shift_ref, gain_ref):
    me, row = ids_ref[0], ids_ref[1]
    width, pair = proj_ref.shape
    frames = own_ref.shape[0]
    depth = width // frames
    part, heads = depth // 2, step_ref.shape[0] // 2
    cols = 2 * width // frames
    for i in range(frames):
        source = jnp.bitwise_xor(me, (i % radix) * radix + i // radix)
        for ref, half in ((own_ref, row), (other_ref, 1 - row)):
            rows = pl.ds(pl.multiple_of(source * depth + half * part, part), part)
            at = 0
            for _, sl in blocks(pair):
                proj_ref[rows, sl] = ref[i, at : at + part, :]
                at += part
            rows = pl.ds(pl.multiple_of(half * heads, heads), heads)
            lanes = pl.ds(pl.multiple_of(source * depth, depth), depth)
            step_ref[rows, lanes] = ref[i, at : at + heads, :]
            at += heads
        own = own_ref[i, at : at + 8, :].astype(f32)
        count = cols // LANES
        lanes_at = jnp.bitwise_and(source, frames // 2 - 1) * cols
        for k in range(count):
            value = own[k : k + 1, :] + own[count + k : count + k + 1, :]
            lanes = pl.ds(pl.multiple_of(lanes_at + k * LANES, LANES), LANES)

            @pl.when(source < frames // 2)
            def _():
                shift_ref[:, lanes] = value

            @pl.when(source >= frames // 2)
            def _():
                gain_ref[:, lanes] = value


def finish_kernel(factor, ids_ref, own_ref, other_ref, active_ref, proj_ref, step_ref, mod_ref):
    row = ids_ref[1]
    pair = proj_ref.shape[1]
    part, heads = proj_ref.shape[0] // 2, step_ref.shape[0] // 2
    for ref, half in ((own_ref, row), (other_ref, 1 - row)):
        rows = pl.ds(pl.multiple_of(half * part, part), part)
        at = 0
        for _, sl in blocks(pair):
            proj_ref[rows, sl] = ref[at : at + part, :] * factor
            at += part
        step_ref[pl.ds(pl.multiple_of(half * heads, heads), heads), :] = ref[at : at + heads, :] * factor
        at += heads
    for k, sl in blocks(mod_ref.shape[1]):
        mod_ref[:, sl] = active_ref[...] * (own_ref[at + k : at + k + 1, :] * factor)


def site_fast_kernel(sites, got_ref, *refs):
    inputs, (small_ref, sent_hbm, x_hbm, gmod_hbm, dc_ref, dl_ref) = refs[:4], refs[4:10]
    inputs = (*inputs, small_ref[0:1, :], small_ref[1:2, :])
    tok_ref, grad_ref, sent_ref, x_ref, gmod_ref, sems = refs[10:16]
    scratch = refs[16:]
    frames, width = got_ref.shape[0], got_ref.shape[3]
    for _, sl in blocks(width):
        for ref, which in ((tok_ref, 0), (grad_ref, 1)):
            value = got_ref[:, which, :, sl].astype(f32)
            ref[:, sl] = value.reshape(frames * sites, LANES).astype(bf16)

    parts = 2
    share = width // parts
    copies = []

    def begin(source, target):
        copy = pltpu.make_async_copy(source, target, sems.at[len(copies)])
        copy.start()
        copies.append(copy)

    def send(which, p):
        at = (slice(None), which, slice(None), slice(p * share, (p + 1) * share))
        begin(sent_ref.at[at], sent_hbm.at[at])

    class Packed:
        def __init__(self, which):
            self.which = which

        def __setitem__(self, at, value):
            if not copies:
                begin(x_ref, x_hbm)
            value = value.astype(f32).reshape(frames, sites, LANES)
            sent_ref[:, self.which, :, at[1]] = value.astype(bf16)
            if at[1].stop % share == 0:
                send(self.which, at[1].stop // share - 1)

    site_kernel(
        sites, tok_ref, grad_ref, *inputs, Packed(0), Packed(1), dc_ref, dl_ref, gmod_ref, x_ref, *scratch
    )
    begin(gmod_ref, gmod_hbm)
    for copy in copies:
        copy.wait()


def site_kernel(
    sites,
    tok_ref,
    grad_ref,
    shift_ref,
    gain_ref,
    proj_ref,
    step_ref,
    bias_ref,
    rate_ref,
    out_ref,
    back_ref,
    gproj_ref,
    gstep_ref,
    gmod_ref,
    x_ref,
    dn_ref,
    a_hi,
    a_lo,
    b_hi,
    b_lo,
):
    length, width = tok_ref.shape
    heads = step_ref.shape[0]
    state = proj_ref.shape[1] // 2
    clips = shift_ref.shape[0]
    inverse = normalize_into(tok_ref, shift_ref, gain_ref, x_ref)
    lanes_of = head_map(heads, width)
    mask = sequence_mask(length, sites)
    coeffs = mm(x_ref[...], proj_ref[...], 1, 0).astype(bf16)
    logits = mm(x_ref[...], step_ref[...], 1, 1).astype(bf16)
    rate = rate_ref[...]
    z, step, cum, cum_rows = steps_of(logits, bias_ref[...], rate, mask)
    b_part, c_part = coeffs[:, :state], coeffs[:, state:]
    scores = mm(c_part, b_part, 1, 1) * (mask / state)
    step_parts = split(step)
    d_scores = jnp.zeros((length, length), f32)
    for j, sl in blocks(width):
        x, grad = x_ref[:, sl], grad_ref[:, sl]
        step_wide = expand(step_parts, lanes_of[:, sl])
        stepped, out, d_stepped, d_scores = scan_block(
            j, x, grad, step_wide, scores, cum, cum_rows, heads, width, d_scores
        )
        out_ref[:, sl] = out.astype(bf16)
        dn_ref[:, sl] = (step_wide * d_stepped).astype(bf16)
        put((a_hi, a_lo), sl, grad.astype(f32) * out - stepped.astype(f32) * d_stepped)
        put((b_hi, b_lo), sl, x.astype(f32) * d_stepped)
    d_cum = head_sums(a_hi, a_lo, lanes_of)
    d_step = head_sums(b_hi, b_lo, lanes_of)
    d_log = exact(mask, d_cum, 0, 0)
    d_logits = (jax.nn.sigmoid(z) * (d_step - rate * d_log)).astype(bf16)
    d_scores = (d_scores * (mask / state)).astype(bf16)
    d_coeffs = jnp.concatenate(
        [mm(d_scores, c_part, 0, 0), mm(d_scores, b_part, 1, 0)], axis=1
    ).astype(bf16)
    for _, sl in blocks(width):
        back = (
            dn_ref[:, sl].astype(f32)
            + mm(d_coeffs, proj_ref[sl, :], 1, 1)
            + mm(d_logits, step_ref[:, sl], 1, 0)
        ).astype(bf16)
        back_ref[:, sl] = back
        back = back.astype(f32)
        scaled = back * (tok_ref[:, sl].astype(f32) * inverse)
        for c in range(clips):
            rows = slice(c * (length // clips), (c + 1) * (length // clips))
            gmod_ref[c : c + 1, sl] = jnp.sum(back[rows], axis=0, keepdims=True)
            gmod_ref[clips + c : clips + c + 1, sl] = jnp.sum(scaled[rows], axis=0, keepdims=True)
        if gproj_ref.shape == (width, 2 * state):
            gproj_ref[sl, :] = mm(x_ref[:, sl], d_coeffs, 0, 0)
            gstep_ref[:, sl] = mm(d_logits, x_ref[:, sl], 0, 0)
    if gproj_ref.shape != (width, 2 * state):
        gproj_ref[...] = d_coeffs
        gstep_ref[...] = d_logits


def band_fast_kernel(ids_ref, *refs):
    small_ref, give_ref = refs[6], refs[-1]
    inputs = (*refs[:6], small_ref[0:1, :], small_ref[2:3, :])
    band_kernel(*inputs, *refs[7:-1], None, give_ref, first=ids_ref[1] == 0)


def band_kernel(
    tok_ref,
    grad_ref,
    shift_ref,
    gain_ref,
    proj_ref,
    step_ref,
    bias_ref,
    rate_ref,
    x_ref,
    coeffs_ref,
    logits_ref,
    inverse_ref,
    decay_ref,
    end_ref,
    own_ref,
    first=None,
):
    length, width = tok_ref.shape
    heads = step_ref.shape[0]
    state = proj_ref.shape[1] // 2
    inverse_ref[...] = normalize_into(tok_ref, shift_ref, gain_ref, x_ref)
    lanes_of = head_map(heads, width)
    mask = sequence_mask(length, 1)
    coeffs = mm(x_ref[...], proj_ref[...], 1, 0).astype(bf16)
    logits = mm(x_ref[...], step_ref[...], 1, 1).astype(bf16)
    coeffs_ref[...] = coeffs
    logits_ref[...] = logits
    _, step, cum, _ = steps_of(logits, bias_ref[...], rate_ref[...], mask)
    last = cum[length - 1 : length, :]
    decay_ref[...] = jnp.exp(last)
    lead = split(jnp.exp(last - cum) * step)
    reach = split(jnp.exp(cum) / state)
    b_part, c_part = coeffs[:, :state], coeffs[:, state:]
    if first is not None:
        gain = split(jnp.where(first, jnp.exp(last - cum) * step, jnp.exp(cum) / state))
        other = jnp.where(first, b_part, c_part)
        for _, sl in blocks(width):
            value = jnp.where(first, x_ref[:, sl], grad_ref[:, sl]).astype(f32)
            value = (value * expand(gain, lanes_of[:, sl])).astype(bf16)
            own_ref[sl, :] = mm(value, other, 0, 0).astype(bf16)
        return
    for _, sl in blocks(width):
        lead_wide = expand(lead, lanes_of[:, sl])
        reach_wide = expand(reach, lanes_of[:, sl])
        scaled = (x_ref[:, sl].astype(f32) * lead_wide).astype(bf16)
        faded = (grad_ref[:, sl].astype(f32) * reach_wide).astype(bf16)
        end_ref[sl, :] = mm(scaled, b_part, 0, 0).astype(bf16)
        own_ref[sl, :] = mm(faded, c_part, 0, 0).astype(bf16)


def terms_kernel(radix, ids_ref, x_ref, dc_ref, dl_ref, gmod_ref, site_x, site_dc, site_dl, site_gmod,
                 keep_ref, give_ref):
    me, first = ids_ref[0], ids_ref[1] == 0
    width = x_ref.shape[1]
    coeffs = jnp.concatenate([dc_ref[...], site_dc[...]], axis=0)
    logits = jnp.concatenate([dl_ref[...], site_dl[...]], axis=0)
    frames = keep_ref.shape[0]
    share = 2 * width // LANES // frames

    def put_halves(j, at, value):
        part = value.shape[0] // 2
        own = jnp.where(first, value[:part], value[part:]).astype(bf16)
        other = jnp.where(first, value[part:], value[:part]).astype(bf16)
        for _, sl in blocks(value.shape[1]):
            keep_ref[j, at : at + part, :] = own[:, sl]
            give_ref[j, at : at + part, :] = other[:, sl]
            at += part
        return at

    for j, sl in blocks(width):
        offset = jnp.bitwise_xor(me, j)
        place = jnp.bitwise_and(offset, radix - 1) * radix + offset // radix
        tall = jnp.concatenate([x_ref[:, sl], site_x[:, sl]], axis=0)
        at = put_halves(place, 0, mm(tall, coeffs, 0, 0))
        at = put_halves(place, at, mm(logits, tall, 0, 0))
        rows = []
        for n in range(j * share, (j + 1) * share):
            which, at_lane = n // (width // LANES), n % (width // LANES) * LANES
            lanes = slice(at_lane, at_lane + LANES)
            rows.append(gmod_ref[which : which + 1, lanes] + site_gmod[which : which + 1, lanes])
        rows.append(jnp.zeros((8 - len(rows), LANES), f32))
        rows = jnp.concatenate(rows, axis=0).astype(bf16)
        keep_ref[place, at : at + 8, :] = rows
        give_ref[place, at : at + 8, :] = rows


def space_fast_kernel(ids_ref, arrived_ref, *refs):
    inputs, small_ref, outs = refs[:8], refs[8], refs[9:]
    inputs = (*inputs, *(small_ref[n : n + 1, :] for n in (0, 2, 3)))
    first = ids_ref[1] == 0

    class Arrived:
        def __init__(self, wanted):
            self.wanted = wanted

        def __getitem__(self, at):
            value = arrived_ref[at]
            return jnp.where(self.wanted, value, jnp.zeros_like(value))

    space_kernel(*inputs, Arrived(jnp.logical_not(first)), Arrived(first), None, None, *outs)


def space_kernel(
    tok_ref,
    grad_ref,
    x_ref,
    coeffs_ref,
    logits_ref,
    inverse_ref,
    proj_ref,
    step_ref,
    bias_ref,
    rate_ref,
    skip_ref,
    state_ref,
    later_ref,
    gproj_in,
    gstep_in,
    mix_ref,
    pre_ref,
    gproj_ref,
    gstep_ref,
    gmod_ref,
    dn_ref,
    a_hi,
    a_lo,
    b_hi,
    b_lo,
    c_hi,
    c_lo,
):
    length, width = tok_ref.shape
    heads = step_ref.shape[0]
    state = proj_ref.shape[1] // 2
    lanes_of = head_map(heads, width)
    mask = sequence_mask(length, 1)
    coeffs = coeffs_ref[...]
    rate = rate_ref[...]
    z, step, cum, cum_rows = steps_of(logits_ref[...], bias_ref[...], rate, mask)
    last = cum[length - 1 : length, :]
    rest = jnp.exp(last - cum)
    lead = rest * step
    b_part, c_part = coeffs[:, :state], coeffs[:, state:]
    scores = mm(c_part, b_part, 1, 1) * (mask / state)
    step_parts, lead_parts, reach_parts = split(step), split(lead), split(jnp.exp(cum) / state)
    skip_parts = split(jnp.broadcast_to(skip_ref[...], (8, heads)))
    d_scores = jnp.zeros((length, length), f32)
    d_b = jnp.zeros((length, state), f32)
    d_c = jnp.zeros((length, state), f32)
    d_end = jnp.zeros((heads, state), f32)
    for j, sl in blocks(width):
        x, grad = x_ref[:, sl], grad_ref[:, sl]
        wide_map = lanes_of[:, sl]
        step_wide = expand(step_parts, wide_map)
        lead_wide = expand(lead_parts, wide_map)
        reach_wide = expand(reach_parts, wide_map)
        stepped, out, d_stepped, d_scores = scan_block(
            j, x, grad, step_wide, scores, cum, cum_rows, heads, width, d_scores
        )
        x, wide = x.astype(f32), grad.astype(f32)
        before, later = state_ref[sl, :], later_ref[sl, :]
        carried = mm(c_part, before, 1, 1) * reach_wide
        d_c = d_c + mm((wide * reach_wide).astype(bf16), before, 1, 0)
        d_b = d_b + mm((x * lead_wide).astype(bf16), later, 1, 0)
        d_scaled = mm(b_part, later, 1, 1)
        both = split(before.astype(f32) * later.astype(f32))
        d_end = d_end + mm(wide_map, both[0], 1, 0) + mm(wide_map, both[1], 1, 0)
        total = out + carried
        skip = expand(skip_parts, wide_map)[0:1, :]
        mix_ref[:, sl] = total + skip * x
        d_x = (step_wide * d_stepped + d_scaled * lead_wide).astype(bf16)
        dn_ref[:, sl] = d_x + (wide * skip).astype(bf16)
        put((a_hi, a_lo), sl, wide * total - stepped.astype(f32) * d_stepped)
        put((b_hi, b_lo), sl, x * d_stepped)
        put((c_hi, c_lo), sl, x * d_scaled)
    d_lead = head_sums(c_hi, c_lo, lanes_of)
    d_step = head_sums(b_hi, b_lo, lanes_of) + d_lead * rest
    fall = d_lead * lead
    d_cum = head_sums(a_hi, a_lo, lanes_of) - fall
    ones = jnp.ones((8, state), f32)
    end_sum = exact(ones, d_end, 1, 1)[0:1, :] * jnp.exp(last)
    end_sum = end_sum + jnp.sum(fall, axis=0, keepdims=True)
    d_log = exact(mask, d_cum, 0, 0) + end_sum
    d_logits = (jax.nn.sigmoid(z) * (d_step - rate * d_log)).astype(bf16)
    d_scores = (d_scores * (mask / state)).astype(bf16)
    d_coeffs = jnp.concatenate(
        [mm(d_scores, c_part, 0, 0) + d_b, mm(d_scores, b_part, 1, 0) + d_c], axis=1
    ).astype(bf16)
    inverse = inverse_ref[...]
    if gproj_in is None:
        gproj_ref[...] = d_coeffs
        gstep_ref[...] = d_logits
    for _, sl in blocks(width):
        pre = (
            dn_ref[:, sl].astype(f32)
            + mm(d_coeffs, proj_ref[sl, :], 1, 1)
            + mm(d_logits, step_ref[:, sl], 1, 0)
        )
        pre_ref[:, sl] = pre
        scaled = pre * (tok_ref[:, sl].astype(f32) * inverse)
        gmod_ref[0:1, sl] = jnp.sum(pre, axis=0, keepdims=True)
        gmod_ref[1:2, sl] = jnp.sum(scaled, axis=0, keepdims=True)
        if gproj_in is not None:
            gproj_ref[sl, :] = (gproj_in[sl, :] + mm(x_ref[:, sl], d_coeffs, 0, 0)).astype(bf16)
            gstep_ref[:, sl] = (gstep_in[:, sl] + mm(d_logits, x_ref[:, sl], 0, 0)).astype(bf16)


def last_kernel(tok_ref, inverse_ref, gain_ref, mix_ref, pre_ref, time_ref, back_ref, out_ref, dtok_ref):
    length, width = tok_ref.shape
    inverse = inverse_ref[...]
    total = jnp.zeros((length, LANES), f32)
    for _, sl in blocks(width):
        out_ref[:, sl] = (mix_ref[:, sl] + time_ref[:, sl].astype(f32)).astype(bf16)
        grad = (pre_ref[:, sl] + back_ref[:, sl].astype(f32)) * (1.0 + gain_ref[:, sl])
        total = total + grad * tok_ref[:, sl].astype(f32)
    inner = jnp.sum(total, axis=1, keepdims=True) / width
    inner = inner * inverse * inverse * inverse
    for _, sl in blocks(width):
        grad = (pre_ref[:, sl] + back_ref[:, sl].astype(f32)) * (1.0 + gain_ref[:, sl])
        dtok_ref[:, sl] = (grad * inverse - tok_ref[:, sl].astype(f32) * inner).astype(bf16)


def last_fast_kernel(tok_ref, inverse_ref, gain_ref, mix_ref, pre_ref, came_ref, *outs):
    class Packed:
        def __init__(self, which):
            self.which = which

        def __getitem__(self, at):
            value = came_ref[:, self.which, :, at[1]].astype(f32)
            return value.reshape(value.shape[0] * value.shape[1], LANES)

    last_kernel(tok_ref, inverse_ref, gain_ref, mix_ref, pre_ref, Packed(0), Packed(1), *outs)


def in_hbm(array):
    return pltpu.with_memory_space_constraint(array, pltpu.MemorySpace.HBM)


def call(kernel, outs, scratch=(), name=None, specs=None, hbm_outs=()):
    shapes = [
        pltpu.MemorySpace.HBM(s, d) if n in hbm_outs else jax.ShapeDtypeStruct(s, d)
        for n, (s, d) in enumerate(outs)
    ]
    where = {"s": pltpu.SMEM, "v": pltpu.VMEM, "h": pltpu.MemorySpace.HBM}
    spaces = {}
    if specs:
        spaces["in_specs"] = [pl.BlockSpec(memory_space=where[c]) for c in specs]
        spaces["out_specs"] = [
            pl.BlockSpec(memory_space=where["h" if n in hbm_outs else "v"]) for n in range(len(outs))
        ]
    return pl.pallas_call(
        kernel,
        out_shape=shapes,
        **spaces,
        scratch_shapes=[pltpu.VMEM(*s) if isinstance(s, tuple) else s for s in scratch],
        compiler_params=pltpu.CompilerParams(vmem_limit_bytes=24 << 20),
        name=name,
    )


def rows_in_order(part):
    if lax.axis_size("row") != 2:
        return lax.all_gather(part, "row")
    other = lax.ppermute(part, "row", [(0, 1), (1, 0)])
    first = lax.axis_index("row") == 0
    return jnp.stack([jnp.where(first, part, other), jnp.where(first, other, part)])


def rows_sum(part):
    if lax.axis_size("row") != 2:
        return lax.psum(part, "row")
    return part + lax.ppermute(part, "row", [(0, 1), (1, 0)])


def chain(own, decay, forward):
    count = lax.axis_size("row")
    hops = [(i, i + 1) if forward else (i + 1, i) for i in range(count - 1)]
    if count == 1:
        return jnp.zeros_like(own)
    arrived = lax.ppermute(own, "row", hops)
    wide = jnp.repeat(decay[0], own.shape[0] // decay.shape[1])[:, None]
    for _ in range(count - 2):
        passed = wide * arrived.astype(f32) + own.astype(f32)
        arrived = lax.ppermute(passed.astype(bf16), "row", hops)
    return arrived


def per_device(
    tokens,
    cotangent,
    timestep,
    mod_weight,
    proj_weight,
    step_weight,
    step_bias,
    rate_space,
    rate_time,
    skip_gain,
):
    frames = lax.axis_size("frame")
    rows = lax.axis_size("row")
    frame_id = lax.axis_index("frame")
    row_id = lax.axis_index("row")
    width = tokens.shape[-1]
    length = tokens.shape[1] * tokens.shape[2]
    clips = timestep.shape[0]
    clip_id = frame_id // (frames // clips)
    sites = length // frames
    heads = rate_space.shape[0]
    depth, pair = proj_weight.shape
    state = pair // 2
    mod_cols = mod_weight.shape[1]
    factor = (frames * rows * length) ** (-0.5)
    tok = tokens.reshape(length, width)
    grad = cotangent.reshape(length, width)

    activated = time_embed(timestep, mod_weight.shape[0]).astype(bf16)
    own_mod = jnp.dot(activated, mod_weight, preferred_element_type=f32)
    high = lax.reduce_precision(own_mod, 8, 7)
    own_mod = jnp.stack([high, own_mod - high]).astype(bf16)

    part = depth // rows
    own_proj = lax.dynamic_slice_in_dim(proj_weight, row_id * part, part, 0)
    to_all = [
        to_tiles(own_proj[None]),
        to_tiles(step_weight.T[None]),
        own_mod.reshape(1, -1, LANES),
    ]
    to_all = jnp.concatenate(to_all, axis=1)
    to_all = jnp.pad(to_all, ((0, 0), (0, -to_all.shape[1] % 8), (0, 0)))
    count = sites * width // LANES
    got = exchange(
        jnp.concatenate(
            [
                to_tiles(tok.reshape(frames, sites, width)),
                to_tiles(grad.reshape(frames, sites, width)),
                jnp.broadcast_to(to_all, (frames,) + to_all.shape[1:]),
            ],
            axis=1,
        )
    )
    site_tok = from_tiles(got[:, :count], sites, width).reshape(length, width)
    site_grad = from_tiles(got[:, count : 2 * count], sites, width).reshape(length, width)
    at = 2 * count
    size = part * pair // LANES
    proj_full = rows_in_order(got[:, at : at + size])
    proj_full = from_tiles(proj_full.reshape(rows * frames, size, LANES), part, pair)
    proj_full = proj_full.reshape(rows, frames, part, pair).transpose(1, 0, 2, 3)
    proj_full = proj_full.reshape(width, pair)
    at += size
    size = heads * depth // LANES
    step_full = from_tiles(got[:, at : at + size], heads, depth)
    step_full = step_full.transpose(1, 0, 2).reshape(heads, width)
    at += size
    size = 2 * clips * mod_cols // LANES
    mod_full = got[:, at : at + size].reshape(frames, 2, clips, mod_cols).astype(f32)
    mod_full = (mod_full[:, 0] + mod_full[:, 1]).transpose(1, 0, 2).reshape(clips, 2 * width)
    shift, gain = mod_full[:, :width], mod_full[:, width:]

    bias = step_bias[None]
    wide = (length, width)
    site_out, site_back, gproj, gstep, site_gmod = call(
        functools.partial(site_kernel, sites),
        [(wide, bf16), (wide, bf16), ((width, pair), f32), ((heads, width), f32), ((2 * clips, width), f32)],
        [(wide, bf16)] * 6,
        name="site",
    )(site_tok, site_grad, shift, gain, proj_full, step_full, bias, rate_time[None])

    came = exchange(
        jnp.concatenate(
            [
                to_tiles(site_out.reshape(frames, sites, width)),
                to_tiles(site_back.reshape(frames, sites, width)),
            ],
            axis=1,
        )
    )
    time_out = from_tiles(came[:, :count], sites, width).reshape(length, width)
    time_back = from_tiles(came[:, count:], sites, width).reshape(length, width)

    own_shift = lax.dynamic_slice_in_dim(shift, clip_id, 1, 0)
    own_gain = lax.dynamic_slice_in_dim(gain, clip_id, 1, 0)
    normed, coeffs, logits, inverse, decay, end_own, start_grad = call(
        band_kernel,
        [
            (wide, bf16),
            ((length, pair), bf16),
            ((length, heads), bf16),
            ((length, 1), f32),
            ((1, heads), f32),
            ((width, state), bf16),
            ((width, state), bf16),
        ],
        name="band",
    )(tok, grad, own_shift, own_gain, proj_full, step_full, bias, rate_space[None])
    state_in = chain(end_own, decay, True)
    later_grad = chain(start_grad, decay, False)
    mix, pre, gproj, gstep, gmod = call(
        space_kernel,
        [(wide, f32), (wide, f32), ((width, pair), bf16), ((heads, width), bf16), ((2, width), f32)],
        [(wide, bf16)] * 7,
        name="space",
    )(
        tok,
        grad,
        normed,
        coeffs,
        logits,
        inverse,
        proj_full,
        step_full,
        bias,
        rate_space[None],
        skip_gain[None],
        state_in,
        later_grad,
        gproj,
        gstep,
    )

    picked = (jnp.arange(clips) == clip_id).astype(f32)[:, None]
    gmod = jnp.concatenate(
        [site_gmod[:clips] + picked * gmod[0:1], site_gmod[clips:] + picked * gmod[1:2]], axis=1
    )
    gmod = gmod.reshape(clips, frames, mod_cols).transpose(1, 0, 2).astype(bf16)
    sent = jnp.concatenate(
        [
            to_tiles(gproj.reshape(frames, depth, pair)),
            to_tiles(gstep.reshape(heads, frames, depth).transpose(1, 0, 2)),
            gmod.reshape(frames, -1, LANES) if (clips * mod_cols) % LANES == 0 else gmod,
        ],
        axis=1,
    )
    size = sent.shape[1]
    sent = jnp.pad(sent, ((0, 0), (0, -size % 8), (0, 0)))
    sums = jnp.sum(exchange(sent).astype(f32), axis=0, keepdims=True)
    sums = rows_sum(sums) * factor
    at = depth * pair // LANES
    grad_proj = from_tiles(sums[:, :at], depth, pair)[0]
    size = heads * depth // LANES
    grad_step = from_tiles(sums[:, at : at + size], heads, depth)[0].T
    at += size
    size = clips * mod_cols // LANES
    mod_sum = sums[0, at : at + size].reshape(clips, mod_cols)
    grad_mod = jnp.dot(activated.astype(f32).T, mod_sum, precision=EXACT)

    mixed, d_tokens = call(last_kernel, [(wide, bf16), (wide, bf16)], name="last")(
        tok, inverse, own_gain, mix, pre, time_out, time_back
    )
    return (mixed.reshape(tokens.shape), d_tokens.reshape(tokens.shape), grad_proj, grad_step, grad_mod)


def fits(mesh, tokens, timestep, proj_weight, step_weight):
    frames, rows = mesh.shape["frame"], mesh.shape["row"]
    length, width = tokens.shape[2] * tokens.shape[1] // rows, tokens.shape[3]
    return (
        rows == 2
        and frames == 16
        and timestep.shape[0] == 1
        and length == LANES
        and length // frames == 8
        and width // frames == LANES
        and proj_weight.shape[1] == 2 * LANES
        and step_weight.shape[1] % 32 == 0
    )


def spread_over_frames(own, radix=4):
    frames = radix * radix

    def others(piece, stride):
        return [piece] + [
            lax.ppermute(piece, "frame", [(i, i ^ (d * stride)) for i in range(frames)])
            for d in range(1, radix)
        ]

    far = jnp.stack(others(own, radix))
    return jnp.concatenate(others(far, 1))


def sum_over_frames(keep, given, radix, ahead):
    frames = radix * radix

    def total(pieces):
        value = pieces[0].astype(f32)
        for piece in pieces[1:]:
            value = value + piece.astype(f32)
        return value

    def partner(piece, offset):
        return lax.ppermute(piece, "frame", [(i, i ^ offset) for i in range(frames)])

    parts = [slice(d * radix, (d + 1) * radix) for d in range(radix)]
    near = [total([keep[p], given[p]]).astype(bf16) for p in parts]
    near = [near[0]] + [partner(near[d], d) for d in range(1, radix)]
    near, ahead = lax.optimization_barrier((near, ahead))
    value = total(near)
    while value.shape[0] > 1:
        half = value.shape[0] // 2
        value = value.astype(bf16)
        value = total([value[:half], partner(value[half:], half * radix)])
    return value[0], *ahead


def per_device_fast(
    tokens,
    cotangent,
    timestep,
    mod_weight,
    proj_weight,
    step_weight,
    step_bias,
    rate_space,
    rate_time,
    skip_gain,
):
    frames = lax.axis_size("frame")
    rows = lax.axis_size("row")
    ids = jnp.stack([lax.axis_index("frame"), lax.axis_index("row")]).astype(jnp.int32)
    width = tokens.shape[-1]
    length = tokens.shape[1] * tokens.shape[2]
    sites = length // frames
    heads = rate_space.shape[0]
    depth, pair = proj_weight.shape
    state = pair // 2
    mod_cols = mod_weight.shape[1]
    factor = (frames * rows * length) ** (-0.5)
    tok = tokens.reshape(length, width)
    grad = cotangent.reshape(length, width)
    wide = (length, width)
    small = jnp.stack([step_bias, rate_time, rate_space, skip_gain])
    swap = [(0, 1), (1, 0)]

    packed = (frames, 2, sites, width)
    size = depth // 2 * pair // LANES + heads // 2 + 8
    activated = time_embed(timestep, mod_weight.shape[0]).astype(bf16)
    sent, payload = call(
        start_kernel,
        [(packed, bf16), ((size, LANES), bf16)],
        [
            ((depth, pair), bf16),
            ((heads, depth), bf16),
            (mod_weight.shape, bf16),
            (packed, bf16),
            pltpu.SemaphoreType.DMA((7,)),
        ],
        name="start",
        specs="shhhhhv",
        hbm_outs=(0,),
    )(
        ids,
        in_hbm(tok.reshape(frames, sites, width)),
        in_hbm(grad.reshape(frames, sites, width)),
        in_hbm(proj_weight),
        in_hbm(step_weight.T),
        in_hbm(mod_weight),
        activated,
    )
    got = exchange(sent)
    payload = spread_over_frames(payload)
    other = lax.ppermute(payload, "row", swap)
    proj_full, step_full, shift, gain = call(
        functools.partial(unpack_kernel, 4),
        [((width, pair), bf16), ((heads, width), bf16), ((1, width), f32), ((1, width), f32)],
        name="unpack",
        specs="svv",
    )(ids, payload, other)

    normed, coeffs, logits, inverse, _, give = call(
        band_fast_kernel,
        [
            (wide, bf16),
            ((length, pair), bf16),
            ((length, heads), bf16),
            ((length, 1), f32),
            ((1, heads), f32),
            ((width, state), bf16),
        ],
        name="band",
        specs="svvvvvvv",
    )(ids, tok, grad, shift, gain, proj_full, step_full, small)
    arrived = lax.ppermute(give, "row", swap)

    sent, site_x, site_gmod, site_dc, site_dl = call(
        functools.partial(site_fast_kernel, sites),
        [
            (packed, bf16),
            (wide, bf16),
            ((2, width), f32),
            ((length, pair), bf16),
            ((length, heads), bf16),
        ],
        [
            (wide, bf16),
            (wide, bf16),
            (packed, bf16),
            (wide, bf16),
            ((2, width), f32),
            pltpu.SemaphoreType.DMA((6,)),
        ]
        + [(wide, bf16)] * 5,
        name="site",
        specs="vvvvvv",
        hbm_outs=(0, 1, 2),
    )(got, shift, gain, proj_full, step_full, small)
    sent, arrived = lax.optimization_barrier((sent, arrived))
    came = exchange(sent)

    halves = (frames, size, LANES)
    mix, pre, own_dc, own_dl, gmod = call(
        space_fast_kernel,
        [(wide, f32), (wide, f32), ((length, pair), bf16), ((length, heads), bf16), ((2, width), f32)],
        [(wide, bf16)] * 7,
        name="space",
        specs="s" + "v" * 10,
    )(
        ids,
        arrived,
        tok,
        grad,
        normed,
        coeffs,
        logits,
        inverse,
        proj_full,
        step_full,
        small,
    )
    keep, give = call(
        functools.partial(terms_kernel, 4),
        [(halves, bf16), (halves, bf16)],
        name="terms",
        specs="svvvvvvvv",
    )(ids, normed, own_dc, own_dl, gmod, site_x, site_dc, site_dl, site_gmod)
    given = lax.ppermute(give, "row", swap)
    mixed, d_tokens = call(last_fast_kernel, [(wide, bf16), (wide, bf16)], name="last")(
        tok, inverse, gain, mix, pre, came
    )
    terms, mixed, d_tokens = sum_over_frames(keep, given, 4, (mixed, d_tokens))
    other = lax.ppermute(terms, "row", swap)
    grad_proj, grad_step, grad_mod = call(
        functools.partial(finish_kernel, factor),
        [((depth, pair), f32), ((heads, depth), f32), ((mod_weight.shape[0], mod_cols), f32)],
        name="finish",
        specs="svvv",
    )(ids, terms, other, activated.astype(f32).T)
    return (mixed.reshape(tokens.shape), d_tokens.reshape(tokens.shape), grad_proj, grad_step.T, grad_mod)


def solution(mesh):
    placed = (
        P("frame", "row", None, None),
        P("frame", "row", None, None),
        P(),
        P(None, "frame"),
        P("frame", None),
        P("frame", None),
        P(),
        P(),
        P(),
        P(),
    )
    outs = (
        P("frame", "row", None, None),
        P("frame", "row", None, None),
        P("frame", None),
        P("frame", None),
        P(None, "frame"),
    )

    def step(tokens, cotangent, timestep, mod_weight, proj_weight, step_weight, *rest):
        fast = fits(mesh, tokens, timestep, proj_weight, step_weight)
        body = per_device_fast if fast else per_device
        return jax.shard_map(
            body, mesh=mesh, in_specs=placed, out_specs=outs, check_vma=False
        )(tokens, cotangent, timestep, mod_weight, proj_weight, step_weight, *rest)

    return step
```

```python
import functools
import math

import jax
import jax.numpy as jnp
from jax import lax
from jax.experimental import pallas as pl
from jax.experimental.pallas import tpu as pltpu
from jax.sharding import PartitionSpec as P

norm_eps = 1e-05
LANES = 128
f32 = jnp.float32
bf16 = jnp.bfloat16
EXACT = lax.Precision.HIGHEST


def time_embed(timestep, embed_dim):
    half_dim = embed_dim // 2
    frequency = jnp.exp(-math.log(10000.0) * jnp.arange(half_dim, dtype=f32) / half_dim)
    angles = timestep.astype(f32)[:, None] * frequency[None, :]
    return jax.nn.silu(jnp.concatenate([jnp.cos(angles), jnp.sin(angles)], axis=1))


def to_tiles(a):
    f, r, c = a.shape
    if r % 8 == 0 and c % LANES == 0:
        a = a.reshape(f, r // 8, 8, c // LANES, LANES).transpose(0, 1, 3, 2, 4)
    return a.reshape(f, r * c // LANES, LANES)


def from_tiles(a, r, c):
    f = a.shape[0]
    if r % 8 == 0 and c % LANES == 0:
        a = a.reshape(f, r // 8, c // LANES, 8, LANES).transpose(0, 1, 3, 2, 4)
    return a.reshape(f, r, c)


def exchange(packed):
    return lax.all_to_all(packed, "frame", split_axis=0, concat_axis=0, tiled=True)


def mm(a, b, ca, cb):
    return lax.dot_general(a, b, (((ca,), (cb,)), ((), ())), preferred_element_type=f32)


def exact(a, b, ca, cb):
    return lax.dot_general(
        a, b, (((ca,), (cb,)), ((), ())), preferred_element_type=f32, precision=EXACT
    )


def split(a):
    high = a.astype(bf16)
    return high, (a - high.astype(f32)).astype(bf16)


def head_map(heads, width):
    size = width // heads
    own = lax.broadcasted_iota(jnp.int32, (heads, width), 0)
    lane = lax.broadcasted_iota(jnp.int32, (heads, width), 1)
    return jnp.where(lane // size == own, 1.0, 0.0).astype(bf16)


def sequence_mask(length, sites):
    later = lax.broadcasted_iota(jnp.int32, (length, length), 0)
    earlier = lax.broadcasted_iota(jnp.int32, (length, length), 1)
    keep = later >= earlier
    if sites > 1:
        keep = keep & (later % sites == earlier % sites)
    return jnp.where(keep, 1.0, 0.0).astype(f32)


def blocks(width):
    return [(j, slice(j * LANES, (j + 1) * LANES)) for j in range(width // LANES)]


def spread_rows(rows, length):
    count = rows.shape[0]
    if count == 1:
        return rows
    part = (length // count, rows.shape[1])
    return jnp.concatenate([jnp.broadcast_to(rows[c : c + 1], part) for c in range(count)], axis=0)


def normalize_into(tok_ref, shift_ref, gain_ref, x_ref):
    length, width = tok_ref.shape
    total = jnp.zeros((length, LANES), f32)
    for _, sl in blocks(width):
        v = tok_ref[:, sl].astype(f32)
        total = total + v * v
    mean = jnp.sum(total, axis=1, keepdims=True) / width
    inverse = lax.rsqrt(mean + norm_eps)
    for _, sl in blocks(width):
        unit = tok_ref[:, sl].astype(f32) * inverse
        gain = spread_rows(gain_ref[:, sl], length)
        shift = spread_rows(shift_ref[:, sl], length)
        x_ref[:, sl] = (unit * (1.0 + gain) + shift).astype(bf16)
    return inverse


def steps_of(logits, bias, rate, mask):
    z = logits.astype(f32) + bias
    step = jnp.maximum(z, 0.0) + jnp.log1p(jnp.exp(-jnp.abs(z)))
    log_decay = -step * rate
    cum = exact(mask, log_decay, 1, 0)
    cum_rows = exact(log_decay, mask, 0, 1)
    return z, step, cum, cum_rows


def expand(parts, lanes_of):
    return mm(parts[0], lanes_of, 1, 0) + mm(parts[1], lanes_of, 1, 0)


def scan_block(j, x, grad, step_wide, scores, cum, cum_rows, heads, width, d_scores):
    size = width // heads
    per_block = LANES // size
    stepped = (x.astype(f32) * step_wide).astype(bf16)
    lane = lax.broadcasted_iota(jnp.int32, x.shape, 1)
    weights, steppeds, grads = [], [], []
    for i in range(per_block):
        h = j * per_block + i
        decay = jnp.exp(jnp.minimum(cum[:, h : h + 1] - cum_rows[h : h + 1, :], 0.0))
        inside = lane // size == i
        own_grad = jnp.where(inside, grad, jnp.zeros_like(grad))
        d_weight = mm(own_grad, stepped, 1, 1)
        d_scores = d_scores + d_weight * decay
        weights.append((scores * decay).astype(bf16))
        steppeds.append(jnp.where(inside, stepped, jnp.zeros_like(stepped)))
        grads.append(own_grad)
    out = mm(jnp.concatenate(weights, axis=1), jnp.concatenate(steppeds, axis=0), 1, 0)
    d_stepped = mm(jnp.concatenate(weights, axis=0), jnp.concatenate(grads, axis=0), 0, 0)
    return stepped, out, d_stepped, d_scores


def head_sums(high_ref, low_ref, lanes_of):
    return mm(high_ref[...], lanes_of, 1, 1) + mm(low_ref[...], lanes_of, 1, 1)


def put(refs, sl, value):
    high, low = split(value)
    refs[0][:, sl] = high
    refs[1][:, sl] = low


def start_kernel(ids_ref, tok_ref, grad_ref, proj_hbm, step_hbm, mod_hbm, active_ref, sent_ref, pay_ref,
                 proj_ref, step_ref, mod_ref, both_ref, sems):
    copies = [
        pltpu.make_async_copy(src, dst, sems.at[n])
        for n, (src, dst) in enumerate(
            [
                (proj_hbm, proj_ref),
                (step_hbm, step_ref),
                (mod_hbm, mod_ref),
                (tok_ref, both_ref.at[:, 0]),
                (grad_ref, both_ref.at[:, 1]),
                (both_ref.at[:, 0], sent_ref.at[:, 0]),
                (both_ref.at[:, 1], sent_ref.at[:, 1]),
            ]
        )
    ]
    for copy in copies[:5]:
        copy.start()
    copies[3].wait()
    copies[5].start()
    copies[4].wait()
    copies[6].start()
    row = ids_ref[1]
    part, pair = proj_ref.shape[0] // 2, proj_ref.shape[1]
    copies[0].wait()
    own = proj_ref[pl.ds(pl.multiple_of(row * part, part), part), :]
    at = 0
    for _, sl in blocks(pair):
        pay_ref[at : at + part, :] = own[:, sl]
        at += part
    copies[1].wait()
    part = step_ref.shape[0] // 2
    pay_ref[at : at + part, :] = step_ref[pl.ds(pl.multiple_of(row * part, part), part), :]
    at += part
    copies[2].wait()
    own = mm(active_ref[...], mod_ref[...], 1, 0)
    high = own.astype(bf16).astype(f32)
    pieces = [piece[:, sl] for piece in (high, own - high) for _, sl in blocks(own.shape[1])]
    pieces.append(jnp.zeros((8 - len(pieces), LANES), f32))
    pay_ref[at : at + 8, :] = jnp.concatenate(pieces, axis=0).astype(bf16)
    copies[5].wait()
    copies[6].wait()


def unpack_kernel(radix, ids_ref, own_ref, other_ref, proj_ref, step_ref, shift_ref, gain_ref):
    me, row = ids_ref[0], ids_ref[1]
    width, pair = proj_ref.shape
    frames = own_ref.shape[0]
    depth = width // frames
    part, heads = depth // 2, step_ref.shape[0] // 2
    cols = 2 * width // frames
    for i in range(frames):
        source = jnp.bitwise_xor(me, (i % radix) * radix + i // radix)
        for ref, half in ((own_ref, row), (other_ref, 1 - row)):
            rows = pl.ds(pl.multiple_of(source * depth + half * part, part), part)
            at = 0
            for _, sl in blocks(pair):
                proj_ref[rows, sl] = ref[i, at : at + part, :]
                at += part
            rows = pl.ds(pl.multiple_of(half * heads, heads), heads)
            lanes = pl.ds(pl.multiple_of(source * depth, depth), depth)
            step_ref[rows, lanes] = ref[i, at : at + heads, :]
            at += heads
        own = own_ref[i, at : at + 8, :].astype(f32)
        count = cols // LANES
        lanes_at = jnp.bitwise_and(source, frames // 2 - 1) * cols
        for k in range(count):
            value = own[k : k + 1, :] + own[count + k : count + k + 1, :]
            lanes = pl.ds(pl.multiple_of(lanes_at + k * LANES, LANES), LANES)

            @pl.when(source < frames // 2)
            def _():
                shift_ref[:, lanes] = value

            @pl.when(source >= frames // 2)
            def _():
                gain_ref[:, lanes] = value


def finish_kernel(factor, ids_ref, own_ref, other_ref, active_ref, proj_ref, step_ref, mod_ref):
    row = ids_ref[1]
    pair = proj_ref.shape[1]
    part, heads = proj_ref.shape[0] // 2, step_ref.shape[0] // 2
    for ref, half in ((own_ref, row), (other_ref, 1 - row)):
        rows = pl.ds(pl.multiple_of(half * part, part), part)
        at = 0
        for _, sl in blocks(pair):
            proj_ref[rows, sl] = ref[at : at + part, :] * factor
            at += part
        step_ref[pl.ds(pl.multiple_of(half * heads, heads), heads), :] = ref[at : at + heads, :] * factor
        at += heads
    for k, sl in blocks(mod_ref.shape[1]):
        mod_ref[:, sl] = active_ref[...] * (own_ref[at + k : at + k + 1, :] * factor)


def site_fast_kernel(sites, got_ref, *refs):
    inputs, (small_ref, sent_hbm, x_hbm, gmod_hbm, dc_ref, dl_ref) = refs[:4], refs[4:10]
    inputs = (*inputs, small_ref[0:1, :], small_ref[1:2, :])
    tok_ref, grad_ref, sent_ref, x_ref, gmod_ref, sems = refs[10:16]
    scratch = refs[16:]
    frames, width = got_ref.shape[0], got_ref.shape[3]
    for _, sl in blocks(width):
        for ref, which in ((tok_ref, 0), (grad_ref, 1)):
            value = got_ref[:, which, :, sl].astype(f32)
            ref[:, sl] = value.reshape(frames * sites, LANES).astype(bf16)

    parts = 2
    share = width // parts
    copies = []

    def begin(source, target):
        copy = pltpu.make_async_copy(source, target, sems.at[len(copies)])
        copy.start()
        copies.append(copy)

    def send(which, p):
        at = (slice(None), which, slice(None), slice(p * share, (p + 1) * share))
        begin(sent_ref.at[at], sent_hbm.at[at])

    class Packed:
        def __init__(self, which):
            self.which = which

        def __setitem__(self, at, value):
            if not copies:
                begin(x_ref, x_hbm)
            value = value.astype(f32).reshape(frames, sites, LANES)
            sent_ref[:, self.which, :, at[1]] = value.astype(bf16)
            if at[1].stop % share == 0:
                send(self.which, at[1].stop // share - 1)

    site_kernel(
        sites, tok_ref, grad_ref, *inputs, Packed(0), Packed(1), dc_ref, dl_ref, gmod_ref, x_ref, *scratch
    )
    begin(gmod_ref, gmod_hbm)
    for copy in copies:
        copy.wait()


def site_kernel(
    sites,
    tok_ref,
    grad_ref,
    shift_ref,
    gain_ref,
    proj_ref,
    step_ref,
    bias_ref,
    rate_ref,
    out_ref,
    back_ref,
    gproj_ref,
    gstep_ref,
    gmod_ref,
    x_ref,
    dn_ref,
    a_hi,
    a_lo,
    b_hi,
    b_lo,
):
    length, width = tok_ref.shape
    heads = step_ref.shape[0]
    state = proj_ref.shape[1] // 2
    clips = shift_ref.shape[0]
    inverse = normalize_into(tok_ref, shift_ref, gain_ref, x_ref)
    lanes_of = head_map(heads, width)
    mask = sequence_mask(length, sites)
    coeffs = mm(x_ref[...], proj_ref[...], 1, 0).astype(bf16)
    logits = mm(x_ref[...], step_ref[...], 1, 1).astype(bf16)
    rate = rate_ref[...]
    z, step, cum, cum_rows = steps_of(logits, bias_ref[...], rate, mask)
    b_part, c_part = coeffs[:, :state], coeffs[:, state:]
    scores = mm(c_part, b_part, 1, 1) * (mask / state)
    step_parts = split(step)
    d_scores = jnp.zeros((length, length), f32)
    for j, sl in blocks(width):
        x, grad = x_ref[:, sl], grad_ref[:, sl]
        step_wide = expand(step_parts, lanes_of[:, sl])
        stepped, out, d_stepped, d_scores = scan_block(
            j, x, grad, step_wide, scores, cum, cum_rows, heads, width, d_scores
        )
        out_ref[:, sl] = out.astype(bf16)
        dn_ref[:, sl] = (step_wide * d_stepped).astype(bf16)
        put((a_hi, a_lo), sl, grad.astype(f32) * out - stepped.astype(f32) * d_stepped)
        put((b_hi, b_lo), sl, x.astype(f32) * d_stepped)
    d_cum = head_sums(a_hi, a_lo, lanes_of)
    d_step = head_sums(b_hi, b_lo, lanes_of)
    d_log = exact(mask, d_cum, 0, 0)
    d_logits = (jax.nn.sigmoid(z) * (d_step - rate * d_log)).astype(bf16)
    d_scores = (d_scores * (mask / state)).astype(bf16)
    d_coeffs = jnp.concatenate(
        [mm(d_scores, c_part, 0, 0), mm(d_scores, b_part, 1, 0)], axis=1
    ).astype(bf16)
    for _, sl in blocks(width):
        back = (
            dn_ref[:, sl].astype(f32)
            + mm(d_coeffs, proj_ref[sl, :], 1, 1)
            + mm(d_logits, step_ref[:, sl], 1, 0)
        ).astype(bf16)
        back_ref[:, sl] = back
        back = back.astype(f32)
        scaled = back * (tok_ref[:, sl].astype(f32) * inverse)
        for c in range(clips):
            rows = slice(c * (length // clips), (c + 1) * (length // clips))
            gmod_ref[c : c + 1, sl] = jnp.sum(back[rows], axis=0, keepdims=True)
            gmod_ref[clips + c : clips + c + 1, sl] = jnp.sum(scaled[rows], axis=0, keepdims=True)
        if gproj_ref.shape == (width, 2 * state):
            gproj_ref[sl, :] = mm(x_ref[:, sl], d_coeffs, 0, 0)
            gstep_ref[:, sl] = mm(d_logits, x_ref[:, sl], 0, 0)
    if gproj_ref.shape != (width, 2 * state):
        gproj_ref[...] = d_coeffs
        gstep_ref[...] = d_logits


def band_fast_kernel(ids_ref, *refs):
    small_ref, give_ref = refs[6], refs[-1]
    inputs = (*refs[:6], small_ref[0:1, :], small_ref[2:3, :])
    band_kernel(*inputs, *refs[7:-1], None, give_ref, first=ids_ref[1] == 0)


def band_kernel(
    tok_ref,
    grad_ref,
    shift_ref,
    gain_ref,
    proj_ref,
    step_ref,
    bias_ref,
    rate_ref,
    x_ref,
    coeffs_ref,
    logits_ref,
    inverse_ref,
    decay_ref,
    end_ref,
    own_ref,
    first=None,
):
    length, width = tok_ref.shape
    heads = step_ref.shape[0]
    state = proj_ref.shape[1] // 2
    inverse_ref[...] = normalize_into(tok_ref, shift_ref, gain_ref, x_ref)
    lanes_of = head_map(heads, width)
    mask = sequence_mask(length, 1)
    coeffs = mm(x_ref[...], proj_ref[...], 1, 0).astype(bf16)
    logits = mm(x_ref[...], step_ref[...], 1, 1).astype(bf16)
    coeffs_ref[...] = coeffs
    logits_ref[...] = logits
    _, step, cum, _ = steps_of(logits, bias_ref[...], rate_ref[...], mask)
    last = cum[length - 1 : length, :]
    decay_ref[...] = jnp.exp(last)
    lead = split(jnp.exp(last - cum) * step)
    reach = split(jnp.exp(cum) / state)
    b_part, c_part = coeffs[:, :state], coeffs[:, state:]
    if first is not None:
        gain = split(jnp.where(first, jnp.exp(last - cum) * step, jnp.exp(cum) / state))
        other = jnp.where(first, b_part, c_part)
        for _, sl in blocks(width):
            value = jnp.where(first, x_ref[:, sl], grad_ref[:, sl]).astype(f32)
            value = (value * expand(gain, lanes_of[:, sl])).astype(bf16)
            own_ref[sl, :] = mm(value, other, 0, 0).astype(bf16)
        return
    for _, sl in blocks(width):
        lead_wide = expand(lead, lanes_of[:, sl])
        reach_wide = expand(reach, lanes_of[:, sl])
        scaled = (x_ref[:, sl].astype(f32) * lead_wide).astype(bf16)
        faded = (grad_ref[:, sl].astype(f32) * reach_wide).astype(bf16)
        end_ref[sl, :] = mm(scaled, b_part, 0, 0).astype(bf16)
        own_ref[sl, :] = mm(faded, c_part, 0, 0).astype(bf16)


def terms_kernel(radix, ids_ref, x_ref, dc_ref, dl_ref, gmod_ref, site_x, site_dc, site_dl, site_gmod,
                 keep_ref, give_ref):
    me, first = ids_ref[0], ids_ref[1] == 0
    width = x_ref.shape[1]
    coeffs = jnp.concatenate([dc_ref[...], site_dc[...]], axis=0)
    logits = jnp.concatenate([dl_ref[...], site_dl[...]], axis=0)
    frames = keep_ref.shape[0]
    share = 2 * width // LANES // frames

    def put_halves(j, at, value):
        part = value.shape[0] // 2
        own = jnp.where(first, value[:part], value[part:]).astype(bf16)
        other = jnp.where(first, value[part:], value[:part]).astype(bf16)
        for _, sl in blocks(value.shape[1]):
            keep_ref[j, at : at + part, :] = own[:, sl]
            give_ref[j, at : at + part, :] = other[:, sl]
            at += part
        return at

    for j, sl in blocks(width):
        offset = jnp.bitwise_xor(me, j)
        place = jnp.bitwise_and(offset, radix - 1) * radix + offset // radix
        tall = jnp.concatenate([x_ref[:, sl], site_x[:, sl]], axis=0)
        at = put_halves(place, 0, mm(tall, coeffs, 0, 0))
        at = put_halves(place, at, mm(logits, tall, 0, 0))
        rows = []
        for n in range(j * share, (j + 1) * share):
            which, at_lane = n // (width // LANES), n % (width // LANES) * LANES
            lanes = slice(at_lane, at_lane + LANES)
            rows.append(gmod_ref[which : which + 1, lanes] + site_gmod[which : which + 1, lanes])
        rows.append(jnp.zeros((8 - len(rows), LANES), f32))
        rows = jnp.concatenate(rows, axis=0).astype(bf16)
        keep_ref[place, at : at + 8, :] = rows
        give_ref[place, at : at + 8, :] = rows


def space_fast_kernel(ids_ref, arrived_ref, *refs):
    inputs, small_ref, outs = refs[:8], refs[8], refs[9:]
    inputs = (*inputs, *(small_ref[n : n + 1, :] for n in (0, 2, 3)))
    first = ids_ref[1] == 0

    class Arrived:
        def __init__(self, wanted):
            self.wanted = wanted

        def __getitem__(self, at):
            value = arrived_ref[at]
            return jnp.where(self.wanted, value, jnp.zeros_like(value))

    space_kernel(*inputs, Arrived(jnp.logical_not(first)), Arrived(first), None, None, *outs)


def space_kernel(
    tok_ref,
    grad_ref,
    x_ref,
    coeffs_ref,
    logits_ref,
    inverse_ref,
    proj_ref,
    step_ref,
    bias_ref,
    rate_ref,
    skip_ref,
    state_ref,
    later_ref,
    gproj_in,
    gstep_in,
    mix_ref,
    pre_ref,
    gproj_ref,
    gstep_ref,
    gmod_ref,
    dn_ref,
    a_hi,
    a_lo,
    b_hi,
    b_lo,
    c_hi,
    c_lo,
):
    length, width = tok_ref.shape
    heads = step_ref.shape[0]
    state = proj_ref.shape[1] // 2
    lanes_of = head_map(heads, width)
    mask = sequence_mask(length, 1)
    coeffs = coeffs_ref[...]
    rate = rate_ref[...]
    z, step, cum, cum_rows = steps_of(logits_ref[...], bias_ref[...], rate, mask)
    last = cum[length - 1 : length, :]
    rest = jnp.exp(last - cum)
    lead = rest * step
    b_part, c_part = coeffs[:, :state], coeffs[:, state:]
    scores = mm(c_part, b_part, 1, 1) * (mask / state)
    step_parts, lead_parts, reach_parts = split(step), split(lead), split(jnp.exp(cum) / state)
    skip_parts = split(jnp.broadcast_to(skip_ref[...], (8, heads)))
    d_scores = jnp.zeros((length, length), f32)
    d_b = jnp.zeros((length, state), f32)
    d_c = jnp.zeros((length, state), f32)
    d_end = jnp.zeros((heads, state), f32)
    for j, sl in blocks(width):
        x, grad = x_ref[:, sl], grad_ref[:, sl]
        wide_map = lanes_of[:, sl]
        step_wide = expand(step_parts, wide_map)
        lead_wide = expand(lead_parts, wide_map)
        reach_wide = expand(reach_parts, wide_map)
        stepped, out, d_stepped, d_scores = scan_block(
            j, x, grad, step_wide, scores, cum, cum_rows, heads, width, d_scores
        )
        x, wide = x.astype(f32), grad.astype(f32)
        before, later = state_ref[sl, :], later_ref[sl, :]
        carried = mm(c_part, before, 1, 1) * reach_wide
        d_c = d_c + mm((wide * reach_wide).astype(bf16), before, 1, 0)
        d_b = d_b + mm((x * lead_wide).astype(bf16), later, 1, 0)
        d_scaled = mm(b_part, later, 1, 1)
        both = split(before.astype(f32) * later.astype(f32))
        d_end = d_end + mm(wide_map, both[0], 1, 0) + mm(wide_map, both[1], 1, 0)
        total = out + carried
        skip = expand(skip_parts, wide_map)[0:1, :]
        mix_ref[:, sl] = total + skip * x
        d_x = (step_wide * d_stepped + d_scaled * lead_wide).astype(bf16)
        dn_ref[:, sl] = d_x + (wide * skip).astype(bf16)
        put((a_hi, a_lo), sl, wide * total - stepped.astype(f32) * d_stepped)
        put((b_hi, b_lo), sl, x * d_stepped)
        put((c_hi, c_lo), sl, x * d_scaled)
    d_lead = head_sums(c_hi, c_lo, lanes_of)
    d_step = head_sums(b_hi, b_lo, lanes_of) + d_lead * rest
    fall = d_lead * lead
    d_cum = head_sums(a_hi, a_lo, lanes_of) - fall
    ones = jnp.ones((8, state), f32)
    end_sum = exact(ones, d_end, 1, 1)[0:1, :] * jnp.exp(last)
    end_sum = end_sum + jnp.sum(fall, axis=0, keepdims=True)
    d_log = exact(mask, d_cum, 0, 0) + end_sum
    d_logits = (jax.nn.sigmoid(z) * (d_step - rate * d_log)).astype(bf16)
    d_scores = (d_scores * (mask / state)).astype(bf16)
    d_coeffs = jnp.concatenate(
        [mm(d_scores, c_part, 0, 0) + d_b, mm(d_scores, b_part, 1, 0) + d_c], axis=1
    ).astype(bf16)
    inverse = inverse_ref[...]
    if gproj_in is None:
        gproj_ref[...] = d_coeffs
        gstep_ref[...] = d_logits
    for _, sl in blocks(width):
        pre = (
            dn_ref[:, sl].astype(f32)
            + mm(d_coeffs, proj_ref[sl, :], 1, 1)
            + mm(d_logits, step_ref[:, sl], 1, 0)
        )
        pre_ref[:, sl] = pre
        scaled = pre * (tok_ref[:, sl].astype(f32) * inverse)
        gmod_ref[0:1, sl] = jnp.sum(pre, axis=0, keepdims=True)
        gmod_ref[1:2, sl] = jnp.sum(scaled, axis=0, keepdims=True)
        if gproj_in is not None:
            gproj_ref[sl, :] = (gproj_in[sl, :] + mm(x_ref[:, sl], d_coeffs, 0, 0)).astype(bf16)
            gstep_ref[:, sl] = (gstep_in[:, sl] + mm(d_logits, x_ref[:, sl], 0, 0)).astype(bf16)


def last_kernel(tok_ref, inverse_ref, gain_ref, mix_ref, pre_ref, time_ref, back_ref, out_ref, dtok_ref):
    length, width = tok_ref.shape
    inverse = inverse_ref[...]
    total = jnp.zeros((length, LANES), f32)
    for _, sl in blocks(width):
        out_ref[:, sl] = (mix_ref[:, sl] + time_ref[:, sl].astype(f32)).astype(bf16)
        grad = (pre_ref[:, sl] + back_ref[:, sl].astype(f32)) * (1.0 + gain_ref[:, sl])
        total = total + grad * tok_ref[:, sl].astype(f32)
    inner = jnp.sum(total, axis=1, keepdims=True) / width
    inner = inner * inverse * inverse * inverse
    for _, sl in blocks(width):
        grad = (pre_ref[:, sl] + back_ref[:, sl].astype(f32)) * (1.0 + gain_ref[:, sl])
        dtok_ref[:, sl] = (grad * inverse - tok_ref[:, sl].astype(f32) * inner).astype(bf16)


def last_fast_kernel(tok_ref, inverse_ref, gain_ref, mix_ref, pre_ref, came_ref, *outs):
    class Packed:
        def __init__(self, which):
            self.which = which

        def __getitem__(self, at):
            value = came_ref[:, self.which, :, at[1]].astype(f32)
            return value.reshape(value.shape[0] * value.shape[1], LANES)

    last_kernel(tok_ref, inverse_ref, gain_ref, mix_ref, pre_ref, Packed(0), Packed(1), *outs)


def in_hbm(array):
    return pltpu.with_memory_space_constraint(array, pltpu.MemorySpace.HBM)


def call(kernel, outs, scratch=(), name=None, specs=None, hbm_outs=()):
    shapes = [
        pltpu.MemorySpace.HBM(s, d) if n in hbm_outs else jax.ShapeDtypeStruct(s, d)
        for n, (s, d) in enumerate(outs)
    ]
    where = {"s": pltpu.SMEM, "v": pltpu.VMEM, "h": pltpu.MemorySpace.HBM}
    spaces = {}
    if specs:
        spaces["in_specs"] = [pl.BlockSpec(memory_space=where[c]) for c in specs]
        spaces["out_specs"] = [
            pl.BlockSpec(memory_space=where["h" if n in hbm_outs else "v"]) for n in range(len(outs))
        ]
    return pl.pallas_call(
        kernel,
        out_shape=shapes,
        **spaces,
        scratch_shapes=[pltpu.VMEM(*s) if isinstance(s, tuple) else s for s in scratch],
        compiler_params=pltpu.CompilerParams(vmem_limit_bytes=24 << 20),
        name=name,
    )


def rows_in_order(part):
    if lax.axis_size("row") != 2:
        return lax.all_gather(part, "row")
    other = lax.ppermute(part, "row", [(0, 1), (1, 0)])
    first = lax.axis_index("row") == 0
    return jnp.stack([jnp.where(first, part, other), jnp.where(first, other, part)])


def rows_sum(part):
    if lax.axis_size("row") != 2:
        return lax.psum(part, "row")
    return part + lax.ppermute(part, "row", [(0, 1), (1, 0)])


def chain(own, decay, forward):
    count = lax.axis_size("row")
    hops = [(i, i + 1) if forward else (i + 1, i) for i in range(count - 1)]
    if count == 1:
        return jnp.zeros_like(own)
    arrived = lax.ppermute(own, "row", hops)
    wide = jnp.repeat(decay[0], own.shape[0] // decay.shape[1])[:, None]
    for _ in range(count - 2):
        passed = wide * arrived.astype(f32) + own.astype(f32)
        arrived = lax.ppermute(passed.astype(bf16), "row", hops)
    return arrived


def per_device(
    tokens,
    cotangent,
    timestep,
    mod_weight,
    proj_weight,
    step_weight,
    step_bias,
    rate_space,
    rate_time,
    skip_gain,
):
    frames = lax.axis_size("frame")
    rows = lax.axis_size("row")
    frame_id = lax.axis_index("frame")
    row_id = lax.axis_index("row")
    width = tokens.shape[-1]
    length = tokens.shape[1] * tokens.shape[2]
    clips = timestep.shape[0]
    clip_id = frame_id // (frames // clips)
    sites = length // frames
    heads = rate_space.shape[0]
    depth, pair = proj_weight.shape
    state = pair // 2
    mod_cols = mod_weight.shape[1]
    factor = (frames * rows * length) ** (-0.5)
    tok = tokens.reshape(length, width)
    grad = cotangent.reshape(length, width)

    activated = time_embed(timestep, mod_weight.shape[0]).astype(bf16)
    own_mod = jnp.dot(activated, mod_weight, preferred_element_type=f32)
    high = lax.reduce_precision(own_mod, 8, 7)
    own_mod = jnp.stack([high, own_mod - high]).astype(bf16)

    part = depth // rows
    own_proj = lax.dynamic_slice_in_dim(proj_weight, row_id * part, part, 0)
    to_all = [
        to_tiles(own_proj[None]),
        to_tiles(step_weight.T[None]),
        own_mod.reshape(1, -1, LANES),
    ]
    to_all = jnp.concatenate(to_all, axis=1)
    to_all = jnp.pad(to_all, ((0, 0), (0, -to_all.shape[1] % 8), (0, 0)))
    count = sites * width // LANES
    got = exchange(
        jnp.concatenate(
            [
                to_tiles(tok.reshape(frames, sites, width)),
                to_tiles(grad.reshape(frames, sites, width)),
                jnp.broadcast_to(to_all, (frames,) + to_all.shape[1:]),
            ],
            axis=1,
        )
    )
    site_tok = from_tiles(got[:, :count], sites, width).reshape(length, width)
    site_grad = from_tiles(got[:, count : 2 * count], sites, width).reshape(length, width)
    at = 2 * count
    size = part * pair // LANES
    proj_full = rows_in_order(got[:, at : at + size])
    proj_full = from_tiles(proj_full.reshape(rows * frames, size, LANES), part, pair)
    proj_full = proj_full.reshape(rows, frames, part, pair).transpose(1, 0, 2, 3)
    proj_full = proj_full.reshape(width, pair)
    at += size
    size = heads * depth // LANES
    step_full = from_tiles(got[:, at : at + size], heads, depth)
    step_full = step_full.transpose(1, 0, 2).reshape(heads, width)
    at += size
    size = 2 * clips * mod_cols // LANES
    mod_full = got[:, at : at + size].reshape(frames, 2, clips, mod_cols).astype(f32)
    mod_full = (mod_full[:, 0] + mod_full[:, 1]).transpose(1, 0, 2).reshape(clips, 2 * width)
    shift, gain = mod_full[:, :width], mod_full[:, width:]

    bias = step_bias[None]
    wide = (length, width)
    site_out, site_back, gproj, gstep, site_gmod = call(
        functools.partial(site_kernel, sites),
        [(wide, bf16), (wide, bf16), ((width, pair), f32), ((heads, width), f32), ((2 * clips, width), f32)],
        [(wide, bf16)] * 6,
        name="site",
    )(site_tok, site_grad, shift, gain, proj_full, step_full, bias, rate_time[None])

    came = exchange(
        jnp.concatenate(
            [
                to_tiles(site_out.reshape(frames, sites, width)),
                to_tiles(site_back.reshape(frames, sites, width)),
            ],
            axis=1,
        )
    )
    time_out = from_tiles(came[:, :count], sites, width).reshape(length, width)
    time_back = from_tiles(came[:, count:], sites, width).reshape(length, width)

    own_shift = lax.dynamic_slice_in_dim(shift, clip_id, 1, 0)
    own_gain = lax.dynamic_slice_in_dim(gain, clip_id, 1, 0)
    normed, coeffs, logits, inverse, decay, end_own, start_grad = call(
        band_kernel,
        [
            (wide, bf16),
            ((length, pair), bf16),
            ((length, heads), bf16),
            ((length, 1), f32),
            ((1, heads), f32),
            ((width, state), bf16),
            ((width, state), bf16),
        ],
        name="band",
    )(tok, grad, own_shift, own_gain, proj_full, step_full, bias, rate_space[None])
    state_in = chain(end_own, decay, True)
    later_grad = chain(start_grad, decay, False)
    mix, pre, gproj, gstep, gmod = call(
        space_kernel,
        [(wide, f32), (wide, f32), ((width, pair), bf16), ((heads, width), bf16), ((2, width), f32)],
        [(wide, bf16)] * 7,
        name="space",
    )(
        tok,
        grad,
        normed,
        coeffs,
        logits,
        inverse,
        proj_full,
        step_full,
        bias,
        rate_space[None],
        skip_gain[None],
        state_in,
        later_grad,
        gproj,
        gstep,
    )

    picked = (jnp.arange(clips) == clip_id).astype(f32)[:, None]
    gmod = jnp.concatenate(
        [site_gmod[:clips] + picked * gmod[0:1], site_gmod[clips:] + picked * gmod[1:2]], axis=1
    )
    gmod = gmod.reshape(clips, frames, mod_cols).transpose(1, 0, 2).astype(bf16)
    sent = jnp.concatenate(
        [
            to_tiles(gproj.reshape(frames, depth, pair)),
            to_tiles(gstep.reshape(heads, frames, depth).transpose(1, 0, 2)),
            gmod.reshape(frames, -1, LANES) if (clips * mod_cols) % LANES == 0 else gmod,
        ],
        axis=1,
    )
    size = sent.shape[1]
    sent = jnp.pad(sent, ((0, 0), (0, -size % 8), (0, 0)))
    sums = jnp.sum(exchange(sent).astype(f32), axis=0, keepdims=True)
    sums = rows_sum(sums) * factor
    at = depth * pair // LANES
    grad_proj = from_tiles(sums[:, :at], depth, pair)[0]
    size = heads * depth // LANES
    grad_step = from_tiles(sums[:, at : at + size], heads, depth)[0].T
    at += size
    size = clips * mod_cols // LANES
    mod_sum = sums[0, at : at + size].reshape(clips, mod_cols)
    grad_mod = jnp.dot(activated.astype(f32).T, mod_sum, precision=EXACT)

    mixed, d_tokens = call(last_kernel, [(wide, bf16), (wide, bf16)], name="last")(
        tok, inverse, own_gain, mix, pre, time_out, time_back
    )
    return (mixed.reshape(tokens.shape), d_tokens.reshape(tokens.shape), grad_proj, grad_step, grad_mod)


def fits(mesh, tokens, timestep, proj_weight, step_weight):
    frames, rows = mesh.shape["frame"], mesh.shape["row"]
    length, width = tokens.shape[2] * tokens.shape[1] // rows, tokens.shape[3]
    return (
        rows == 2
        and frames == 16
        and timestep.shape[0] == 1
        and length == LANES
        and length // frames == 8
        and width // frames == LANES
        and proj_weight.shape[1] == 2 * LANES
        and step_weight.shape[1] % 32 == 0
    )


def spread_over_frames(own, radix=4):
    frames = radix * radix

    def others(piece, stride):
        return [piece] + [
            lax.ppermute(piece, "frame", [(i, i ^ (d * stride)) for i in range(frames)])
            for d in range(1, radix)
        ]

    far = jnp.stack(others(own, radix))
    return jnp.concatenate(others(far, 1))


def sum_over_frames(keep, given, radix, ahead):
    frames = radix * radix

    def total(pieces):
        value = pieces[0].astype(f32)
        for piece in pieces[1:]:
            value = value + piece.astype(f32)
        return value

    def partner(piece, offset):
        return lax.ppermute(piece, "frame", [(i, i ^ offset) for i in range(frames)])

    parts = [slice(d * radix, (d + 1) * radix) for d in range(radix)]
    near = [total([keep[p], given[p]]).astype(bf16) for p in parts]
    near = [near[0]] + [partner(near[d], d) for d in range(1, radix)]
    near, ahead = lax.optimization_barrier((near, ahead))
    near = total(near).astype(bf16)
    far = [near[0]] + [partner(near[d], d * radix) for d in range(1, radix)]
    return total(far), *ahead


def per_device_fast(
    tokens,
    cotangent,
    timestep,
    mod_weight,
    proj_weight,
    step_weight,
    step_bias,
    rate_space,
    rate_time,
    skip_gain,
):
    frames = lax.axis_size("frame")
    rows = lax.axis_size("row")
    ids = jnp.stack([lax.axis_index("frame"), lax.axis_index("row")]).astype(jnp.int32)
    width = tokens.shape[-1]
    length = tokens.shape[1] * tokens.shape[2]
    sites = length // frames
    heads = rate_space.shape[0]
    depth, pair = proj_weight.shape
    state = pair // 2
    mod_cols = mod_weight.shape[1]
    factor = (frames * rows * length) ** (-0.5)
    tok = tokens.reshape(length, width)
    grad = cotangent.reshape(length, width)
    wide = (length, width)
    small = jnp.stack([step_bias, rate_time, rate_space, skip_gain])
    swap = [(0, 1), (1, 0)]

    packed = (frames, 2, sites, width)
    size = depth // 2 * pair // LANES + heads // 2 + 8
    activated = time_embed(timestep, mod_weight.shape[0]).astype(bf16)
    sent, payload = call(
        start_kernel,
        [(packed, bf16), ((size, LANES), bf16)],
        [
            ((depth, pair), bf16),
            ((heads, depth), bf16),
            (mod_weight.shape, bf16),
            (packed, bf16),
            pltpu.SemaphoreType.DMA((7,)),
        ],
        name="start",
        specs="shhhhhv",
        hbm_outs=(0,),
    )(
        ids,
        in_hbm(tok.reshape(frames, sites, width)),
        in_hbm(grad.reshape(frames, sites, width)),
        in_hbm(proj_weight),
        in_hbm(step_weight.T),
        in_hbm(mod_weight),
        activated,
    )
    got = exchange(sent)
    payload = spread_over_frames(payload)
    other = lax.ppermute(payload, "row", swap)
    proj_full, step_full, shift, gain = call(
        functools.partial(unpack_kernel, 4),
        [((width, pair), bf16), ((heads, width), bf16), ((1, width), f32), ((1, width), f32)],
        name="unpack",
        specs="svv",
    )(ids, payload, other)

    sent, site_x, site_gmod, site_dc, site_dl = call(
        functools.partial(site_fast_kernel, sites),
        [
            (packed, bf16),
            (wide, bf16),
            ((2, width), f32),
            ((length, pair), bf16),
            ((length, heads), bf16),
        ],
        [
            (wide, bf16),
            (wide, bf16),
            (packed, bf16),
            (wide, bf16),
            ((2, width), f32),
            pltpu.SemaphoreType.DMA((6,)),
        ]
        + [(wide, bf16)] * 5,
        name="site",
        specs="vvvvvv",
        hbm_outs=(0, 1, 2),
    )(got, shift, gain, proj_full, step_full, small)
    sent, proj_full = lax.optimization_barrier((sent, proj_full))
    came = exchange(sent)

    normed, coeffs, logits, inverse, _, give = call(
        band_fast_kernel,
        [
            (wide, bf16),
            ((length, pair), bf16),
            ((length, heads), bf16),
            ((length, 1), f32),
            ((1, heads), f32),
            ((width, state), bf16),
        ],
        name="band",
        specs="svvvvvvv",
    )(ids, tok, grad, shift, gain, proj_full, step_full, small)
    arrived = lax.ppermute(give, "row", swap)

    halves = (frames, size, LANES)
    mix, pre, own_dc, own_dl, gmod = call(
        space_fast_kernel,
        [(wide, f32), (wide, f32), ((length, pair), bf16), ((length, heads), bf16), ((2, width), f32)],
        [(wide, bf16)] * 7,
        name="space",
        specs="s" + "v" * 10,
    )(
        ids,
        arrived,
        tok,
        grad,
        normed,
        coeffs,
        logits,
        inverse,
        proj_full,
        step_full,
        small,
    )
    keep, give = call(
        functools.partial(terms_kernel, 4),
        [(halves, bf16), (halves, bf16)],
        name="terms",
        specs="svvvvvvvv",
    )(ids, normed, own_dc, own_dl, gmod, site_x, site_dc, site_dl, site_gmod)
    given = lax.ppermute(give, "row", swap)
    mixed, d_tokens = call(last_fast_kernel, [(wide, bf16), (wide, bf16)], name="last")(
        tok, inverse, gain, mix, pre, came
    )
    terms, mixed, d_tokens = sum_over_frames(keep, given, 4, (mixed, d_tokens))
    other = lax.ppermute(terms, "row", swap)
    grad_proj, grad_step, grad_mod = call(
        functools.partial(finish_kernel, factor),
        [((depth, pair), f32), ((heads, depth), f32), ((mod_weight.shape[0], mod_cols), f32)],
        name="finish",
        specs="svvv",
    )(ids, terms, other, activated.astype(f32).T)
    return (mixed.reshape(tokens.shape), d_tokens.reshape(tokens.shape), grad_proj, grad_step.T, grad_mod)


def solution(mesh):
    placed = (
        P("frame", "row", None, None),
        P("frame", "row", None, None),
        P(),
        P(None, "frame"),
        P("frame", None),
        P("frame", None),
        P(),
        P(),
        P(),
        P(),
    )
    outs = (
        P("frame", "row", None, None),
        P("frame", "row", None, None),
        P("frame", None),
        P("frame", None),
        P(None, "frame"),
    )

    def step(tokens, cotangent, timestep, mod_weight, proj_weight, step_weight, *rest):
        fast = fits(mesh, tokens, timestep, proj_weight, step_weight)
        body = per_device_fast if fast else per_device
        return jax.shard_map(
            body, mesh=mesh, in_specs=placed, out_specs=outs, check_vma=False
        )(tokens, cotangent, timestep, mod_weight, proj_weight, step_weight, *rest)

    return step
```

```python
import functools
import math

import jax
import jax.numpy as jnp
from jax import lax
from jax.experimental import pallas as pl
from jax.experimental.pallas import tpu as pltpu
from jax.sharding import PartitionSpec as P

norm_eps = 1e-05
LANES = 128
f32 = jnp.float32
bf16 = jnp.bfloat16
EXACT = lax.Precision.HIGHEST


def time_embed(timestep, embed_dim):
    half_dim = embed_dim // 2
    place = (jnp.arange(embed_dim) % half_dim).astype(f32)
    frequency = jnp.exp(-math.log(10000.0) * place / half_dim)
    angles = timestep.astype(f32)[:, None] * frequency[None, :]
    lower = jnp.arange(embed_dim)[None, :] < half_dim
    return jax.nn.silu(jnp.where(lower, jnp.cos(angles), jnp.sin(angles)))


def to_tiles(a):
    f, r, c = a.shape
    if r % 8 == 0 and c % LANES == 0:
        a = a.reshape(f, r // 8, 8, c // LANES, LANES).transpose(0, 1, 3, 2, 4)
    return a.reshape(f, r * c // LANES, LANES)


def from_tiles(a, r, c):
    f = a.shape[0]
    if r % 8 == 0 and c % LANES == 0:
        a = a.reshape(f, r // 8, c // LANES, 8, LANES).transpose(0, 1, 3, 2, 4)
    return a.reshape(f, r, c)


def exchange(packed):
    return lax.all_to_all(packed, "frame", split_axis=0, concat_axis=0, tiled=True)


def mm(a, b, ca, cb):
    return lax.dot_general(a, b, (((ca,), (cb,)), ((), ())), preferred_element_type=f32)


def exact(a, b, ca, cb):
    return lax.dot_general(
        a, b, (((ca,), (cb,)), ((), ())), preferred_element_type=f32, precision=EXACT
    )


def split(a):
    high = a.astype(bf16)
    return high, (a - high.astype(f32)).astype(bf16)


def head_map(heads, width):
    size = width // heads
    own = lax.broadcasted_iota(jnp.int32, (heads, width), 0)
    lane = lax.broadcasted_iota(jnp.int32, (heads, width), 1)
    return jnp.where(lane // size == own, 1.0, 0.0).astype(bf16)


def sequence_mask(length, sites):
    later = lax.broadcasted_iota(jnp.int32, (length, length), 0)
    earlier = lax.broadcasted_iota(jnp.int32, (length, length), 1)
    keep = later >= earlier
    if sites > 1:
        keep = keep & (later % sites == earlier % sites)
    return jnp.where(keep, 1.0, 0.0).astype(f32)


def blocks(width):
    return [(j, slice(j * LANES, (j + 1) * LANES)) for j in range(width // LANES)]


def spread_rows(rows, length):
    count = rows.shape[0]
    if count == 1:
        return rows
    part = (length // count, rows.shape[1])
    return jnp.concatenate([jnp.broadcast_to(rows[c : c + 1], part) for c in range(count)], axis=0)


def normalize_into(tok_ref, shift_ref, gain_ref, x_ref):
    length, width = tok_ref.shape
    total = jnp.zeros((length, LANES), f32)
    for _, sl in blocks(width):
        v = tok_ref[:, sl].astype(f32)
        total = total + v * v
    mean = jnp.sum(total, axis=1, keepdims=True) / width
    inverse = lax.rsqrt(mean + norm_eps)
    for _, sl in blocks(width):
        unit = tok_ref[:, sl].astype(f32) * inverse
        gain = spread_rows(gain_ref[:, sl], length)
        shift = spread_rows(shift_ref[:, sl], length)
        x_ref[:, sl] = (unit * (1.0 + gain) + shift).astype(bf16)
    return inverse


def steps_of(logits, bias, rate, mask):
    z = logits.astype(f32) + bias
    step = jnp.maximum(z, 0.0) + jnp.log1p(jnp.exp(-jnp.abs(z)))
    log_decay = -step * rate
    cum = exact(mask, log_decay, 1, 0)
    cum_rows = exact(log_decay, mask, 0, 1)
    return z, step, cum, cum_rows


def halves_of(a):
    return jnp.concatenate(split(a), axis=1)


def doubled(lanes_of):
    return jnp.concatenate([lanes_of, lanes_of], axis=0)


def scan_block(j, x, grad, step_wide, scores, cum, cum_rows, heads, width, d_scores):
    size = width // heads
    per_block = LANES // size
    length = x.shape[0]
    stepped = (x.astype(f32) * step_wide).astype(bf16)
    lane = lax.broadcasted_iota(jnp.int32, x.shape, 1)
    inside = [lane // size == i for i in range(per_block)]
    zero = jnp.zeros_like(x)
    steppeds = jnp.concatenate([jnp.where(own, stepped, zero) for own in inside], axis=0)
    grads = jnp.concatenate([jnp.where(own, grad, zero) for own in inside], axis=0)
    d_weights = mm(grads, stepped, 1, 1)
    weights = []
    for i in range(per_block):
        h = j * per_block + i
        decay = jnp.exp(jnp.minimum(cum[:, h : h + 1] - cum_rows[h : h + 1, :], 0.0))
        d_scores = d_scores + d_weights[i * length : (i + 1) * length] * decay
        weights.append((scores * decay).astype(bf16))
    out = mm(jnp.concatenate(weights, axis=1), steppeds, 1, 0)
    d_stepped = mm(jnp.concatenate(weights, axis=0), grads, 0, 0)
    return stepped, out, d_stepped, d_scores


def put(sums_ref, which, sl, value):
    length = value.shape[0]
    for n, part in enumerate(split(value)):
        at = (2 * which + n) * length
        sums_ref[at : at + length, sl] = part


def head_sums(sums_ref, lanes_of, length):
    sums = mm(sums_ref[...], lanes_of, 1, 1)
    sums = [sums[at : at + length] for at in range(0, sums.shape[0], length)]
    return [sums[n] + sums[n + 1] for n in range(0, len(sums), 2)]


def wide_blocks(width):
    return [(slice(at, at + 2 * LANES)) for at in range(0, width, 2 * LANES)]


def start_kernel(ids_ref, tok_ref, grad_ref, proj_hbm, step_hbm, mod_hbm, active_ref, sent_ref, pay_ref,
                 proj_ref, step_ref, mod_ref, both_ref, sems):
    copies = [
        pltpu.make_async_copy(src, dst, sems.at[n])
        for n, (src, dst) in enumerate(
            [
                (proj_hbm, proj_ref),
                (step_hbm, step_ref),
                (mod_hbm, mod_ref),
                (tok_ref, both_ref.at[:, 0]),
                (grad_ref, both_ref.at[:, 1]),
                (both_ref.at[:, 0], sent_ref.at[:, 0]),
                (both_ref.at[:, 1], sent_ref.at[:, 1]),
            ]
        )
    ]
    for copy in copies[:5]:
        copy.start()
    copies[3].wait()
    copies[5].start()
    copies[4].wait()
    copies[6].start()
    row = ids_ref[1]
    part, pair = proj_ref.shape[0] // 2, proj_ref.shape[1]
    copies[0].wait()
    own = proj_ref[pl.ds(pl.multiple_of(row * part, part), part), :]
    at = 0
    for _, sl in blocks(pair):
        pay_ref[at : at + part, :] = own[:, sl]
        at += part
    copies[1].wait()
    part = step_ref.shape[0] // 2
    pay_ref[at : at + part, :] = step_ref[pl.ds(pl.multiple_of(row * part, part), part), :]
    at += part
    copies[2].wait()
    own = mm(active_ref[...], mod_ref[...], 1, 0)
    high = own.astype(bf16).astype(f32)
    pieces = [piece[:, sl] for piece in (high, own - high) for _, sl in blocks(own.shape[1])]
    pieces.append(jnp.zeros((8 - len(pieces), LANES), f32))
    pay_ref[at : at + 8, :] = jnp.concatenate(pieces, axis=0).astype(bf16)
    copies[5].wait()
    copies[6].wait()


def unpack_kernel(radix, ids_ref, own_ref, other_ref, proj_ref, step_ref, shift_ref, gain_ref):
    me, row = ids_ref[0], ids_ref[1]
    width, pair = proj_ref.shape
    frames = own_ref.shape[0]
    depth = width // frames
    part, heads = depth // 2, step_ref.shape[0] // 2
    cols = 2 * width // frames
    for i in range(frames):
        source = jnp.bitwise_xor(me, (i % radix) * radix + i // radix)
        for ref, half in ((own_ref, row), (other_ref, 1 - row)):
            rows = pl.ds(pl.multiple_of(source * depth + half * part, part), part)
            at = 0
            for _, sl in blocks(pair):
                proj_ref[rows, sl] = ref[i, at : at + part, :]
                at += part
            rows = pl.ds(pl.multiple_of(half * heads, heads), heads)
            lanes = pl.ds(pl.multiple_of(source * depth, depth), depth)
            step_ref[rows, lanes] = ref[i, at : at + heads, :]
            at += heads
        own = own_ref[i, at : at + 8, :].astype(f32)
        count = cols // LANES
        lanes_at = jnp.bitwise_and(source, frames // 2 - 1) * cols
        for k in range(count):
            value = own[k : k + 1, :] + own[count + k : count + k + 1, :]
            lanes = pl.ds(pl.multiple_of(lanes_at + k * LANES, LANES), LANES)

            @pl.when(source < frames // 2)
            def _():
                shift_ref[:, lanes] = value

            @pl.when(source >= frames // 2)
            def _():
                gain_ref[:, lanes] = value


def finish_kernel(factor, ids_ref, own_ref, other_ref, active_ref, proj_ref, step_ref, mod_ref):
    row = ids_ref[1]
    pair = proj_ref.shape[1]
    part, heads = proj_ref.shape[0] // 2, step_ref.shape[0] // 2
    for ref, half in ((own_ref, row), (other_ref, 1 - row)):
        rows = pl.ds(pl.multiple_of(half * part, part), part)
        at = 0
        for _, sl in blocks(pair):
            proj_ref[rows, sl] = ref[at : at + part, :] * factor
            at += part
        step_ref[pl.ds(pl.multiple_of(half * heads, heads), heads), :] = ref[at : at + heads, :] * factor
        at += heads
    rest = jnp.zeros((7, active_ref.shape[1]), f32)
    active = jnp.concatenate([active_ref[...].astype(f32), rest], axis=0)
    for k, sl in blocks(mod_ref.shape[1]):
        own = jnp.broadcast_to(own_ref[at + k : at + k + 1, :] * factor, (8, LANES))
        mod_ref[:, sl] = exact(active, own, 0, 0)


def site_fast_kernel(sites, got_ref, *refs):
    inputs, (small_ref, sent_hbm, x_hbm, gmod_hbm, dc_ref, dl_ref) = refs[:4], refs[4:10]
    inputs = (*inputs, small_ref[0:1, :], small_ref[1:2, :])
    tok_ref, grad_ref, sent_ref, x_ref, gmod_ref, sems = refs[10:16]
    scratch = refs[16:]
    frames, width = got_ref.shape[0], got_ref.shape[3]
    for _, sl in blocks(width):
        for ref, which in ((tok_ref, 0), (grad_ref, 1)):
            value = got_ref[:, which, :, sl].astype(f32)
            ref[:, sl] = value.reshape(frames * sites, LANES).astype(bf16)

    parts = 4
    share = width // parts
    copies = []

    def begin(source, target):
        copy = pltpu.make_async_copy(source, target, sems.at[len(copies)])
        copy.start()
        copies.append(copy)

    def send(which, p):
        at = (slice(None), which, slice(None), slice(p * share, (p + 1) * share))
        begin(sent_ref.at[at], sent_hbm.at[at])

    class Packed:
        def __init__(self, which):
            self.which = which

        def __setitem__(self, at, value):
            if not copies:
                begin(x_ref, x_hbm)
            value = value.astype(f32).reshape(frames, sites, value.shape[1])
            sent_ref[:, self.which, :, at[1]] = value.astype(bf16)
            if at[1].stop % share == 0:
                send(self.which, at[1].stop // share - 1)

    site_kernel(
        sites, tok_ref, grad_ref, *inputs, Packed(0), Packed(1), dc_ref, dl_ref, gmod_ref, x_ref, *scratch
    )
    begin(gmod_ref, gmod_hbm)
    for copy in copies:
        copy.wait()


def site_kernel(
    sites,
    tok_ref,
    grad_ref,
    shift_ref,
    gain_ref,
    proj_ref,
    step_ref,
    bias_ref,
    rate_ref,
    out_ref,
    back_ref,
    gproj_ref,
    gstep_ref,
    gmod_ref,
    x_ref,
    dn_ref,
    sums_ref,
):
    length, width = tok_ref.shape
    heads = step_ref.shape[0]
    state = proj_ref.shape[1] // 2
    clips = shift_ref.shape[0]
    inverse = normalize_into(tok_ref, shift_ref, gain_ref, x_ref)
    lanes_of = head_map(heads, width)
    mask = sequence_mask(length, sites)
    coeffs = mm(x_ref[...], proj_ref[...], 1, 0).astype(bf16)
    logits = mm(x_ref[...], step_ref[...], 1, 1).astype(bf16)
    rate = rate_ref[...]
    z, step, cum, cum_rows = steps_of(logits, bias_ref[...], rate, mask)
    b_part, c_part = coeffs[:, :state], coeffs[:, state:]
    scores = mm(c_part, b_part, 1, 1) * (mask / state)
    step_parts, twice = halves_of(step), doubled(lanes_of)
    d_scores = jnp.zeros((length, length), f32)
    for j, sl in blocks(width):
        x, grad = x_ref[:, sl], grad_ref[:, sl]
        step_wide = mm(step_parts, twice[:, sl], 1, 0)
        stepped, out, d_stepped, d_scores = scan_block(
            j, x, grad, step_wide, scores, cum, cum_rows, heads, width, d_scores
        )
        out_ref[:, sl] = out.astype(bf16)
        dn_ref[:, sl] = (step_wide * d_stepped).astype(bf16)
        put(sums_ref, 0, sl, grad.astype(f32) * out - stepped.astype(f32) * d_stepped)
        put(sums_ref, 1, sl, x.astype(f32) * d_stepped)
    d_cum, d_step = head_sums(sums_ref, lanes_of, length)
    d_log = exact(mask, d_cum, 0, 0)
    d_logits = (jax.nn.sigmoid(z) * (d_step - rate * d_log)).astype(bf16)
    d_scores = (d_scores * (mask / state)).astype(bf16)
    d_coeffs = jnp.concatenate(
        [mm(d_scores, c_part, 0, 0), mm(d_scores, b_part, 1, 0)], axis=1
    ).astype(bf16)
    for sl in wide_blocks(width):
        back = (
            dn_ref[:, sl].astype(f32)
            + mm(d_coeffs, proj_ref[sl, :], 1, 1)
            + mm(d_logits, step_ref[:, sl], 1, 0)
        ).astype(bf16)
        back_ref[:, sl] = back
        back = back.astype(f32)
        scaled = back * (tok_ref[:, sl].astype(f32) * inverse)
        for c in range(clips):
            rows = slice(c * (length // clips), (c + 1) * (length // clips))
            gmod_ref[c : c + 1, sl] = jnp.sum(back[rows], axis=0, keepdims=True)
            gmod_ref[clips + c : clips + c + 1, sl] = jnp.sum(scaled[rows], axis=0, keepdims=True)
        if gproj_ref.shape == (width, 2 * state):
            gproj_ref[sl, :] = mm(x_ref[:, sl], d_coeffs, 0, 0)
            gstep_ref[:, sl] = mm(d_logits, x_ref[:, sl], 0, 0)
    if gproj_ref.shape != (width, 2 * state):
        gproj_ref[...] = d_coeffs
        gstep_ref[...] = d_logits


def band_fast_kernel(ids_ref, *refs):
    small_ref, give_ref = refs[6], refs[-1]
    inputs = (*refs[:6], small_ref[0:1, :], small_ref[2:3, :])
    band_kernel(*inputs, *refs[7:-1], None, None, give_ref, first=ids_ref[1] == 0)


def band_kernel(
    tok_ref,
    grad_ref,
    shift_ref,
    gain_ref,
    proj_ref,
    step_ref,
    bias_ref,
    rate_ref,
    x_ref,
    coeffs_ref,
    logits_ref,
    inverse_ref,
    decay_ref,
    end_ref,
    own_ref,
    first=None,
):
    length, width = tok_ref.shape
    heads = step_ref.shape[0]
    state = proj_ref.shape[1] // 2
    inverse_ref[...] = normalize_into(tok_ref, shift_ref, gain_ref, x_ref)
    twice = doubled(head_map(heads, width))
    mask = sequence_mask(length, 1)
    coeffs = mm(x_ref[...], proj_ref[...], 1, 0).astype(bf16)
    logits = mm(x_ref[...], step_ref[...], 1, 1).astype(bf16)
    coeffs_ref[...] = coeffs
    logits_ref[...] = logits
    _, step, cum, _ = steps_of(logits, bias_ref[...], rate_ref[...], mask)
    last = cum[length - 1 : length, :]
    b_part, c_part = coeffs[:, :state], coeffs[:, state:]
    if first is not None:
        gain = halves_of(jnp.where(first, jnp.exp(last - cum) * step, jnp.exp(cum) / state))
        other = jnp.where(first, b_part, c_part)
        for _, sl in blocks(width):
            value = jnp.where(first, x_ref[:, sl], grad_ref[:, sl]).astype(f32)
            value = (value * mm(gain, twice[:, sl], 1, 0)).astype(bf16)
            own_ref[sl, :] = mm(value, other, 0, 0).astype(bf16)
        return
    decay_ref[...] = jnp.exp(last)
    lead = halves_of(jnp.exp(last - cum) * step)
    reach = halves_of(jnp.exp(cum) / state)
    for _, sl in blocks(width):
        lead_wide = mm(lead, twice[:, sl], 1, 0)
        reach_wide = mm(reach, twice[:, sl], 1, 0)
        scaled = (x_ref[:, sl].astype(f32) * lead_wide).astype(bf16)
        faded = (grad_ref[:, sl].astype(f32) * reach_wide).astype(bf16)
        end_ref[sl, :] = mm(scaled, b_part, 0, 0).astype(bf16)
        own_ref[sl, :] = mm(faded, c_part, 0, 0).astype(bf16)


def terms_kernel(radix, ids_ref, x_ref, dc_ref, dl_ref, gmod_ref, site_x, site_dc, site_dl, site_gmod,
                 keep_ref, give_ref):
    me, first = ids_ref[0], ids_ref[1] == 0
    width = x_ref.shape[1]
    coeffs = jnp.concatenate([dc_ref[...], site_dc[...]], axis=0)
    logits = jnp.concatenate([dl_ref[...], site_dl[...]], axis=0)
    frames = keep_ref.shape[0]
    share = 2 * width // LANES // frames

    def put_halves(j, at, value):
        part = value.shape[0] // 2
        own = jnp.where(first, value[:part], value[part:]).astype(bf16)
        other = jnp.where(first, value[part:], value[:part]).astype(bf16)
        for _, sl in blocks(value.shape[1]):
            keep_ref[j, at : at + part, :] = own[:, sl]
            give_ref[j, at : at + part, :] = other[:, sl]
            at += part
        return at

    for j, sl in blocks(width):
        offset = jnp.bitwise_xor(me, j)
        place = jnp.bitwise_and(offset, radix - 1) * radix + j // radix
        tall = jnp.concatenate([x_ref[:, sl], site_x[:, sl]], axis=0)
        at = put_halves(place, 0, mm(tall, coeffs, 0, 0))
        at = put_halves(place, at, mm(logits, tall, 0, 0))
        rows = []
        for n in range(j * share, (j + 1) * share):
            which, at_lane = n // (width // LANES), n % (width // LANES) * LANES
            lanes = slice(at_lane, at_lane + LANES)
            rows.append(gmod_ref[which : which + 1, lanes] + site_gmod[which : which + 1, lanes])
        rows.append(jnp.zeros((8 - len(rows), LANES), f32))
        rows = jnp.concatenate(rows, axis=0).astype(bf16)
        keep_ref[place, at : at + 8, :] = rows
        give_ref[place, at : at + 8, :] = rows


def space_fast_kernel(ids_ref, arrived_ref, *refs):
    inputs, small_ref, outs = refs[:8], refs[8], refs[9:]
    inputs = (*inputs, *(small_ref[n : n + 1, :] for n in (0, 2, 3)))
    space_kernel(*inputs, arrived_ref, None, None, None, *outs, first=ids_ref[1] == 0)


def space_kernel(
    tok_ref,
    grad_ref,
    x_ref,
    coeffs_ref,
    logits_ref,
    inverse_ref,
    proj_ref,
    step_ref,
    bias_ref,
    rate_ref,
    skip_ref,
    state_ref,
    later_ref,
    gproj_in,
    gstep_in,
    mix_ref,
    pre_ref,
    gproj_ref,
    gstep_ref,
    gmod_ref,
    dn_ref,
    sums_ref,
    first=None,
):
    length, width = tok_ref.shape
    heads = step_ref.shape[0]
    state = proj_ref.shape[1] // 2
    lanes_of = head_map(heads, width)
    twice = doubled(lanes_of)
    mask = sequence_mask(length, 1)
    coeffs = coeffs_ref[...]
    rate = rate_ref[...]
    z, step, cum, cum_rows = steps_of(logits_ref[...], bias_ref[...], rate, mask)
    last = cum[length - 1 : length, :]
    rest = jnp.exp(last - cum)
    lead, reach = rest * step, jnp.exp(cum) / state
    b_part, c_part = coeffs[:, :state], coeffs[:, state:]
    scores = mm(c_part, b_part, 1, 1) * (mask / state)
    skip = jnp.broadcast_to(skip_ref[...], (8, heads))
    if first is None:
        parts = [step, lead, reach, skip]
    else:
        parts = [step, jnp.where(first, lead, reach), skip]
        chosen = jnp.where(first, b_part, c_part)
        is_first = jnp.where(first, 1.0, 0.0).astype(f32)
        is_second = 1.0 - is_first
    parts = jnp.concatenate([halves_of(part) for part in parts], axis=0)
    d_scores = jnp.zeros((length, length), f32)
    d_b = jnp.zeros((length, state), f32)
    d_c = jnp.zeros((length, state), f32)
    d_end = jnp.zeros((heads, state), f32)
    for j, sl in blocks(width):
        x, grad = x_ref[:, sl], grad_ref[:, sl]
        wide_parts = mm(parts, twice[:, sl], 1, 0)
        step_wide, lead_wide = wide_parts[:length], wide_parts[length : 2 * length]
        skip = wide_parts[-8:-7]
        stepped, out, d_stepped, d_scores = scan_block(
            j, x, grad, step_wide, scores, cum, cum_rows, heads, width, d_scores
        )
        if first is None:
            x, wide = x.astype(f32), grad.astype(f32)
            reach_wide = wide_parts[2 * length : 3 * length]
            before, later = state_ref[sl, :], later_ref[sl, :]
            total = out + mm(c_part, before, 1, 1) * reach_wide
            d_c = d_c + mm((wide * reach_wide).astype(bf16), before, 1, 0)
            d_b = d_b + mm((x * lead_wide).astype(bf16), later, 1, 0)
            d_scaled = mm(b_part, later, 1, 1)
            d_x = step_wide * d_stepped + d_scaled * lead_wide
            both = split(before.astype(f32) * later.astype(f32))
            d_end = d_end + mm(lanes_of[:, sl], both[0], 1, 0) + mm(lanes_of[:, sl], both[1], 1, 0)
        else:
            arrived = state_ref[sl, :]
            value = jnp.where(first, x, grad).astype(f32)
            d_b = d_b + mm((value * lead_wide).astype(bf16), arrived, 1, 0)
            x, wide = x.astype(f32), grad.astype(f32)
            d_scaled = mm(chosen, arrived, 1, 1)
            carried = d_scaled * lead_wide
            total = out + carried * is_second
            d_x = step_wide * d_stepped + carried * is_first
            d_scaled = d_scaled * is_first
        mix_ref[:, sl] = total + skip * x
        dn_ref[:, sl] = d_x.astype(bf16) + (wide * skip).astype(bf16)
        put(sums_ref, 0, sl, wide * total - stepped.astype(f32) * d_stepped)
        put(sums_ref, 1, sl, x * d_stepped)
        put(sums_ref, 2, sl, x * d_scaled)
    d_cum, d_step, d_lead = head_sums(sums_ref, lanes_of, length)
    d_step = d_step + d_lead * rest
    fall = d_lead * lead
    d_cum = d_cum - fall
    end_sum = jnp.sum(fall, axis=0, keepdims=True)
    if first is None:
        ones = jnp.ones((8, state), f32)
        end_sum = end_sum + exact(ones, d_end, 1, 1)[0:1, :] * jnp.exp(last)
    else:
        d_b, d_c = d_b * is_first, d_b * is_second
    d_log = exact(mask, d_cum, 0, 0) + end_sum
    d_logits = (jax.nn.sigmoid(z) * (d_step - rate * d_log)).astype(bf16)
    d_scores = (d_scores * (mask / state)).astype(bf16)
    d_coeffs = jnp.concatenate(
        [mm(d_scores, c_part, 0, 0) + d_b, mm(d_scores, b_part, 1, 0) + d_c], axis=1
    ).astype(bf16)
    inverse = inverse_ref[...]
    if gproj_in is None:
        gproj_ref[...] = d_coeffs
        gstep_ref[...] = d_logits
    for sl in wide_blocks(width):
        pre = (
            dn_ref[:, sl].astype(f32)
            + mm(d_coeffs, proj_ref[sl, :], 1, 1)
            + mm(d_logits, step_ref[:, sl], 1, 0)
        )
        pre_ref[:, sl] = pre
        scaled = pre * (tok_ref[:, sl].astype(f32) * inverse)
        gmod_ref[0:1, sl] = jnp.sum(pre, axis=0, keepdims=True)
        gmod_ref[1:2, sl] = jnp.sum(scaled, axis=0, keepdims=True)
        if gproj_in is not None:
            gproj_ref[sl, :] = (gproj_in[sl, :] + mm(x_ref[:, sl], d_coeffs, 0, 0)).astype(bf16)
            gstep_ref[:, sl] = (gstep_in[:, sl] + mm(d_logits, x_ref[:, sl], 0, 0)).astype(bf16)


def last_kernel(tok_ref, inverse_ref, gain_ref, mix_ref, pre_ref, time_ref, back_ref, out_ref, dtok_ref):
    length, width = tok_ref.shape
    inverse = inverse_ref[...]
    total = jnp.zeros((length, LANES), f32)
    for _, sl in blocks(width):
        out_ref[:, sl] = (mix_ref[:, sl] + time_ref[:, sl].astype(f32)).astype(bf16)
        grad = (pre_ref[:, sl] + back_ref[:, sl].astype(f32)) * (1.0 + gain_ref[:, sl])
        total = total + grad * tok_ref[:, sl].astype(f32)
    inner = jnp.sum(total, axis=1, keepdims=True) / width
    inner = inner * inverse * inverse * inverse
    for _, sl in blocks(width):
        grad = (pre_ref[:, sl] + back_ref[:, sl].astype(f32)) * (1.0 + gain_ref[:, sl])
        dtok_ref[:, sl] = (grad * inverse - tok_ref[:, sl].astype(f32) * inner).astype(bf16)


def last_fast_kernel(tok_ref, inverse_ref, gain_ref, mix_ref, pre_ref, came_ref, *outs):
    class Packed:
        def __init__(self, which):
            self.which = which

        def __getitem__(self, at):
            value = came_ref[:, self.which, :, at[1]].astype(f32)
            return value.reshape(value.shape[0] * value.shape[1], LANES)

    last_kernel(tok_ref, inverse_ref, gain_ref, mix_ref, pre_ref, Packed(0), Packed(1), *outs)


def in_hbm(array):
    return pltpu.with_memory_space_constraint(array, pltpu.MemorySpace.HBM)


def call(kernel, outs, scratch=(), name=None, specs=None, hbm_outs=()):
    shapes = [
        pltpu.MemorySpace.HBM(s, d) if n in hbm_outs else jax.ShapeDtypeStruct(s, d)
        for n, (s, d) in enumerate(outs)
    ]
    where = {"s": pltpu.SMEM, "v": pltpu.VMEM, "h": pltpu.MemorySpace.HBM}
    spaces = {}
    if specs:
        spaces["in_specs"] = [pl.BlockSpec(memory_space=where[c]) for c in specs]
        spaces["out_specs"] = [
            pl.BlockSpec(memory_space=where["h" if n in hbm_outs else "v"]) for n in range(len(outs))
        ]
    return pl.pallas_call(
        kernel,
        out_shape=shapes,
        **spaces,
        scratch_shapes=[pltpu.VMEM(*s) if isinstance(s, tuple) else s for s in scratch],
        compiler_params=pltpu.CompilerParams(vmem_limit_bytes=24 << 20),
        name=name,
    )


def rows_in_order(part):
    if lax.axis_size("row") != 2:
        return lax.all_gather(part, "row")
    other = lax.ppermute(part, "row", [(0, 1), (1, 0)])
    first = lax.axis_index("row") == 0
    return jnp.stack([jnp.where(first, part, other), jnp.where(first, other, part)])


def rows_sum(part):
    if lax.axis_size("row") != 2:
        return lax.psum(part, "row")
    return part + lax.ppermute(part, "row", [(0, 1), (1, 0)])


def chain(own, decay, forward):
    count = lax.axis_size("row")
    hops = [(i, i + 1) if forward else (i + 1, i) for i in range(count - 1)]
    if count == 1:
        return jnp.zeros_like(own)
    arrived = lax.ppermute(own, "row", hops)
    wide = jnp.repeat(decay[0], own.shape[0] // decay.shape[1])[:, None]
    for _ in range(count - 2):
        passed = wide * arrived.astype(f32) + own.astype(f32)
        arrived = lax.ppermute(passed.astype(bf16), "row", hops)
    return arrived


def per_device(
    tokens,
    cotangent,
    timestep,
    mod_weight,
    proj_weight,
    step_weight,
    step_bias,
    rate_space,
    rate_time,
    skip_gain,
):
    frames = lax.axis_size("frame")
    rows = lax.axis_size("row")
    frame_id = lax.axis_index("frame")
    row_id = lax.axis_index("row")
    width = tokens.shape[-1]
    length = tokens.shape[1] * tokens.shape[2]
    clips = timestep.shape[0]
    clip_id = frame_id // (frames // clips)
    sites = length // frames
    heads = rate_space.shape[0]
    depth, pair = proj_weight.shape
    state = pair // 2
    mod_cols = mod_weight.shape[1]
    factor = (frames * rows * length) ** (-0.5)
    tok = tokens.reshape(length, width)
    grad = cotangent.reshape(length, width)

    activated = time_embed(timestep, mod_weight.shape[0]).astype(bf16)
    own_mod = jnp.dot(activated, mod_weight, preferred_element_type=f32)
    high = lax.reduce_precision(own_mod, 8, 7)
    own_mod = jnp.stack([high, own_mod - high]).astype(bf16)

    part = depth // rows
    own_proj = lax.dynamic_slice_in_dim(proj_weight, row_id * part, part, 0)
    to_all = [
        to_tiles(own_proj[None]),
        to_tiles(step_weight.T[None]),
        own_mod.reshape(1, -1, LANES),
    ]
    to_all = jnp.concatenate(to_all, axis=1)
    to_all = jnp.pad(to_all, ((0, 0), (0, -to_all.shape[1] % 8), (0, 0)))
    count = sites * width // LANES
    got = exchange(
        jnp.concatenate(
            [
                to_tiles(tok.reshape(frames, sites, width)),
                to_tiles(grad.reshape(frames, sites, width)),
                jnp.broadcast_to(to_all, (frames,) + to_all.shape[1:]),
            ],
            axis=1,
        )
    )
    site_tok = from_tiles(got[:, :count], sites, width).reshape(length, width)
    site_grad = from_tiles(got[:, count : 2 * count], sites, width).reshape(length, width)
    at = 2 * count
    size = part * pair // LANES
    proj_full = rows_in_order(got[:, at : at + size])
    proj_full = from_tiles(proj_full.reshape(rows * frames, size, LANES), part, pair)
    proj_full = proj_full.reshape(rows, frames, part, pair).transpose(1, 0, 2, 3)
    proj_full = proj_full.reshape(width, pair)
    at += size
    size = heads * depth // LANES
    step_full = from_tiles(got[:, at : at + size], heads, depth)
    step_full = step_full.transpose(1, 0, 2).reshape(heads, width)
    at += size
    size = 2 * clips * mod_cols // LANES
    mod_full = got[:, at : at + size].reshape(frames, 2, clips, mod_cols).astype(f32)
    mod_full = (mod_full[:, 0] + mod_full[:, 1]).transpose(1, 0, 2).reshape(clips, 2 * width)
    shift, gain = mod_full[:, :width], mod_full[:, width:]

    bias = step_bias[None]
    wide = (length, width)
    site_out, site_back, gproj, gstep, site_gmod = call(
        functools.partial(site_kernel, sites),
        [(wide, bf16), (wide, bf16), ((width, pair), f32), ((heads, width), f32), ((2 * clips, width), f32)],
        [(wide, bf16)] * 2 + [((4 * length, width), bf16)],
        name="site",
    )(site_tok, site_grad, shift, gain, proj_full, step_full, bias, rate_time[None])

    came = exchange(
        jnp.concatenate(
            [
                to_tiles(site_out.reshape(frames, sites, width)),
                to_tiles(site_back.reshape(frames, sites, width)),
            ],
            axis=1,
        )
    )
    time_out = from_tiles(came[:, :count], sites, width).reshape(length, width)
    time_back = from_tiles(came[:, count:], sites, width).reshape(length, width)

    own_shift = lax.dynamic_slice_in_dim(shift, clip_id, 1, 0)
    own_gain = lax.dynamic_slice_in_dim(gain, clip_id, 1, 0)
    normed, coeffs, logits, inverse, decay, end_own, start_grad = call(
        band_kernel,
        [
            (wide, bf16),
            ((length, pair), bf16),
            ((length, heads), bf16),
            ((length, 1), f32),
            ((1, heads), f32),
            ((width, state), bf16),
            ((width, state), bf16),
        ],
        name="band",
    )(tok, grad, own_shift, own_gain, proj_full, step_full, bias, rate_space[None])
    state_in = chain(end_own, decay, True)
    later_grad = chain(start_grad, decay, False)
    mix, pre, gproj, gstep, gmod = call(
        space_kernel,
        [(wide, f32), (wide, f32), ((width, pair), bf16), ((heads, width), bf16), ((2, width), f32)],
        [(wide, bf16), ((6 * length, width), bf16)],
        name="space",
    )(
        tok,
        grad,
        normed,
        coeffs,
        logits,
        inverse,
        proj_full,
        step_full,
        bias,
        rate_space[None],
        skip_gain[None],
        state_in,
        later_grad,
        gproj,
        gstep,
    )

    picked = (jnp.arange(clips) == clip_id).astype(f32)[:, None]
    gmod = jnp.concatenate(
        [site_gmod[:clips] + picked * gmod[0:1], site_gmod[clips:] + picked * gmod[1:2]], axis=1
    )
    gmod = gmod.reshape(clips, frames, mod_cols).transpose(1, 0, 2).astype(bf16)
    sent = jnp.concatenate(
        [
            to_tiles(gproj.reshape(frames, depth, pair)),
            to_tiles(gstep.reshape(heads, frames, depth).transpose(1, 0, 2)),
            gmod.reshape(frames, -1, LANES) if (clips * mod_cols) % LANES == 0 else gmod,
        ],
        axis=1,
    )
    size = sent.shape[1]
    sent = jnp.pad(sent, ((0, 0), (0, -size % 8), (0, 0)))
    sums = jnp.sum(exchange(sent).astype(f32), axis=0, keepdims=True)
    sums = rows_sum(sums) * factor
    at = depth * pair // LANES
    grad_proj = from_tiles(sums[:, :at], depth, pair)[0]
    size = heads * depth // LANES
    grad_step = from_tiles(sums[:, at : at + size], heads, depth)[0].T
    at += size
    size = clips * mod_cols // LANES
    mod_sum = sums[0, at : at + size].reshape(clips, mod_cols)
    grad_mod = jnp.dot(activated.astype(f32).T, mod_sum, precision=EXACT)

    mixed, d_tokens = call(last_kernel, [(wide, bf16), (wide, bf16)], name="last")(
        tok, inverse, own_gain, mix, pre, time_out, time_back
    )
    return (mixed.reshape(tokens.shape), d_tokens.reshape(tokens.shape), grad_proj, grad_step, grad_mod)


def fits(mesh, tokens, timestep, proj_weight, step_weight):
    frames, rows = mesh.shape["frame"], mesh.shape["row"]
    length, width = tokens.shape[2] * tokens.shape[1] // rows, tokens.shape[3]
    return (
        rows == 2
        and frames == 16
        and timestep.shape[0] == 1
        and length == LANES
        and length // frames == 8
        and width // frames == LANES
        and proj_weight.shape[1] == 2 * LANES
        and step_weight.shape[1] % 32 == 0
    )


def spread_over_frames(own, radix=4):
    frames = radix * radix

    def others(piece, stride):
        return [piece] + [
            lax.ppermute(piece, "frame", [(i, i ^ (d * stride)) for i in range(frames)])
            for d in range(1, radix)
        ]

    far = jnp.stack(others(own, radix))
    return jnp.concatenate(others(far, 1))


def sum_over_frames(keep, given, radix, ahead):
    frames = radix * radix

    def total(pieces):
        value = pieces[0].astype(f32)
        for piece in pieces[1:]:
            value = value + piece.astype(f32)
        return value

    def partner(piece, offset):
        return lax.ppermute(piece, "frame", [(i, i ^ offset) for i in range(frames)])

    parts = [slice(d * radix, (d + 1) * radix) for d in range(radix)]
    near = [total([keep[p], given[p]]).astype(bf16) for p in parts]
    near = [near[0]] + [partner(near[d], d) for d in range(1, radix)]
    near, ahead = lax.optimization_barrier((near, ahead))
    near = total(near).astype(bf16)
    planes = [[p * radix + i for p in range(radix)] for i in range(radix)]
    far = lax.all_to_all(near, "frame", 0, 0, tiled=True, axis_index_groups=planes)
    return jnp.sum(far.astype(f32), axis=0), *ahead


def per_device_fast(
    tokens,
    cotangent,
    timestep,
    mod_weight,
    proj_weight,
    step_weight,
    step_bias,
    rate_space,
    rate_time,
    skip_gain,
):
    frames = lax.axis_size("frame")
    rows = lax.axis_size("row")
    ids = jnp.stack([lax.axis_index("frame"), lax.axis_index("row")]).astype(jnp.int32)
    width = tokens.shape[-1]
    length = tokens.shape[1] * tokens.shape[2]
    sites = length // frames
    heads = rate_space.shape[0]
    depth, pair = proj_weight.shape
    state = pair // 2
    mod_cols = mod_weight.shape[1]
    factor = (frames * rows * length) ** (-0.5)
    tok = tokens.reshape(length, width)
    grad = cotangent.reshape(length, width)
    wide = (length, width)
    small = jnp.stack([step_bias, rate_time, rate_space, skip_gain])
    swap = [(0, 1), (1, 0)]

    packed = (frames, 2, sites, width)
    size = depth // 2 * pair // LANES + heads // 2 + 8
    activated = time_embed(timestep, mod_weight.shape[0]).astype(bf16)
    sent, payload = call(
        start_kernel,
        [(packed, bf16), ((size, LANES), bf16)],
        [
            ((depth, pair), bf16),
            ((heads, depth), bf16),
            (mod_weight.shape, bf16),
            (packed, bf16),
            pltpu.SemaphoreType.DMA((7,)),
        ],
        name="start",
        specs="shhhhhv",
        hbm_outs=(0,),
    )(
        ids,
        in_hbm(tok.reshape(frames, sites, width)),
        in_hbm(grad.reshape(frames, sites, width)),
        in_hbm(proj_weight),
        in_hbm(step_weight.T),
        in_hbm(mod_weight),
        activated,
    )
    got = exchange(sent)
    payload = spread_over_frames(payload)
    other = lax.ppermute(payload, "row", swap)
    proj_full, step_full, shift, gain = call(
        functools.partial(unpack_kernel, 4),
        [((width, pair), bf16), ((heads, width), bf16), ((1, width), f32), ((1, width), f32)],
        name="unpack",
        specs="svv",
    )(ids, payload, other)

    sent, site_x, site_gmod, site_dc, site_dl = call(
        functools.partial(site_fast_kernel, sites),
        [
            (packed, bf16),
            (wide, bf16),
            ((2, width), f32),
            ((length, pair), bf16),
            ((length, heads), bf16),
        ],
        [
            (wide, bf16),
            (wide, bf16),
            (packed, bf16),
            (wide, bf16),
            ((2, width), f32),
            pltpu.SemaphoreType.DMA((10,)),
        ]
        + [(wide, bf16), ((4 * length, width), bf16)],
        name="site",
        specs="vvvvvv",
        hbm_outs=(0, 1, 2),
    )(got, shift, gain, proj_full, step_full, small)
    sent, proj_full = lax.optimization_barrier((sent, proj_full))
    came = exchange(sent)

    normed, coeffs, logits, inverse, give = call(
        band_fast_kernel,
        [
            (wide, bf16),
            ((length, pair), bf16),
            ((length, heads), bf16),
            ((length, 1), f32),
            ((width, state), bf16),
        ],
        name="band",
        specs="svvvvvvv",
    )(ids, tok, grad, shift, gain, proj_full, step_full, small)
    arrived = lax.ppermute(give, "row", swap)

    halves = (frames, size, LANES)
    mix, pre, own_dc, own_dl, gmod = call(
        space_fast_kernel,
        [(wide, f32), (wide, f32), ((length, pair), bf16), ((length, heads), bf16), ((2, width), f32)],
        [(wide, bf16), ((6 * length, width), bf16)],
        name="space",
        specs="s" + "v" * 10,
    )(
        ids,
        arrived,
        tok,
        grad,
        normed,
        coeffs,
        logits,
        inverse,
        proj_full,
        step_full,
        small,
    )
    keep, give = call(
        functools.partial(terms_kernel, 4),
        [(halves, bf16), (halves, bf16)],
        name="terms",
        specs="svvvvvvvv",
    )(ids, normed, own_dc, own_dl, gmod, site_x, site_dc, site_dl, site_gmod)
    given = lax.ppermute(give, "row", swap)
    mixed, d_tokens = call(last_fast_kernel, [(wide, bf16), (wide, bf16)], name="last")(
        tok, inverse, gain, mix, pre, came
    )
    terms, mixed, d_tokens = sum_over_frames(keep, given, 4, (mixed, d_tokens))
    other = lax.ppermute(terms, "row", swap)
    grad_proj, grad_step, grad_mod = call(
        functools.partial(finish_kernel, factor),
        [((depth, pair), f32), ((heads, depth), f32), ((mod_weight.shape[0], mod_cols), f32)],
        name="finish",
        specs="svvv",
    )(ids, terms, other, activated)
    return (mixed.reshape(tokens.shape), d_tokens.reshape(tokens.shape), grad_proj, grad_step.T, grad_mod)


def solution(mesh):
    placed = (
        P("frame", "row", None, None),
        P("frame", "row", None, None),
        P(),
        P(None, "frame"),
        P("frame", None),
        P("frame", None),
        P(),
        P(),
        P(),
        P(),
    )
    outs = (
        P("frame", "row", None, None),
        P("frame", "row", None, None),
        P("frame", None),
        P("frame", None),
        P(None, "frame"),
    )

    def step(tokens, cotangent, timestep, mod_weight, proj_weight, step_weight, *rest):
        fast = fits(mesh, tokens, timestep, proj_weight, step_weight)
        body = per_device_fast if fast else per_device
        return jax.shard_map(
            body, mesh=mesh, in_specs=placed, out_specs=outs, check_vma=False
        )(tokens, cotangent, timestep, mod_weight, proj_weight, step_weight, *rest)

    return step
```

```python
import functools
import math

import jax
import jax.numpy as jnp
from jax import lax
from jax.experimental import pallas as pl
from jax.experimental.pallas import tpu as pltpu
from jax.sharding import PartitionSpec as P

norm_eps = 1e-05
LANES = 128
LOG2E = math.log2(math.e)
f32 = jnp.float32
bf16 = jnp.bfloat16
EXACT = lax.Precision.HIGHEST


def time_embed(timestep, embed_dim):
    half_dim = embed_dim // 2
    place = (jnp.arange(embed_dim) % half_dim).astype(f32)
    frequency = jnp.exp(-math.log(10000.0) * place / half_dim)
    angles = timestep.astype(f32)[:, None] * frequency[None, :]
    lower = jnp.arange(embed_dim)[None, :] < half_dim
    return jax.nn.silu(jnp.where(lower, jnp.cos(angles), jnp.sin(angles)))


def to_tiles(a):
    f, r, c = a.shape
    if r % 8 == 0 and c % LANES == 0:
        a = a.reshape(f, r // 8, 8, c // LANES, LANES).transpose(0, 1, 3, 2, 4)
    return a.reshape(f, r * c // LANES, LANES)


def from_tiles(a, r, c):
    f = a.shape[0]
    if r % 8 == 0 and c % LANES == 0:
        a = a.reshape(f, r // 8, c // LANES, 8, LANES).transpose(0, 1, 3, 2, 4)
    return a.reshape(f, r, c)


def exchange(packed):
    return lax.all_to_all(packed, "frame", split_axis=0, concat_axis=0, tiled=True)


def mm(a, b, ca, cb):
    return lax.dot_general(a, b, (((ca,), (cb,)), ((), ())), preferred_element_type=f32)


def exact(a, b, ca, cb):
    return lax.dot_general(
        a, b, (((ca,), (cb,)), ((), ())), preferred_element_type=f32, precision=EXACT
    )


def split(a):
    high = a.astype(bf16)
    return high, (a - high.astype(f32)).astype(bf16)


def head_map(heads, width):
    size = width // heads
    own = lax.broadcasted_iota(jnp.int32, (heads, width), 0)
    lane = lax.broadcasted_iota(jnp.int32, (heads, width), 1)
    return jnp.where(lane // size == own, 1.0, 0.0).astype(bf16)


def sequence_mask(length, sites):
    later = lax.broadcasted_iota(jnp.int32, (length, length), 0)
    earlier = lax.broadcasted_iota(jnp.int32, (length, length), 1)
    keep = later >= earlier
    if sites > 1:
        keep = keep & (later % sites == earlier % sites)
    return jnp.where(keep, 1.0, 0.0).astype(f32)


def blocks(width):
    return [(j, slice(j * LANES, (j + 1) * LANES)) for j in range(width // LANES)]


def spread_rows(rows, length):
    count = rows.shape[0]
    if count == 1:
        return rows
    part = (length // count, rows.shape[1])
    return jnp.concatenate([jnp.broadcast_to(rows[c : c + 1], part) for c in range(count)], axis=0)


def normalize_into(tok_ref, shift_ref, gain_ref, x_ref, read=None):
    length, width = tok_ref.shape
    total = jnp.zeros((length, LANES), f32)
    for _, sl in blocks(width):
        if read is None:
            v = tok_ref[:, sl].astype(f32)
        else:
            v = read(sl)
            tok_ref[:, sl] = v.astype(bf16)
        total = total + v * v
    mean = jnp.sum(total, axis=1, keepdims=True) / width
    inverse = lax.rsqrt(mean + norm_eps)
    for _, sl in blocks(width):
        unit = tok_ref[:, sl].astype(f32) * inverse
        gain = spread_rows(gain_ref[:, sl], length)
        shift = spread_rows(shift_ref[:, sl], length)
        x_ref[:, sl] = (unit * (1.0 + gain) + shift).astype(bf16)
    return inverse


def steps_of(logits, bias, rate, mask):
    z = logits.astype(f32) + bias
    step = jnp.maximum(z, 0.0) + jnp.log1p(jnp.exp(-jnp.abs(z)))
    log_decay = -step * rate
    cum = exact(mask, log_decay, 1, 0)
    return z, step, cum, (cum * LOG2E, exact(log_decay * LOG2E, mask, 0, 1))


def halves_of(a):
    return jnp.concatenate(split(a), axis=1)


def doubled(lanes_of):
    return jnp.concatenate([lanes_of, lanes_of], axis=0)


def scan_block(j, x, grad, step_wide, scores, cums, heads, width, d_scores):
    size = width // heads
    per_block = LANES // size
    length = x.shape[0]
    stepped = (x.astype(f32) * step_wide).astype(bf16)
    lane = lax.broadcasted_iota(jnp.int32, x.shape, 1)
    inside = [lane // size == i for i in range(per_block)]
    zero = jnp.zeros_like(x)
    steppeds = jnp.concatenate([jnp.where(own, stepped, zero) for own in inside], axis=0)
    grads = jnp.concatenate([jnp.where(own, grad, zero) for own in inside], axis=0)
    d_weights = mm(grads, stepped, 1, 1)
    weights = []
    for i in range(per_block):
        h = j * per_block + i
        decay = jnp.exp2(jnp.minimum(cums[0][:, h : h + 1] - cums[1][h : h + 1, :], 0.0))
        d_scores = d_scores + d_weights[i * length : (i + 1) * length] * decay
        weights.append((scores * decay).astype(bf16))
    out = mm(jnp.concatenate(weights, axis=1), steppeds, 1, 0)
    d_stepped = mm(jnp.concatenate(weights, axis=0), grads, 0, 0)
    return stepped, out, d_stepped, d_scores


def put(sums_ref, which, sl, value):
    length = value.shape[0]
    sums_ref[which * length : (which + 1) * length, sl] = value.astype(bf16)


def head_sums(sums_ref, lanes_of, length):
    sums = mm(sums_ref[...], lanes_of, 1, 1)
    return [sums[at : at + length] for at in range(0, sums.shape[0], length)]


def wide_blocks(width):
    return [(slice(at, at + 2 * LANES)) for at in range(0, width, 2 * LANES)]


def start_kernel(ids_ref, tok_ref, grad_ref, proj_hbm, step_hbm, mod_hbm, active_ref, sent_ref, pay_ref,
                 proj_ref, step_ref, mod_ref, both_ref, sems):
    copies = [
        pltpu.make_async_copy(src, dst, sems.at[n])
        for n, (src, dst) in enumerate(
            [
                (proj_hbm, proj_ref),
                (step_hbm, step_ref),
                (mod_hbm, mod_ref),
                (tok_ref, both_ref.at[:, 0]),
                (grad_ref, both_ref.at[:, 1]),
                (both_ref.at[:, 0], sent_ref.at[:, 0]),
                (both_ref.at[:, 1], sent_ref.at[:, 1]),
            ]
        )
    ]
    for copy in copies[:5]:
        copy.start()
    copies[3].wait()
    copies[5].start()
    copies[4].wait()
    copies[6].start()
    row = ids_ref[1]
    part, pair = proj_ref.shape[0] // 2, proj_ref.shape[1]
    copies[0].wait()
    own = proj_ref[pl.ds(pl.multiple_of(row * part, part), part), :]
    at = 0
    for _, sl in blocks(pair):
        pay_ref[at : at + part, :] = own[:, sl]
        at += part
    copies[1].wait()
    part = step_ref.shape[0] // 2
    pay_ref[at : at + part, :] = step_ref[pl.ds(pl.multiple_of(row * part, part), part), :]
    at += part
    copies[2].wait()
    own = mm(active_ref[...], mod_ref[...], 1, 0)
    high = own.astype(bf16).astype(f32)
    pieces = [piece[:, sl] for piece in (high, own - high) for _, sl in blocks(own.shape[1])]
    pieces.append(jnp.zeros((8 - len(pieces), LANES), f32))
    pay_ref[at : at + 8, :] = jnp.concatenate(pieces, axis=0).astype(bf16)
    copies[5].wait()
    copies[6].wait()


def unpack_kernel(radix, ids_ref, own_ref, other_ref, proj_ref, step_ref, shift_ref, gain_ref):
    me, row = ids_ref[0], ids_ref[1]
    width, pair = proj_ref.shape
    frames = own_ref.shape[0]
    depth = width // frames
    part, heads = depth // 2, step_ref.shape[0] // 2
    cols = 2 * width // frames
    for i in range(frames):
        source = jnp.bitwise_xor(me, (i % radix) * radix + i // radix)
        for ref, half in ((own_ref, row), (other_ref, 1 - row)):
            rows = pl.ds(pl.multiple_of(source * depth + half * part, part), part)
            at = 0
            for _, sl in blocks(pair):
                proj_ref[rows, sl] = ref[i, at : at + part, :]
                at += part
            rows = pl.ds(pl.multiple_of(half * heads, heads), heads)
            lanes = pl.ds(pl.multiple_of(source * depth, depth), depth)
            step_ref[rows, lanes] = ref[i, at : at + heads, :]
            at += heads
        own = own_ref[i, at : at + 8, :].astype(f32)
        count = cols // LANES
        lanes_at = jnp.bitwise_and(source, frames // 2 - 1) * cols
        for k in range(count):
            value = own[k : k + 1, :] + own[count + k : count + k + 1, :]
            lanes = pl.ds(pl.multiple_of(lanes_at + k * LANES, LANES), LANES)

            @pl.when(source < frames // 2)
            def _():
                shift_ref[:, lanes] = value

            @pl.when(source >= frames // 2)
            def _():
                gain_ref[:, lanes] = value


def finish_kernel(factor, ids_ref, own_ref, other_ref, active_ref, proj_ref, step_ref, mod_ref):
    row = ids_ref[1]
    pair = proj_ref.shape[1]
    part, heads = proj_ref.shape[0] // 2, step_ref.shape[0] // 2
    for ref, half in ((own_ref, row), (other_ref, 1 - row)):
        rows = pl.ds(pl.multiple_of(half * part, part), part)
        at = 0
        for _, sl in blocks(pair):
            proj_ref[rows, sl] = ref[at : at + part, :] * factor
            at += part
        step_ref[pl.ds(pl.multiple_of(half * heads, heads), heads), :] = ref[at : at + heads, :] * factor
        at += heads
    for k, sl in blocks(mod_ref.shape[1]):
        mod_ref[:, sl] = active_ref[...] * (own_ref[at + k : at + k + 1, :] * factor)


def site_fast_kernel(sites, got_ref, *refs):
    inputs, (small_ref, sent_hbm, x_hbm, gmod_hbm, dc_ref, dl_ref) = refs[:4], refs[4:10]
    inputs = (*inputs, small_ref[0:1, :], small_ref[1:2, :])
    tok_ref, sent_ref, x_ref, gmod_ref, sems = refs[10:15]
    scratch = refs[15:]
    frames, width = got_ref.shape[0], got_ref.shape[3]
    def read(which):
        return lambda sl: got_ref[:, which, :, sl].astype(f32).reshape(frames * sites, LANES)

    class Grad:
        def __getitem__(self, at):
            return read(1)(at[1]).astype(bf16)

    parts = 4
    share = width // parts
    copies = []

    def begin(source, target):
        copy = pltpu.make_async_copy(source, target, sems.at[len(copies)])
        copy.start()
        copies.append(copy)

    def send(which, p):
        at = (slice(None), which, slice(None), slice(p * share, (p + 1) * share))
        begin(sent_ref.at[at], sent_hbm.at[at])

    class Packed:
        def __init__(self, which):
            self.which = which

        def __setitem__(self, at, value):
            if not copies:
                begin(x_ref, x_hbm)
            value = value.astype(f32).reshape(frames, sites, value.shape[1])
            sent_ref[:, self.which, :, at[1]] = value.astype(bf16)
            if at[1].stop % share == 0:
                send(self.which, at[1].stop // share - 1)

    site_kernel(
        sites,
        tok_ref,
        Grad(),
        *inputs,
        Packed(0),
        Packed(1),
        dc_ref,
        dl_ref,
        gmod_ref,
        x_ref,
        *scratch,
        read=read(0),
    )
    begin(gmod_ref, gmod_hbm)
    for copy in copies:
        copy.wait()


def site_kernel(
    sites,
    tok_ref,
    grad_ref,
    shift_ref,
    gain_ref,
    proj_ref,
    step_ref,
    bias_ref,
    rate_ref,
    out_ref,
    back_ref,
    gproj_ref,
    gstep_ref,
    gmod_ref,
    x_ref,
    dn_ref,
    sums_ref,
    read=None,
):
    length, width = tok_ref.shape
    heads = step_ref.shape[0]
    state = proj_ref.shape[1] // 2
    clips = shift_ref.shape[0]
    inverse = normalize_into(tok_ref, shift_ref, gain_ref, x_ref, read)
    lanes_of = head_map(heads, width)
    mask = sequence_mask(length, sites)
    coeffs = mm(x_ref[...], proj_ref[...], 1, 0).astype(bf16)
    logits = mm(x_ref[...], step_ref[...], 1, 1).astype(bf16)
    rate = rate_ref[...]
    z, step, cum, cums = steps_of(logits, bias_ref[...], rate, mask)
    b_part, c_part = coeffs[:, :state], coeffs[:, state:]
    scores = mm(c_part, b_part, 1, 1) * (mask / state)
    step_parts, twice = halves_of(step), doubled(lanes_of)
    d_scores = jnp.zeros((length, length), f32)
    for j, sl in blocks(width):
        x, grad = x_ref[:, sl], grad_ref[:, sl]
        step_wide = mm(step_parts, twice[:, sl], 1, 0)
        stepped, out, d_stepped, d_scores = scan_block(
            j, x, grad, step_wide, scores, cums, heads, width, d_scores
        )
        out_ref[:, sl] = out.astype(bf16)
        dn_ref[:, sl] = (step_wide * d_stepped).astype(bf16)
        put(sums_ref, 0, sl, grad.astype(f32) * out - stepped.astype(f32) * d_stepped)
        put(sums_ref, 1, sl, x.astype(f32) * d_stepped)
    d_cum, d_step = head_sums(sums_ref, lanes_of, length)
    d_log = exact(mask, d_cum, 0, 0)
    d_logits = (jax.nn.sigmoid(z) * (d_step - rate * d_log)).astype(bf16)
    d_scores = (d_scores * (mask / state)).astype(bf16)
    d_coeffs = jnp.concatenate(
        [mm(d_scores, c_part, 0, 0), mm(d_scores, b_part, 1, 0)], axis=1
    ).astype(bf16)
    for sl in wide_blocks(width):
        back = (
            dn_ref[:, sl].astype(f32)
            + mm(d_coeffs, proj_ref[sl, :], 1, 1)
            + mm(d_logits, step_ref[:, sl], 1, 0)
        )
        back_ref[:, sl] = back.astype(bf16)
        scaled = back * (tok_ref[:, sl].astype(f32) * inverse)
        for c in range(clips):
            rows = slice(c * (length // clips), (c + 1) * (length // clips))
            gmod_ref[c : c + 1, sl] = jnp.sum(back[rows], axis=0, keepdims=True)
            gmod_ref[clips + c : clips + c + 1, sl] = jnp.sum(scaled[rows], axis=0, keepdims=True)
        if gproj_ref.shape == (width, 2 * state):
            gproj_ref[sl, :] = mm(x_ref[:, sl], d_coeffs, 0, 0)
            gstep_ref[:, sl] = mm(d_logits, x_ref[:, sl], 0, 0)
    if gproj_ref.shape != (width, 2 * state):
        gproj_ref[...] = d_coeffs
        gstep_ref[...] = d_logits


def band_fast_kernel(ids_ref, *refs):
    small_ref, give_ref = refs[6], refs[-1]
    inputs = (*refs[:6], small_ref[0:1, :], small_ref[2:3, :])
    band_kernel(*inputs, *refs[7:-1], None, None, give_ref, first=ids_ref[1] == 0)


def band_kernel(
    tok_ref,
    grad_ref,
    shift_ref,
    gain_ref,
    proj_ref,
    step_ref,
    bias_ref,
    rate_ref,
    x_ref,
    coeffs_ref,
    logits_ref,
    inverse_ref,
    decay_ref,
    end_ref,
    own_ref,
    first=None,
):
    length, width = tok_ref.shape
    heads = step_ref.shape[0]
    state = proj_ref.shape[1] // 2
    inverse_ref[...] = normalize_into(tok_ref, shift_ref, gain_ref, x_ref)
    twice = doubled(head_map(heads, width))
    mask = sequence_mask(length, 1)
    coeffs = mm(x_ref[...], proj_ref[...], 1, 0).astype(bf16)
    logits = mm(x_ref[...], step_ref[...], 1, 1).astype(bf16)
    coeffs_ref[...] = coeffs
    logits_ref[...] = logits
    _, step, cum, _ = steps_of(logits, bias_ref[...], rate_ref[...], mask)
    last = cum[length - 1 : length, :]
    b_part, c_part = coeffs[:, :state], coeffs[:, state:]
    if first is not None:
        gain = halves_of(jnp.where(first, jnp.exp(last - cum) * step, jnp.exp(cum) / state))
        other = jnp.where(first, b_part, c_part)
        for _, sl in blocks(width):
            value = jnp.where(first, x_ref[:, sl], grad_ref[:, sl]).astype(f32)
            value = (value * mm(gain, twice[:, sl], 1, 0)).astype(bf16)
            own_ref[sl, :] = mm(value, other, 0, 0).astype(bf16)
        return
    decay_ref[...] = jnp.exp(last)
    lead = halves_of(jnp.exp(last - cum) * step)
    reach = halves_of(jnp.exp(cum) / state)
    for _, sl in blocks(width):
        lead_wide = mm(lead, twice[:, sl], 1, 0)
        reach_wide = mm(reach, twice[:, sl], 1, 0)
        scaled = (x_ref[:, sl].astype(f32) * lead_wide).astype(bf16)
        faded = (grad_ref[:, sl].astype(f32) * reach_wide).astype(bf16)
        end_ref[sl, :] = mm(scaled, b_part, 0, 0).astype(bf16)
        own_ref[sl, :] = mm(faded, c_part, 0, 0).astype(bf16)


def terms_kernel(radix, ids_ref, x_ref, dc_ref, dl_ref, gmod_ref, site_x, site_dc, site_dl, site_gmod,
                 keep_ref, give_ref):
    me, first = ids_ref[0], ids_ref[1] == 0
    width = x_ref.shape[1]
    coeffs = jnp.concatenate([dc_ref[...], site_dc[...]], axis=0)
    logits = jnp.concatenate([dl_ref[...], site_dl[...]], axis=0)
    frames = keep_ref.shape[0]
    share = 2 * width // LANES // frames

    def put_halves(j, at, value):
        part = value.shape[0] // 2
        own = jnp.where(first, value[:part], value[part:]).astype(bf16)
        other = jnp.where(first, value[part:], value[:part]).astype(bf16)
        for _, sl in blocks(value.shape[1]):
            keep_ref[j, at : at + part, :] = own[:, sl]
            give_ref[j, at : at + part, :] = other[:, sl]
            at += part
        return at

    for j, sl in blocks(width):
        offset = jnp.bitwise_xor(me, j)
        place = jnp.bitwise_and(offset, radix - 1) * radix + offset // radix
        tall = jnp.concatenate([x_ref[:, sl], site_x[:, sl]], axis=0)
        at = put_halves(place, 0, mm(tall, coeffs, 0, 0))
        at = put_halves(place, at, mm(logits, tall, 0, 0))
        rows = []
        for n in range(j * share, (j + 1) * share):
            which, at_lane = n // (width // LANES), n % (width // LANES) * LANES
            lanes = slice(at_lane, at_lane + LANES)
            rows.append(gmod_ref[which : which + 1, lanes] + site_gmod[which : which + 1, lanes])
        rows.append(jnp.zeros((8 - len(rows), LANES), f32))
        rows = jnp.concatenate(rows, axis=0).astype(bf16)
        keep_ref[place, at : at + 8, :] = rows
        give_ref[place, at : at + 8, :] = rows


def space_fast_kernel(ids_ref, arrived_ref, *refs):
    inputs, small_ref, outs = refs[:8], refs[8], refs[9:]
    inputs = (*inputs, *(small_ref[n : n + 1, :] for n in (0, 2, 3)))
    space_kernel(*inputs, arrived_ref, None, None, None, *outs, first=ids_ref[1] == 0)


def space_kernel(
    tok_ref,
    grad_ref,
    x_ref,
    coeffs_ref,
    logits_ref,
    inverse_ref,
    proj_ref,
    step_ref,
    bias_ref,
    rate_ref,
    skip_ref,
    state_ref,
    later_ref,
    gproj_in,
    gstep_in,
    mix_ref,
    pre_ref,
    gproj_ref,
    gstep_ref,
    gmod_ref,
    dn_ref,
    sums_ref,
    first=None,
):
    length, width = tok_ref.shape
    heads = step_ref.shape[0]
    state = proj_ref.shape[1] // 2
    lanes_of = head_map(heads, width)
    twice = doubled(lanes_of)
    mask = sequence_mask(length, 1)
    coeffs = coeffs_ref[...]
    rate = rate_ref[...]
    z, step, cum, cums = steps_of(logits_ref[...], bias_ref[...], rate, mask)
    last = cum[length - 1 : length, :]
    rest = jnp.exp(last - cum)
    lead, reach = rest * step, jnp.exp(cum) / state
    b_part, c_part = coeffs[:, :state], coeffs[:, state:]
    scores = mm(c_part, b_part, 1, 1) * (mask / state)
    skip = jnp.broadcast_to(skip_ref[...], (8, heads))
    if first is None:
        parts = [step, lead, reach, skip]
    else:
        parts = [step, jnp.where(first, lead, reach), skip]
        chosen = jnp.where(first, b_part, c_part)
        is_first = jnp.where(first, 1.0, 0.0).astype(f32)
        is_second = 1.0 - is_first
    parts = jnp.concatenate([halves_of(part) for part in parts], axis=0)
    d_scores = jnp.zeros((length, length), f32)
    d_b = jnp.zeros((length, state), f32)
    d_c = jnp.zeros((length, state), f32)
    d_end = jnp.zeros((heads, state), f32)
    for j, sl in blocks(width):
        x, grad = x_ref[:, sl], grad_ref[:, sl]
        wide_parts = mm(parts, twice[:, sl], 1, 0)
        step_wide, lead_wide = wide_parts[:length], wide_parts[length : 2 * length]
        skip = wide_parts[-8:-7]
        stepped, out, d_stepped, d_scores = scan_block(
            j, x, grad, step_wide, scores, cums, heads, width, d_scores
        )
        if first is None:
            x, wide = x.astype(f32), grad.astype(f32)
            reach_wide = wide_parts[2 * length : 3 * length]
            before, later = state_ref[sl, :], later_ref[sl, :]
            total = out + mm(c_part, before, 1, 1) * reach_wide
            d_c = d_c + mm((wide * reach_wide).astype(bf16), before, 1, 0)
            d_b = d_b + mm((x * lead_wide).astype(bf16), later, 1, 0)
            d_scaled = mm(b_part, later, 1, 1)
            d_x = step_wide * d_stepped + d_scaled * lead_wide
            both = split(before.astype(f32) * later.astype(f32))
            d_end = d_end + mm(lanes_of[:, sl], both[0], 1, 0) + mm(lanes_of[:, sl], both[1], 1, 0)
        else:
            arrived = state_ref[sl, :]
            value = jnp.where(first, x, grad).astype(f32)
            d_b = d_b + mm((value * lead_wide).astype(bf16), arrived, 1, 0)
            x, wide = x.astype(f32), grad.astype(f32)
            d_scaled = mm(chosen, arrived, 1, 1)
            carried = d_scaled * lead_wide
            total = out + carried * is_second
            d_x = step_wide * d_stepped + carried * is_first
            d_scaled = d_scaled * is_first
        mix_ref[:, sl] = total + skip * x
        dn_ref[:, sl] = d_x.astype(bf16) + (wide * skip).astype(bf16)
        put(sums_ref, 0, sl, wide * total - stepped.astype(f32) * d_stepped)
        put(sums_ref, 1, sl, x * d_stepped)
        put(sums_ref, 2, sl, x * d_scaled)
    d_cum, d_step, d_lead = head_sums(sums_ref, lanes_of, length)
    d_step = d_step + d_lead * rest
    fall = d_lead * lead
    d_cum = d_cum - fall
    end_sum = jnp.sum(fall, axis=0, keepdims=True)
    if first is None:
        ones = jnp.ones((8, state), f32)
        end_sum = end_sum + exact(ones, d_end, 1, 1)[0:1, :] * jnp.exp(last)
    else:
        d_b, d_c = d_b * is_first, d_b * is_second
    d_log = exact(mask, d_cum, 0, 0) + end_sum
    d_logits = (jax.nn.sigmoid(z) * (d_step - rate * d_log)).astype(bf16)
    d_scores = (d_scores * (mask / state)).astype(bf16)
    d_coeffs = jnp.concatenate(
        [mm(d_scores, c_part, 0, 0) + d_b, mm(d_scores, b_part, 1, 0) + d_c], axis=1
    ).astype(bf16)
    inverse = inverse_ref[...]
    if gproj_in is None:
        gproj_ref[...] = d_coeffs
        gstep_ref[...] = d_logits
    for sl in wide_blocks(width):
        pre = (
            dn_ref[:, sl].astype(f32)
            + mm(d_coeffs, proj_ref[sl, :], 1, 1)
            + mm(d_logits, step_ref[:, sl], 1, 0)
        )
        pre_ref[:, sl] = pre
        scaled = pre * (tok_ref[:, sl].astype(f32) * inverse)
        gmod_ref[0:1, sl] = jnp.sum(pre, axis=0, keepdims=True)
        gmod_ref[1:2, sl] = jnp.sum(scaled, axis=0, keepdims=True)
        if gproj_in is not None:
            gproj_ref[sl, :] = (gproj_in[sl, :] + mm(x_ref[:, sl], d_coeffs, 0, 0)).astype(bf16)
            gstep_ref[:, sl] = (gstep_in[:, sl] + mm(d_logits, x_ref[:, sl], 0, 0)).astype(bf16)


def last_kernel(tok_ref, inverse_ref, gain_ref, mix_ref, pre_ref, time_ref, back_ref, out_ref, dtok_ref):
    length, width = tok_ref.shape
    inverse = inverse_ref[...]
    total = jnp.zeros((length, LANES), f32)
    for _, sl in blocks(width):
        out_ref[:, sl] = (mix_ref[:, sl] + time_ref[:, sl].astype(f32)).astype(bf16)
        grad = (pre_ref[:, sl] + back_ref[:, sl].astype(f32)) * (1.0 + gain_ref[:, sl])
        total = total + grad * tok_ref[:, sl].astype(f32)
    inner = jnp.sum(total, axis=1, keepdims=True) / width
    inner = inner * inverse * inverse * inverse
    for _, sl in blocks(width):
        grad = (pre_ref[:, sl] + back_ref[:, sl].astype(f32)) * (1.0 + gain_ref[:, sl])
        dtok_ref[:, sl] = (grad * inverse - tok_ref[:, sl].astype(f32) * inner).astype(bf16)


def last_fast_kernel(tok_ref, inverse_ref, gain_ref, mix_ref, pre_ref, came_ref, *outs):
    class Packed:
        def __init__(self, which):
            self.which = which

        def __getitem__(self, at):
            value = came_ref[:, self.which, :, at[1]].astype(f32)
            return value.reshape(value.shape[0] * value.shape[1], LANES)

    last_kernel(tok_ref, inverse_ref, gain_ref, mix_ref, pre_ref, Packed(0), Packed(1), *outs)


def in_hbm(array):
    return pltpu.with_memory_space_constraint(array, pltpu.MemorySpace.HBM)


def call(kernel, outs, scratch=(), name=None, specs=None, hbm_outs=()):
    shapes = [
        pltpu.MemorySpace.HBM(s, d) if n in hbm_outs else jax.ShapeDtypeStruct(s, d)
        for n, (s, d) in enumerate(outs)
    ]
    where = {"s": pltpu.SMEM, "v": pltpu.VMEM, "h": pltpu.MemorySpace.HBM}
    spaces = {}
    if specs:
        spaces["in_specs"] = [pl.BlockSpec(memory_space=where[c]) for c in specs]
        spaces["out_specs"] = [
            pl.BlockSpec(memory_space=where["h" if n in hbm_outs else "v"]) for n in range(len(outs))
        ]
    return pl.pallas_call(
        kernel,
        out_shape=shapes,
        **spaces,
        scratch_shapes=[pltpu.VMEM(*s) if isinstance(s, tuple) else s for s in scratch],
        compiler_params=pltpu.CompilerParams(vmem_limit_bytes=24 << 20),
        name=name,
    )


def rows_in_order(part):
    if lax.axis_size("row") != 2:
        return lax.all_gather(part, "row")
    other = lax.ppermute(part, "row", [(0, 1), (1, 0)])
    first = lax.axis_index("row") == 0
    return jnp.stack([jnp.where(first, part, other), jnp.where(first, other, part)])


def rows_sum(part):
    if lax.axis_size("row") != 2:
        return lax.psum(part, "row")
    return part + lax.ppermute(part, "row", [(0, 1), (1, 0)])


def chain(own, decay, forward):
    count = lax.axis_size("row")
    hops = [(i, i + 1) if forward else (i + 1, i) for i in range(count - 1)]
    if count == 1:
        return jnp.zeros_like(own)
    arrived = lax.ppermute(own, "row", hops)
    wide = jnp.repeat(decay[0], own.shape[0] // decay.shape[1])[:, None]
    for _ in range(count - 2):
        passed = wide * arrived.astype(f32) + own.astype(f32)
        arrived = lax.ppermute(passed.astype(bf16), "row", hops)
    return arrived


def per_device(
    tokens,
    cotangent,
    timestep,
    mod_weight,
    proj_weight,
    step_weight,
    step_bias,
    rate_space,
    rate_time,
    skip_gain,
):
    frames = lax.axis_size("frame")
    rows = lax.axis_size("row")
    frame_id = lax.axis_index("frame")
    row_id = lax.axis_index("row")
    width = tokens.shape[-1]
    length = tokens.shape[1] * tokens.shape[2]
    clips = timestep.shape[0]
    clip_id = frame_id // (frames // clips)
    sites = length // frames
    heads = rate_space.shape[0]
    depth, pair = proj_weight.shape
    state = pair // 2
    mod_cols = mod_weight.shape[1]
    factor = (frames * rows * length) ** (-0.5)
    tok = tokens.reshape(length, width)
    grad = cotangent.reshape(length, width)

    activated = time_embed(timestep, mod_weight.shape[0]).astype(bf16)
    own_mod = jnp.dot(activated, mod_weight, preferred_element_type=f32)
    high = lax.reduce_precision(own_mod, 8, 7)
    own_mod = jnp.stack([high, own_mod - high]).astype(bf16)

    part = depth // rows
    own_proj = lax.dynamic_slice_in_dim(proj_weight, row_id * part, part, 0)
    to_all = [
        to_tiles(own_proj[None]),
        to_tiles(step_weight.T[None]),
        own_mod.reshape(1, -1, LANES),
    ]
    to_all = jnp.concatenate(to_all, axis=1)
    to_all = jnp.pad(to_all, ((0, 0), (0, -to_all.shape[1] % 8), (0, 0)))
    count = sites * width // LANES
    got = exchange(
        jnp.concatenate(
            [
                to_tiles(tok.reshape(frames, sites, width)),
                to_tiles(grad.reshape(frames, sites, width)),
                jnp.broadcast_to(to_all, (frames,) + to_all.shape[1:]),
            ],
            axis=1,
        )
    )
    site_tok = from_tiles(got[:, :count], sites, width).reshape(length, width)
    site_grad = from_tiles(got[:, count : 2 * count], sites, width).reshape(length, width)
    at = 2 * count
    size = part * pair // LANES
    proj_full = rows_in_order(got[:, at : at + size])
    proj_full = from_tiles(proj_full.reshape(rows * frames, size, LANES), part, pair)
    proj_full = proj_full.reshape(rows, frames, part, pair).transpose(1, 0, 2, 3)
    proj_full = proj_full.reshape(width, pair)
    at += size
    size = heads * depth // LANES
    step_full = from_tiles(got[:, at : at + size], heads, depth)
    step_full = step_full.transpose(1, 0, 2).reshape(heads, width)
    at += size
    size = 2 * clips * mod_cols // LANES
    mod_full = got[:, at : at + size].reshape(frames, 2, clips, mod_cols).astype(f32)
    mod_full = (mod_full[:, 0] + mod_full[:, 1]).transpose(1, 0, 2).reshape(clips, 2 * width)
    shift, gain = mod_full[:, :width], mod_full[:, width:]

    bias = step_bias[None]
    wide = (length, width)
    site_out, site_back, gproj, gstep, site_gmod = call(
        functools.partial(site_kernel, sites),
        [(wide, bf16), (wide, bf16), ((width, pair), f32), ((heads, width), f32), ((2 * clips, width), f32)],
        [(wide, bf16)] * 2 + [((2 * length, width), bf16)],
        name="site",
    )(site_tok, site_grad, shift, gain, proj_full, step_full, bias, rate_time[None])

    came = exchange(
        jnp.concatenate(
            [
                to_tiles(site_out.reshape(frames, sites, width)),
                to_tiles(site_back.reshape(frames, sites, width)),
            ],
            axis=1,
        )
    )
    time_out = from_tiles(came[:, :count], sites, width).reshape(length, width)
    time_back = from_tiles(came[:, count:], sites, width).reshape(length, width)

    own_shift = lax.dynamic_slice_in_dim(shift, clip_id, 1, 0)
    own_gain = lax.dynamic_slice_in_dim(gain, clip_id, 1, 0)
    normed, coeffs, logits, inverse, decay, end_own, start_grad = call(
        band_kernel,
        [
            (wide, bf16),
            ((length, pair), bf16),
            ((length, heads), bf16),
            ((length, 1), f32),
            ((1, heads), f32),
            ((width, state), bf16),
            ((width, state), bf16),
        ],
        name="band",
    )(tok, grad, own_shift, own_gain, proj_full, step_full, bias, rate_space[None])
    state_in = chain(end_own, decay, True)
    later_grad = chain(start_grad, decay, False)
    mix, pre, gproj, gstep, gmod = call(
        space_kernel,
        [(wide, f32), (wide, f32), ((width, pair), bf16), ((heads, width), bf16), ((2, width), f32)],
        [(wide, bf16), ((3 * length, width), bf16)],
        name="space",
    )(
        tok,
        grad,
        normed,
        coeffs,
        logits,
        inverse,
        proj_full,
        step_full,
        bias,
        rate_space[None],
        skip_gain[None],
        state_in,
        later_grad,
        gproj,
        gstep,
    )

    picked = (jnp.arange(clips) == clip_id).astype(f32)[:, None]
    gmod = jnp.concatenate(
        [site_gmod[:clips] + picked * gmod[0:1], site_gmod[clips:] + picked * gmod[1:2]], axis=1
    )
    gmod = gmod.reshape(clips, frames, mod_cols).transpose(1, 0, 2).astype(bf16)
    sent = jnp.concatenate(
        [
            to_tiles(gproj.reshape(frames, depth, pair)),
            to_tiles(gstep.reshape(heads, frames, depth).transpose(1, 0, 2)),
            gmod.reshape(frames, -1, LANES) if (clips * mod_cols) % LANES == 0 else gmod,
        ],
        axis=1,
    )
    size = sent.shape[1]
    sent = jnp.pad(sent, ((0, 0), (0, -size % 8), (0, 0)))
    sums = jnp.sum(exchange(sent).astype(f32), axis=0, keepdims=True)
    sums = rows_sum(sums) * factor
    at = depth * pair // LANES
    grad_proj = from_tiles(sums[:, :at], depth, pair)[0]
    size = heads * depth // LANES
    grad_step = from_tiles(sums[:, at : at + size], heads, depth)[0].T
    at += size
    size = clips * mod_cols // LANES
    mod_sum = sums[0, at : at + size].reshape(clips, mod_cols)
    grad_mod = jnp.dot(activated.astype(f32).T, mod_sum, precision=EXACT)

    mixed, d_tokens = call(last_kernel, [(wide, bf16), (wide, bf16)], name="last")(
        tok, inverse, own_gain, mix, pre, time_out, time_back
    )
    return (mixed.reshape(tokens.shape), d_tokens.reshape(tokens.shape), grad_proj, grad_step, grad_mod)


def fits(mesh, tokens, timestep, proj_weight, step_weight):
    frames, rows = mesh.shape["frame"], mesh.shape["row"]
    length, width = tokens.shape[2] * tokens.shape[1] // rows, tokens.shape[3]
    return (
        rows == 2
        and frames == 16
        and timestep.shape[0] == 1
        and length == LANES
        and length // frames == 8
        and width // frames == LANES
        and proj_weight.shape[1] == 2 * LANES
        and step_weight.shape[1] % 32 == 0
    )


def spread_over_frames(own, radix=4):
    frames = radix * radix

    def others(piece, stride):
        return [piece] + [
            lax.ppermute(piece, "frame", [(i, i ^ (d * stride)) for i in range(frames)])
            for d in range(1, radix)
        ]

    far = jnp.stack(others(own, radix))
    return jnp.concatenate(others(far, 1))


def sum_over_frames(keep, given, radix, ahead):
    frames = radix * radix

    def total(pieces):
        value = pieces[0].astype(f32)
        for piece in pieces[1:]:
            value = value + piece.astype(f32)
        return value

    def partner(piece, offset):
        return lax.ppermute(piece, "frame", [(i, i ^ offset) for i in range(frames)])

    parts = [slice(d * radix, (d + 1) * radix) for d in range(radix)]
    near = [total([keep[p], given[p]]).astype(bf16) for p in parts]
    near = [near[0]] + [partner(near[d], d) for d in range(1, radix)]
    near, ahead = lax.optimization_barrier((near, ahead))
    near = total(near).astype(bf16)
    far = [near[0]] + [partner(near[d], d * radix) for d in range(1, radix)]
    return total(far), *ahead


def per_device_fast(
    tokens,
    cotangent,
    timestep,
    mod_weight,
    proj_weight,
    step_weight,
    step_bias,
    rate_space,
    rate_time,
    skip_gain,
):
    frames = lax.axis_size("frame")
    rows = lax.axis_size("row")
    ids = jnp.stack([lax.axis_index("frame"), lax.axis_index("row")]).astype(jnp.int32)
    width = tokens.shape[-1]
    length = tokens.shape[1] * tokens.shape[2]
    sites = length // frames
    heads = rate_space.shape[0]
    depth, pair = proj_weight.shape
    state = pair // 2
    mod_cols = mod_weight.shape[1]
    factor = (frames * rows * length) ** (-0.5)
    tok = tokens.reshape(length, width)
    grad = cotangent.reshape(length, width)
    wide = (length, width)
    small = jnp.stack([step_bias, rate_time, rate_space, skip_gain])
    swap = [(0, 1), (1, 0)]

    packed = (frames, 2, sites, width)
    size = depth // 2 * pair // LANES + heads // 2 + 8
    activated = time_embed(timestep, mod_weight.shape[0]).astype(bf16)
    sent, payload = call(
        start_kernel,
        [(packed, bf16), ((size, LANES), bf16)],
        [
            ((depth, pair), bf16),
            ((heads, depth), bf16),
            (mod_weight.shape, bf16),
            (packed, bf16),
            pltpu.SemaphoreType.DMA((7,)),
        ],
        name="start",
        specs="shhhhhv",
        hbm_outs=(0,),
    )(
        ids,
        in_hbm(tok.reshape(frames, sites, width)),
        in_hbm(grad.reshape(frames, sites, width)),
        in_hbm(proj_weight),
        in_hbm(step_weight.T),
        in_hbm(mod_weight),
        activated,
    )
    got = exchange(sent)
    payload = spread_over_frames(payload)
    other = lax.ppermute(payload, "row", swap)
    proj_full, step_full, shift, gain = call(
        functools.partial(unpack_kernel, 4),
        [((width, pair), bf16), ((heads, width), bf16), ((1, width), f32), ((1, width), f32)],
        name="unpack",
        specs="svv",
    )(ids, payload, other)

    sent, site_x, site_gmod, site_dc, site_dl = call(
        functools.partial(site_fast_kernel, sites),
        [
            (packed, bf16),
            (wide, bf16),
            ((2, width), f32),
            ((length, pair), bf16),
            ((length, heads), bf16),
        ],
        [
            (wide, bf16),
            (packed, bf16),
            (wide, bf16),
            ((2, width), f32),
            pltpu.SemaphoreType.DMA((10,)),
        ]
        + [(wide, bf16), ((2 * length, width), bf16)],
        name="site",
        specs="vvvvvv",
        hbm_outs=(0, 1, 2),
    )(got, shift, gain, proj_full, step_full, small)
    sent, proj_full = lax.optimization_barrier((sent, proj_full))
    came = exchange(sent)

    normed, coeffs, logits, inverse, give = call(
        band_fast_kernel,
        [
            (wide, bf16),
            ((length, pair), bf16),
            ((length, heads), bf16),
            ((length, 1), f32),
            ((width, state), bf16),
        ],
        name="band",
        specs="svvvvvvv",
    )(ids, tok, grad, shift, gain, proj_full, step_full, small)
    arrived = lax.ppermute(give, "row", swap)

    halves = (frames, size, LANES)
    mix, pre, own_dc, own_dl, gmod = call(
        space_fast_kernel,
        [(wide, f32), (wide, f32), ((length, pair), bf16), ((length, heads), bf16), ((2, width), f32)],
        [(wide, bf16), ((3 * length, width), bf16)],
        name="space",
        specs="s" + "v" * 10,
    )(
        ids,
        arrived,
        tok,
        grad,
        normed,
        coeffs,
        logits,
        inverse,
        proj_full,
        step_full,
        small,
    )
    keep, give = call(
        functools.partial(terms_kernel, 4),
        [(halves, bf16), (halves, bf16)],
        name="terms",
        specs="svvvvvvvv",
    )(ids, normed, own_dc, own_dl, gmod, site_x, site_dc, site_dl, site_gmod)
    given = lax.ppermute(give, "row", swap)
    mixed, d_tokens = call(last_fast_kernel, [(wide, bf16), (wide, bf16)], name="last")(
        tok, inverse, gain, mix, pre, came
    )
    terms, mixed, d_tokens = sum_over_frames(keep, given, 4, (mixed, d_tokens))
    other = lax.ppermute(terms, "row", swap)
    grad_proj, grad_step, grad_mod = call(
        functools.partial(finish_kernel, factor),
        [((depth, pair), f32), ((heads, depth), f32), ((mod_weight.shape[0], mod_cols), f32)],
        name="finish",
        specs="svvv",
    )(ids, terms, other, activated.astype(f32).T)
    return (mixed.reshape(tokens.shape), d_tokens.reshape(tokens.shape), grad_proj, grad_step.T, grad_mod)


def solution(mesh):
    placed = (
        P("frame", "row", None, None),
        P("frame", "row", None, None),
        P(),
        P(None, "frame"),
        P("frame", None),
        P("frame", None),
        P(),
        P(),
        P(),
        P(),
    )
    outs = (
        P("frame", "row", None, None),
        P("frame", "row", None, None),
        P("frame", None),
        P("frame", None),
        P(None, "frame"),
    )

    def step(tokens, cotangent, timestep, mod_weight, proj_weight, step_weight, *rest):
        fast = fits(mesh, tokens, timestep, proj_weight, step_weight)
        body = per_device_fast if fast else per_device
        return jax.shard_map(
            body, mesh=mesh, in_specs=placed, out_specs=outs, check_vma=False
        )(tokens, cotangent, timestep, mod_weight, proj_weight, step_weight, *rest)

    return step
```

```python
import functools
import math

import jax
import jax.numpy as jnp
from jax import lax
from jax.experimental import pallas as pl
from jax.experimental.pallas import tpu as pltpu
from jax.sharding import PartitionSpec as P

norm_eps = 1e-05
LANES = 128
LOG2E = math.log2(math.e)
f32 = jnp.float32
bf16 = jnp.bfloat16
EXACT = lax.Precision.HIGHEST


def time_embed(timestep, embed_dim):
    half_dim = embed_dim // 2
    place = (jnp.arange(embed_dim) % half_dim).astype(f32)
    frequency = jnp.exp(-math.log(10000.0) * place / half_dim)
    angles = timestep.astype(f32)[:, None] * frequency[None, :]
    lower = jnp.arange(embed_dim)[None, :] < half_dim
    return jax.nn.silu(jnp.where(lower, jnp.cos(angles), jnp.sin(angles)))


def to_tiles(a):
    f, r, c = a.shape
    if r % 8 == 0 and c % LANES == 0:
        a = a.reshape(f, r // 8, 8, c // LANES, LANES).transpose(0, 1, 3, 2, 4)
    return a.reshape(f, r * c // LANES, LANES)


def from_tiles(a, r, c):
    f = a.shape[0]
    if r % 8 == 0 and c % LANES == 0:
        a = a.reshape(f, r // 8, c // LANES, 8, LANES).transpose(0, 1, 3, 2, 4)
    return a.reshape(f, r, c)


def exchange(packed):
    return lax.all_to_all(packed, "frame", split_axis=0, concat_axis=0, tiled=True)


def mm(a, b, ca, cb):
    return lax.dot_general(a, b, (((ca,), (cb,)), ((), ())), preferred_element_type=f32)


def exact(a, b, ca, cb):
    return lax.dot_general(
        a, b, (((ca,), (cb,)), ((), ())), preferred_element_type=f32, precision=EXACT
    )


def split(a):
    high = a.astype(bf16)
    return high, (a - high.astype(f32)).astype(bf16)


def head_map(heads, width):
    size = width // heads
    own = lax.broadcasted_iota(jnp.int32, (heads, width), 0)
    lane = lax.broadcasted_iota(jnp.int32, (heads, width), 1)
    return jnp.where(lane // size == own, 1.0, 0.0).astype(bf16)


def sequence_mask(length, sites):
    later = lax.broadcasted_iota(jnp.int32, (length, length), 0)
    earlier = lax.broadcasted_iota(jnp.int32, (length, length), 1)
    keep = later >= earlier
    if sites > 1:
        keep = keep & (later % sites == earlier % sites)
    return jnp.where(keep, 1.0, 0.0).astype(f32)


def blocks(width):
    return [(j, slice(j * LANES, (j + 1) * LANES)) for j in range(width // LANES)]


def spread_rows(rows, length):
    count = rows.shape[0]
    if count == 1:
        return rows
    part = (length // count, rows.shape[1])
    return jnp.concatenate([jnp.broadcast_to(rows[c : c + 1], part) for c in range(count)], axis=0)


def normalize_into(tok_ref, shift_ref, gain_ref, x_ref, read=None):
    length, width = tok_ref.shape
    total = jnp.zeros((length, LANES), f32)
    for _, sl in blocks(width):
        if read is None:
            v = tok_ref[:, sl].astype(f32)
        else:
            v = read(sl)
            tok_ref[:, sl] = v.astype(bf16)
        total = total + v * v
    mean = jnp.sum(total, axis=1, keepdims=True) / width
    inverse = lax.rsqrt(mean + norm_eps)
    for _, sl in blocks(width):
        unit = tok_ref[:, sl].astype(f32) * inverse
        gain = spread_rows(gain_ref[:, sl], length)
        shift = spread_rows(shift_ref[:, sl], length)
        x_ref[:, sl] = (unit * (1.0 + gain) + shift).astype(bf16)
    return inverse


def steps_of(logits, bias, rate, mask):
    z = logits.astype(f32) + bias
    step = jnp.maximum(z, 0.0) + jnp.log1p(jnp.exp(-jnp.abs(z)))
    log_decay = -step * rate
    cum = exact(mask, log_decay, 1, 0)
    return z, step, cum, (cum * LOG2E, exact(log_decay * LOG2E, mask, 0, 1))


def halves_of(a):
    return jnp.concatenate(split(a), axis=1)


def doubled(lanes_of):
    return jnp.concatenate([lanes_of, lanes_of], axis=0)


def scan_block(j, x, grad, step_wide, scores, cums, heads, width, d_scores):
    size = width // heads
    per_block = LANES // size
    length = x.shape[0]
    stepped = (x.astype(f32) * step_wide).astype(bf16)
    lane = lax.broadcasted_iota(jnp.int32, x.shape, 1)
    inside = [lane // size == i for i in range(per_block)]
    zero = jnp.zeros_like(x)
    steppeds = jnp.concatenate([jnp.where(own, stepped, zero) for own in inside], axis=0)
    grads = jnp.concatenate([jnp.where(own, grad, zero) for own in inside], axis=0)
    d_weights = mm(grads, stepped, 1, 1)
    weights = []
    for i in range(per_block):
        h = j * per_block + i
        decay = jnp.exp2(jnp.minimum(cums[0][:, h : h + 1] - cums[1][h : h + 1, :], 0.0))
        d_scores = d_scores + d_weights[i * length : (i + 1) * length] * decay
        weights.append((scores * decay).astype(bf16))
    out = mm(jnp.concatenate(weights, axis=1), steppeds, 1, 0)
    d_stepped = mm(jnp.concatenate(weights, axis=0), grads, 0, 0)
    return stepped, out, d_stepped, d_scores


def put(sums_ref, which, sl, value):
    length = value.shape[0]
    sums_ref[which * length : (which + 1) * length, sl] = value.astype(bf16)


def head_sums(sums_ref, lanes_of, length):
    sums = mm(sums_ref[...], lanes_of, 1, 1)
    return [sums[at : at + length] for at in range(0, sums.shape[0], length)]


def wide_blocks(width):
    return [(slice(at, at + 2 * LANES)) for at in range(0, width, 2 * LANES)]


def start_kernel(ids_ref, tok_ref, grad_ref, proj_hbm, step_hbm, mod_hbm, active_ref, sent_ref, pay_ref,
                 proj_ref, step_ref, mod_ref, both_ref, sems):
    parts = 4
    share = tok_ref.shape[0] // parts
    pairs = [(proj_hbm, proj_ref), (step_hbm, step_ref), (mod_hbm, mod_ref)]
    for p in range(parts):
        at = slice(p * share, (p + 1) * share)
        pairs += [(tok_ref.at[at], both_ref.at[at, 0]), (grad_ref.at[at], both_ref.at[at, 1])]
    for p in range(parts):
        at = slice(p * share, (p + 1) * share)
        pairs.append((both_ref.at[at], sent_ref.at[at]))
    copies = [
        pltpu.make_async_copy(src, dst, sems.at[n]) for n, (src, dst) in enumerate(pairs)
    ]
    inward, outward = copies[: 3 + 2 * parts], copies[3 + 2 * parts :]
    for copy in inward:
        copy.start()
    for p, copy in enumerate(outward):
        inward[3 + 2 * p].wait()
        inward[4 + 2 * p].wait()
        copy.start()
    row = ids_ref[1]
    part, pair = proj_ref.shape[0] // 2, proj_ref.shape[1]
    copies[0].wait()
    own = proj_ref[pl.ds(pl.multiple_of(row * part, part), part), :]
    at = 0
    for _, sl in blocks(pair):
        pay_ref[at : at + part, :] = own[:, sl]
        at += part
    copies[1].wait()
    part = step_ref.shape[0] // 2
    pay_ref[at : at + part, :] = step_ref[pl.ds(pl.multiple_of(row * part, part), part), :]
    at += part
    copies[2].wait()
    own = mm(active_ref[...], mod_ref[...], 1, 0)
    high = own.astype(bf16).astype(f32)
    pieces = [piece[:, sl] for piece in (high, own - high) for _, sl in blocks(own.shape[1])]
    pieces.append(jnp.zeros((8 - len(pieces), LANES), f32))
    pay_ref[at : at + 8, :] = jnp.concatenate(pieces, axis=0).astype(bf16)
    for copy in outward:
        copy.wait()


def unpack_kernel(radix, ids_ref, own_ref, other_ref, proj_ref, step_ref, shift_ref, gain_ref):
    me, row = ids_ref[0], ids_ref[1]
    width, pair = proj_ref.shape
    frames = own_ref.shape[0]
    depth = width // frames
    part, heads = depth // 2, step_ref.shape[0] // 2
    cols = 2 * width // frames
    for i in range(frames):
        source = jnp.bitwise_xor(me, (i % radix) * radix + i // radix)
        for ref, half in ((own_ref, row), (other_ref, 1 - row)):
            rows = pl.ds(pl.multiple_of(source * depth + half * part, part), part)
            at = 0
            for _, sl in blocks(pair):
                proj_ref[rows, sl] = ref[i, at : at + part, :]
                at += part
            rows = pl.ds(pl.multiple_of(half * heads, heads), heads)
            lanes = pl.ds(pl.multiple_of(source * depth, depth), depth)
            step_ref[rows, lanes] = ref[i, at : at + heads, :]
            at += heads
        own = own_ref[i, at : at + 8, :].astype(f32)
        count = cols // LANES
        lanes_at = jnp.bitwise_and(source, frames // 2 - 1) * cols
        for k in range(count):
            value = own[k : k + 1, :] + own[count + k : count + k + 1, :]
            lanes = pl.ds(pl.multiple_of(lanes_at + k * LANES, LANES), LANES)

            @pl.when(source < frames // 2)
            def _():
                shift_ref[:, lanes] = value

            @pl.when(source >= frames // 2)
            def _():
                gain_ref[:, lanes] = value


def finish_mod_kernel(factor, at, sums_ref, active_ref, mod_ref):
    rest = jnp.zeros((7, active_ref.shape[1]), f32)
    active = jnp.concatenate([active_ref[...].astype(f32), rest], axis=0)
    for k, sl in blocks(mod_ref.shape[1]):
        own = jnp.broadcast_to(sums_ref[at + k : at + k + 1, :] * factor, (8, LANES))
        mod_ref[:, sl] = exact(active, own, 0, 0)


def finish_kernel(factor, ids_ref, own_ref, other_ref, proj_ref, step_ref):
    row = ids_ref[1]
    pair = proj_ref.shape[1]
    part, heads = proj_ref.shape[0] // 2, step_ref.shape[0] // 2
    for ref, half in ((own_ref, row), (other_ref, 1 - row)):
        rows = pl.ds(pl.multiple_of(half * part, part), part)
        at = 0
        for _, sl in blocks(pair):
            proj_ref[rows, sl] = ref[at : at + part, :] * factor
            at += part
        step_ref[pl.ds(pl.multiple_of(half * heads, heads), heads), :] = ref[at : at + heads, :] * factor


def site_fast_kernel(sites, got_ref, *refs):
    inputs, (small_ref, sent_hbm, x_hbm, gmod_hbm, dc_ref, dl_ref) = refs[:4], refs[4:10]
    inputs = (*inputs, small_ref[0:1, :], small_ref[1:2, :])
    tok_ref, sent_ref, x_ref, gmod_ref, sems = refs[10:15]
    scratch = refs[15:]
    frames, width = got_ref.shape[0], got_ref.shape[3]
    def read(which):
        return lambda sl: got_ref[:, which, :, sl].astype(f32).reshape(frames * sites, LANES)

    class Grad:
        def __getitem__(self, at):
            return read(1)(at[1]).astype(bf16)

    parts = 8
    share = width // parts
    copies = []

    def begin(source, target):
        copy = pltpu.make_async_copy(source, target, sems.at[len(copies)])
        copy.start()
        copies.append(copy)

    def send(which, p):
        at = (slice(None), which, slice(None), slice(p * share, (p + 1) * share))
        begin(sent_ref.at[at], sent_hbm.at[at])

    class Packed:
        def __init__(self, which):
            self.which = which

        def __setitem__(self, at, value):
            if not copies:
                begin(x_ref, x_hbm)
            value = value.astype(f32).reshape(frames, sites, value.shape[1])
            sent_ref[:, self.which, :, at[1]] = value.astype(bf16)
            if at[1].stop % share == 0:
                send(self.which, at[1].stop // share - 1)

    site_kernel(
        sites,
        tok_ref,
        Grad(),
        *inputs,
        Packed(0),
        Packed(1),
        dc_ref,
        dl_ref,
        gmod_ref,
        x_ref,
        *scratch,
        read=read(0),
    )
    begin(gmod_ref, gmod_hbm)
    for copy in copies:
        copy.wait()


def site_kernel(
    sites,
    tok_ref,
    grad_ref,
    shift_ref,
    gain_ref,
    proj_ref,
    step_ref,
    bias_ref,
    rate_ref,
    out_ref,
    back_ref,
    gproj_ref,
    gstep_ref,
    gmod_ref,
    x_ref,
    dn_ref,
    sums_ref,
    read=None,
):
    length, width = tok_ref.shape
    heads = step_ref.shape[0]
    state = proj_ref.shape[1] // 2
    clips = shift_ref.shape[0]
    inverse = normalize_into(tok_ref, shift_ref, gain_ref, x_ref, read)
    lanes_of = head_map(heads, width)
    mask = sequence_mask(length, sites)
    coeffs = mm(x_ref[...], proj_ref[...], 1, 0).astype(bf16)
    logits = mm(x_ref[...], step_ref[...], 1, 1).astype(bf16)
    rate = rate_ref[...]
    z, step, cum, cums = steps_of(logits, bias_ref[...], rate, mask)
    b_part, c_part = coeffs[:, :state], coeffs[:, state:]
    scores = mm(c_part, b_part, 1, 1) * (mask / state)
    step_parts, twice = halves_of(step), doubled(lanes_of)
    d_scores = jnp.zeros((length, length), f32)
    for j, sl in blocks(width):
        x, grad = x_ref[:, sl], grad_ref[:, sl]
        step_wide = mm(step_parts, twice[:, sl], 1, 0)
        stepped, out, d_stepped, d_scores = scan_block(
            j, x, grad, step_wide, scores, cums, heads, width, d_scores
        )
        out_ref[:, sl] = out.astype(bf16)
        dn_ref[:, sl] = (step_wide * d_stepped).astype(bf16)
        put(sums_ref, 0, sl, grad.astype(f32) * out - stepped.astype(f32) * d_stepped)
        put(sums_ref, 1, sl, x.astype(f32) * d_stepped)
    d_cum, d_step = head_sums(sums_ref, lanes_of, length)
    d_log = exact(mask, d_cum, 0, 0)
    d_logits = (jax.nn.sigmoid(z) * (d_step - rate * d_log)).astype(bf16)
    d_scores = (d_scores * (mask / state)).astype(bf16)
    d_coeffs = jnp.concatenate(
        [mm(d_scores, c_part, 0, 0), mm(d_scores, b_part, 1, 0)], axis=1
    ).astype(bf16)
    for sl in wide_blocks(width):
        back = (
            dn_ref[:, sl].astype(f32)
            + mm(d_coeffs, proj_ref[sl, :], 1, 1)
            + mm(d_logits, step_ref[:, sl], 1, 0)
        )
        back_ref[:, sl] = back.astype(bf16)
        scaled = back * (tok_ref[:, sl].astype(f32) * inverse)
        for c in range(clips):
            rows = slice(c * (length // clips), (c + 1) * (length // clips))
            gmod_ref[c : c + 1, sl] = jnp.sum(back[rows], axis=0, keepdims=True)
            gmod_ref[clips + c : clips + c + 1, sl] = jnp.sum(scaled[rows], axis=0, keepdims=True)
        if gproj_ref.shape == (width, 2 * state):
            gproj_ref[sl, :] = mm(x_ref[:, sl], d_coeffs, 0, 0)
            gstep_ref[:, sl] = mm(d_logits, x_ref[:, sl], 0, 0)
    if gproj_ref.shape != (width, 2 * state):
        gproj_ref[...] = d_coeffs
        gstep_ref[...] = d_logits


def band_fast_kernel(ids_ref, *refs):
    small_ref, give_ref = refs[6], refs[-1]
    inputs = (*refs[:6], small_ref[0:1, :], small_ref[2:3, :])
    band_kernel(*inputs, *refs[7:-1], None, None, give_ref, first=ids_ref[1] == 0)


def band_kernel(
    tok_ref,
    grad_ref,
    shift_ref,
    gain_ref,
    proj_ref,
    step_ref,
    bias_ref,
    rate_ref,
    x_ref,
    coeffs_ref,
    logits_ref,
    inverse_ref,
    decay_ref,
    end_ref,
    own_ref,
    first=None,
):
    length, width = tok_ref.shape
    heads = step_ref.shape[0]
    state = proj_ref.shape[1] // 2
    inverse_ref[...] = normalize_into(tok_ref, shift_ref, gain_ref, x_ref)
    twice = doubled(head_map(heads, width))
    mask = sequence_mask(length, 1)
    coeffs = mm(x_ref[...], proj_ref[...], 1, 0).astype(bf16)
    logits = mm(x_ref[...], step_ref[...], 1, 1).astype(bf16)
    coeffs_ref[...] = coeffs
    logits_ref[...] = logits
    _, step, cum, _ = steps_of(logits, bias_ref[...], rate_ref[...], mask)
    last = cum[length - 1 : length, :]
    b_part, c_part = coeffs[:, :state], coeffs[:, state:]
    if first is not None:
        gain = halves_of(jnp.where(first, jnp.exp(last - cum) * step, jnp.exp(cum) / state))
        other = jnp.where(first, b_part, c_part)
        for _, sl in blocks(width):
            value = jnp.where(first, x_ref[:, sl], grad_ref[:, sl]).astype(f32)
            value = (value * mm(gain, twice[:, sl], 1, 0)).astype(bf16)
            own_ref[sl, :] = mm(value, other, 0, 0).astype(bf16)
        return
    decay_ref[...] = jnp.exp(last)
    lead = halves_of(jnp.exp(last - cum) * step)
    reach = halves_of(jnp.exp(cum) / state)
    for _, sl in blocks(width):
        lead_wide = mm(lead, twice[:, sl], 1, 0)
        reach_wide = mm(reach, twice[:, sl], 1, 0)
        scaled = (x_ref[:, sl].astype(f32) * lead_wide).astype(bf16)
        faded = (grad_ref[:, sl].astype(f32) * reach_wide).astype(bf16)
        end_ref[sl, :] = mm(scaled, b_part, 0, 0).astype(bf16)
        own_ref[sl, :] = mm(faded, c_part, 0, 0).astype(bf16)


def terms_kernel(radix, ids_ref, x_ref, dc_ref, dl_ref, gmod_ref, site_x, site_dc, site_dl, site_gmod,
                 keep_ref, give_ref):
    me, first = ids_ref[0], ids_ref[1] == 0
    width = x_ref.shape[1]
    coeffs = jnp.concatenate([dc_ref[...], site_dc[...]], axis=0)
    logits = jnp.concatenate([dl_ref[...], site_dl[...]], axis=0)
    frames = keep_ref.shape[0]
    share = 2 * width // LANES // frames

    def put_halves(j, at, value):
        part = value.shape[0] // 2
        own = jnp.where(first, value[:part], value[part:]).astype(bf16)
        other = jnp.where(first, value[part:], value[:part]).astype(bf16)
        for _, sl in blocks(value.shape[1]):
            keep_ref[j, at : at + part, :] = own[:, sl]
            give_ref[j, at : at + part, :] = other[:, sl]
            at += part
        return at

    for j, sl in blocks(width):
        offset = jnp.bitwise_xor(me, j)
        place = jnp.bitwise_and(offset, radix - 1) * radix + offset // radix
        tall = jnp.concatenate([x_ref[:, sl], site_x[:, sl]], axis=0)
        at = put_halves(place, 0, mm(tall, coeffs, 0, 0))
        at = put_halves(place, at, mm(logits, tall, 0, 0))
        rows = []
        for n in range(j * share, (j + 1) * share):
            which, at_lane = n // (width // LANES), n % (width // LANES) * LANES
            lanes = slice(at_lane, at_lane + LANES)
            rows.append(gmod_ref[which : which + 1, lanes] + site_gmod[which : which + 1, lanes])
        rows.append(jnp.zeros((8 - len(rows), LANES), f32))
        rows = jnp.concatenate(rows, axis=0).astype(bf16)
        keep_ref[place, at : at + 8, :] = rows
        give_ref[place, at : at + 8, :] = rows


def space_fast_kernel(ids_ref, arrived_ref, *refs):
    inputs, small_ref, outs = refs[:8], refs[8], refs[9:]
    inputs = (*inputs, *(small_ref[n : n + 1, :] for n in (0, 2, 3)))
    space_kernel(*inputs, arrived_ref, None, None, None, *outs, first=ids_ref[1] == 0)


def space_kernel(
    tok_ref,
    grad_ref,
    x_ref,
    coeffs_ref,
    logits_ref,
    inverse_ref,
    proj_ref,
    step_ref,
    bias_ref,
    rate_ref,
    skip_ref,
    state_ref,
    later_ref,
    gproj_in,
    gstep_in,
    mix_ref,
    pre_ref,
    gproj_ref,
    gstep_ref,
    gmod_ref,
    dn_ref,
    sums_ref,
    first=None,
):
    length, width = tok_ref.shape
    heads = step_ref.shape[0]
    state = proj_ref.shape[1] // 2
    lanes_of = head_map(heads, width)
    twice = doubled(lanes_of)
    mask = sequence_mask(length, 1)
    coeffs = coeffs_ref[...]
    rate = rate_ref[...]
    z, step, cum, cums = steps_of(logits_ref[...], bias_ref[...], rate, mask)
    last = cum[length - 1 : length, :]
    rest = jnp.exp(last - cum)
    lead, reach = rest * step, jnp.exp(cum) / state
    b_part, c_part = coeffs[:, :state], coeffs[:, state:]
    scores = mm(c_part, b_part, 1, 1) * (mask / state)
    skip = jnp.broadcast_to(skip_ref[...], (8, heads))
    if first is None:
        parts = [step, lead, reach, skip]
    else:
        parts = [step, jnp.where(first, lead, reach), skip]
        chosen = jnp.where(first, b_part, c_part)
        is_first = jnp.where(first, 1.0, 0.0).astype(f32)
        is_second = 1.0 - is_first
    parts = jnp.concatenate([halves_of(part) for part in parts], axis=0)
    d_scores = jnp.zeros((length, length), f32)
    d_b = jnp.zeros((length, state), f32)
    d_c = jnp.zeros((length, state), f32)
    d_end = jnp.zeros((heads, state), f32)
    for j, sl in blocks(width):
        x, grad = x_ref[:, sl], grad_ref[:, sl]
        wide_parts = mm(parts, twice[:, sl], 1, 0)
        step_wide, lead_wide = wide_parts[:length], wide_parts[length : 2 * length]
        skip = wide_parts[-8:-7]
        stepped, out, d_stepped, d_scores = scan_block(
            j, x, grad, step_wide, scores, cums, heads, width, d_scores
        )
        if first is None:
            x, wide = x.astype(f32), grad.astype(f32)
            reach_wide = wide_parts[2 * length : 3 * length]
            before, later = state_ref[sl, :], later_ref[sl, :]
            total = out + mm(c_part, before, 1, 1) * reach_wide
            d_c = d_c + mm((wide * reach_wide).astype(bf16), before, 1, 0)
            d_b = d_b + mm((x * lead_wide).astype(bf16), later, 1, 0)
            d_scaled = mm(b_part, later, 1, 1)
            d_x = step_wide * d_stepped + d_scaled * lead_wide
            both = split(before.astype(f32) * later.astype(f32))
            d_end = d_end + mm(lanes_of[:, sl], both[0], 1, 0) + mm(lanes_of[:, sl], both[1], 1, 0)
        else:
            arrived = state_ref[sl, :]
            value = jnp.where(first, x, grad).astype(f32)
            d_b = d_b + mm((value * lead_wide).astype(bf16), arrived, 1, 0)
            x, wide = x.astype(f32), grad.astype(f32)
            d_scaled = mm(chosen, arrived, 1, 1)
            carried = d_scaled * lead_wide
            total = out + carried * is_second
            d_x = step_wide * d_stepped + carried * is_first
            d_scaled = d_scaled * is_first
        mix_ref[:, sl] = total + skip * x
        dn_ref[:, sl] = d_x.astype(bf16) + (wide * skip).astype(bf16)
        put(sums_ref, 0, sl, wide * total - stepped.astype(f32) * d_stepped)
        put(sums_ref, 1, sl, x * d_stepped)
        put(sums_ref, 2, sl, x * d_scaled)
    d_cum, d_step, d_lead = head_sums(sums_ref, lanes_of, length)
    d_step = d_step + d_lead * rest
    fall = d_lead * lead
    d_cum = d_cum - fall
    end_sum = jnp.sum(fall, axis=0, keepdims=True)
    if first is None:
        ones = jnp.ones((8, state), f32)
        end_sum = end_sum + exact(ones, d_end, 1, 1)[0:1, :] * jnp.exp(last)
    else:
        d_b, d_c = d_b * is_first, d_b * is_second
    d_log = exact(mask, d_cum, 0, 0) + end_sum
    d_logits = (jax.nn.sigmoid(z) * (d_step - rate * d_log)).astype(bf16)
    d_scores = (d_scores * (mask / state)).astype(bf16)
    d_coeffs = jnp.concatenate(
        [mm(d_scores, c_part, 0, 0) + d_b, mm(d_scores, b_part, 1, 0) + d_c], axis=1
    ).astype(bf16)
    inverse = inverse_ref[...]
    if gproj_in is None:
        gproj_ref[...] = d_coeffs
        gstep_ref[...] = d_logits
    for sl in wide_blocks(width):
        pre = (
            dn_ref[:, sl].astype(f32)
            + mm(d_coeffs, proj_ref[sl, :], 1, 1)
            + mm(d_logits, step_ref[:, sl], 1, 0)
        )
        pre_ref[:, sl] = pre
        scaled = pre * (tok_ref[:, sl].astype(f32) * inverse)
        gmod_ref[0:1, sl] = jnp.sum(pre, axis=0, keepdims=True)
        gmod_ref[1:2, sl] = jnp.sum(scaled, axis=0, keepdims=True)
        if gproj_in is not None:
            gproj_ref[sl, :] = (gproj_in[sl, :] + mm(x_ref[:, sl], d_coeffs, 0, 0)).astype(bf16)
            gstep_ref[:, sl] = (gstep_in[:, sl] + mm(d_logits, x_ref[:, sl], 0, 0)).astype(bf16)


def last_kernel(tok_ref, inverse_ref, gain_ref, mix_ref, pre_ref, time_ref, back_ref, out_ref, dtok_ref):
    length, width = tok_ref.shape
    inverse = inverse_ref[...]
    total = jnp.zeros((length, LANES), f32)
    for _, sl in blocks(width):
        out_ref[:, sl] = (mix_ref[:, sl] + time_ref[:, sl].astype(f32)).astype(bf16)
        grad = (pre_ref[:, sl] + back_ref[:, sl].astype(f32)) * (1.0 + gain_ref[:, sl])
        total = total + grad * tok_ref[:, sl].astype(f32)
    inner = jnp.sum(total, axis=1, keepdims=True) / width
    inner = inner * inverse * inverse * inverse
    for _, sl in blocks(width):
        grad = (pre_ref[:, sl] + back_ref[:, sl].astype(f32)) * (1.0 + gain_ref[:, sl])
        dtok_ref[:, sl] = (grad * inverse - tok_ref[:, sl].astype(f32) * inner).astype(bf16)


def last_fast_kernel(tok_ref, inverse_ref, gain_ref, mix_ref, pre_ref, came_ref, *outs):
    class Packed:
        def __init__(self, which):
            self.which = which

        def __getitem__(self, at):
            value = came_ref[:, self.which, :, at[1]].astype(f32)
            return value.reshape(value.shape[0] * value.shape[1], LANES)

    last_kernel(tok_ref, inverse_ref, gain_ref, mix_ref, pre_ref, Packed(0), Packed(1), *outs)


def in_hbm(array):
    return pltpu.with_memory_space_constraint(array, pltpu.MemorySpace.HBM)


def call(kernel, outs, scratch=(), name=None, specs=None, hbm_outs=()):
    shapes = [
        pltpu.MemorySpace.HBM(s, d) if n in hbm_outs else jax.ShapeDtypeStruct(s, d)
        for n, (s, d) in enumerate(outs)
    ]
    where = {"s": pltpu.SMEM, "v": pltpu.VMEM, "h": pltpu.MemorySpace.HBM}
    spaces = {}
    if specs:
        spaces["in_specs"] = [pl.BlockSpec(memory_space=where[c]) for c in specs]
        spaces["out_specs"] = [
            pl.BlockSpec(memory_space=where["h" if n in hbm_outs else "v"]) for n in range(len(outs))
        ]
    return pl.pallas_call(
        kernel,
        out_shape=shapes,
        **spaces,
        scratch_shapes=[pltpu.VMEM(*s) if isinstance(s, tuple) else s for s in scratch],
        compiler_params=pltpu.CompilerParams(vmem_limit_bytes=24 << 20),
        name=name,
    )


def rows_in_order(part):
    if lax.axis_size("row") != 2:
        return lax.all_gather(part, "row")
    other = lax.ppermute(part, "row", [(0, 1), (1, 0)])
    first = lax.axis_index("row") == 0
    return jnp.stack([jnp.where(first, part, other), jnp.where(first, other, part)])


def rows_sum(part):
    if lax.axis_size("row") != 2:
        return lax.psum(part, "row")
    return part + lax.ppermute(part, "row", [(0, 1), (1, 0)])


def chain(own, decay, forward):
    count = lax.axis_size("row")
    hops = [(i, i + 1) if forward else (i + 1, i) for i in range(count - 1)]
    if count == 1:
        return jnp.zeros_like(own)
    arrived = lax.ppermute(own, "row", hops)
    wide = jnp.repeat(decay[0], own.shape[0] // decay.shape[1])[:, None]
    for _ in range(count - 2):
        passed = wide * arrived.astype(f32) + own.astype(f32)
        arrived = lax.ppermute(passed.astype(bf16), "row", hops)
    return arrived


def per_device(
    tokens,
    cotangent,
    timestep,
    mod_weight,
    proj_weight,
    step_weight,
    step_bias,
    rate_space,
    rate_time,
    skip_gain,
):
    frames = lax.axis_size("frame")
    rows = lax.axis_size("row")
    frame_id = lax.axis_index("frame")
    row_id = lax.axis_index("row")
    width = tokens.shape[-1]
    length = tokens.shape[1] * tokens.shape[2]
    clips = timestep.shape[0]
    clip_id = frame_id // (frames // clips)
    sites = length // frames
    heads = rate_space.shape[0]
    depth, pair = proj_weight.shape
    state = pair // 2
    mod_cols = mod_weight.shape[1]
    factor = (frames * rows * length) ** (-0.5)
    tok = tokens.reshape(length, width)
    grad = cotangent.reshape(length, width)

    activated = time_embed(timestep, mod_weight.shape[0]).astype(bf16)
    own_mod = jnp.dot(activated, mod_weight, preferred_element_type=f32)
    high = lax.reduce_precision(own_mod, 8, 7)
    own_mod = jnp.stack([high, own_mod - high]).astype(bf16)

    part = depth // rows
    own_proj = lax.dynamic_slice_in_dim(proj_weight, row_id * part, part, 0)
    to_all = [
        to_tiles(own_proj[None]),
        to_tiles(step_weight.T[None]),
        own_mod.reshape(1, -1, LANES),
    ]
    to_all = jnp.concatenate(to_all, axis=1)
    to_all = jnp.pad(to_all, ((0, 0), (0, -to_all.shape[1] % 8), (0, 0)))
    count = sites * width // LANES
    got = exchange(
        jnp.concatenate(
            [
                to_tiles(tok.reshape(frames, sites, width)),
                to_tiles(grad.reshape(frames, sites, width)),
                jnp.broadcast_to(to_all, (frames,) + to_all.shape[1:]),
            ],
            axis=1,
        )
    )
    site_tok = from_tiles(got[:, :count], sites, width).reshape(length, width)
    site_grad = from_tiles(got[:, count : 2 * count], sites, width).reshape(length, width)
    at = 2 * count
    size = part * pair // LANES
    proj_full = rows_in_order(got[:, at : at + size])
    proj_full = from_tiles(proj_full.reshape(rows * frames, size, LANES), part, pair)
    proj_full = proj_full.reshape(rows, frames, part, pair).transpose(1, 0, 2, 3)
    proj_full = proj_full.reshape(width, pair)
    at += size
    size = heads * depth // LANES
    step_full = from_tiles(got[:, at : at + size], heads, depth)
    step_full = step_full.transpose(1, 0, 2).reshape(heads, width)
    at += size
    size = 2 * clips * mod_cols // LANES
    mod_full = got[:, at : at + size].reshape(frames, 2, clips, mod_cols).astype(f32)
    mod_full = (mod_full[:, 0] + mod_full[:, 1]).transpose(1, 0, 2).reshape(clips, 2 * width)
    shift, gain = mod_full[:, :width], mod_full[:, width:]

    bias = step_bias[None]
    wide = (length, width)
    site_out, site_back, gproj, gstep, site_gmod = call(
        functools.partial(site_kernel, sites),
        [(wide, bf16), (wide, bf16), ((width, pair), f32), ((heads, width), f32), ((2 * clips, width), f32)],
        [(wide, bf16)] * 2 + [((2 * length, width), bf16)],
        name="site",
    )(site_tok, site_grad, shift, gain, proj_full, step_full, bias, rate_time[None])

    came = exchange(
        jnp.concatenate(
            [
                to_tiles(site_out.reshape(frames, sites, width)),
                to_tiles(site_back.reshape(frames, sites, width)),
            ],
            axis=1,
        )
    )
    time_out = from_tiles(came[:, :count], sites, width).reshape(length, width)
    time_back = from_tiles(came[:, count:], sites, width).reshape(length, width)

    own_shift = lax.dynamic_slice_in_dim(shift, clip_id, 1, 0)
    own_gain = lax.dynamic_slice_in_dim(gain, clip_id, 1, 0)
    normed, coeffs, logits, inverse, decay, end_own, start_grad = call(
        band_kernel,
        [
            (wide, bf16),
            ((length, pair), bf16),
            ((length, heads), bf16),
            ((length, 1), f32),
            ((1, heads), f32),
            ((width, state), bf16),
            ((width, state), bf16),
        ],
        name="band",
    )(tok, grad, own_shift, own_gain, proj_full, step_full, bias, rate_space[None])
    state_in = chain(end_own, decay, True)
    later_grad = chain(start_grad, decay, False)
    mix, pre, gproj, gstep, gmod = call(
        space_kernel,
        [(wide, f32), (wide, f32), ((width, pair), bf16), ((heads, width), bf16), ((2, width), f32)],
        [(wide, bf16), ((3 * length, width), bf16)],
        name="space",
    )(
        tok,
        grad,
        normed,
        coeffs,
        logits,
        inverse,
        proj_full,
        step_full,
        bias,
        rate_space[None],
        skip_gain[None],
        state_in,
        later_grad,
        gproj,
        gstep,
    )

    picked = (jnp.arange(clips) == clip_id).astype(f32)[:, None]
    gmod = jnp.concatenate(
        [site_gmod[:clips] + picked * gmod[0:1], site_gmod[clips:] + picked * gmod[1:2]], axis=1
    )
    gmod = gmod.reshape(clips, frames, mod_cols).transpose(1, 0, 2).astype(bf16)
    sent = jnp.concatenate(
        [
            to_tiles(gproj.reshape(frames, depth, pair)),
            to_tiles(gstep.reshape(heads, frames, depth).transpose(1, 0, 2)),
            gmod.reshape(frames, -1, LANES) if (clips * mod_cols) % LANES == 0 else gmod,
        ],
        axis=1,
    )
    size = sent.shape[1]
    sent = jnp.pad(sent, ((0, 0), (0, -size % 8), (0, 0)))
    sums = jnp.sum(exchange(sent).astype(f32), axis=0, keepdims=True)
    sums = rows_sum(sums) * factor
    at = depth * pair // LANES
    grad_proj = from_tiles(sums[:, :at], depth, pair)[0]
    size = heads * depth // LANES
    grad_step = from_tiles(sums[:, at : at + size], heads, depth)[0].T
    at += size
    size = clips * mod_cols // LANES
    mod_sum = sums[0, at : at + size].reshape(clips, mod_cols)
    grad_mod = jnp.dot(activated.astype(f32).T, mod_sum, precision=EXACT)

    mixed, d_tokens = call(last_kernel, [(wide, bf16), (wide, bf16)], name="last")(
        tok, inverse, own_gain, mix, pre, time_out, time_back
    )
    return (mixed.reshape(tokens.shape), d_tokens.reshape(tokens.shape), grad_proj, grad_step, grad_mod)


def fits(mesh, tokens, timestep, proj_weight, step_weight):
    frames, rows = mesh.shape["frame"], mesh.shape["row"]
    length, width = tokens.shape[2] * tokens.shape[1] // rows, tokens.shape[3]
    return (
        rows == 2
        and frames == 16
        and timestep.shape[0] == 1
        and length == LANES
        and length // frames == 8
        and width // frames == LANES
        and proj_weight.shape[1] == 2 * LANES
        and step_weight.shape[1] % 32 == 0
    )


def spread_over_frames(own, radix=4):
    frames = radix * radix

    def others(piece, stride):
        return [piece] + [
            lax.ppermute(piece, "frame", [(i, i ^ (d * stride)) for i in range(frames)])
            for d in range(1, radix)
        ]

    far = jnp.stack(others(own, radix))
    return jnp.concatenate(others(far, 1))


def sum_over_frames(keep, given, radix, ahead):
    frames = radix * radix

    def total(pieces):
        value = pieces[0].astype(f32)
        for piece in pieces[1:]:
            value = value + piece.astype(f32)
        return value

    def partner(piece, offset):
        return lax.ppermute(piece, "frame", [(i, i ^ offset) for i in range(frames)])

    parts = [slice(d * radix, (d + 1) * radix) for d in range(radix)]
    near = [total([keep[p], given[p]]).astype(bf16) for p in parts]
    near = [near[0]] + [partner(near[d], d) for d in range(1, radix)]
    near, ahead = lax.optimization_barrier((near, ahead))
    near = total(near).astype(bf16)
    far = [near[0]] + [partner(near[d], d * radix) for d in range(1, radix)]
    return total(far), *ahead


def per_device_fast(
    tokens,
    cotangent,
    timestep,
    mod_weight,
    proj_weight,
    step_weight,
    step_bias,
    rate_space,
    rate_time,
    skip_gain,
):
    frames = lax.axis_size("frame")
    rows = lax.axis_size("row")
    ids = jnp.stack([lax.axis_index("frame"), lax.axis_index("row")]).astype(jnp.int32)
    width = tokens.shape[-1]
    length = tokens.shape[1] * tokens.shape[2]
    sites = length // frames
    heads = rate_space.shape[0]
    depth, pair = proj_weight.shape
    state = pair // 2
    mod_cols = mod_weight.shape[1]
    factor = (frames * rows * length) ** (-0.5)
    tok = tokens.reshape(length, width)
    grad = cotangent.reshape(length, width)
    wide = (length, width)
    small = jnp.stack([step_bias, rate_time, rate_space, skip_gain])
    swap = [(0, 1), (1, 0)]

    packed = (frames, 2, sites, width)
    size = depth // 2 * pair // LANES + heads // 2 + 8
    activated = time_embed(timestep, mod_weight.shape[0]).astype(bf16)
    sent, payload = call(
        start_kernel,
        [(packed, bf16), ((size, LANES), bf16)],
        [
            ((depth, pair), bf16),
            ((heads, depth), bf16),
            (mod_weight.shape, bf16),
            (packed, bf16),
            pltpu.SemaphoreType.DMA((15,)),
        ],
        name="start",
        specs="shhhhhv",
        hbm_outs=(0,),
    )(
        ids,
        in_hbm(tok.reshape(frames, sites, width)),
        in_hbm(grad.reshape(frames, sites, width)),
        in_hbm(proj_weight),
        in_hbm(step_weight.T),
        in_hbm(mod_weight),
        activated,
    )
    got = exchange(sent)
    payload = spread_over_frames(payload)
    other = lax.ppermute(payload, "row", swap)
    proj_full, step_full, shift, gain = call(
        functools.partial(unpack_kernel, 4),
        [((width, pair), bf16), ((heads, width), bf16), ((1, width), f32), ((1, width), f32)],
        name="unpack",
        specs="svv",
    )(ids, payload, other)

    sent, site_x, site_gmod, site_dc, site_dl = call(
        functools.partial(site_fast_kernel, sites),
        [
            (packed, bf16),
            (wide, bf16),
            ((2, width), f32),
            ((length, pair), bf16),
            ((length, heads), bf16),
        ],
        [
            (wide, bf16),
            (packed, bf16),
            (wide, bf16),
            ((2, width), f32),
            pltpu.SemaphoreType.DMA((18,)),
        ]
        + [(wide, bf16), ((2 * length, width), bf16)],
        name="site",
        specs="vvvvvv",
        hbm_outs=(0, 1, 2),
    )(got, shift, gain, proj_full, step_full, small)
    sent, proj_full = lax.optimization_barrier((sent, proj_full))
    came = exchange(sent)

    normed, coeffs, logits, inverse, give = call(
        band_fast_kernel,
        [
            (wide, bf16),
            ((length, pair), bf16),
            ((length, heads), bf16),
            ((length, 1), f32),
            ((width, state), bf16),
        ],
        name="band",
        specs="svvvvvvv",
    )(ids, tok, grad, shift, gain, proj_full, step_full, small)
    arrived = lax.ppermute(give, "row", swap)

    halves = (frames, size, LANES)
    mix, pre, own_dc, own_dl, gmod = call(
        space_fast_kernel,
        [(wide, f32), (wide, f32), ((length, pair), bf16), ((length, heads), bf16), ((2, width), f32)],
        [(wide, bf16), ((3 * length, width), bf16)],
        name="space",
        specs="s" + "v" * 10,
    )(
        ids,
        arrived,
        tok,
        grad,
        normed,
        coeffs,
        logits,
        inverse,
        proj_full,
        step_full,
        small,
    )
    keep, give = call(
        functools.partial(terms_kernel, 4),
        [(halves, bf16), (halves, bf16)],
        name="terms",
        specs="svvvvvvvv",
    )(ids, normed, own_dc, own_dl, gmod, site_x, site_dc, site_dl, site_gmod)
    given = lax.ppermute(give, "row", swap)
    mixed, d_tokens = call(last_fast_kernel, [(wide, bf16), (wide, bf16)], name="last")(
        tok, inverse, gain, mix, pre, came
    )
    terms, mixed, d_tokens = sum_over_frames(keep, given, 4, (mixed, d_tokens))
    other = lax.ppermute(terms, "row", swap)
    (grad_mod,) = call(
        functools.partial(finish_mod_kernel, factor, size - 8),
        [((mod_weight.shape[0], mod_cols), f32)],
        name="finish_mod",
        specs="vv",
    )(terms, activated)
    other, grad_mod = lax.optimization_barrier((other, grad_mod))
    grad_proj, grad_step = call(
        functools.partial(finish_kernel, factor),
        [((depth, pair), f32), ((heads, depth), f32)],
        name="finish",
        specs="svv",
    )(ids, terms, other)
    return (mixed.reshape(tokens.shape), d_tokens.reshape(tokens.shape), grad_proj, grad_step.T, grad_mod)


def solution(mesh):
    placed = (
        P("frame", "row", None, None),
        P("frame", "row", None, None),
        P(),
        P(None, "frame"),
        P("frame", None),
        P("frame", None),
        P(),
        P(),
        P(),
        P(),
    )
    outs = (
        P("frame", "row", None, None),
        P("frame", "row", None, None),
        P("frame", None),
        P("frame", None),
        P(None, "frame"),
    )

    def step(tokens, cotangent, timestep, mod_weight, proj_weight, step_weight, *rest):
        fast = fits(mesh, tokens, timestep, proj_weight, step_weight)
        body = per_device_fast if fast else per_device
        return jax.shard_map(
            body, mesh=mesh, in_specs=placed, out_specs=outs, check_vma=False
        )(tokens, cotangent, timestep, mod_weight, proj_weight, step_weight, *rest)

    return step
```

```python
import functools
import math

import jax
import jax.numpy as jnp
from jax import lax
from jax.experimental import pallas as pl
from jax.experimental.pallas import tpu as pltpu
from jax.sharding import PartitionSpec as P


norm_eps = 1e-05
LANES = 128
LOG2E = math.log2(math.e)
f32 = jnp.float32
bf16 = jnp.bfloat16
EXACT = lax.Precision.HIGHEST


def time_embed(timestep, embed_dim):
    half_dim = embed_dim // 2
    place = (jnp.arange(embed_dim) % half_dim).astype(f32)
    frequency = jnp.exp(-math.log(10000.0) * place / half_dim)
    angles = timestep.astype(f32)[:, None] * frequency[None, :]
    lower = jnp.arange(embed_dim)[None, :] < half_dim
    return jax.nn.silu(jnp.where(lower, jnp.cos(angles), jnp.sin(angles)))


def to_tiles(a):
    f, r, c = a.shape
    if r % 8 == 0 and c % LANES == 0:
        a = a.reshape(f, r // 8, 8, c // LANES, LANES).transpose(0, 1, 3, 2, 4)
    return a.reshape(f, r * c // LANES, LANES)


def from_tiles(a, r, c):
    f = a.shape[0]
    if r % 8 == 0 and c % LANES == 0:
        a = a.reshape(f, r // 8, c // LANES, 8, LANES).transpose(0, 1, 3, 2, 4)
    return a.reshape(f, r, c)


def exchange(packed):
    return lax.all_to_all(packed, "frame", split_axis=0, concat_axis=0, tiled=True)


def mm(a, b, ca, cb):
    return lax.dot_general(a, b, (((ca,), (cb,)), ((), ())), preferred_element_type=f32)


def exact(a, b, ca, cb):
    return lax.dot_general(
        a, b, (((ca,), (cb,)), ((), ())), preferred_element_type=f32, precision=EXACT
    )


def split(a):
    high = a.astype(bf16)
    return high, (a - high.astype(f32)).astype(bf16)


def head_map(heads, width):
    size = width // heads
    own = lax.broadcasted_iota(jnp.int32, (heads, width), 0)
    lane = lax.broadcasted_iota(jnp.int32, (heads, width), 1)
    return jnp.where(lane // size == own, 1.0, 0.0).astype(bf16)


def sequence_mask(length, sites):
    later = lax.broadcasted_iota(jnp.int32, (length, length), 0)
    earlier = lax.broadcasted_iota(jnp.int32, (length, length), 1)
    keep = later >= earlier
    if sites > 1:
        keep = keep & (later % sites == earlier % sites)
    return jnp.where(keep, 1.0, 0.0).astype(f32)


def blocks(width):
    return [(j, slice(j * LANES, (j + 1) * LANES)) for j in range(width // LANES)]


def spread_rows(rows, length):
    count = rows.shape[0]
    if count == 1:
        return rows
    part = (length // count, rows.shape[1])
    return jnp.concatenate([jnp.broadcast_to(rows[c : c + 1], part) for c in range(count)], axis=0)


def normalize_into(tok_ref, shift_ref, gain_ref, x_ref, read=None):
    length, width = tok_ref.shape
    total = jnp.zeros((length, LANES), f32)
    for _, sl in blocks(width):
        if read is None:
            v = tok_ref[:, sl].astype(f32)
        else:
            v = read(sl)
            tok_ref[:, sl] = v.astype(bf16)
        total = total + v * v
    mean = jnp.sum(total, axis=1, keepdims=True) / width
    inverse = lax.rsqrt(mean + norm_eps)
    for _, sl in blocks(width):
        unit = tok_ref[:, sl].astype(f32) * inverse
        gain = spread_rows(gain_ref[:, sl], length)
        shift = spread_rows(shift_ref[:, sl], length)
        x_ref[:, sl] = (unit * (1.0 + gain) + shift).astype(bf16)
    return inverse


def steps_of(logits, bias, rate, mask):
    z = logits.astype(f32) + bias
    step = jnp.maximum(z, 0.0) + jnp.log1p(jnp.exp(-jnp.abs(z)))
    log_decay = -step * rate
    cum = exact(mask, log_decay, 1, 0)
    return z, step, cum, (cum * LOG2E, exact(log_decay * LOG2E, mask, 0, 1))


def halves_of(a):
    return jnp.concatenate(split(a), axis=1)


def doubled(lanes_of):
    return jnp.concatenate([lanes_of, lanes_of], axis=0)


def scan_block(j, x, grad, step_wide, scores, cums, heads, width, d_scores):
    size = width // heads
    per_block = LANES // size
    length = x.shape[0]
    stepped = (x.astype(f32) * step_wide).astype(bf16)
    lane = lax.broadcasted_iota(jnp.int32, x.shape, 1)
    inside = [lane // size == i for i in range(per_block)]
    zero = jnp.zeros_like(x)
    steppeds = jnp.concatenate([jnp.where(own, stepped, zero) for own in inside], axis=0)
    grads = jnp.concatenate([jnp.where(own, grad, zero) for own in inside], axis=0)
    d_weights = mm(grads, stepped, 1, 1)
    weights = []
    for i in range(per_block):
        h = j * per_block + i
        decay = jnp.exp2(jnp.minimum(cums[0][:, h : h + 1] - cums[1][h : h + 1, :], 0.0))
        d_scores = d_scores + d_weights[i * length : (i + 1) * length] * decay
        weights.append((scores * decay).astype(bf16))
    out = mm(jnp.concatenate(weights, axis=1), steppeds, 1, 0)
    d_stepped = mm(jnp.concatenate(weights, axis=0), grads, 0, 0)
    return stepped, out, d_stepped, d_scores


def put(sums_ref, which, sl, value):
    length = value.shape[0]
    sums_ref[which * length : (which + 1) * length, sl] = value.astype(bf16)


def head_sums(sums_ref, lanes_of, length):
    sums = mm(sums_ref[...], lanes_of, 1, 1)
    return [sums[at : at + length] for at in range(0, sums.shape[0], length)]


def wide_blocks(width):
    return [(slice(at, at + 2 * LANES)) for at in range(0, width, 2 * LANES)]


def start_kernel(ids_ref, tok_ref, grad_ref, proj_hbm, step_hbm, mod_hbm, active_ref, sent_ref, pay_ref,
                 proj_ref, step_ref, mod_ref, both_ref, sems):
    parts = 4
    share = tok_ref.shape[0] // parts
    pairs = [(proj_hbm, proj_ref), (step_hbm, step_ref), (mod_hbm, mod_ref)]
    for p in range(parts):
        at = slice(p * share, (p + 1) * share)
        pairs += [(tok_ref.at[at], both_ref.at[at, 0]), (grad_ref.at[at], both_ref.at[at, 1])]
    for p in range(parts):
        at = slice(p * share, (p + 1) * share)
        pairs.append((both_ref.at[at], sent_ref.at[at]))
    copies = [
        pltpu.make_async_copy(src, dst, sems.at[n]) for n, (src, dst) in enumerate(pairs)
    ]
    inward, outward = copies[: 3 + 2 * parts], copies[3 + 2 * parts :]
    for copy in inward:
        copy.start()
    for p, copy in enumerate(outward):
        inward[3 + 2 * p].wait()
        inward[4 + 2 * p].wait()
        copy.start()
    row = ids_ref[1]
    part, pair = proj_ref.shape[0] // 2, proj_ref.shape[1]
    copies[0].wait()
    own = proj_ref[pl.ds(pl.multiple_of(row * part, part), part), :]
    at = 0
    for _, sl in blocks(pair):
        pay_ref[at : at + part, :] = own[:, sl]
        at += part
    copies[1].wait()
    part = step_ref.shape[0] // 2
    pay_ref[at : at + part, :] = step_ref[pl.ds(pl.multiple_of(row * part, part), part), :]
    at += part
    copies[2].wait()
    own = mm(active_ref[...], mod_ref[...], 1, 0)
    high = own.astype(bf16).astype(f32)
    pieces = [piece[:, sl] for piece in (high, own - high) for _, sl in blocks(own.shape[1])]
    pieces.append(jnp.zeros((8 - len(pieces), LANES), f32))
    pay_ref[at : at + 8, :] = jnp.concatenate(pieces, axis=0).astype(bf16)
    for copy in outward:
        copy.wait()


def unpack_kernel(radix, ids_ref, *refs):
    own_refs, other_refs = refs[:radix], refs[radix : 2 * radix]
    proj_ref, step_ref, shift_ref, gain_ref = refs[2 * radix :]
    me, row = ids_ref[0], ids_ref[1]
    width, pair = proj_ref.shape
    frames = radix * radix
    depth = width // frames
    part, heads = depth // 2, step_ref.shape[0] // 2
    cols = 2 * width // frames
    for i in range(frames):
        source = jnp.bitwise_xor(me, (i % radix) * radix + i // radix)
        near, far = i // radix, i % radix
        for ref, half in ((own_refs[near], row), (other_refs[near], 1 - row)):
            rows = pl.ds(pl.multiple_of(source * depth + half * part, part), part)
            at = 0
            for _, sl in blocks(pair):
                proj_ref[rows, sl] = ref[far, at : at + part, :]
                at += part
            rows = pl.ds(pl.multiple_of(half * heads, heads), heads)
            lanes = pl.ds(pl.multiple_of(source * depth, depth), depth)
            step_ref[rows, lanes] = ref[far, at : at + heads, :]
            at += heads
        own = own_refs[near][far, at : at + 8, :].astype(f32)
        count = cols // LANES
        lanes_at = jnp.bitwise_and(source, frames // 2 - 1) * cols
        for k in range(count):
            value = own[k : k + 1, :] + own[count + k : count + k + 1, :]
            lanes = pl.ds(pl.multiple_of(lanes_at + k * LANES, LANES), LANES)

            @pl.when(source < frames // 2)
            def _():
                shift_ref[:, lanes] = value

            @pl.when(source >= frames // 2)
            def _():
                gain_ref[:, lanes] = value


def finish_mod_kernel(factor, at, sums_ref, active_ref, mod_ref):
    rest = jnp.zeros((7, active_ref.shape[1]), f32)
    active = jnp.concatenate([active_ref[...].astype(f32), rest], axis=0)
    for k, sl in blocks(mod_ref.shape[1]):
        own = jnp.broadcast_to(sums_ref[at + k : at + k + 1, :] * factor, (8, LANES))
        mod_ref[:, sl] = exact(active, own, 0, 0)


def finish_kernel(factor, ids_ref, own_ref, other_ref, proj_ref, step_ref):
    row = ids_ref[1]
    pair = proj_ref.shape[1]
    part, heads = proj_ref.shape[0] // 2, step_ref.shape[0] // 2
    for ref, half in ((own_ref, row), (other_ref, 1 - row)):
        rows = pl.ds(pl.multiple_of(half * part, part), part)
        at = 0
        for _, sl in blocks(pair):
            proj_ref[rows, sl] = ref[at : at + part, :] * factor
            at += part
        step_ref[pl.ds(pl.multiple_of(half * heads, heads), heads), :] = ref[at : at + heads, :] * factor


def site_fast_kernel(sites, got_ref, *refs):
    inputs, (small_ref, sent_hbm, x_hbm, gmod_hbm, dc_ref, dl_ref) = refs[:4], refs[4:10]
    inputs = (*inputs, small_ref[0:1, :], small_ref[1:2, :])
    tok_ref, sent_ref, x_ref, gmod_ref, sems = refs[10:15]
    scratch = refs[15:]
    frames, width = got_ref.shape[0], got_ref.shape[3]

    def read(which):
        return lambda sl: got_ref[:, which, :, sl].astype(f32).reshape(frames * sites, LANES)

    class Grad:
        def __getitem__(self, at):
            return read(1)(at[1]).astype(bf16)

    parts = 8
    share = width // parts
    copies = []

    def begin(source, target):
        copy = pltpu.make_async_copy(source, target, sems.at[len(copies)])
        copy.start()
        copies.append(copy)

    def send(which, p):
        at = (slice(None), which, slice(None), slice(p * share, (p + 1) * share))
        begin(sent_ref.at[at], sent_hbm.at[at])

    class Packed:
        def __init__(self, which):
            self.which = which

        def __setitem__(self, at, value):
            if not copies:
                begin(x_ref, x_hbm)
            value = value.astype(f32).reshape(frames, sites, value.shape[1])
            sent_ref[:, self.which, :, at[1]] = value.astype(bf16)
            if at[1].stop % share == 0:
                send(self.which, at[1].stop // share - 1)

    site_kernel(
        sites,
        tok_ref,
        Grad(),
        *inputs,
        Packed(0),
        Packed(1),
        dc_ref,
        dl_ref,
        gmod_ref,
        x_ref,
        *scratch,
        read=read(0),
    )
    begin(gmod_ref, gmod_hbm)
    for copy in copies:
        copy.wait()


def site_kernel(
    sites,
    tok_ref,
    grad_ref,
    shift_ref,
    gain_ref,
    proj_ref,
    step_ref,
    bias_ref,
    rate_ref,
    out_ref,
    back_ref,
    gproj_ref,
    gstep_ref,
    gmod_ref,
    x_ref,
    dn_ref,
    sums_ref,
    read=None,
):
    length, width = tok_ref.shape
    heads = step_ref.shape[0]
    state = proj_ref.shape[1] // 2
    clips = shift_ref.shape[0]
    inverse = normalize_into(tok_ref, shift_ref, gain_ref, x_ref, read)
    lanes_of = head_map(heads, width)
    mask = sequence_mask(length, sites)
    coeffs = mm(x_ref[...], proj_ref[...], 1, 0).astype(bf16)
    logits = mm(x_ref[...], step_ref[...], 1, 1).astype(bf16)
    rate = rate_ref[...]
    z, step, _, cums = steps_of(logits, bias_ref[...], rate, mask)
    b_part, c_part = coeffs[:, :state], coeffs[:, state:]
    scores = mm(c_part, b_part, 1, 1) * (mask / state)
    step_parts, twice = halves_of(step), doubled(lanes_of)
    d_scores = jnp.zeros((length, length), f32)
    for j, sl in blocks(width):
        x, grad = x_ref[:, sl], grad_ref[:, sl]
        step_wide = mm(step_parts, twice[:, sl], 1, 0)
        stepped, out, d_stepped, d_scores = scan_block(
            j, x, grad, step_wide, scores, cums, heads, width, d_scores
        )
        out_ref[:, sl] = out.astype(bf16)
        dn_ref[:, sl] = (step_wide * d_stepped).astype(bf16)
        put(sums_ref, 0, sl, grad.astype(f32) * out - stepped.astype(f32) * d_stepped)
        put(sums_ref, 1, sl, x.astype(f32) * d_stepped)
    d_cum, d_step = head_sums(sums_ref, lanes_of, length)
    d_log = exact(mask, d_cum, 0, 0)
    d_logits = (jax.nn.sigmoid(z) * (d_step - rate * d_log)).astype(bf16)
    d_scores = (d_scores * (mask / state)).astype(bf16)
    d_coeffs = jnp.concatenate(
        [mm(d_scores, c_part, 0, 0), mm(d_scores, b_part, 1, 0)], axis=1
    ).astype(bf16)
    for sl in wide_blocks(width):
        back = (
            dn_ref[:, sl].astype(f32)
            + mm(d_coeffs, proj_ref[sl, :], 1, 1)
            + mm(d_logits, step_ref[:, sl], 1, 0)
        )
        back_ref[:, sl] = back.astype(bf16)
        scaled = back * (tok_ref[:, sl].astype(f32) * inverse)
        for c in range(clips):
            rows = slice(c * (length // clips), (c + 1) * (length // clips))
            gmod_ref[c : c + 1, sl] = jnp.sum(back[rows], axis=0, keepdims=True)
            gmod_ref[clips + c : clips + c + 1, sl] = jnp.sum(scaled[rows], axis=0, keepdims=True)
        if gproj_ref.shape == (width, 2 * state):
            gproj_ref[sl, :] = mm(x_ref[:, sl], d_coeffs, 0, 0)
            gstep_ref[:, sl] = mm(d_logits, x_ref[:, sl], 0, 0)
    if gproj_ref.shape != (width, 2 * state):
        gproj_ref[...] = d_coeffs
        gstep_ref[...] = d_logits


def band_fast_kernel(ids_ref, *refs):
    small_ref, give_ref = refs[6], refs[-1]
    inputs = (*refs[:6], small_ref[0:1, :], small_ref[2:3, :])
    band_kernel(*inputs, *refs[7:-1], None, None, give_ref, first=ids_ref[1] == 0)


def band_kernel(
    tok_ref,
    grad_ref,
    shift_ref,
    gain_ref,
    proj_ref,
    step_ref,
    bias_ref,
    rate_ref,
    x_ref,
    coeffs_ref,
    logits_ref,
    inverse_ref,
    decay_ref,
    end_ref,
    own_ref,
    first=None,
):
    length, width = tok_ref.shape
    heads = step_ref.shape[0]
    state = proj_ref.shape[1] // 2
    inverse_ref[...] = normalize_into(tok_ref, shift_ref, gain_ref, x_ref)
    twice = doubled(head_map(heads, width))
    mask = sequence_mask(length, 1)
    coeffs = mm(x_ref[...], proj_ref[...], 1, 0).astype(bf16)
    logits = mm(x_ref[...], step_ref[...], 1, 1).astype(bf16)
    coeffs_ref[...] = coeffs
    logits_ref[...] = logits
    _, step, cum, _ = steps_of(logits, bias_ref[...], rate_ref[...], mask)
    last = cum[length - 1 : length, :]
    b_part, c_part = coeffs[:, :state], coeffs[:, state:]
    if first is not None:
        gain = halves_of(jnp.where(first, jnp.exp(last - cum) * step, jnp.exp(cum) / state))
        other = jnp.where(first, b_part, c_part)
        for _, sl in blocks(width):
            value = jnp.where(first, x_ref[:, sl], grad_ref[:, sl]).astype(f32)
            value = (value * mm(gain, twice[:, sl], 1, 0)).astype(bf16)
            own_ref[sl, :] = mm(value, other, 0, 0).astype(bf16)
        return
    decay_ref[...] = jnp.exp(last)
    lead = halves_of(jnp.exp(last - cum) * step)
    reach = halves_of(jnp.exp(cum) / state)
    for _, sl in blocks(width):
        lead_wide = mm(lead, twice[:, sl], 1, 0)
        reach_wide = mm(reach, twice[:, sl], 1, 0)
        scaled = (x_ref[:, sl].astype(f32) * lead_wide).astype(bf16)
        faded = (grad_ref[:, sl].astype(f32) * reach_wide).astype(bf16)
        end_ref[sl, :] = mm(scaled, b_part, 0, 0).astype(bf16)
        own_ref[sl, :] = mm(faded, c_part, 0, 0).astype(bf16)


def terms_kernel(radix, ids_ref, x_ref, dc_ref, dl_ref, gmod_ref, site_x, site_dc, site_dl, site_gmod, *refs):
    me, first = ids_ref[0], ids_ref[1] == 0
    width = x_ref.shape[1]
    coeffs = jnp.concatenate([dc_ref[...], site_dc[...]], axis=0)
    logits = jnp.concatenate([dl_ref[...], site_dl[...]], axis=0)
    share = 2 * width // LANES // (radix * radix)
    half = radix * radix // 2

    def put_halves(keep_ref, give_ref, e, at, value):
        part = value.shape[0] // 2
        own = jnp.where(first, value[:part], value[part:]).astype(bf16)
        other = jnp.where(first, value[part:], value[:part]).astype(bf16)
        for _, sl in blocks(value.shape[1]):
            keep_ref[e, at : at + part, :] = own[:, sl]
            give_ref[e, at : at + part, :] = other[:, sl]
            at += part
        return at

    for d in (*range(1, radix), 0):
        keep_ref, give_ref = refs[d], refs[radix + d]
        for e in range(radix):
            frame = jnp.bitwise_xor(me, e * radix + d)
            sl = pl.ds(pl.multiple_of(frame * LANES, LANES), LANES)
            tall = jnp.concatenate([x_ref[:, sl], site_x[:, sl]], axis=0)
            at = put_halves(keep_ref, give_ref, e, 0, mm(tall, coeffs, 0, 0))
            at = put_halves(keep_ref, give_ref, e, at, mm(logits, tall, 0, 0))
            start = jnp.bitwise_and(frame, half - 1) * share * LANES
            rows = []
            for k in range(share):
                lanes = pl.ds(pl.multiple_of(start + k * LANES, LANES), LANES)
                both = gmod_ref[:, lanes] + site_gmod[:, lanes]
                rows.append(jnp.where(frame < half, both[0:1], both[1:2]))
            rows.append(jnp.zeros((8 - len(rows), LANES), f32))
            rows = jnp.concatenate(rows, axis=0).astype(bf16)
            keep_ref[e, at : at + 8, :] = rows
            give_ref[e, at : at + 8, :] = rows


def space_fast_kernel(ids_ref, arrived_ref, *refs):
    inputs, small_ref, outs = refs[:8], refs[8], refs[9:]
    inputs = (*inputs, *(small_ref[n : n + 1, :] for n in (0, 2, 3)))
    space_kernel(*inputs, arrived_ref, None, None, None, *outs, first=ids_ref[1] == 0)


def space_kernel(
    tok_ref,
    grad_ref,
    x_ref,
    coeffs_ref,
    logits_ref,
    inverse_ref,
    proj_ref,
    step_ref,
    bias_ref,
    rate_ref,
    skip_ref,
    state_ref,
    later_ref,
    gproj_in,
    gstep_in,
    mix_ref,
    pre_ref,
    gproj_ref,
    gstep_ref,
    gmod_ref,
    dn_ref,
    sums_ref,
    first=None,
):
    length, width = tok_ref.shape
    heads = step_ref.shape[0]
    state = proj_ref.shape[1] // 2
    lanes_of = head_map(heads, width)
    twice = doubled(lanes_of)
    mask = sequence_mask(length, 1)
    coeffs = coeffs_ref[...]
    rate = rate_ref[...]
    z, step, cum, cums = steps_of(logits_ref[...], bias_ref[...], rate, mask)
    last = cum[length - 1 : length, :]
    rest = jnp.exp(last - cum)
    lead, reach = rest * step, jnp.exp(cum) / state
    b_part, c_part = coeffs[:, :state], coeffs[:, state:]
    scores = mm(c_part, b_part, 1, 1) * (mask / state)
    skip = jnp.broadcast_to(skip_ref[...], (8, heads))
    if first is None:
        parts = [step, lead, reach, skip]
    else:
        parts = [step, jnp.where(first, lead, reach), skip]
        chosen = jnp.where(first, b_part, c_part)
        is_first = jnp.where(first, 1.0, 0.0).astype(f32)
        is_second = 1.0 - is_first
    parts = jnp.concatenate([halves_of(part) for part in parts], axis=0)
    d_scores = jnp.zeros((length, length), f32)
    d_b = jnp.zeros((length, state), f32)
    d_c = jnp.zeros((length, state), f32)
    d_end = jnp.zeros((heads, state), f32)
    for j, sl in blocks(width):
        x, grad = x_ref[:, sl], grad_ref[:, sl]
        wide_parts = mm(parts, twice[:, sl], 1, 0)
        step_wide, lead_wide = wide_parts[:length], wide_parts[length : 2 * length]
        skip = wide_parts[-8:-7]
        stepped, out, d_stepped, d_scores = scan_block(
            j, x, grad, step_wide, scores, cums, heads, width, d_scores
        )
        if first is None:
            x, wide = x.astype(f32), grad.astype(f32)
            reach_wide = wide_parts[2 * length : 3 * length]
            before, later = state_ref[sl, :], later_ref[sl, :]
            total = out + mm(c_part, before, 1, 1) * reach_wide
            d_c = d_c + mm((wide * reach_wide).astype(bf16), before, 1, 0)
            d_b = d_b + mm((x * lead_wide).astype(bf16), later, 1, 0)
            d_scaled = mm(b_part, later, 1, 1)
            d_x = step_wide * d_stepped + d_scaled * lead_wide
            both = split(before.astype(f32) * later.astype(f32))
            d_end = d_end + mm(lanes_of[:, sl], both[0], 1, 0) + mm(lanes_of[:, sl], both[1], 1, 0)
        else:
            arrived = state_ref[sl, :]
            value = jnp.where(first, x, grad).astype(f32)
            d_b = d_b + mm((value * lead_wide).astype(bf16), arrived, 1, 0)
            x, wide = x.astype(f32), grad.astype(f32)
            d_scaled = mm(chosen, arrived, 1, 1)
            carried = d_scaled * lead_wide
            total = out + carried * is_second
            d_x = step_wide * d_stepped + carried * is_first
            d_scaled = d_scaled * is_first
        mix_ref[:, sl] = total + skip * x
        dn_ref[:, sl] = d_x.astype(bf16) + (wide * skip).astype(bf16)
        put(sums_ref, 0, sl, wide * total - stepped.astype(f32) * d_stepped)
        put(sums_ref, 1, sl, x * d_stepped)
        put(sums_ref, 2, sl, x * d_scaled)
    d_cum, d_step, d_lead = head_sums(sums_ref, lanes_of, length)
    d_step = d_step + d_lead * rest
    fall = d_lead * lead
    d_cum = d_cum - fall
    end_sum = jnp.sum(fall, axis=0, keepdims=True)
    if first is None:
        ones = jnp.ones((8, state), f32)
        end_sum = end_sum + exact(ones, d_end, 1, 1)[0:1, :] * jnp.exp(last)
    else:
        d_b, d_c = d_b * is_first, d_b * is_second
    d_log = exact(mask, d_cum, 0, 0) + end_sum
    d_logits = (jax.nn.sigmoid(z) * (d_step - rate * d_log)).astype(bf16)
    d_scores = (d_scores * (mask / state)).astype(bf16)
    d_coeffs = jnp.concatenate(
        [mm(d_scores, c_part, 0, 0) + d_b, mm(d_scores, b_part, 1, 0) + d_c], axis=1
    ).astype(bf16)
    inverse = inverse_ref[...]
    if gproj_in is None:
        gproj_ref[...] = d_coeffs
        gstep_ref[...] = d_logits
    for sl in wide_blocks(width):
        pre = (
            dn_ref[:, sl].astype(f32)
            + mm(d_coeffs, proj_ref[sl, :], 1, 1)
            + mm(d_logits, step_ref[:, sl], 1, 0)
        )
        pre_ref[:, sl] = pre
        scaled = pre * (tok_ref[:, sl].astype(f32) * inverse)
        gmod_ref[0:1, sl] = jnp.sum(pre, axis=0, keepdims=True)
        gmod_ref[1:2, sl] = jnp.sum(scaled, axis=0, keepdims=True)
        if gproj_in is not None:
            gproj_ref[sl, :] = (gproj_in[sl, :] + mm(x_ref[:, sl], d_coeffs, 0, 0)).astype(bf16)
            gstep_ref[:, sl] = (gstep_in[:, sl] + mm(d_logits, x_ref[:, sl], 0, 0)).astype(bf16)


def last_kernel(tok_ref, inverse_ref, gain_ref, mix_ref, pre_ref, time_ref, back_ref, out_ref, dtok_ref):
    length, width = tok_ref.shape
    inverse = inverse_ref[...]
    total = jnp.zeros((length, LANES), f32)
    for _, sl in blocks(width):
        out_ref[:, sl] = (mix_ref[:, sl] + time_ref[:, sl].astype(f32)).astype(bf16)
        grad = (pre_ref[:, sl] + back_ref[:, sl].astype(f32)) * (1.0 + gain_ref[:, sl])
        total = total + grad * tok_ref[:, sl].astype(f32)
    inner = jnp.sum(total, axis=1, keepdims=True) / width
    inner = inner * inverse * inverse * inverse
    for _, sl in blocks(width):
        grad = (pre_ref[:, sl] + back_ref[:, sl].astype(f32)) * (1.0 + gain_ref[:, sl])
        dtok_ref[:, sl] = (grad * inverse - tok_ref[:, sl].astype(f32) * inner).astype(bf16)


def last_fast_kernel(tok_ref, inverse_ref, gain_ref, mix_ref, pre_ref, came_ref, *outs):
    class Packed:
        def __init__(self, which):
            self.which = which

        def __getitem__(self, at):
            value = came_ref[:, self.which, :, at[1]].astype(f32)
            return value.reshape(value.shape[0] * value.shape[1], LANES)

    last_kernel(tok_ref, inverse_ref, gain_ref, mix_ref, pre_ref, Packed(0), Packed(1), *outs)


def in_hbm(array):
    return pltpu.with_memory_space_constraint(array, pltpu.MemorySpace.HBM)


def call(kernel, outs, scratch=(), specs=None, hbm_outs=()):
    shapes = [
        pltpu.MemorySpace.HBM(s, d) if n in hbm_outs else jax.ShapeDtypeStruct(s, d)
        for n, (s, d) in enumerate(outs)
    ]
    where = {"s": pltpu.SMEM, "v": pltpu.VMEM, "h": pltpu.MemorySpace.HBM}
    spaces = {}
    if specs:
        spaces["in_specs"] = [pl.BlockSpec(memory_space=where[c]) for c in specs]
        spaces["out_specs"] = [
            pl.BlockSpec(memory_space=where["h" if n in hbm_outs else "v"]) for n in range(len(outs))
        ]
    return pl.pallas_call(
        kernel,
        out_shape=shapes,
        **spaces,
        scratch_shapes=[pltpu.VMEM(*s) if isinstance(s, tuple) else s for s in scratch],
        compiler_params=pltpu.CompilerParams(vmem_limit_bytes=24 << 20),
    )


def rows_in_order(part):
    if lax.axis_size("row") != 2:
        return lax.all_gather(part, "row")
    other = lax.ppermute(part, "row", [(0, 1), (1, 0)])
    first = lax.axis_index("row") == 0
    return jnp.stack([jnp.where(first, part, other), jnp.where(first, other, part)])


def rows_sum(part):
    if lax.axis_size("row") != 2:
        return lax.psum(part, "row")
    return part + lax.ppermute(part, "row", [(0, 1), (1, 0)])


def chain(own, decay, forward):
    count = lax.axis_size("row")
    hops = [(i, i + 1) if forward else (i + 1, i) for i in range(count - 1)]
    if count == 1:
        return jnp.zeros_like(own)
    arrived = lax.ppermute(own, "row", hops)
    wide = jnp.repeat(decay[0], own.shape[0] // decay.shape[1])[:, None]
    for _ in range(count - 2):
        passed = wide * arrived.astype(f32) + own.astype(f32)
        arrived = lax.ppermute(passed.astype(bf16), "row", hops)
    return arrived


def per_device(
    tokens,
    cotangent,
    timestep,
    mod_weight,
    proj_weight,
    step_weight,
    step_bias,
    rate_space,
    rate_time,
    skip_gain,
):
    frames = lax.axis_size("frame")
    rows = lax.axis_size("row")
    frame_id = lax.axis_index("frame")
    row_id = lax.axis_index("row")
    width = tokens.shape[-1]
    length = tokens.shape[1] * tokens.shape[2]
    clips = timestep.shape[0]
    clip_id = frame_id // (frames // clips)
    sites = length // frames
    heads = rate_space.shape[0]
    depth, pair = proj_weight.shape
    state = pair // 2
    mod_cols = mod_weight.shape[1]
    factor = (frames * rows * length) ** (-0.5)
    tok = tokens.reshape(length, width)
    grad = cotangent.reshape(length, width)

    activated = time_embed(timestep, mod_weight.shape[0]).astype(bf16)
    own_mod = jnp.dot(activated, mod_weight, preferred_element_type=f32)
    high = lax.reduce_precision(own_mod, 8, 7)
    own_mod = jnp.stack([high, own_mod - high]).astype(bf16)

    part = depth // rows
    own_proj = lax.dynamic_slice_in_dim(proj_weight, row_id * part, part, 0)
    to_all = [
        to_tiles(own_proj[None]),
        to_tiles(step_weight.T[None]),
        own_mod.reshape(1, -1, LANES),
    ]
    to_all = jnp.concatenate(to_all, axis=1)
    to_all = jnp.pad(to_all, ((0, 0), (0, -to_all.shape[1] % 8), (0, 0)))
    count = sites * width // LANES
    got = exchange(
        jnp.concatenate(
            [
                to_tiles(tok.reshape(frames, sites, width)),
                to_tiles(grad.reshape(frames, sites, width)),
                jnp.broadcast_to(to_all, (frames,) + to_all.shape[1:]),
            ],
            axis=1,
        )
    )
    site_tok = from_tiles(got[:, :count], sites, width).reshape(length, width)
    site_grad = from_tiles(got[:, count : 2 * count], sites, width).reshape(length, width)
    at = 2 * count
    size = part * pair // LANES
    proj_full = rows_in_order(got[:, at : at + size])
    proj_full = from_tiles(proj_full.reshape(rows * frames, size, LANES), part, pair)
    proj_full = proj_full.reshape(rows, frames, part, pair).transpose(1, 0, 2, 3)
    proj_full = proj_full.reshape(width, pair)
    at += size
    size = heads * depth // LANES
    step_full = from_tiles(got[:, at : at + size], heads, depth)
    step_full = step_full.transpose(1, 0, 2).reshape(heads, width)
    at += size
    size = 2 * clips * mod_cols // LANES
    mod_full = got[:, at : at + size].reshape(frames, 2, clips, mod_cols).astype(f32)
    mod_full = (mod_full[:, 0] + mod_full[:, 1]).transpose(1, 0, 2).reshape(clips, 2 * width)
    shift, gain = mod_full[:, :width], mod_full[:, width:]

    bias = step_bias[None]
    wide = (length, width)
    site_out, site_back, gproj, gstep, site_gmod = call(
        functools.partial(site_kernel, sites),
        [(wide, bf16), (wide, bf16), ((width, pair), f32), ((heads, width), f32), ((2 * clips, width), f32)],
        [(wide, bf16)] * 2 + [((2 * length, width), bf16)],
    )(site_tok, site_grad, shift, gain, proj_full, step_full, bias, rate_time[None])

    came = exchange(
        jnp.concatenate(
            [
                to_tiles(site_out.reshape(frames, sites, width)),
                to_tiles(site_back.reshape(frames, sites, width)),
            ],
            axis=1,
        )
    )
    time_out = from_tiles(came[:, :count], sites, width).reshape(length, width)
    time_back = from_tiles(came[:, count:], sites, width).reshape(length, width)

    own_shift = lax.dynamic_slice_in_dim(shift, clip_id, 1, 0)
    own_gain = lax.dynamic_slice_in_dim(gain, clip_id, 1, 0)
    normed, coeffs, logits, inverse, decay, end_own, start_grad = call(
        band_kernel,
        [
            (wide, bf16),
            ((length, pair), bf16),
            ((length, heads), bf16),
            ((length, 1), f32),
            ((1, heads), f32),
            ((width, state), bf16),
            ((width, state), bf16),
        ],
    )(tok, grad, own_shift, own_gain, proj_full, step_full, bias, rate_space[None])
    state_in = chain(end_own, decay, True)
    later_grad = chain(start_grad, decay, False)
    mix, pre, gproj, gstep, gmod = call(
        space_kernel,
        [(wide, f32), (wide, f32), ((width, pair), bf16), ((heads, width), bf16), ((2, width), f32)],
        [(wide, bf16), ((3 * length, width), bf16)],
    )(
        tok,
        grad,
        normed,
        coeffs,
        logits,
        inverse,
        proj_full,
        step_full,
        bias,
        rate_space[None],
        skip_gain[None],
        state_in,
        later_grad,
        gproj,
        gstep,
    )

    picked = (jnp.arange(clips) == clip_id).astype(f32)[:, None]
    gmod = jnp.concatenate(
        [site_gmod[:clips] + picked * gmod[0:1], site_gmod[clips:] + picked * gmod[1:2]], axis=1
    )
    gmod = gmod.reshape(clips, frames, mod_cols).transpose(1, 0, 2).astype(bf16)
    sent = jnp.concatenate(
        [
            to_tiles(gproj.reshape(frames, depth, pair)),
            to_tiles(gstep.reshape(heads, frames, depth).transpose(1, 0, 2)),
            gmod.reshape(frames, -1, LANES) if (clips * mod_cols) % LANES == 0 else gmod,
        ],
        axis=1,
    )
    size = sent.shape[1]
    sent = jnp.pad(sent, ((0, 0), (0, -size % 8), (0, 0)))
    sums = jnp.sum(exchange(sent).astype(f32), axis=0, keepdims=True)
    sums = rows_sum(sums) * factor
    at = depth * pair // LANES
    grad_proj = from_tiles(sums[:, :at], depth, pair)[0]
    size = heads * depth // LANES
    grad_step = from_tiles(sums[:, at : at + size], heads, depth)[0].T
    at += size
    size = clips * mod_cols // LANES
    mod_sum = sums[0, at : at + size].reshape(clips, mod_cols)
    grad_mod = jnp.dot(activated.astype(f32).T, mod_sum, precision=EXACT)

    mixed, d_tokens = call(last_kernel, [(wide, bf16), (wide, bf16)])(
        tok, inverse, own_gain, mix, pre, time_out, time_back
    )
    return (mixed.reshape(tokens.shape), d_tokens.reshape(tokens.shape), grad_proj, grad_step, grad_mod)


def fits(mesh, tokens, timestep, proj_weight, step_weight):
    frames, rows = mesh.shape["frame"], mesh.shape["row"]
    length, width = tokens.shape[2] * tokens.shape[1] // rows, tokens.shape[3]
    return (
        rows == 2
        and frames == 16
        and timestep.shape[0] == 1
        and length == LANES
        and length // frames == 8
        and width // frames == LANES
        and proj_weight.shape[1] == 2 * LANES
        and step_weight.shape[1] % 32 == 0
    )


def spread_over_frames(own, radix=4):
    frames = radix * radix

    def others(piece, stride):
        return [piece] + [
            lax.ppermute(piece, "frame", [(i, i ^ (d * stride)) for i in range(frames)])
            for d in range(1, radix)
        ]

    far = jnp.stack(others(own, radix))
    return others(far, 1)


def sum_over_frames(keep, given, radix, ahead):
    frames = radix * radix

    def total(pieces):
        value = pieces[0].astype(f32)
        for piece in pieces[1:]:
            value = value + piece.astype(f32)
        return value

    def partner(piece, offset):
        return lax.ppermute(piece, "frame", [(i, i ^ offset) for i in range(frames)])

    near = [total([keep[d], given[d]]).astype(bf16) for d in range(radix)]
    near = [near[0]] + [partner(near[d], d) for d in range(1, radix)]
    near, ahead = lax.optimization_barrier((near, ahead))
    near = total(near).astype(bf16)
    far = [near[0]] + [partner(near[d], d * radix) for d in range(1, radix)]
    return total(far), *ahead


def per_device_fast(
    tokens,
    cotangent,
    timestep,
    mod_weight,
    proj_weight,
    step_weight,
    step_bias,
    rate_space,
    rate_time,
    skip_gain,
):
    frames = lax.axis_size("frame")
    rows = lax.axis_size("row")
    ids = jnp.stack([lax.axis_index("frame"), lax.axis_index("row")]).astype(jnp.int32)
    width = tokens.shape[-1]
    length = tokens.shape[1] * tokens.shape[2]
    sites = length // frames
    heads = rate_space.shape[0]
    depth, pair = proj_weight.shape
    state = pair // 2
    mod_cols = mod_weight.shape[1]
    factor = (frames * rows * length) ** (-0.5)
    tok = tokens.reshape(length, width)
    grad = cotangent.reshape(length, width)
    wide = (length, width)
    small = jnp.stack([step_bias, rate_time, rate_space, skip_gain])
    swap = [(0, 1), (1, 0)]

    packed = (frames, 2, sites, width)
    size = depth // 2 * pair // LANES + heads // 2 + 8
    activated = time_embed(timestep, mod_weight.shape[0]).astype(bf16)
    sent, payload = call(
        start_kernel,
        [(packed, bf16), ((size, LANES), bf16)],
        [
            ((depth, pair), bf16),
            ((heads, depth), bf16),
            (mod_weight.shape, bf16),
            (packed, bf16),
            pltpu.SemaphoreType.DMA((15,)),
        ],
        specs="shhhhhv",
        hbm_outs=(0,),
    )(
        ids,
        in_hbm(tok.reshape(frames, sites, width)),
        in_hbm(grad.reshape(frames, sites, width)),
        in_hbm(proj_weight),
        in_hbm(step_weight.T),
        in_hbm(mod_weight),
        activated,
    )
    got = exchange(sent)
    payload = spread_over_frames(payload)
    other = [lax.ppermute(piece, "row", swap) for piece in payload]
    proj_full, step_full, shift, gain = call(
        functools.partial(unpack_kernel, 4),
        [((width, pair), bf16), ((heads, width), bf16), ((1, width), f32), ((1, width), f32)],
        specs="s" + "v" * 8,
    )(ids, *payload, *other)

    sent, site_x, site_gmod, site_dc, site_dl = call(
        functools.partial(site_fast_kernel, sites),
        [
            (packed, bf16),
            (wide, bf16),
            ((2, width), f32),
            ((length, pair), bf16),
            ((length, heads), bf16),
        ],
        [
            (wide, bf16),
            (packed, bf16),
            (wide, bf16),
            ((2, width), f32),
            pltpu.SemaphoreType.DMA((18,)),
        ]
        + [(wide, bf16), ((2 * length, width), bf16)],
        specs="vvvvvv",
        hbm_outs=(0, 1, 2),
    )(got, shift, gain, proj_full, step_full, small)
    sent, proj_full = lax.optimization_barrier((sent, proj_full))
    came = exchange(sent)

    normed, coeffs, logits, inverse, give = call(
        band_fast_kernel,
        [
            (wide, bf16),
            ((length, pair), bf16),
            ((length, heads), bf16),
            ((length, 1), f32),
            ((width, state), bf16),
        ],
        specs="svvvvvvv",
    )(ids, tok, grad, shift, gain, proj_full, step_full, small)
    arrived = lax.ppermute(give, "row", swap)

    mix, pre, own_dc, own_dl, gmod = call(
        space_fast_kernel,
        [(wide, f32), (wide, f32), ((length, pair), bf16), ((length, heads), bf16), ((2, width), f32)],
        [(wide, bf16), ((3 * length, width), bf16)],
        specs="s" + "v" * 10,
    )(
        ids,
        arrived,
        tok,
        grad,
        normed,
        coeffs,
        logits,
        inverse,
        proj_full,
        step_full,
        small,
    )
    pieces = call(
        functools.partial(terms_kernel, 4), [((4, size, LANES), bf16)] * 8, specs="svvvvvvvv"
    )(ids, normed, own_dc, own_dl, gmod, site_x, site_dc, site_dl, site_gmod)
    keep, given = pieces[:4], [lax.ppermute(piece, "row", swap) for piece in pieces[4:]]
    mixed, d_tokens = call(last_fast_kernel, [(wide, bf16), (wide, bf16)])(
        tok, inverse, gain, mix, pre, came
    )
    terms, mixed, d_tokens = sum_over_frames(keep, given, 4, (mixed, d_tokens))
    other = lax.ppermute(terms, "row", swap)
    (grad_mod,) = call(
        functools.partial(finish_mod_kernel, factor, size - 8),
        [((mod_weight.shape[0], mod_cols), f32)],
        specs="vv",
    )(terms, activated)
    other, grad_mod = lax.optimization_barrier((other, grad_mod))
    grad_proj, grad_step = call(
        functools.partial(finish_kernel, factor),
        [((depth, pair), f32), ((heads, depth), f32)],
        specs="svv",
    )(ids, terms, other)
    return (mixed.reshape(tokens.shape), d_tokens.reshape(tokens.shape), grad_proj, grad_step.T, grad_mod)


def solution(mesh):
    placed = (
        P("frame", "row", None, None),
        P("frame", "row", None, None),
        P(),
        P(None, "frame"),
        P("frame", None),
        P("frame", None),
        P(),
        P(),
        P(),
        P(),
    )
    outs = (
        P("frame", "row", None, None),
        P("frame", "row", None, None),
        P("frame", None),
        P("frame", None),
        P(None, "frame"),
    )

    def step(tokens, cotangent, timestep, mod_weight, proj_weight, step_weight, *rest):
        fast = fits(mesh, tokens, timestep, proj_weight, step_weight)
        body = per_device_fast if fast else per_device
        return jax.shard_map(
            body, mesh=mesh, in_specs=placed, out_specs=outs, check_vma=False
        )(tokens, cotangent, timestep, mod_weight, proj_weight, step_weight, *rest)

    return step
```

```python
import functools
import math

import jax
import jax.numpy as jnp
from jax import lax
from jax.experimental import pallas as pl
from jax.experimental.pallas import tpu as pltpu
from jax.sharding import PartitionSpec as P


norm_eps = 1e-05
LANES = 128
LOG2E = math.log2(math.e)
f32 = jnp.float32
bf16 = jnp.bfloat16
EXACT = lax.Precision.HIGHEST


def time_embed(timestep, embed_dim):
    half_dim = embed_dim // 2
    place = (jnp.arange(embed_dim) % half_dim).astype(f32)
    frequency = jnp.exp(-math.log(10000.0) * place / half_dim)
    angles = timestep.astype(f32)[:, None] * frequency[None, :]
    lower = jnp.arange(embed_dim)[None, :] < half_dim
    return jax.nn.silu(jnp.where(lower, jnp.cos(angles), jnp.sin(angles)))


def to_tiles(a):
    f, r, c = a.shape
    if r % 8 == 0 and c % LANES == 0:
        a = a.reshape(f, r // 8, 8, c // LANES, LANES).transpose(0, 1, 3, 2, 4)
    return a.reshape(f, r * c // LANES, LANES)


def from_tiles(a, r, c):
    f = a.shape[0]
    if r % 8 == 0 and c % LANES == 0:
        a = a.reshape(f, r // 8, c // LANES, 8, LANES).transpose(0, 1, 3, 2, 4)
    return a.reshape(f, r, c)


def exchange(packed):
    return lax.all_to_all(packed, "frame", split_axis=0, concat_axis=0, tiled=True)


def mm(a, b, ca, cb):
    return lax.dot_general(a, b, (((ca,), (cb,)), ((), ())), preferred_element_type=f32)


def exact(a, b, ca, cb):
    return lax.dot_general(
        a, b, (((ca,), (cb,)), ((), ())), preferred_element_type=f32, precision=EXACT
    )


def split(a):
    high = a.astype(bf16)
    return high, (a - high.astype(f32)).astype(bf16)


def head_map(heads, width):
    size = width // heads
    own = lax.broadcasted_iota(jnp.int32, (heads, width), 0)
    lane = lax.broadcasted_iota(jnp.int32, (heads, width), 1)
    return jnp.where(lane // size == own, 1.0, 0.0).astype(bf16)


def sequence_mask(length, sites):
    later = lax.broadcasted_iota(jnp.int32, (length, length), 0)
    earlier = lax.broadcasted_iota(jnp.int32, (length, length), 1)
    keep = later >= earlier
    if sites > 1:
        keep = keep & (later % sites == earlier % sites)
    return jnp.where(keep, 1.0, 0.0).astype(f32)


def blocks(width):
    return [(j, slice(j * LANES, (j + 1) * LANES)) for j in range(width // LANES)]


def spread_rows(rows, length):
    count = rows.shape[0]
    if count == 1:
        return rows
    part = (length // count, rows.shape[1])
    return jnp.concatenate([jnp.broadcast_to(rows[c : c + 1], part) for c in range(count)], axis=0)


def normalize_into(tok_ref, shift_ref, gain_ref, x_ref, read=None):
    length, width = tok_ref.shape
    total = jnp.zeros((length, LANES), f32)
    for _, sl in blocks(width):
        if read is None:
            v = tok_ref[:, sl].astype(f32)
        else:
            v = read(sl)
            tok_ref[:, sl] = v.astype(bf16)
        total = total + v * v
    mean = jnp.sum(total, axis=1, keepdims=True) / width
    inverse = lax.rsqrt(mean + norm_eps)
    for _, sl in blocks(width):
        unit = tok_ref[:, sl].astype(f32) * inverse
        gain = spread_rows(gain_ref[:, sl], length)
        shift = spread_rows(shift_ref[:, sl], length)
        x_ref[:, sl] = (unit * (1.0 + gain) + shift).astype(bf16)
    return inverse


def steps_of(logits, bias, rate, mask):
    z = logits.astype(f32) + bias
    step = jnp.maximum(z, 0.0) + jnp.log1p(jnp.exp(-jnp.abs(z)))
    log_decay = -step * rate
    parts, mask = thirds_of(log_decay), tripled(mask, 1)
    cum = mm(mask, parts, 1, 0)
    return z, step, cum, (cum * LOG2E, mm(parts, mask, 0, 1) * LOG2E)


def thirds_of(a):
    high, rest = split(a)
    high_rest = a - high.astype(f32)
    return jnp.concatenate([high, rest, (high_rest - rest.astype(f32)).astype(bf16)], axis=0)


def tripled(mask, axis):
    return jnp.concatenate([mask.astype(bf16)] * 3, axis=axis)


def halves_of(a):
    return jnp.concatenate(split(a), axis=1)


def doubled(lanes_of):
    return jnp.concatenate([lanes_of, lanes_of], axis=0)


def scan_block(j, x, grad, step_wide, scores, cums, heads, width, d_scores):
    size = width // heads
    per_block = LANES // size
    length = x.shape[0]
    stepped = (x.astype(f32) * step_wide).astype(bf16)
    lane = lax.broadcasted_iota(jnp.int32, x.shape, 1)
    inside = [lane // size == i for i in range(per_block)]
    zero = jnp.zeros_like(x)
    steppeds = jnp.concatenate([jnp.where(own, stepped, zero) for own in inside], axis=0)
    grads = jnp.concatenate([jnp.where(own, grad, zero) for own in inside], axis=0)
    d_weights = mm(grads, stepped, 1, 1)
    weights = []
    for i in range(per_block):
        h = j * per_block + i
        decay = jnp.exp2(jnp.minimum(cums[0][:, h : h + 1] - cums[1][h : h + 1, :], 0.0))
        d_scores = d_scores + d_weights[i * length : (i + 1) * length] * decay
        weights.append((scores * decay).astype(bf16))
    out = mm(jnp.concatenate(weights, axis=1), steppeds, 1, 0)
    d_stepped = mm(jnp.concatenate(weights, axis=0), grads, 0, 0)
    return stepped, out, d_stepped, d_scores


def put(sums_ref, which, sl, value):
    length = value.shape[0]
    sums_ref[which * length : (which + 1) * length, sl] = value.astype(bf16)


def head_sums(sums_ref, lanes_of, length):
    sums = mm(sums_ref[...], lanes_of, 1, 1)
    return [sums[at : at + length] for at in range(0, sums.shape[0], length)]


def wide_blocks(width):
    return [(slice(at, at + 2 * LANES)) for at in range(0, width, 2 * LANES)]


def start_kernel(ids_ref, tok_ref, grad_ref, proj_hbm, step_hbm, mod_hbm, active_ref, sent_ref, pay_ref,
                 proj_ref, step_ref, mod_ref, sems):
    pairs = [(proj_hbm, proj_ref), (step_hbm, step_ref), (mod_hbm, mod_ref)]
    pairs += [(tok_ref, sent_ref.at[:, 0]), (grad_ref, sent_ref.at[:, 1])]
    copies = [
        pltpu.make_async_copy(src, dst, sems.at[n]) for n, (src, dst) in enumerate(pairs)
    ]
    for copy in copies:
        copy.start()
    row = ids_ref[1]
    part, pair = proj_ref.shape[0] // 2, proj_ref.shape[1]
    copies[0].wait()
    own = proj_ref[pl.ds(pl.multiple_of(row * part, part), part), :]
    at = 0
    for _, sl in blocks(pair):
        pay_ref[at : at + part, :] = own[:, sl]
        at += part
    copies[1].wait()
    part = step_ref.shape[0] // 2
    pay_ref[at : at + part, :] = step_ref[pl.ds(pl.multiple_of(row * part, part), part), :]
    at += part
    copies[2].wait()
    own = mm(active_ref[...], mod_ref[...], 1, 0)
    high = own.astype(bf16).astype(f32)
    pieces = [piece[:, sl] for piece in (high, own - high) for _, sl in blocks(own.shape[1])]
    pieces.append(jnp.zeros((8 - len(pieces), LANES), f32))
    pay_ref[at : at + 8, :] = jnp.concatenate(pieces, axis=0).astype(bf16)
    copies[3].wait()
    copies[4].wait()


def unpack_kernel(radix, ids_ref, *refs):
    own_refs, other_refs = refs[:radix], refs[radix : 2 * radix]
    proj_ref, step_ref, shift_ref, gain_ref = refs[2 * radix :]
    me, row = ids_ref[0], ids_ref[1]
    width, pair = proj_ref.shape
    frames = radix * radix
    depth = width // frames
    part, heads = depth // 2, step_ref.shape[0] // 2
    cols = 2 * width // frames
    for i in range(frames):
        source = jnp.bitwise_xor(me, (i % radix) * radix + i // radix)
        near, far = i // radix, i % radix
        for ref, half in ((own_refs[near], row), (other_refs[near], 1 - row)):
            rows = pl.ds(pl.multiple_of(source * depth + half * part, part), part)
            at = 0
            for _, sl in blocks(pair):
                proj_ref[rows, sl] = ref[far, at : at + part, :]
                at += part
            rows = pl.ds(pl.multiple_of(half * heads, heads), heads)
            lanes = pl.ds(pl.multiple_of(source * depth, depth), depth)
            step_ref[rows, lanes] = ref[far, at : at + heads, :]
            at += heads
        own = own_refs[near][far, at : at + 8, :].astype(f32)
        count = cols // LANES
        lanes_at = jnp.bitwise_and(source, frames // 2 - 1) * cols
        for k in range(count):
            value = own[k : k + 1, :] + own[count + k : count + k + 1, :]
            lanes = pl.ds(pl.multiple_of(lanes_at + k * LANES, LANES), LANES)

            @pl.when(source < frames // 2)
            def _():
                shift_ref[:, lanes] = value

            @pl.when(source >= frames // 2)
            def _():
                gain_ref[:, lanes] = value


def finish_mod_kernel(factor, at, sums_ref, active_ref, mod_ref):
    rest = jnp.zeros((7, active_ref.shape[1]), f32)
    active = jnp.concatenate([active_ref[...].astype(f32), rest], axis=0)
    for k, sl in blocks(mod_ref.shape[1]):
        own = jnp.broadcast_to(sums_ref[at + k : at + k + 1, :] * factor, (8, LANES))
        mod_ref[:, sl] = exact(active, own, 0, 0)


def finish_kernel(factor, ids_ref, own_ref, other_ref, proj_ref, step_ref):
    row = ids_ref[1]
    pair = proj_ref.shape[1]
    part, heads = proj_ref.shape[0] // 2, step_ref.shape[0] // 2
    for ref, half in ((own_ref, row), (other_ref, 1 - row)):
        rows = pl.ds(pl.multiple_of(half * part, part), part)
        at = 0
        for _, sl in blocks(pair):
            proj_ref[rows, sl] = ref[at : at + part, :] * factor
            at += part
        step_ref[pl.ds(pl.multiple_of(half * heads, heads), heads), :] = ref[at : at + heads, :] * factor


def site_fast_kernel(sites, got_ref, *refs):
    inputs, (small_ref, sent_hbm, x_hbm, gmod_hbm, dc_ref, dl_ref) = refs[:4], refs[4:10]
    inputs = (*inputs, small_ref[0:1, :], small_ref[1:2, :])
    tok_ref, sent_ref, x_ref, gmod_ref, sems = refs[10:15]
    scratch = refs[15:]
    frames, width = got_ref.shape[0], got_ref.shape[3]

    def read(which):
        return lambda sl: got_ref[:, which, :, sl].astype(f32).reshape(frames * sites, LANES)

    class Grad:
        def __getitem__(self, at):
            return read(1)(at[1]).astype(bf16)

    parts = 8
    share = width // parts
    copies = []

    def begin(source, target):
        copy = pltpu.make_async_copy(source, target, sems.at[len(copies)])
        copy.start()
        copies.append(copy)

    def send(which, p):
        at = (slice(None), which, slice(None), slice(p * share, (p + 1) * share))
        begin(sent_ref.at[at], sent_hbm.at[at])

    class Packed:
        def __init__(self, which):
            self.which = which

        def __setitem__(self, at, value):
            if not copies:
                begin(x_ref, x_hbm)
            value = value.astype(f32).reshape(frames, sites, value.shape[1])
            sent_ref[:, self.which, :, at[1]] = value.astype(bf16)
            if at[1].stop % share == 0:
                send(self.which, at[1].stop // share - 1)

    site_kernel(
        sites,
        tok_ref,
        Grad(),
        *inputs,
        Packed(0),
        Packed(1),
        dc_ref,
        dl_ref,
        gmod_ref,
        x_ref,
        *scratch,
        read=read(0),
    )
    begin(gmod_ref, gmod_hbm)
    for copy in copies:
        copy.wait()


def site_kernel(
    sites,
    tok_ref,
    grad_ref,
    shift_ref,
    gain_ref,
    proj_ref,
    step_ref,
    bias_ref,
    rate_ref,
    out_ref,
    back_ref,
    gproj_ref,
    gstep_ref,
    gmod_ref,
    x_ref,
    dn_ref,
    sums_ref,
    read=None,
):
    length, width = tok_ref.shape
    heads = step_ref.shape[0]
    state = proj_ref.shape[1] // 2
    clips = shift_ref.shape[0]
    inverse = normalize_into(tok_ref, shift_ref, gain_ref, x_ref, read)
    lanes_of = head_map(heads, width)
    mask = sequence_mask(length, sites)
    coeffs = mm(x_ref[...], proj_ref[...], 1, 0).astype(bf16)
    logits = mm(x_ref[...], step_ref[...], 1, 1).astype(bf16)
    rate = rate_ref[...]
    z, step, _, cums = steps_of(logits, bias_ref[...], rate, mask)
    b_part, c_part = coeffs[:, :state], coeffs[:, state:]
    scores = mm(c_part, b_part, 1, 1) * (mask / state)
    step_parts, twice = halves_of(step), doubled(lanes_of)
    d_scores = jnp.zeros((length, length), f32)
    for j, sl in blocks(width):
        x, grad = x_ref[:, sl], grad_ref[:, sl]
        step_wide = mm(step_parts, twice[:, sl], 1, 0)
        stepped, out, d_stepped, d_scores = scan_block(
            j, x, grad, step_wide, scores, cums, heads, width, d_scores
        )
        out_ref[:, sl] = out.astype(bf16)
        dn_ref[:, sl] = (step_wide * d_stepped).astype(bf16)
        put(sums_ref, 0, sl, grad.astype(f32) * out - stepped.astype(f32) * d_stepped)
        put(sums_ref, 1, sl, x.astype(f32) * d_stepped)
    d_cum, d_step = head_sums(sums_ref, lanes_of, length)
    d_log = mm(tripled(mask, 0), thirds_of(d_cum), 0, 0)
    d_logits = (jax.nn.sigmoid(z) * (d_step - rate * d_log)).astype(bf16)
    d_scores = (d_scores * (mask / state)).astype(bf16)
    d_coeffs = jnp.concatenate(
        [mm(d_scores, c_part, 0, 0), mm(d_scores, b_part, 1, 0)], axis=1
    ).astype(bf16)
    clip = lax.broadcasted_iota(jnp.int32, (8, length), 1) // (length // clips)
    clip_row = lax.broadcasted_iota(jnp.int32, (8, length), 0)
    pick = jnp.where(clip == clip_row, 1.0, 0.0).astype(bf16)
    for sl in wide_blocks(width):
        back = (
            dn_ref[:, sl].astype(f32)
            + mm(d_coeffs, proj_ref[sl, :], 1, 1)
            + mm(d_logits, step_ref[:, sl], 1, 0)
        )
        low = back.astype(bf16)
        back_ref[:, sl] = low
        scaled = (back * (tok_ref[:, sl].astype(f32) * inverse)).astype(bf16)
        gmod_ref[0:clips, sl] = mm(pick, low, 1, 0)[0:clips]
        gmod_ref[clips : 2 * clips, sl] = mm(pick, scaled, 1, 0)[0:clips]
        if gproj_ref.shape == (width, 2 * state):
            gproj_ref[sl, :] = mm(x_ref[:, sl], d_coeffs, 0, 0)
            gstep_ref[:, sl] = mm(d_logits, x_ref[:, sl], 0, 0)
    if gproj_ref.shape != (width, 2 * state):
        gproj_ref[...] = d_coeffs
        gstep_ref[...] = d_logits


def band_fast_kernel(ids_ref, *refs):
    small_ref, give_ref = refs[6], refs[-1]
    inputs = (*refs[:6], small_ref[0:1, :], small_ref[2:3, :])
    band_kernel(*inputs, *refs[7:-1], None, None, give_ref, first=ids_ref[1] == 0)


def band_kernel(
    tok_ref,
    grad_ref,
    shift_ref,
    gain_ref,
    proj_ref,
    step_ref,
    bias_ref,
    rate_ref,
    x_ref,
    coeffs_ref,
    logits_ref,
    inverse_ref,
    decay_ref,
    end_ref,
    own_ref,
    first=None,
):
    length, width = tok_ref.shape
    heads = step_ref.shape[0]
    state = proj_ref.shape[1] // 2
    inverse_ref[...] = normalize_into(tok_ref, shift_ref, gain_ref, x_ref)
    twice = doubled(head_map(heads, width))
    mask = sequence_mask(length, 1)
    coeffs = mm(x_ref[...], proj_ref[...], 1, 0).astype(bf16)
    logits = mm(x_ref[...], step_ref[...], 1, 1).astype(bf16)
    coeffs_ref[...] = coeffs
    logits_ref[...] = logits
    _, step, cum, _ = steps_of(logits, bias_ref[...], rate_ref[...], mask)
    last = cum[length - 1 : length, :]
    b_part, c_part = coeffs[:, :state], coeffs[:, state:]
    if first is not None:
        gain = halves_of(jnp.where(first, jnp.exp(last - cum) * step, jnp.exp(cum) / state))
        other = jnp.where(first, b_part, c_part)
        for _, sl in blocks(width):
            value = jnp.where(first, x_ref[:, sl], grad_ref[:, sl]).astype(f32)
            value = (value * mm(gain, twice[:, sl], 1, 0)).astype(bf16)
            own_ref[sl, :] = mm(value, other, 0, 0).astype(bf16)
        return
    decay_ref[...] = jnp.exp(last)
    lead = halves_of(jnp.exp(last - cum) * step)
    reach = halves_of(jnp.exp(cum) / state)
    for _, sl in blocks(width):
        lead_wide = mm(lead, twice[:, sl], 1, 0)
        reach_wide = mm(reach, twice[:, sl], 1, 0)
        scaled = (x_ref[:, sl].astype(f32) * lead_wide).astype(bf16)
        faded = (grad_ref[:, sl].astype(f32) * reach_wide).astype(bf16)
        end_ref[sl, :] = mm(scaled, b_part, 0, 0).astype(bf16)
        own_ref[sl, :] = mm(faded, c_part, 0, 0).astype(bf16)


def terms_kernel(radix, ids_ref, x_ref, dc_ref, dl_ref, gmod_ref, site_x, site_dc, site_dl, site_gmod, *refs):
    me, first = ids_ref[0], ids_ref[1] == 0
    width = x_ref.shape[1]
    coeffs = jnp.concatenate([dc_ref[...], site_dc[...]], axis=0)
    logits = jnp.concatenate([dl_ref[...], site_dl[...]], axis=0)
    share = 2 * width // LANES // (radix * radix)
    half = radix * radix // 2

    def put_halves(keep_ref, give_ref, e, at, value):
        part = value.shape[0] // 2
        own = jnp.where(first, value[:part], value[part:]).astype(bf16)
        other = jnp.where(first, value[part:], value[:part]).astype(bf16)
        for _, sl in blocks(value.shape[1]):
            keep_ref[e, at : at + part, :] = own[:, sl]
            give_ref[e, at : at + part, :] = other[:, sl]
            at += part
        return at

    for d in (*range(1, radix), 0):
        keep_ref, give_ref = refs[d], refs[radix + d]
        for e in range(radix):
            frame = jnp.bitwise_xor(me, e * radix + d)
            sl = pl.ds(pl.multiple_of(frame * LANES, LANES), LANES)
            tall = jnp.concatenate([x_ref[:, sl], site_x[:, sl]], axis=0)
            at = put_halves(keep_ref, give_ref, e, 0, mm(tall, coeffs, 0, 0))
            at = put_halves(keep_ref, give_ref, e, at, mm(logits, tall, 0, 0))
            start = jnp.bitwise_and(frame, half - 1) * share * LANES
            rows = []
            for k in range(share):
                lanes = pl.ds(pl.multiple_of(start + k * LANES, LANES), LANES)
                both = gmod_ref[:, lanes] + site_gmod[:, lanes]
                rows.append(jnp.where(frame < half, both[0:1], both[1:2]))
            rows.append(jnp.zeros((8 - len(rows), LANES), f32))
            rows = jnp.concatenate(rows, axis=0).astype(bf16)
            keep_ref[e, at : at + 8, :] = rows
            give_ref[e, at : at + 8, :] = rows


def space_fast_kernel(ids_ref, arrived_ref, *refs):
    inputs, small_ref, outs = refs[:8], refs[8], refs[9:]
    inputs = (*inputs, *(small_ref[n : n + 1, :] for n in (0, 2, 3)))
    space_kernel(*inputs, arrived_ref, None, None, None, *outs, first=ids_ref[1] == 0)


def space_kernel(
    tok_ref,
    grad_ref,
    x_ref,
    coeffs_ref,
    logits_ref,
    inverse_ref,
    proj_ref,
    step_ref,
    bias_ref,
    rate_ref,
    skip_ref,
    state_ref,
    later_ref,
    gproj_in,
    gstep_in,
    mix_ref,
    pre_ref,
    gproj_ref,
    gstep_ref,
    gmod_ref,
    dn_ref,
    sums_ref,
    first=None,
):
    length, width = tok_ref.shape
    heads = step_ref.shape[0]
    state = proj_ref.shape[1] // 2
    lanes_of = head_map(heads, width)
    twice = doubled(lanes_of)
    mask = sequence_mask(length, 1)
    coeffs = coeffs_ref[...]
    rate = rate_ref[...]
    z, step, cum, cums = steps_of(logits_ref[...], bias_ref[...], rate, mask)
    last = cum[length - 1 : length, :]
    rest = jnp.exp(last - cum)
    lead, reach = rest * step, jnp.exp(cum) / state
    b_part, c_part = coeffs[:, :state], coeffs[:, state:]
    scores = mm(c_part, b_part, 1, 1) * (mask / state)
    skip = jnp.broadcast_to(skip_ref[...], (8, heads))
    if first is None:
        parts = [step, lead, reach, skip]
    else:
        parts = [step, jnp.where(first, lead, reach), skip]
        chosen = jnp.where(first, b_part, c_part)
        is_first = jnp.where(first, 1.0, 0.0).astype(f32)
        is_second = 1.0 - is_first
    parts = jnp.concatenate([halves_of(part) for part in parts], axis=0)
    d_scores = jnp.zeros((length, length), f32)
    d_b = jnp.zeros((length, state), f32)
    d_c = jnp.zeros((length, state), f32)
    d_end = jnp.zeros((heads, state), f32)
    for j, sl in blocks(width):
        x, grad = x_ref[:, sl], grad_ref[:, sl]
        wide_parts = mm(parts, twice[:, sl], 1, 0)
        step_wide, lead_wide = wide_parts[:length], wide_parts[length : 2 * length]
        skip = wide_parts[-8:-7]
        stepped, out, d_stepped, d_scores = scan_block(
            j, x, grad, step_wide, scores, cums, heads, width, d_scores
        )
        if first is None:
            x, wide = x.astype(f32), grad.astype(f32)
            reach_wide = wide_parts[2 * length : 3 * length]
            before, later = state_ref[sl, :], later_ref[sl, :]
            total = out + mm(c_part, before, 1, 1) * reach_wide
            d_c = d_c + mm((wide * reach_wide).astype(bf16), before, 1, 0)
            d_b = d_b + mm((x * lead_wide).astype(bf16), later, 1, 0)
            d_scaled = mm(b_part, later, 1, 1)
            d_x = step_wide * d_stepped + d_scaled * lead_wide
            both = split(before.astype(f32) * later.astype(f32))
            d_end = d_end + mm(lanes_of[:, sl], both[0], 1, 0) + mm(lanes_of[:, sl], both[1], 1, 0)
        else:
            arrived = state_ref[sl, :]
            value = jnp.where(first, x, grad).astype(f32)
            d_b = d_b + mm((value * lead_wide).astype(bf16), arrived, 1, 0)
            x, wide = x.astype(f32), grad.astype(f32)
            d_scaled = mm(chosen, arrived, 1, 1)
            carried = d_scaled * lead_wide
            total = out + carried * is_second
            d_x = step_wide * d_stepped + carried * is_first
            d_scaled = d_scaled * is_first
        mix_ref[:, sl] = total + skip * x
        dn_ref[:, sl] = d_x.astype(bf16) + (wide * skip).astype(bf16)
        put(sums_ref, 0, sl, wide * total - stepped.astype(f32) * d_stepped)
        put(sums_ref, 1, sl, x * d_stepped)
        put(sums_ref, 2, sl, x * d_scaled)
    d_cum, d_step, d_lead = head_sums(sums_ref, lanes_of, length)
    d_step = d_step + d_lead * rest
    fall = d_lead * lead
    d_cum = d_cum - fall
    end_sum = jnp.sum(fall, axis=0, keepdims=True)
    if first is None:
        ones = jnp.ones((8, state), f32)
        end_sum = end_sum + exact(ones, d_end, 1, 1)[0:1, :] * jnp.exp(last)
    else:
        d_b, d_c = d_b * is_first, d_b * is_second
    d_log = mm(tripled(mask, 0), thirds_of(d_cum), 0, 0) + end_sum
    d_logits = (jax.nn.sigmoid(z) * (d_step - rate * d_log)).astype(bf16)
    d_scores = (d_scores * (mask / state)).astype(bf16)
    d_coeffs = jnp.concatenate(
        [mm(d_scores, c_part, 0, 0) + d_b, mm(d_scores, b_part, 1, 0) + d_c], axis=1
    ).astype(bf16)
    inverse = inverse_ref[...]
    if gproj_in is None:
        gproj_ref[...] = d_coeffs
        gstep_ref[...] = d_logits
    for sl in wide_blocks(width):
        pre = (
            dn_ref[:, sl].astype(f32)
            + mm(d_coeffs, proj_ref[sl, :], 1, 1)
            + mm(d_logits, step_ref[:, sl], 1, 0)
        )
        pre_ref[:, sl] = pre
        scaled = pre * (tok_ref[:, sl].astype(f32) * inverse)
        gmod_ref[0:1, sl] = jnp.sum(pre, axis=0, keepdims=True)
        gmod_ref[1:2, sl] = jnp.sum(scaled, axis=0, keepdims=True)
        if gproj_in is not None:
            gproj_ref[sl, :] = (gproj_in[sl, :] + mm(x_ref[:, sl], d_coeffs, 0, 0)).astype(bf16)
            gstep_ref[:, sl] = (gstep_in[:, sl] + mm(d_logits, x_ref[:, sl], 0, 0)).astype(bf16)


def last_kernel(tok_ref, inverse_ref, gain_ref, mix_ref, pre_ref, time_ref, back_ref, out_ref, dtok_ref):
    length, width = tok_ref.shape
    inverse = inverse_ref[...]
    total = jnp.zeros((length, LANES), f32)
    for _, sl in blocks(width):
        out_ref[:, sl] = (mix_ref[:, sl] + time_ref[:, sl].astype(f32)).astype(bf16)
        grad = (pre_ref[:, sl] + back_ref[:, sl].astype(f32)) * (1.0 + gain_ref[:, sl])
        total = total + grad * tok_ref[:, sl].astype(f32)
    inner = jnp.sum(total, axis=1, keepdims=True) / width
    inner = inner * inverse * inverse * inverse
    for _, sl in blocks(width):
        grad = (pre_ref[:, sl] + back_ref[:, sl].astype(f32)) * (1.0 + gain_ref[:, sl])
        dtok_ref[:, sl] = (grad * inverse - tok_ref[:, sl].astype(f32) * inner).astype(bf16)


def last_fast_kernel(tok_ref, inverse_ref, gain_ref, mix_ref, pre_ref, came_ref, *outs):
    class Packed:
        def __init__(self, which):
            self.which = which

        def __getitem__(self, at):
            value = came_ref[:, self.which, :, at[1]].astype(f32)
            return value.reshape(value.shape[0] * value.shape[1], LANES)

    last_kernel(tok_ref, inverse_ref, gain_ref, mix_ref, pre_ref, Packed(0), Packed(1), *outs)


def in_hbm(array):
    return pltpu.with_memory_space_constraint(array, pltpu.MemorySpace.HBM)


def call(kernel, outs, scratch=(), specs=None, hbm_outs=()):
    shapes = [
        pltpu.MemorySpace.HBM(s, d) if n in hbm_outs else jax.ShapeDtypeStruct(s, d)
        for n, (s, d) in enumerate(outs)
    ]
    where = {"s": pltpu.SMEM, "v": pltpu.VMEM, "h": pltpu.MemorySpace.HBM}
    spaces = {}
    if specs:
        spaces["in_specs"] = [pl.BlockSpec(memory_space=where[c]) for c in specs]
        spaces["out_specs"] = [
            pl.BlockSpec(memory_space=where["h" if n in hbm_outs else "v"]) for n in range(len(outs))
        ]
    return pl.pallas_call(
        kernel,
        out_shape=shapes,
        **spaces,
        scratch_shapes=[pltpu.VMEM(*s) if isinstance(s, tuple) else s for s in scratch],
        compiler_params=pltpu.CompilerParams(vmem_limit_bytes=24 << 20),
    )


def rows_in_order(part):
    if lax.axis_size("row") != 2:
        return lax.all_gather(part, "row")
    other = lax.ppermute(part, "row", [(0, 1), (1, 0)])
    first = lax.axis_index("row") == 0
    return jnp.stack([jnp.where(first, part, other), jnp.where(first, other, part)])


def rows_sum(part):
    if lax.axis_size("row") != 2:
        return lax.psum(part, "row")
    return part + lax.ppermute(part, "row", [(0, 1), (1, 0)])


def chain(own, decay, forward):
    count = lax.axis_size("row")
    hops = [(i, i + 1) if forward else (i + 1, i) for i in range(count - 1)]
    if count == 1:
        return jnp.zeros_like(own)
    arrived = lax.ppermute(own, "row", hops)
    wide = jnp.repeat(decay[0], own.shape[0] // decay.shape[1])[:, None]
    for _ in range(count - 2):
        passed = wide * arrived.astype(f32) + own.astype(f32)
        arrived = lax.ppermute(passed.astype(bf16), "row", hops)
    return arrived


def per_device(
    tokens,
    cotangent,
    timestep,
    mod_weight,
    proj_weight,
    step_weight,
    step_bias,
    rate_space,
    rate_time,
    skip_gain,
):
    frames = lax.axis_size("frame")
    rows = lax.axis_size("row")
    frame_id = lax.axis_index("frame")
    row_id = lax.axis_index("row")
    width = tokens.shape[-1]
    length = tokens.shape[1] * tokens.shape[2]
    clips = timestep.shape[0]
    clip_id = frame_id // (frames // clips)
    sites = length // frames
    heads = rate_space.shape[0]
    depth, pair = proj_weight.shape
    state = pair // 2
    mod_cols = mod_weight.shape[1]
    factor = (frames * rows * length) ** (-0.5)
    tok = tokens.reshape(length, width)
    grad = cotangent.reshape(length, width)

    activated = time_embed(timestep, mod_weight.shape[0]).astype(bf16)
    own_mod = jnp.dot(activated, mod_weight, preferred_element_type=f32)
    high = lax.reduce_precision(own_mod, 8, 7)
    own_mod = jnp.stack([high, own_mod - high]).astype(bf16)

    part = depth // rows
    own_proj = lax.dynamic_slice_in_dim(proj_weight, row_id * part, part, 0)
    to_all = [
        to_tiles(own_proj[None]),
        to_tiles(step_weight.T[None]),
        own_mod.reshape(1, -1, LANES),
    ]
    to_all = jnp.concatenate(to_all, axis=1)
    to_all = jnp.pad(to_all, ((0, 0), (0, -to_all.shape[1] % 8), (0, 0)))
    count = sites * width // LANES
    got = exchange(
        jnp.concatenate(
            [
                to_tiles(tok.reshape(frames, sites, width)),
                to_tiles(grad.reshape(frames, sites, width)),
                jnp.broadcast_to(to_all, (frames,) + to_all.shape[1:]),
            ],
            axis=1,
        )
    )
    site_tok = from_tiles(got[:, :count], sites, width).reshape(length, width)
    site_grad = from_tiles(got[:, count : 2 * count], sites, width).reshape(length, width)
    at = 2 * count
    size = part * pair // LANES
    proj_full = rows_in_order(got[:, at : at + size])
    proj_full = from_tiles(proj_full.reshape(rows * frames, size, LANES), part, pair)
    proj_full = proj_full.reshape(rows, frames, part, pair).transpose(1, 0, 2, 3)
    proj_full = proj_full.reshape(width, pair)
    at += size
    size = heads * depth // LANES
    step_full = from_tiles(got[:, at : at + size], heads, depth)
    step_full = step_full.transpose(1, 0, 2).reshape(heads, width)
    at += size
    size = 2 * clips * mod_cols // LANES
    mod_full = got[:, at : at + size].reshape(frames, 2, clips, mod_cols).astype(f32)
    mod_full = (mod_full[:, 0] + mod_full[:, 1]).transpose(1, 0, 2).reshape(clips, 2 * width)
    shift, gain = mod_full[:, :width], mod_full[:, width:]

    bias = step_bias[None]
    wide = (length, width)
    site_out, site_back, gproj, gstep, site_gmod = call(
        functools.partial(site_kernel, sites),
        [(wide, bf16), (wide, bf16), ((width, pair), f32), ((heads, width), f32), ((2 * clips, width), f32)],
        [(wide, bf16)] * 2 + [((2 * length, width), bf16)],
    )(site_tok, site_grad, shift, gain, proj_full, step_full, bias, rate_time[None])

    came = exchange(
        jnp.concatenate(
            [
                to_tiles(site_out.reshape(frames, sites, width)),
                to_tiles(site_back.reshape(frames, sites, width)),
            ],
            axis=1,
        )
    )
    time_out = from_tiles(came[:, :count], sites, width).reshape(length, width)
    time_back = from_tiles(came[:, count:], sites, width).reshape(length, width)

    own_shift = lax.dynamic_slice_in_dim(shift, clip_id, 1, 0)
    own_gain = lax.dynamic_slice_in_dim(gain, clip_id, 1, 0)
    normed, coeffs, logits, inverse, decay, end_own, start_grad = call(
        band_kernel,
        [
            (wide, bf16),
            ((length, pair), bf16),
            ((length, heads), bf16),
            ((length, 1), f32),
            ((1, heads), f32),
            ((width, state), bf16),
            ((width, state), bf16),
        ],
    )(tok, grad, own_shift, own_gain, proj_full, step_full, bias, rate_space[None])
    state_in = chain(end_own, decay, True)
    later_grad = chain(start_grad, decay, False)
    mix, pre, gproj, gstep, gmod = call(
        space_kernel,
        [(wide, f32), (wide, f32), ((width, pair), bf16), ((heads, width), bf16), ((2, width), f32)],
        [(wide, bf16), ((3 * length, width), bf16)],
    )(
        tok,
        grad,
        normed,
        coeffs,
        logits,
        inverse,
        proj_full,
        step_full,
        bias,
        rate_space[None],
        skip_gain[None],
        state_in,
        later_grad,
        gproj,
        gstep,
    )

    picked = (jnp.arange(clips) == clip_id).astype(f32)[:, None]
    gmod = jnp.concatenate(
        [site_gmod[:clips] + picked * gmod[0:1], site_gmod[clips:] + picked * gmod[1:2]], axis=1
    )
    gmod = gmod.reshape(clips, frames, mod_cols).transpose(1, 0, 2).astype(bf16)
    sent = jnp.concatenate(
        [
            to_tiles(gproj.reshape(frames, depth, pair)),
            to_tiles(gstep.reshape(heads, frames, depth).transpose(1, 0, 2)),
            gmod.reshape(frames, -1, LANES) if (clips * mod_cols) % LANES == 0 else gmod,
        ],
        axis=1,
    )
    size = sent.shape[1]
    sent = jnp.pad(sent, ((0, 0), (0, -size % 8), (0, 0)))
    sums = jnp.sum(exchange(sent).astype(f32), axis=0, keepdims=True)
    sums = rows_sum(sums) * factor
    at = depth * pair // LANES
    grad_proj = from_tiles(sums[:, :at], depth, pair)[0]
    size = heads * depth // LANES
    grad_step = from_tiles(sums[:, at : at + size], heads, depth)[0].T
    at += size
    size = clips * mod_cols // LANES
    mod_sum = sums[0, at : at + size].reshape(clips, mod_cols)
    grad_mod = jnp.dot(activated.astype(f32).T, mod_sum, precision=EXACT)

    mixed, d_tokens = call(last_kernel, [(wide, bf16), (wide, bf16)])(
        tok, inverse, own_gain, mix, pre, time_out, time_back
    )
    return (mixed.reshape(tokens.shape), d_tokens.reshape(tokens.shape), grad_proj, grad_step, grad_mod)


def fits(mesh, tokens, timestep, proj_weight, step_weight):
    frames, rows = mesh.shape["frame"], mesh.shape["row"]
    length, width = tokens.shape[2] * tokens.shape[1] // rows, tokens.shape[3]
    return (
        rows == 2
        and frames == 16
        and timestep.shape[0] == 1
        and length == LANES
        and length // frames == 8
        and width // frames == LANES
        and proj_weight.shape[1] == 2 * LANES
        and step_weight.shape[1] % 32 == 0
    )


def spread_over_frames(own, radix=4):
    frames = radix * radix

    def others(piece, stride):
        return [piece] + [
            lax.ppermute(piece, "frame", [(i, i ^ (d * stride)) for i in range(frames)])
            for d in range(1, radix)
        ]

    far = jnp.stack(others(own, radix))
    return others(far, 1)


def sum_over_frames(keep, given, radix, ahead):
    frames = radix * radix

    def total(pieces):
        value = pieces[0].astype(f32)
        for piece in pieces[1:]:
            value = value + piece.astype(f32)
        return value

    def partner(piece, offset):
        return lax.ppermute(piece, "frame", [(i, i ^ offset) for i in range(frames)])

    near = [total([keep[d], given[d]]).astype(bf16) for d in range(radix)]
    near = [near[0]] + [partner(near[d], d) for d in range(1, radix)]
    near, ahead = lax.optimization_barrier((near, ahead))
    near = total(near).astype(bf16)
    far = [near[0]] + [partner(near[d], d * radix) for d in range(1, radix)]
    return total(far), *ahead


def per_device_fast(
    tokens,
    cotangent,
    timestep,
    mod_weight,
    proj_weight,
    step_weight,
    step_bias,
    rate_space,
    rate_time,
    skip_gain,
):
    frames = lax.axis_size("frame")
    rows = lax.axis_size("row")
    ids = jnp.stack([lax.axis_index("frame"), lax.axis_index("row")]).astype(jnp.int32)
    width = tokens.shape[-1]
    length = tokens.shape[1] * tokens.shape[2]
    sites = length // frames
    heads = rate_space.shape[0]
    depth, pair = proj_weight.shape
    state = pair // 2
    mod_cols = mod_weight.shape[1]
    factor = (frames * rows * length) ** (-0.5)
    tok = tokens.reshape(length, width)
    grad = cotangent.reshape(length, width)
    wide = (length, width)
    small = jnp.stack([step_bias, rate_time, rate_space, skip_gain])
    swap = [(0, 1), (1, 0)]

    packed = (frames, 2, sites, width)
    size = depth // 2 * pair // LANES + heads // 2 + 8
    activated = time_embed(timestep, mod_weight.shape[0]).astype(bf16)
    sent, payload = call(
        start_kernel,
        [(packed, bf16), ((size, LANES), bf16)],
        [
            ((depth, pair), bf16),
            ((heads, depth), bf16),
            (mod_weight.shape, bf16),
            pltpu.SemaphoreType.DMA((5,)),
        ],
        specs="shhhhhv",
    )(
        ids,
        in_hbm(tok.reshape(frames, sites, width)),
        in_hbm(grad.reshape(frames, sites, width)),
        in_hbm(proj_weight),
        in_hbm(step_weight.T),
        in_hbm(mod_weight),
        activated,
    )
    got = exchange(sent)
    payload = spread_over_frames(payload)
    other = [lax.ppermute(piece, "row", swap) for piece in payload]
    proj_full, step_full, shift, gain = call(
        functools.partial(unpack_kernel, 4),
        [((width, pair), bf16), ((heads, width), bf16), ((1, width), f32), ((1, width), f32)],
        specs="s" + "v" * 8,
    )(ids, *payload, *other)

    sent, site_x, site_gmod, site_dc, site_dl = call(
        functools.partial(site_fast_kernel, sites),
        [
            (packed, bf16),
            (wide, bf16),
            ((2, width), f32),
            ((length, pair), bf16),
            ((length, heads), bf16),
        ],
        [
            (wide, bf16),
            (packed, bf16),
            (wide, bf16),
            ((2, width), f32),
            pltpu.SemaphoreType.DMA((18,)),
        ]
        + [(wide, bf16), ((2 * length, width), bf16)],
        specs="vvvvvv",
        hbm_outs=(0, 1, 2),
    )(got, shift, gain, proj_full, step_full, small)
    sent, proj_full = lax.optimization_barrier((sent, proj_full))
    came = exchange(sent)

    normed, coeffs, logits, inverse, give = call(
        band_fast_kernel,
        [
            (wide, bf16),
            ((length, pair), bf16),
            ((length, heads), bf16),
            ((length, 1), f32),
            ((width, state), bf16),
        ],
        specs="svvvvvvv",
    )(ids, tok, grad, shift, gain, proj_full, step_full, small)
    arrived = lax.ppermute(give, "row", swap)

    mix, pre, own_dc, own_dl, gmod = call(
        space_fast_kernel,
        [(wide, f32), (wide, f32), ((length, pair), bf16), ((length, heads), bf16), ((2, width), f32)],
        [(wide, bf16), ((3 * length, width), bf16)],
        specs="s" + "v" * 10,
    )(
        ids,
        arrived,
        tok,
        grad,
        normed,
        coeffs,
        logits,
        inverse,
        proj_full,
        step_full,
        small,
    )
    pieces = call(
        functools.partial(terms_kernel, 4), [((4, size, LANES), bf16)] * 8, specs="svvvvvvvv"
    )(ids, normed, own_dc, own_dl, gmod, site_x, site_dc, site_dl, site_gmod)
    keep, given = pieces[:4], [lax.ppermute(piece, "row", swap) for piece in pieces[4:]]
    mixed, d_tokens = call(last_fast_kernel, [(wide, bf16), (wide, bf16)])(
        tok, inverse, gain, mix, pre, came
    )
    terms, mixed, d_tokens = sum_over_frames(keep, given, 4, (mixed, d_tokens))
    other = lax.ppermute(terms, "row", swap)
    (grad_mod,) = call(
        functools.partial(finish_mod_kernel, factor, size - 8),
        [((mod_weight.shape[0], mod_cols), f32)],
        specs="vv",
    )(terms, activated)
    other, grad_mod = lax.optimization_barrier((other, grad_mod))
    grad_proj, grad_step = call(
        functools.partial(finish_kernel, factor),
        [((depth, pair), f32), ((heads, depth), f32)],
        specs="svv",
    )(ids, terms, other)
    return (mixed.reshape(tokens.shape), d_tokens.reshape(tokens.shape), grad_proj, grad_step.T, grad_mod)


def solution(mesh):
    placed = (
        P("frame", "row", None, None),
        P("frame", "row", None, None),
        P(),
        P(None, "frame"),
        P("frame", None),
        P("frame", None),
        P(),
        P(),
        P(),
        P(),
    )
    outs = (
        P("frame", "row", None, None),
        P("frame", "row", None, None),
        P("frame", None),
        P("frame", None),
        P(None, "frame"),
    )

    def step(tokens, cotangent, timestep, mod_weight, proj_weight, step_weight, *rest):
        fast = fits(mesh, tokens, timestep, proj_weight, step_weight)
        body = per_device_fast if fast else per_device
        return jax.shard_map(
            body, mesh=mesh, in_specs=placed, out_specs=outs, check_vma=False
        )(tokens, cotangent, timestep, mod_weight, proj_weight, step_weight, *rest)

    return step
```

```python
import functools
import math

import jax
import jax.numpy as jnp
from jax import lax
from jax.experimental import pallas as pl
from jax.experimental.pallas import tpu as pltpu
from jax.sharding import PartitionSpec as P


norm_eps = 1e-05
LANES = 128
LOG2E = math.log2(math.e)
f32 = jnp.float32
bf16 = jnp.bfloat16
EXACT = lax.Precision.HIGHEST


def time_embed(timestep, embed_dim):
    half_dim = embed_dim // 2
    place = (jnp.arange(embed_dim) % half_dim).astype(f32)
    frequency = jnp.exp(-math.log(10000.0) * place / half_dim)
    angles = timestep.astype(f32)[:, None] * frequency[None, :]
    lower = jnp.arange(embed_dim)[None, :] < half_dim
    return jax.nn.silu(jnp.where(lower, jnp.cos(angles), jnp.sin(angles)))


def to_tiles(a):
    f, r, c = a.shape
    if r % 8 == 0 and c % LANES == 0:
        a = a.reshape(f, r // 8, 8, c // LANES, LANES).transpose(0, 1, 3, 2, 4)
    return a.reshape(f, r * c // LANES, LANES)


def from_tiles(a, r, c):
    f = a.shape[0]
    if r % 8 == 0 and c % LANES == 0:
        a = a.reshape(f, r // 8, c // LANES, 8, LANES).transpose(0, 1, 3, 2, 4)
    return a.reshape(f, r, c)


def exchange(packed):
    return lax.all_to_all(packed, "frame", split_axis=0, concat_axis=0, tiled=True)


def mm(a, b, ca, cb):
    return lax.dot_general(a, b, (((ca,), (cb,)), ((), ())), preferred_element_type=f32)


def exact(a, b, ca, cb):
    return lax.dot_general(
        a, b, (((ca,), (cb,)), ((), ())), preferred_element_type=f32, precision=EXACT
    )


def split(a):
    high = a.astype(bf16)
    return high, (a - high.astype(f32)).astype(bf16)


def head_map(heads, width):
    size = width // heads
    own = lax.broadcasted_iota(jnp.int32, (heads, width), 0)
    lane = lax.broadcasted_iota(jnp.int32, (heads, width), 1)
    return jnp.where(lane // size == own, 1.0, 0.0).astype(bf16)


def sequence_mask(length, sites):
    later = lax.broadcasted_iota(jnp.int32, (length, length), 0)
    earlier = lax.broadcasted_iota(jnp.int32, (length, length), 1)
    keep = later >= earlier
    if sites > 1:
        keep = keep & (later % sites == earlier % sites)
    return jnp.where(keep, 1.0, 0.0).astype(f32)


def blocks(width):
    return [(j, slice(j * LANES, (j + 1) * LANES)) for j in range(width // LANES)]


def spread_rows(rows, length):
    count = rows.shape[0]
    if count == 1:
        return rows
    part = (length // count, rows.shape[1])
    return jnp.concatenate([jnp.broadcast_to(rows[c : c + 1], part) for c in range(count)], axis=0)


def normalize_into(tok_ref, shift_ref, gain_ref, x_ref, read=None):
    length, width = tok_ref.shape
    total = jnp.zeros((length, LANES), f32)
    for _, sl in blocks(width):
        if read is None:
            v = tok_ref[:, sl].astype(f32)
        else:
            v = read(sl)
            tok_ref[:, sl] = v.astype(bf16)
        total = total + v * v
    mean = jnp.sum(total, axis=1, keepdims=True) / width
    inverse = lax.rsqrt(mean + norm_eps)
    for _, sl in blocks(width):
        unit = tok_ref[:, sl].astype(f32) * inverse
        gain = spread_rows(gain_ref[:, sl], length)
        shift = spread_rows(shift_ref[:, sl], length)
        x_ref[:, sl] = (unit * (1.0 + gain) + shift).astype(bf16)
    return inverse


def steps_of(logits, bias, rate, mask):
    z = logits.astype(f32) + bias
    step = jnp.maximum(z, 0.0) + jnp.log1p(jnp.exp(-jnp.abs(z)))
    log_decay = -step * rate
    parts, mask = thirds_of(log_decay), tripled(mask, 1)
    cum = mm(mask, parts, 1, 0)
    return z, step, cum, (cum * LOG2E, mm(parts, mask, 0, 1) * LOG2E)


def thirds_of(a):
    high, rest = split(a)
    high_rest = a - high.astype(f32)
    return jnp.concatenate([high, rest, (high_rest - rest.astype(f32)).astype(bf16)], axis=0)


def tripled(mask, axis):
    return jnp.concatenate([mask.astype(bf16)] * 3, axis=axis)


def halves_of(a):
    return jnp.concatenate(split(a), axis=1)


def doubled(lanes_of):
    return jnp.concatenate([lanes_of, lanes_of], axis=0)


def scan_block(j, x, grad, step_wide, scores, cums, heads, width, d_scores):
    size = width // heads
    per_block = LANES // size
    length = x.shape[0]
    stepped = (x.astype(f32) * step_wide).astype(bf16)
    lane = lax.broadcasted_iota(jnp.int32, x.shape, 1)
    inside = [lane // size == i for i in range(per_block)]
    zero = jnp.zeros_like(x)
    steppeds = jnp.concatenate([jnp.where(own, stepped, zero) for own in inside], axis=0)
    grads = jnp.concatenate([jnp.where(own, grad, zero) for own in inside], axis=0)
    d_weights = mm(grads, stepped, 1, 1)
    weights = []
    low_scores = scores.astype(bf16)
    for i in range(per_block):
        h = j * per_block + i
        decay = jnp.exp2(jnp.minimum(cums[0][:, h : h + 1] - cums[1][h : h + 1, :], 0.0))
        d_scores = d_scores + d_weights[i * length : (i + 1) * length] * decay
        weights.append(low_scores * decay.astype(bf16))
    out = mm(jnp.concatenate(weights, axis=1), steppeds, 1, 0)
    d_stepped = mm(jnp.concatenate(weights, axis=0), grads, 0, 0)
    return stepped, out, d_stepped, d_scores


def put(sums_ref, which, sl, value):
    length = value.shape[0]
    sums_ref[which * length : (which + 1) * length, sl] = value.astype(bf16)


def head_sums(sums_ref, lanes_of, length):
    sums = mm(sums_ref[...], lanes_of, 1, 1)
    return [sums[at : at + length] for at in range(0, sums.shape[0], length)]


def wide_blocks(width):
    return [(slice(at, at + 2 * LANES)) for at in range(0, width, 2 * LANES)]


def start_kernel(ids_ref, tok_ref, grad_ref, proj_hbm, step_hbm, mod_hbm, active_ref, sent_ref, pay_ref,
                 proj_ref, step_ref, mod_ref, sems):
    pairs = [(proj_hbm, proj_ref), (step_hbm, step_ref), (mod_hbm, mod_ref)]
    pairs += [(tok_ref, sent_ref.at[:, 0]), (grad_ref, sent_ref.at[:, 1])]
    copies = [
        pltpu.make_async_copy(src, dst, sems.at[n]) for n, (src, dst) in enumerate(pairs)
    ]
    for copy in copies:
        copy.start()
    row = ids_ref[1]
    part, pair = proj_ref.shape[0] // 2, proj_ref.shape[1]
    copies[0].wait()
    own = proj_ref[pl.ds(pl.multiple_of(row * part, part), part), :]
    at = 0
    for _, sl in blocks(pair):
        pay_ref[at : at + part, :] = own[:, sl]
        at += part
    copies[1].wait()
    part = step_ref.shape[0] // 2
    pay_ref[at : at + part, :] = step_ref[pl.ds(pl.multiple_of(row * part, part), part), :]
    at += part
    copies[2].wait()
    own = mm(active_ref[...], mod_ref[...], 1, 0)
    high = own.astype(bf16).astype(f32)
    pieces = [piece[:, sl] for piece in (high, own - high) for _, sl in blocks(own.shape[1])]
    pieces.append(jnp.zeros((8 - len(pieces), LANES), f32))
    pay_ref[at : at + 8, :] = jnp.concatenate(pieces, axis=0).astype(bf16)
    copies[3].wait()
    copies[4].wait()


def unpack_kernel(radix, ids_ref, *refs):
    own_refs, other_refs = refs[:radix], refs[radix : 2 * radix]
    proj_ref, step_ref, shift_ref, gain_ref = refs[2 * radix :]
    me, row = ids_ref[0], ids_ref[1]
    width, pair = proj_ref.shape
    frames = radix * radix
    depth = width // frames
    part, heads = depth // 2, step_ref.shape[0] // 2
    cols = 2 * width // frames
    for i in range(frames):
        source = jnp.bitwise_xor(me, (i % radix) * radix + i // radix)
        near, far = i // radix, i % radix
        for ref, half in ((own_refs[near], row), (other_refs[near], 1 - row)):
            rows = pl.ds(pl.multiple_of(source * depth + half * part, part), part)
            at = 0
            for _, sl in blocks(pair):
                proj_ref[rows, sl] = ref[far, at : at + part, :]
                at += part
            rows = pl.ds(pl.multiple_of(half * heads, heads), heads)
            lanes = pl.ds(pl.multiple_of(source * depth, depth), depth)
            step_ref[rows, lanes] = ref[far, at : at + heads, :]
            at += heads
        own = own_refs[near][far, at : at + 8, :].astype(f32)
        count = cols // LANES
        lanes_at = jnp.bitwise_and(source, frames // 2 - 1) * cols
        for k in range(count):
            value = own[k : k + 1, :] + own[count + k : count + k + 1, :]
            lanes = pl.ds(pl.multiple_of(lanes_at + k * LANES, LANES), LANES)

            @pl.when(source < frames // 2)
            def _():
                shift_ref[:, lanes] = value

            @pl.when(source >= frames // 2)
            def _():
                gain_ref[:, lanes] = value


def finish_mod_kernel(factor, at, sums_ref, active_ref, mod_ref):
    rest = jnp.zeros((7, active_ref.shape[1]), f32)
    active = jnp.concatenate([active_ref[...].astype(f32), rest], axis=0)
    for k, sl in blocks(mod_ref.shape[1]):
        own = jnp.broadcast_to(sums_ref[at + k : at + k + 1, :] * factor, (8, LANES))
        mod_ref[:, sl] = exact(active, own, 0, 0)


def finish_kernel(factor, ids_ref, own_ref, other_ref, proj_ref, step_ref):
    row = ids_ref[1]
    pair = proj_ref.shape[1]
    part, heads = proj_ref.shape[0] // 2, step_ref.shape[0] // 2
    for ref, half in ((own_ref, row), (other_ref, 1 - row)):
        rows = pl.ds(pl.multiple_of(half * part, part), part)
        at = 0
        for _, sl in blocks(pair):
            proj_ref[rows, sl] = ref[at : at + part, :] * factor
            at += part
        step_ref[pl.ds(pl.multiple_of(half * heads, heads), heads), :] = ref[at : at + heads, :] * factor


def site_fast_kernel(sites, got_ref, *refs):
    inputs, (small_ref, sent_hbm, x_hbm, gmod_hbm, dc_ref, dl_ref) = refs[:4], refs[4:10]
    inputs = (*inputs, small_ref[0:1, :], small_ref[1:2, :])
    tok_ref, sent_ref, x_ref, gmod_ref, sems = refs[10:15]
    scratch = refs[15:]
    frames, width = got_ref.shape[0], got_ref.shape[3]

    def read(which):
        return lambda sl: got_ref[:, which, :, sl].astype(f32).reshape(frames * sites, LANES)

    class Grad:
        def __getitem__(self, at):
            return read(1)(at[1]).astype(bf16)

    parts = 8
    share = width // parts
    copies = []

    def begin(source, target):
        copy = pltpu.make_async_copy(source, target, sems.at[len(copies)])
        copy.start()
        copies.append(copy)

    def send(which, p):
        at = (slice(None), which, slice(None), slice(p * share, (p + 1) * share))
        begin(sent_ref.at[at], sent_hbm.at[at])

    class Packed:
        def __init__(self, which):
            self.which = which

        def __setitem__(self, at, value):
            if not copies:
                begin(x_ref, x_hbm)
            value = value.astype(f32).reshape(frames, sites, value.shape[1])
            sent_ref[:, self.which, :, at[1]] = value.astype(bf16)
            if at[1].stop % share == 0:
                send(self.which, at[1].stop // share - 1)

    site_kernel(
        sites,
        tok_ref,
        Grad(),
        *inputs,
        Packed(0),
        Packed(1),
        dc_ref,
        dl_ref,
        gmod_ref,
        x_ref,
        *scratch,
        read=read(0),
    )
    begin(gmod_ref, gmod_hbm)
    for copy in copies:
        copy.wait()


def site_kernel(
    sites,
    tok_ref,
    grad_ref,
    shift_ref,
    gain_ref,
    proj_ref,
    step_ref,
    bias_ref,
    rate_ref,
    out_ref,
    back_ref,
    gproj_ref,
    gstep_ref,
    gmod_ref,
    x_ref,
    dn_ref,
    sums_ref,
    read=None,
):
    length, width = tok_ref.shape
    heads = step_ref.shape[0]
    state = proj_ref.shape[1] // 2
    clips = shift_ref.shape[0]
    inverse = normalize_into(tok_ref, shift_ref, gain_ref, x_ref, read)
    lanes_of = head_map(heads, width)
    mask = sequence_mask(length, sites)
    coeffs = mm(x_ref[...], proj_ref[...], 1, 0).astype(bf16)
    logits = mm(x_ref[...], step_ref[...], 1, 1).astype(bf16)
    rate = rate_ref[...]
    z, step, _, cums = steps_of(logits, bias_ref[...], rate, mask)
    b_part, c_part = coeffs[:, :state], coeffs[:, state:]
    scores = mm(c_part, b_part, 1, 1) * (mask / state)
    step_parts, twice = halves_of(step), doubled(lanes_of)
    d_scores = jnp.zeros((length, length), f32)
    for j, sl in blocks(width):
        x, grad = x_ref[:, sl], grad_ref[:, sl]
        step_wide = mm(step_parts, twice[:, sl], 1, 0)
        stepped, out, d_stepped, d_scores = scan_block(
            j, x, grad, step_wide, scores, cums, heads, width, d_scores
        )
        out_ref[:, sl] = out.astype(bf16)
        dn_ref[:, sl] = (step_wide * d_stepped).astype(bf16)
        put(sums_ref, 0, sl, grad.astype(f32) * out - stepped.astype(f32) * d_stepped)
        put(sums_ref, 1, sl, x.astype(f32) * d_stepped)
    d_cum, d_step = head_sums(sums_ref, lanes_of, length)
    d_log = mm(tripled(mask, 0), thirds_of(d_cum), 0, 0)
    d_logits = (jax.nn.sigmoid(z) * (d_step - rate * d_log)).astype(bf16)
    d_scores = (d_scores * (mask / state)).astype(bf16)
    d_coeffs = jnp.concatenate(
        [mm(d_scores, c_part, 0, 0), mm(d_scores, b_part, 1, 0)], axis=1
    ).astype(bf16)
    for sl in wide_blocks(width):
        back = (
            dn_ref[:, sl].astype(f32)
            + mm(d_coeffs, proj_ref[sl, :], 1, 1)
            + mm(d_logits, step_ref[:, sl], 1, 0)
        )
        back_ref[:, sl] = back.astype(bf16)
        scaled = back * (tok_ref[:, sl].astype(f32) * inverse)
        for c in range(clips):
            rows = slice(c * (length // clips), (c + 1) * (length // clips))
            gmod_ref[c : c + 1, sl] = jnp.sum(back[rows], axis=0, keepdims=True)
            gmod_ref[clips + c : clips + c + 1, sl] = jnp.sum(scaled[rows], axis=0, keepdims=True)
        if gproj_ref.shape == (width, 2 * state):
            gproj_ref[sl, :] = mm(x_ref[:, sl], d_coeffs, 0, 0)
            gstep_ref[:, sl] = mm(d_logits, x_ref[:, sl], 0, 0)
    if gproj_ref.shape != (width, 2 * state):
        gproj_ref[...] = d_coeffs
        gstep_ref[...] = d_logits


def band_fast_kernel(ids_ref, *refs):
    small_ref, give_ref = refs[6], refs[-1]
    inputs = (*refs[:6], small_ref[0:1, :], small_ref[2:3, :])
    band_kernel(*inputs, *refs[7:-1], None, None, give_ref, first=ids_ref[1] == 0)


def band_kernel(
    tok_ref,
    grad_ref,
    shift_ref,
    gain_ref,
    proj_ref,
    step_ref,
    bias_ref,
    rate_ref,
    x_ref,
    coeffs_ref,
    logits_ref,
    inverse_ref,
    decay_ref,
    end_ref,
    own_ref,
    first=None,
):
    length, width = tok_ref.shape
    heads = step_ref.shape[0]
    state = proj_ref.shape[1] // 2
    inverse_ref[...] = normalize_into(tok_ref, shift_ref, gain_ref, x_ref)
    twice = doubled(head_map(heads, width))
    mask = sequence_mask(length, 1)
    coeffs = mm(x_ref[...], proj_ref[...], 1, 0).astype(bf16)
    logits = mm(x_ref[...], step_ref[...], 1, 1).astype(bf16)
    coeffs_ref[...] = coeffs
    logits_ref[...] = logits
    _, step, cum, _ = steps_of(logits, bias_ref[...], rate_ref[...], mask)
    last = cum[length - 1 : length, :]
    b_part, c_part = coeffs[:, :state], coeffs[:, state:]
    if first is not None:
        gain = halves_of(jnp.where(first, jnp.exp(last - cum) * step, jnp.exp(cum) / state))
        other = jnp.where(first, b_part, c_part)
        for _, sl in blocks(width):
            value = jnp.where(first, x_ref[:, sl], grad_ref[:, sl]).astype(f32)
            value = (value * mm(gain, twice[:, sl], 1, 0)).astype(bf16)
            own_ref[sl, :] = mm(value, other, 0, 0).astype(bf16)
        return
    decay_ref[...] = jnp.exp(last)
    lead = halves_of(jnp.exp(last - cum) * step)
    reach = halves_of(jnp.exp(cum) / state)
    for _, sl in blocks(width):
        lead_wide = mm(lead, twice[:, sl], 1, 0)
        reach_wide = mm(reach, twice[:, sl], 1, 0)
        scaled = (x_ref[:, sl].astype(f32) * lead_wide).astype(bf16)
        faded = (grad_ref[:, sl].astype(f32) * reach_wide).astype(bf16)
        end_ref[sl, :] = mm(scaled, b_part, 0, 0).astype(bf16)
        own_ref[sl, :] = mm(faded, c_part, 0, 0).astype(bf16)


def terms_kernel(radix, ids_ref, x_ref, dc_ref, dl_ref, gmod_ref, site_x, site_dc, site_dl, site_gmod, *refs):
    me, first = ids_ref[0], ids_ref[1] == 0
    width = x_ref.shape[1]
    coeffs = jnp.concatenate([dc_ref[...], site_dc[...]], axis=0)
    logits = jnp.concatenate([dl_ref[...], site_dl[...]], axis=0)
    share = 2 * width // LANES // (radix * radix)
    half = radix * radix // 2

    def put_halves(keep_ref, give_ref, e, at, value):
        part = value.shape[0] // 2
        own = jnp.where(first, value[:part], value[part:]).astype(bf16)
        other = jnp.where(first, value[part:], value[:part]).astype(bf16)
        for _, sl in blocks(value.shape[1]):
            keep_ref[e, at : at + part, :] = own[:, sl]
            give_ref[e, at : at + part, :] = other[:, sl]
            at += part
        return at

    for d in (*range(1, radix), 0):
        keep_ref, give_ref = refs[d], refs[radix + d]
        for e in range(radix):
            frame = jnp.bitwise_xor(me, e * radix + d)
            sl = pl.ds(pl.multiple_of(frame * LANES, LANES), LANES)
            tall = jnp.concatenate([x_ref[:, sl], site_x[:, sl]], axis=0)
            at = put_halves(keep_ref, give_ref, e, 0, mm(tall, coeffs, 0, 0))
            at = put_halves(keep_ref, give_ref, e, at, mm(logits, tall, 0, 0))
            start = jnp.bitwise_and(frame, half - 1) * share * LANES
            rows = []
            for k in range(share):
                lanes = pl.ds(pl.multiple_of(start + k * LANES, LANES), LANES)
                both = gmod_ref[:, lanes] + site_gmod[:, lanes]
                rows.append(jnp.where(frame < half, both[0:1], both[1:2]))
            rows.append(jnp.zeros((8 - len(rows), LANES), f32))
            rows = jnp.concatenate(rows, axis=0).astype(bf16)
            keep_ref[e, at : at + 8, :] = rows
            give_ref[e, at : at + 8, :] = rows


def space_fast_kernel(ids_ref, arrived_ref, *refs):
    inputs, small_ref, outs = refs[:8], refs[8], refs[9:]
    inputs = (*inputs, *(small_ref[n : n + 1, :] for n in (0, 2, 3)))
    space_kernel(*inputs, arrived_ref, None, None, None, *outs, first=ids_ref[1] == 0)


def space_kernel(
    tok_ref,
    grad_ref,
    x_ref,
    coeffs_ref,
    logits_ref,
    inverse_ref,
    proj_ref,
    step_ref,
    bias_ref,
    rate_ref,
    skip_ref,
    state_ref,
    later_ref,
    gproj_in,
    gstep_in,
    mix_ref,
    pre_ref,
    gproj_ref,
    gstep_ref,
    gmod_ref,
    dn_ref,
    sums_ref,
    first=None,
):
    length, width = tok_ref.shape
    heads = step_ref.shape[0]
    state = proj_ref.shape[1] // 2
    lanes_of = head_map(heads, width)
    twice = doubled(lanes_of)
    mask = sequence_mask(length, 1)
    coeffs = coeffs_ref[...]
    rate = rate_ref[...]
    z, step, cum, cums = steps_of(logits_ref[...], bias_ref[...], rate, mask)
    last = cum[length - 1 : length, :]
    rest = jnp.exp(last - cum)
    lead, reach = rest * step, jnp.exp(cum) / state
    b_part, c_part = coeffs[:, :state], coeffs[:, state:]
    scores = mm(c_part, b_part, 1, 1) * (mask / state)
    skip = jnp.broadcast_to(skip_ref[...], (8, heads))
    if first is None:
        parts = [step, lead, reach, skip]
    else:
        parts = [step, jnp.where(first, lead, reach), skip]
        chosen = jnp.where(first, b_part, c_part)
        is_first = jnp.where(first, 1.0, 0.0).astype(f32)
        is_second = 1.0 - is_first
    parts = jnp.concatenate([halves_of(part) for part in parts], axis=0)
    d_scores = jnp.zeros((length, length), f32)
    d_b = jnp.zeros((length, state), f32)
    d_c = jnp.zeros((length, state), f32)
    d_end = jnp.zeros((heads, state), f32)
    for j, sl in blocks(width):
        x, grad = x_ref[:, sl], grad_ref[:, sl]
        wide_parts = mm(parts, twice[:, sl], 1, 0)
        step_wide, lead_wide = wide_parts[:length], wide_parts[length : 2 * length]
        skip = wide_parts[-8:-7]
        stepped, out, d_stepped, d_scores = scan_block(
            j, x, grad, step_wide, scores, cums, heads, width, d_scores
        )
        if first is None:
            x, wide = x.astype(f32), grad.astype(f32)
            reach_wide = wide_parts[2 * length : 3 * length]
            before, later = state_ref[sl, :], later_ref[sl, :]
            total = out + mm(c_part, before, 1, 1) * reach_wide
            d_c = d_c + mm((wide * reach_wide).astype(bf16), before, 1, 0)
            d_b = d_b + mm((x * lead_wide).astype(bf16), later, 1, 0)
            d_scaled = mm(b_part, later, 1, 1)
            d_x = step_wide * d_stepped + d_scaled * lead_wide
            both = split(before.astype(f32) * later.astype(f32))
            d_end = d_end + mm(lanes_of[:, sl], both[0], 1, 0) + mm(lanes_of[:, sl], both[1], 1, 0)
        else:
            arrived = state_ref[sl, :]
            value = jnp.where(first, x, grad).astype(f32)
            d_b = d_b + mm((value * lead_wide).astype(bf16), arrived, 1, 0)
            x, wide = x.astype(f32), grad.astype(f32)
            d_scaled = mm(chosen, arrived, 1, 1)
            carried = d_scaled * lead_wide
            total = out + carried * is_second
            d_x = step_wide * d_stepped + carried * is_first
            d_scaled = d_scaled * is_first
        mix_ref[:, sl] = total + skip * x
        dn_ref[:, sl] = d_x.astype(bf16) + (wide * skip).astype(bf16)
        put(sums_ref, 0, sl, wide * total - stepped.astype(f32) * d_stepped)
        put(sums_ref, 1, sl, x * d_stepped)
        put(sums_ref, 2, sl, x * d_scaled)
    d_cum, d_step, d_lead = head_sums(sums_ref, lanes_of, length)
    d_step = d_step + d_lead * rest
    fall = d_lead * lead
    d_cum = d_cum - fall
    end_sum = jnp.sum(fall, axis=0, keepdims=True)
    if first is None:
        ones = jnp.ones((8, state), f32)
        end_sum = end_sum + exact(ones, d_end, 1, 1)[0:1, :] * jnp.exp(last)
    else:
        d_b, d_c = d_b * is_first, d_b * is_second
    d_log = mm(tripled(mask, 0), thirds_of(d_cum), 0, 0) + end_sum
    d_logits = (jax.nn.sigmoid(z) * (d_step - rate * d_log)).astype(bf16)
    d_scores = (d_scores * (mask / state)).astype(bf16)
    d_coeffs = jnp.concatenate(
        [mm(d_scores, c_part, 0, 0) + d_b, mm(d_scores, b_part, 1, 0) + d_c], axis=1
    ).astype(bf16)
    inverse = inverse_ref[...]
    if gproj_in is None:
        gproj_ref[...] = d_coeffs
        gstep_ref[...] = d_logits
    for sl in wide_blocks(width):
        pre = (
            dn_ref[:, sl].astype(f32)
            + mm(d_coeffs, proj_ref[sl, :], 1, 1)
            + mm(d_logits, step_ref[:, sl], 1, 0)
        )
        pre_ref[:, sl] = pre
        scaled = pre * (tok_ref[:, sl].astype(f32) * inverse)
        gmod_ref[0:1, sl] = jnp.sum(pre, axis=0, keepdims=True)
        gmod_ref[1:2, sl] = jnp.sum(scaled, axis=0, keepdims=True)
        if gproj_in is not None:
            gproj_ref[sl, :] = (gproj_in[sl, :] + mm(x_ref[:, sl], d_coeffs, 0, 0)).astype(bf16)
            gstep_ref[:, sl] = (gstep_in[:, sl] + mm(d_logits, x_ref[:, sl], 0, 0)).astype(bf16)


def last_kernel(tok_ref, inverse_ref, gain_ref, mix_ref, pre_ref, time_ref, back_ref, out_ref, dtok_ref):
    length, width = tok_ref.shape
    inverse = inverse_ref[...]
    total = jnp.zeros((length, LANES), f32)
    for _, sl in blocks(width):
        out_ref[:, sl] = (mix_ref[:, sl] + time_ref[:, sl].astype(f32)).astype(bf16)
        grad = (pre_ref[:, sl] + back_ref[:, sl].astype(f32)) * (1.0 + gain_ref[:, sl])
        total = total + grad * tok_ref[:, sl].astype(f32)
    inner = jnp.sum(total, axis=1, keepdims=True) / width
    inner = inner * inverse * inverse * inverse
    for _, sl in blocks(width):
        grad = (pre_ref[:, sl] + back_ref[:, sl].astype(f32)) * (1.0 + gain_ref[:, sl])
        dtok_ref[:, sl] = (grad * inverse - tok_ref[:, sl].astype(f32) * inner).astype(bf16)


def last_fast_kernel(tok_ref, inverse_ref, gain_ref, mix_ref, pre_ref, came_ref, *outs):
    class Packed:
        def __init__(self, which):
            self.which = which

        def __getitem__(self, at):
            value = came_ref[:, self.which, :, at[1]].astype(f32)
            return value.reshape(value.shape[0] * value.shape[1], LANES)

    last_kernel(tok_ref, inverse_ref, gain_ref, mix_ref, pre_ref, Packed(0), Packed(1), *outs)


def in_hbm(array):
    return pltpu.with_memory_space_constraint(array, pltpu.MemorySpace.HBM)


def call(kernel, outs, scratch=(), specs=None, hbm_outs=()):
    shapes = [
        pltpu.MemorySpace.HBM(s, d) if n in hbm_outs else jax.ShapeDtypeStruct(s, d)
        for n, (s, d) in enumerate(outs)
    ]
    where = {"s": pltpu.SMEM, "v": pltpu.VMEM, "h": pltpu.MemorySpace.HBM}
    spaces = {}
    if specs:
        spaces["in_specs"] = [pl.BlockSpec(memory_space=where[c]) for c in specs]
        spaces["out_specs"] = [
            pl.BlockSpec(memory_space=where["h" if n in hbm_outs else "v"]) for n in range(len(outs))
        ]
    return pl.pallas_call(
        kernel,
        out_shape=shapes,
        **spaces,
        scratch_shapes=[pltpu.VMEM(*s) if isinstance(s, tuple) else s for s in scratch],
        compiler_params=pltpu.CompilerParams(vmem_limit_bytes=24 << 20),
    )


def rows_in_order(part):
    if lax.axis_size("row") != 2:
        return lax.all_gather(part, "row")
    other = lax.ppermute(part, "row", [(0, 1), (1, 0)])
    first = lax.axis_index("row") == 0
    return jnp.stack([jnp.where(first, part, other), jnp.where(first, other, part)])


def rows_sum(part):
    if lax.axis_size("row") != 2:
        return lax.psum(part, "row")
    return part + lax.ppermute(part, "row", [(0, 1), (1, 0)])


def chain(own, decay, forward):
    count = lax.axis_size("row")
    hops = [(i, i + 1) if forward else (i + 1, i) for i in range(count - 1)]
    if count == 1:
        return jnp.zeros_like(own)
    arrived = lax.ppermute(own, "row", hops)
    wide = jnp.repeat(decay[0], own.shape[0] // decay.shape[1])[:, None]
    for _ in range(count - 2):
        passed = wide * arrived.astype(f32) + own.astype(f32)
        arrived = lax.ppermute(passed.astype(bf16), "row", hops)
    return arrived


def per_device(
    tokens,
    cotangent,
    timestep,
    mod_weight,
    proj_weight,
    step_weight,
    step_bias,
    rate_space,
    rate_time,
    skip_gain,
):
    frames = lax.axis_size("frame")
    rows = lax.axis_size("row")
    frame_id = lax.axis_index("frame")
    row_id = lax.axis_index("row")
    width = tokens.shape[-1]
    length = tokens.shape[1] * tokens.shape[2]
    clips = timestep.shape[0]
    clip_id = frame_id // (frames // clips)
    sites = length // frames
    heads = rate_space.shape[0]
    depth, pair = proj_weight.shape
    state = pair // 2
    mod_cols = mod_weight.shape[1]
    factor = (frames * rows * length) ** (-0.5)
    tok = tokens.reshape(length, width)
    grad = cotangent.reshape(length, width)

    activated = time_embed(timestep, mod_weight.shape[0]).astype(bf16)
    own_mod = jnp.dot(activated, mod_weight, preferred_element_type=f32)
    high = lax.reduce_precision(own_mod, 8, 7)
    own_mod = jnp.stack([high, own_mod - high]).astype(bf16)

    part = depth // rows
    own_proj = lax.dynamic_slice_in_dim(proj_weight, row_id * part, part, 0)
    to_all = [
        to_tiles(own_proj[None]),
        to_tiles(step_weight.T[None]),
        own_mod.reshape(1, -1, LANES),
    ]
    to_all = jnp.concatenate(to_all, axis=1)
    to_all = jnp.pad(to_all, ((0, 0), (0, -to_all.shape[1] % 8), (0, 0)))
    count = sites * width // LANES
    got = exchange(
        jnp.concatenate(
            [
                to_tiles(tok.reshape(frames, sites, width)),
                to_tiles(grad.reshape(frames, sites, width)),
                jnp.broadcast_to(to_all, (frames,) + to_all.shape[1:]),
            ],
            axis=1,
        )
    )
    site_tok = from_tiles(got[:, :count], sites, width).reshape(length, width)
    site_grad = from_tiles(got[:, count : 2 * count], sites, width).reshape(length, width)
    at = 2 * count
    size = part * pair // LANES
    proj_full = rows_in_order(got[:, at : at + size])
    proj_full = from_tiles(proj_full.reshape(rows * frames, size, LANES), part, pair)
    proj_full = proj_full.reshape(rows, frames, part, pair).transpose(1, 0, 2, 3)
    proj_full = proj_full.reshape(width, pair)
    at += size
    size = heads * depth // LANES
    step_full = from_tiles(got[:, at : at + size], heads, depth)
    step_full = step_full.transpose(1, 0, 2).reshape(heads, width)
    at += size
    size = 2 * clips * mod_cols // LANES
    mod_full = got[:, at : at + size].reshape(frames, 2, clips, mod_cols).astype(f32)
    mod_full = (mod_full[:, 0] + mod_full[:, 1]).transpose(1, 0, 2).reshape(clips, 2 * width)
    shift, gain = mod_full[:, :width], mod_full[:, width:]

    bias = step_bias[None]
    wide = (length, width)
    site_out, site_back, gproj, gstep, site_gmod = call(
        functools.partial(site_kernel, sites),
        [(wide, bf16), (wide, bf16), ((width, pair), f32), ((heads, width), f32), ((2 * clips, width), f32)],
        [(wide, bf16)] * 2 + [((2 * length, width), bf16)],
    )(site_tok, site_grad, shift, gain, proj_full, step_full, bias, rate_time[None])

    came = exchange(
        jnp.concatenate(
            [
                to_tiles(site_out.reshape(frames, sites, width)),
                to_tiles(site_back.reshape(frames, sites, width)),
            ],
            axis=1,
        )
    )
    time_out = from_tiles(came[:, :count], sites, width).reshape(length, width)
    time_back = from_tiles(came[:, count:], sites, width).reshape(length, width)

    own_shift = lax.dynamic_slice_in_dim(shift, clip_id, 1, 0)
    own_gain = lax.dynamic_slice_in_dim(gain, clip_id, 1, 0)
    normed, coeffs, logits, inverse, decay, end_own, start_grad = call(
        band_kernel,
        [
            (wide, bf16),
            ((length, pair), bf16),
            ((length, heads), bf16),
            ((length, 1), f32),
            ((1, heads), f32),
            ((width, state), bf16),
            ((width, state), bf16),
        ],
    )(tok, grad, own_shift, own_gain, proj_full, step_full, bias, rate_space[None])
    state_in = chain(end_own, decay, True)
    later_grad = chain(start_grad, decay, False)
    mix, pre, gproj, gstep, gmod = call(
        space_kernel,
        [(wide, f32), (wide, f32), ((width, pair), bf16), ((heads, width), bf16), ((2, width), f32)],
        [(wide, bf16), ((3 * length, width), bf16)],
    )(
        tok,
        grad,
        normed,
        coeffs,
        logits,
        inverse,
        proj_full,
        step_full,
        bias,
        rate_space[None],
        skip_gain[None],
        state_in,
        later_grad,
        gproj,
        gstep,
    )

    picked = (jnp.arange(clips) == clip_id).astype(f32)[:, None]
    gmod = jnp.concatenate(
        [site_gmod[:clips] + picked * gmod[0:1], site_gmod[clips:] + picked * gmod[1:2]], axis=1
    )
    gmod = gmod.reshape(clips, frames, mod_cols).transpose(1, 0, 2).astype(bf16)
    sent = jnp.concatenate(
        [
            to_tiles(gproj.reshape(frames, depth, pair)),
            to_tiles(gstep.reshape(heads, frames, depth).transpose(1, 0, 2)),
            gmod.reshape(frames, -1, LANES) if (clips * mod_cols) % LANES == 0 else gmod,
        ],
        axis=1,
    )
    size = sent.shape[1]
    sent = jnp.pad(sent, ((0, 0), (0, -size % 8), (0, 0)))
    sums = jnp.sum(exchange(sent).astype(f32), axis=0, keepdims=True)
    sums = rows_sum(sums) * factor
    at = depth * pair // LANES
    grad_proj = from_tiles(sums[:, :at], depth, pair)[0]
    size = heads * depth // LANES
    grad_step = from_tiles(sums[:, at : at + size], heads, depth)[0].T
    at += size
    size = clips * mod_cols // LANES
    mod_sum = sums[0, at : at + size].reshape(clips, mod_cols)
    grad_mod = jnp.dot(activated.astype(f32).T, mod_sum, precision=EXACT)

    mixed, d_tokens = call(last_kernel, [(wide, bf16), (wide, bf16)])(
        tok, inverse, own_gain, mix, pre, time_out, time_back
    )
    return (mixed.reshape(tokens.shape), d_tokens.reshape(tokens.shape), grad_proj, grad_step, grad_mod)


def fits(mesh, tokens, timestep, proj_weight, step_weight):
    frames, rows = mesh.shape["frame"], mesh.shape["row"]
    length, width = tokens.shape[2] * tokens.shape[1] // rows, tokens.shape[3]
    return (
        rows == 2
        and frames == 16
        and timestep.shape[0] == 1
        and length == LANES
        and length // frames == 8
        and width // frames == LANES
        and proj_weight.shape[1] == 2 * LANES
        and step_weight.shape[1] % 32 == 0
    )


def spread_over_frames(own, radix=4):
    frames = radix * radix

    def others(piece, stride):
        return [piece] + [
            lax.ppermute(piece, "frame", [(i, i ^ (d * stride)) for i in range(frames)])
            for d in range(1, radix)
        ]

    far = jnp.stack(others(own, radix))
    return others(far, 1)


def sum_over_frames(keep, given, radix, ahead):
    frames = radix * radix

    def total(pieces):
        value = pieces[0].astype(f32)
        for piece in pieces[1:]:
            value = value + piece.astype(f32)
        return value

    def partner(piece, offset):
        return lax.ppermute(piece, "frame", [(i, i ^ offset) for i in range(frames)])

    near = [total([keep[d], given[d]]).astype(bf16) for d in range(radix)]
    near = [near[0]] + [partner(near[d], d) for d in range(1, radix)]
    near, ahead = lax.optimization_barrier((near, ahead))
    near = total(near).astype(bf16)
    far = [near[0]] + [partner(near[d], d * radix) for d in range(1, radix)]
    return total(far), *ahead


def per_device_fast(
    tokens,
    cotangent,
    timestep,
    mod_weight,
    proj_weight,
    step_weight,
    step_bias,
    rate_space,
    rate_time,
    skip_gain,
):
    frames = lax.axis_size("frame")
    rows = lax.axis_size("row")
    ids = jnp.stack([lax.axis_index("frame"), lax.axis_index("row")]).astype(jnp.int32)
    width = tokens.shape[-1]
    length = tokens.shape[1] * tokens.shape[2]
    sites = length // frames
    heads = rate_space.shape[0]
    depth, pair = proj_weight.shape
    state = pair // 2
    mod_cols = mod_weight.shape[1]
    factor = (frames * rows * length) ** (-0.5)
    tok = tokens.reshape(length, width)
    grad = cotangent.reshape(length, width)
    wide = (length, width)
    small = jnp.stack([step_bias, rate_time, rate_space, skip_gain])
    swap = [(0, 1), (1, 0)]

    packed = (frames, 2, sites, width)
    size = depth // 2 * pair // LANES + heads // 2 + 8
    activated = time_embed(timestep, mod_weight.shape[0]).astype(bf16)
    sent, payload = call(
        start_kernel,
        [(packed, bf16), ((size, LANES), bf16)],
        [
            ((depth, pair), bf16),
            ((heads, depth), bf16),
            (mod_weight.shape, bf16),
            pltpu.SemaphoreType.DMA((5,)),
        ],
        specs="shhhhhv",
    )(
        ids,
        in_hbm(tok.reshape(frames, sites, width)),
        in_hbm(grad.reshape(frames, sites, width)),
        in_hbm(proj_weight),
        in_hbm(step_weight.T),
        in_hbm(mod_weight),
        activated,
    )
    got = exchange(sent)
    payload = spread_over_frames(payload)
    other = [lax.ppermute(piece, "row", swap) for piece in payload]
    proj_full, step_full, shift, gain = call(
        functools.partial(unpack_kernel, 4),
        [((width, pair), bf16), ((heads, width), bf16), ((1, width), f32), ((1, width), f32)],
        specs="s" + "v" * 8,
    )(ids, *payload, *other)

    sent, site_x, site_gmod, site_dc, site_dl = call(
        functools.partial(site_fast_kernel, sites),
        [
            (packed, bf16),
            (wide, bf16),
            ((2, width), f32),
            ((length, pair), bf16),
            ((length, heads), bf16),
        ],
        [
            (wide, bf16),
            (packed, bf16),
            (wide, bf16),
            ((2, width), f32),
            pltpu.SemaphoreType.DMA((18,)),
        ]
        + [(wide, bf16), ((2 * length, width), bf16)],
        specs="vvvvvv",
        hbm_outs=(0, 1, 2),
    )(got, shift, gain, proj_full, step_full, small)
    sent, proj_full = lax.optimization_barrier((sent, proj_full))
    came = exchange(sent)

    normed, coeffs, logits, inverse, give = call(
        band_fast_kernel,
        [
            (wide, bf16),
            ((length, pair), bf16),
            ((length, heads), bf16),
            ((length, 1), f32),
            ((width, state), bf16),
        ],
        specs="svvvvvvv",
    )(ids, tok, grad, shift, gain, proj_full, step_full, small)
    arrived = lax.ppermute(give, "row", swap)

    mix, pre, own_dc, own_dl, gmod = call(
        space_fast_kernel,
        [(wide, f32), (wide, f32), ((length, pair), bf16), ((length, heads), bf16), ((2, width), f32)],
        [(wide, bf16), ((3 * length, width), bf16)],
        specs="s" + "v" * 10,
    )(
        ids,
        arrived,
        tok,
        grad,
        normed,
        coeffs,
        logits,
        inverse,
        proj_full,
        step_full,
        small,
    )
    pieces = call(
        functools.partial(terms_kernel, 4), [((4, size, LANES), bf16)] * 8, specs="svvvvvvvv"
    )(ids, normed, own_dc, own_dl, gmod, site_x, site_dc, site_dl, site_gmod)
    keep, given = pieces[:4], [lax.ppermute(piece, "row", swap) for piece in pieces[4:]]
    mixed, d_tokens = call(last_fast_kernel, [(wide, bf16), (wide, bf16)])(
        tok, inverse, gain, mix, pre, came
    )
    terms, mixed, d_tokens = sum_over_frames(keep, given, 4, (mixed, d_tokens))
    other = lax.ppermute(terms, "row", swap)
    (grad_mod,) = call(
        functools.partial(finish_mod_kernel, factor, size - 8),
        [((mod_weight.shape[0], mod_cols), f32)],
        specs="vv",
    )(terms, activated)
    other, grad_mod = lax.optimization_barrier((other, grad_mod))
    grad_proj, grad_step = call(
        functools.partial(finish_kernel, factor),
        [((depth, pair), f32), ((heads, depth), f32)],
        specs="svv",
    )(ids, terms, other)
    return (mixed.reshape(tokens.shape), d_tokens.reshape(tokens.shape), grad_proj, grad_step.T, grad_mod)


def solution(mesh):
    placed = (
        P("frame", "row", None, None),
        P("frame", "row", None, None),
        P(),
        P(None, "frame"),
        P("frame", None),
        P("frame", None),
        P(),
        P(),
        P(),
        P(),
    )
    outs = (
        P("frame", "row", None, None),
        P("frame", "row", None, None),
        P("frame", None),
        P("frame", None),
        P(None, "frame"),
    )

    def step(tokens, cotangent, timestep, mod_weight, proj_weight, step_weight, *rest):
        fast = fits(mesh, tokens, timestep, proj_weight, step_weight)
        body = per_device_fast if fast else per_device
        return jax.shard_map(
            body, mesh=mesh, in_specs=placed, out_specs=outs, check_vma=False
        )(tokens, cotangent, timestep, mod_weight, proj_weight, step_weight, *rest)

    return step
```
